32 devices in a mesh: seq: 8 (over z, core), tp: 4 (over y, x).
Axes of the slice: x: 2, y: 2, z: 4, core: 2. Of those that a mesh axis runs over, the one named last changes fastest.
Arguments:
- inputs: bfloat16 [4, 1024, 2048], P('tp', 'seq'), may hold values from -6 to 6
- query_weight: bfloat16 [2048, 2048], P(None, 'tp'), may hold values from -0.125 to 0.125
- key_weight: bfloat16 [2048, 2048], P(None, 'tp'), may hold values from -0.125 to 0.125
- value_weight: bfloat16 [2048, 4096], P(None, 'tp'), may hold values from -0.125 to 0.125
- swish_weight: bfloat16 [2048, 4096], P(None, 'tp'), may hold values from -0.125 to 0.125
- output_weight: bfloat16 [4096, 2048], P('tp'), may hold values from -0.1875 to 0.1875
- gate_weight: bfloat16 [2048, 4096], P(None, 'tp'), may hold values from -0.125 to 0.125
- up_weight: bfloat16 [2048, 4096], P(None, 'tp'), may hold values from -0.125 to 0.125
- down_weight: bfloat16 [4096, 2048], P('tp'), may hold values from -0.09375 to 0.09375
- attn_gain: float32 [2048], replicated, may hold values from 0.1 to 1.9
- attn_bias: float32 [2048], replicated, may hold values from -3 to 3
- mlp_gain: float32 [2048], replicated, may hold values from 0.1 to 1.9
- mlp_bias: float32 [2048], replicated, may hold values from -3 to 3
- output_grad: bfloat16 [4, 1024, 2048], P('tp', 'seq'), may hold values from -6 to 6
Outputs:
- outputs: bfloat16 [4, 1024, 2048], P('tp', 'seq')
- input_grad: bfloat16 [4, 1024, 2048], P('tp', 'seq')
- query_grad: float32 [2048, 2048], P('seq', 'tp')
- key_grad: float32 [2048, 2048], P('seq', 'tp')
- value_grad: float32 [2048, 4096], P('seq', 'tp')
- swish_grad: float32 [2048, 4096], P('seq', 'tp')
- mixer_grad: float32 [4096, 2048], P('tp', 'seq')
- gate_grad: float32 [2048, 4096], P('seq', 'tp')
- up_grad: float32 [2048, 4096], P('seq', 'tp')
- down_grad: float32 [4096, 2048], P('tp', 'seq')
- attngain_grad: float32 [2048], P(('seq', 'tp'))
- attnbias_grad: float32 [2048], P(('seq', 'tp'))
- mlpgain_grad: float32 [2048], P(('seq', 'tp'))
- mlpbias_grad: float32 [2048], P(('seq', 'tp'))
The draws below stay inside these ranges and needn't reach their ends.
All inputs are finite; a program needn't handle non-finite values.
Results may differ from the reference program's by a relative error of at most 0.02.
Values may be sent and summed in bfloat16 or wider, within the bound.
A program may use at most 256 MiB of HBM per device.

```python
import jax
import jax.numpy as jnp
from jax import lax

D = 2048
HEADS = 8
DK = 256
DV = 512
FF = 4096
BLOCK = 128
KEYS = 2048
VALS = 4096
SEQS = 4
LEN = 1024


def steps_of(key, dims, cuts, smallest, high):
    def one(position, blocks):
        draws = jax.random.uniform(jax.random.fold_in(jax.random.fold_in(key, 6), position), (blocks,), jnp.float32, smallest / len(cuts), high / len(cuts))
        return jnp.repeat(jnp.exp(draws), dims[position] // blocks).reshape((-1,) + (1,) * (len(dims) - position - 1))

    level = one(*cuts[0])
    for cut in cuts[1:]:
        level = level * one(*cut)
    return level


def normal_values(stream_key, shape, deviation, most, shards=(), held_as=jnp.bfloat16):
    values = jax.random.normal(stream_key, shape, jnp.float32) * deviation
    if len(shards) > 0:
        values = steps_of(stream_key, shape, shards, -0.22, 0.18) * values
    return jnp.clip(values, min=-most, max=most).astype(held_as)


def setup_inputs(seed: int = 0) -> dict:
    key_list = jax.random.split(jax.random.key(seed), 15)
    return {
        "inputs": normal_values(key_list[0], (SEQS, LEN, D), 1.0, 6.0, ((0, 4), (1, 8))),
        "query_weight": normal_values(key_list[1], (D, KEYS), D ** -0.5, 0.125, ((1, 4),)),
        "key_weight": normal_values(key_list[2], (D, KEYS), D ** -0.5, 0.125, ((1, 4),)),
        "value_weight": normal_values(key_list[3], (D, VALS), D ** -0.5, 0.125, ((1, 4),)),
        "swish_weight": normal_values(key_list[4], (D, VALS), D ** -0.5, 0.125, ((1, 4),)),
        "output_weight": normal_values(key_list[5], (VALS, D), (VALS // 4) ** -0.5, 0.1875, ((0, 4),)),
        "gate_weight": normal_values(key_list[6], (D, FF), D ** -0.5, 0.125, ((1, 4),)),
        "up_weight": normal_values(key_list[7], (D, FF), D ** -0.5, 0.125, ((1, 4),)),
        "down_weight": normal_values(key_list[8], (FF, D), FF ** -0.5, 0.09375, ((0, 4),)),
        "attn_gain": jnp.clip(1.0 + 0.18 * jax.random.normal(key_list[9], (D,), jnp.float32), 0.1, 1.9),
        "attn_bias": normal_values(key_list[10], (D,), 0.5, 3.0, (), jnp.float32),
        "mlp_gain": jnp.clip(1.0 + 0.18 * jax.random.normal(key_list[11], (D,), jnp.float32), 0.1, 1.9),
        "mlp_bias": normal_values(key_list[12], (D,), 0.5, 3.0, (), jnp.float32),
        "output_grad": normal_values(key_list[13], (SEQS, LEN, D), 1.0, 6.0, ((0, 4), (1, 8))),
    }


EPS = 1e-05
HIGHEST_PREC = lax.Precision.HIGHEST

@jax.custom_vjp
def low(v):
    return lax.optimization_barrier(v.astype(jnp.bfloat16)).astype(jnp.float32)

@jax.custom_vjp
def low_back(v):
    return v

def low_keep(v):
    return (low(v), None)

def low_pass(kept, grad):
    return (grad,)

def back_keep(v):
    return (v, None)

def back_low(kept, grad):
    return (low(grad),)
low.defvjp(low_keep, low_pass)
low_back.defvjp(back_keep, back_low)

def layer_norm(values, gain, bias):
    center = values - lax.optimization_barrier(jnp.mean(values, -1, keepdims=True))
    spread = lax.optimization_barrier(jnp.mean(center * center, -1, keepdims=True))
    return center * lax.rsqrt(spread + EPS) * gain + bias

def head_norm(values):
    center = values - lax.optimization_barrier(jnp.mean(values, -1, keepdims=True))
    spread = lax.optimization_barrier(jnp.mean(center * center, -1, keepdims=True))
    return center * lax.rsqrt(spread + EPS)

def rotation(values, angles):
    half_width = values.shape[-1] // 2
    cosine = jnp.cos(angles)
    sine = jnp.sin(angles)
    cosine = jnp.concatenate([cosine, cosine], -1)[:, None, :]
    sine = jnp.concatenate([sine, sine], -1)[:, None, :]
    turned = jnp.concatenate([-values[..., half_width:], values[..., :half_width]], -1)
    return values * cosine + turned * sine

def matmul(left, right):
    return jnp.dot(left, right, precision=HIGHEST_PREC, preferred_element_type=jnp.float32)

def forward(inputs, query_weight, key_weight, value_weight, swish_weight, output_weight, gate_weight, up_weight, down_weight, attn_gain, attn_bias, mlp_gain, mlp_bias):
    seq_count, length, model_width = inputs.shape
    normed_one = low(layer_norm(inputs, attn_gain, attn_bias))
    query = low_back(matmul(normed_one, query_weight)).reshape(seq_count, length, HEADS, DK)
    keys_pre = low_back(matmul(normed_one, key_weight)).reshape(seq_count, length, HEADS, DK)
    value = low(low_back(matmul(normed_one, value_weight))).reshape(seq_count, length, HEADS, DV)
    swish_pre = low_back(matmul(normed_one, swish_weight)).reshape(seq_count, length, HEADS, DV)
    half_width = DK // 2
    frequencies = jnp.power(10000.0, -jnp.arange(half_width, dtype=jnp.float32) / half_width)
    positions = jnp.arange(length, dtype=jnp.float32)
    angles = positions[:, None] * frequencies[None, :]
    query_rot = low(rotation(query, angles))
    key_rot = low(rotation(keys_pre, angles))
    decays = 1.0 - jnp.exp2(-5.0 - jnp.arange(HEADS, dtype=jnp.float32))
    steps_in = jnp.arange(BLOCK, dtype=jnp.float32)
    lag = steps_in[:, None] - steps_in[None, :]
    decay_mat = jnp.where(lag[None] >= 0, jnp.power(decays[:, None, None], jnp.maximum(lag, 0.0)[None]), 0.0)
    query_fac = jnp.power(decays[None, :], steps_in[:, None] + 1.0)
    key_fac = jnp.power(decays[None, :], BLOCK - 1.0 - steps_in[:, None])
    block_fac = jnp.power(decays, BLOCK * 1.0)
    block_count = length // BLOCK

    def to_blocks(values):
        return jnp.moveaxis(values.reshape(seq_count, block_count, BLOCK, HEADS, values.shape[-1]), 1, 0)

    def block_step(state, pieces):
        query_piece, key_piece, value_piece = pieces
        raw = low_back(jnp.einsum('sthk,suhk->shtu', query_piece, key_piece, precision=HIGHEST_PREC))
        scores = low(raw * decay_mat[None])
        intra = jnp.einsum('shtu,suhv->sthv', scores, value_piece, precision=HIGHEST_PREC)
        query_dec = low(query_piece * query_fac[None, :, :, None])
        cross = jnp.einsum('sthk,shkv->sthv', query_dec, low(state), precision=HIGHEST_PREC)
        key_dec = low(key_piece * key_fac[None, :, :, None])
        local_state = low_back(jnp.einsum('suhk,suhv->shkv', key_dec, value_piece, precision=HIGHEST_PREC))
        new_state = block_fac[None, :, None, None] * state + local_state
        return (new_state, low_back(intra + cross))
    initial = jnp.zeros((seq_count, HEADS, DK, DV), jnp.float32)
    _, mixed_blocks = lax.scan(jax.checkpoint(block_step), initial, (to_blocks(query_rot), to_blocks(key_rot), to_blocks(value)))
    mixed = jnp.moveaxis(mixed_blocks, 0, 1).reshape(seq_count, length, HEADS, DV)
    gated = low(jax.nn.silu(swish_pre) * head_norm(mixed)).reshape(seq_count, length, HEADS * DV)
    hidden_res = inputs + low_back(matmul(gated, output_weight))
    normed_two = low(layer_norm(hidden_res, mlp_gain, mlp_bias))
    gate = low_back(matmul(normed_two, gate_weight))
    upper = low_back(matmul(normed_two, up_weight))
    hidden = low(jax.nn.gelu(gate, approximate=True) * upper)
    return hidden_res + low_back(matmul(hidden, down_weight))

def reference(inputs, query_weight, key_weight, value_weight, swish_weight, output_weight, gate_weight, up_weight, down_weight, attn_gain, attn_bias, mlp_gain, mlp_bias, output_grad):
    result, pull = jax.vjp(forward, inputs.astype(jnp.float32), query_weight.astype(jnp.float32), key_weight.astype(jnp.float32), value_weight.astype(jnp.float32), swish_weight.astype(jnp.float32), output_weight.astype(jnp.float32), gate_weight.astype(jnp.float32), up_weight.astype(jnp.float32), down_weight.astype(jnp.float32), attn_gain.astype(jnp.float32), attn_bias.astype(jnp.float32), mlp_gain.astype(jnp.float32), mlp_bias.astype(jnp.float32))
    grads = pull(output_grad.astype(jnp.float32))
    return (result.astype(jnp.bfloat16), grads[0].astype(jnp.bfloat16), grads[1], grads[2], grads[3], grads[4], grads[5], grads[6], grads[7], grads[8], grads[9], grads[10], grads[11], grads[12])
```

```python
import functools

import jax
import jax.numpy as jnp
from jax import lax
from jax.experimental import pallas as pl
from jax.experimental.pallas import tpu as pltpu
from jax.sharding import PartitionSpec as P

DK = 256
DV = 512


EPS = 1e-05
MESH = pl.DeviceIdType.MESH
BF = jnp.bfloat16
F32 = jnp.float32
VMEM_LIMIT = 60 * 1024 * 1024


def remote(src, dst, ssem, rsem, slot, dev):
    return pltpu.make_async_remote_copy(
        src_ref=src,
        dst_ref=dst,
        send_sem=ssem.at[slot],
        recv_sem=rsem.at[slot],
        device_id=dev,
        device_id_type=MESH,
    )


def greet(devs):
    barrier = pltpu.get_barrier_semaphore()
    for dev in devs:
        pl.semaphore_signal(barrier, inc=1, device_id=dev, device_id_type=MESH)
    pl.semaphore_wait(barrier, len(devs))


def params(cid):
    return pltpu.CompilerParams(
        collective_id=cid, has_side_effects=True, vmem_limit_bytes=VMEM_LIMIT
    )


def gather_kernel(n, x_ref, o_ref, ssem, rsem):
    s = lax.axis_index("seq")
    t = lax.axis_index("tp")
    b, length, _ = x_ref.shape
    if n == 4:
        px, py = t + 1 - 2 * (t % 2), (t + 2) % 4
        half = length // 2
        lo, hi = pl.ds(0, half), pl.ds(half, half)
        mine, from_x, from_y = pl.ds(t * b, b), pl.ds(px * b, b), pl.ds(py * b, b)
        dx, dy = (s, px), (s, py)
        greet([dx, dy])
        first = [
            remote(x_ref.at[:, lo], o_ref.at[mine, lo], ssem, rsem, 0, dx),
            remote(x_ref.at[:, hi], o_ref.at[mine, hi], ssem, rsem, 1, dy),
            remote(x_ref.at[:, hi], o_ref.at[mine, hi], ssem, rsem, 2, dx),
            remote(x_ref.at[:, lo], o_ref.at[mine, lo], ssem, rsem, 3, dy),
        ]
        for copy in first:
            copy.start()
        o_ref[mine] = x_ref[...]
        first[0].wait_recv()
        relay_x = remote(o_ref.at[from_x, lo], o_ref.at[from_x, lo], ssem, rsem, 4, dy)
        relay_x.start()
        first[1].wait_recv()
        relay_y = remote(o_ref.at[from_y, hi], o_ref.at[from_y, hi], ssem, rsem, 5, dx)
        relay_y.start()
        first[2].wait_recv()
        first[3].wait_recv()
        relay_x.wait_recv()
        relay_y.wait_recv()
        for copy in first:
            copy.wait_send()
        relay_x.wait_send()
        relay_y.wait_send()
    else:
        peers = [(s, (t + k) % n) for k in range(1, n)]
        greet(peers)
        mine = pl.ds(t * b, b)
        copies = [
            remote(x_ref, o_ref.at[mine], ssem, rsem, k, dev) for k, dev in enumerate(peers)
        ]
        for copy in copies:
            copy.start()
        o_ref[mine] = x_ref[...]
        for copy in copies:
            copy.wait()


def gather_tp(x, cid):
    n = lax.axis_size("tp")
    sems = max(6, n - 1)
    return pl.pallas_call(
        functools.partial(gather_kernel, n),
        out_shape=jax.ShapeDtypeStruct((n * x.shape[0],) + x.shape[1:], x.dtype),
        in_specs=[pl.BlockSpec(memory_space=pltpu.VMEM)],
        out_specs=pl.BlockSpec(memory_space=pltpu.VMEM),
        scratch_shapes=[pltpu.SemaphoreType.DMA((sems,)), pltpu.SemaphoreType.DMA((sems,))],
        compiler_params=params(cid),
        name=f"gather_tp_{cid}",
    )(x)


def scatter_kernel(n, p_ref, o_ref, near, far, hold, ssem, rsem):
    s = lax.axis_index("seq")
    t = lax.axis_index("tp")
    b, _, width = o_ref.shape
    if n == 4:
        px, py, pd = t + 1 - 2 * (t % 2), (t + 2) % 4, 3 - t
        half = width // 2
        cols = (pl.ds(0, half), pl.ds(half, half))
        dx, dy = (s, px), (s, py)
        greet([dx, dy])

        def own(who, side):
            return p_ref.at[pl.ds(who * b, b), :, cols[side]]

        steps = []
        for side, (who, dev) in enumerate(((px, dx), (py, dy))):
            steps.append(remote(own(pd, side), near.at[side, 1], ssem, rsem, 2 * side, dev))
            steps.append(remote(own(who, side), near.at[side, 0], ssem, rsem, 2 * side + 1, dev))
        steps[0].start()
        steps[2].start()
        steps[1].start()
        steps[3].start()
        later = []
        for side, (who, dev) in enumerate(((py, dy), (px, dx))):
            steps[2 * side].wait_recv()
            total = own(who, side)[...].astype(F32) + near[side, 1].astype(F32)
            hold[side] = total.astype(BF)
            copy = remote(hold.at[side], far.at[side], ssem, rsem, 4 + side, dev)
            copy.start()
            later.append(copy)
        for side in range(2):
            steps[2 * side + 1].wait_recv()
            partial = own(t, side)[...].astype(F32) + near[side, 0].astype(F32)
            later[side].wait_recv()
            o_ref[:, :, cols[side]] = partial + far[side].astype(F32)
        for copy in steps + later:
            copy.wait_send()
    else:
        peers = [(s, (t + k) % n) for k in range(1, n)]
        greet(peers)
        copies = [
            remote(p_ref.at[pl.ds(((t + k) % n) * b, b)], near.at[k - 1], ssem, rsem, k - 1, (s, (t + k) % n))
            for k in range(1, n)
        ]
        for copy in copies:
            copy.start()
        total = p_ref[pl.ds(t * b, b)].astype(F32)
        for k, copy in enumerate(copies):
            copy.wait_recv()
            total = total + near[k].astype(F32)
        o_ref[...] = total
        for copy in copies:
            copy.wait_send()


def scatter_tp(parts, cid):
    n = lax.axis_size("tp")
    rows, length, width = parts.shape
    b = rows // n
    sems = max(6, n - 1)
    if n == 4:
        near, far = (2, 2, b, length, width // 2), (2, b, length, width // 2)
    else:
        near, far = (n - 1, b, length, width), (1, b, 16, 128)
    return pl.pallas_call(
        functools.partial(scatter_kernel, n),
        out_shape=jax.ShapeDtypeStruct((b, length, width), F32),
        in_specs=[pl.BlockSpec(memory_space=pltpu.VMEM)],
        out_specs=pl.BlockSpec(memory_space=pltpu.VMEM),
        scratch_shapes=[
            pltpu.VMEM(near, BF),
            pltpu.VMEM(far, BF),
            pltpu.VMEM(far, BF),
            pltpu.SemaphoreType.DMA((sems,)),
            pltpu.SemaphoreType.DMA((sems,)),
        ],
        compiler_params=params(cid),
        name=f"scatter_tp_{cid}",
    )(parts)


def chain_kernel(chips, heads, flip, fac_ref, l_ref, o_ref, pair, enter, leave, ps, pr, zs, zr, bs, br):
    s = lax.axis_index("seq")
    t = lax.axis_index("tp")
    core = s % 2
    chip = s // 2
    pieces = l_ref.shape[0]
    partner = (s + 1 - 2 * core, t)
    if flip:
        first, place, ahead = core == 1, chips - 1 - chip, (s - 2 + 2 * chips) % (2 * chips)
        behind = (s + 2) % (2 * chips)
    else:
        first, place, ahead = core == 0, chip, (s + 2) % (2 * chips)
        behind = (s - 2 + 2 * chips) % (2 * chips)
    last = jnp.logical_not(first)
    barrier = pltpu.get_barrier_semaphore()
    for dev in (partner, (ahead, t), (behind, t)):
        pl.semaphore_signal(barrier, inc=1, device_id=dev, device_id_type=MESH)
    pl.semaphore_wait(barrier, 3)

    def give(p):
        return remote(l_ref.at[p], pair.at[p], ps, pr, p, partner)

    def back(p):
        return remote(enter.at[p], o_ref.at[p], bs, br, p, partner)

    def onward(p):
        return remote(leave.at[p], enter.at[p], zs, zr, p, (ahead, t))

    @pl.when(first)
    def _():
        @pl.loop(0, pieces)
        def _(p):
            give(p).start()

        @pl.when(place == 0)
        def _():
            o_ref[...] = jnp.zeros_like(o_ref)

        @pl.when(place > 0)
        def _():
            @pl.loop(0, pieces)
            def _(p):
                back(p).wait_recv()

        @pl.loop(0, pieces)
        def _(p):
            give(p).wait_send()

    @pl.when(last)
    def _():
        @pl.loop(0, pieces)
        def _(p):
            fac = fac_ref[p % heads]
            give(p).wait_recv()
            early = pair[p].astype(F32)
            chip_sum = early * fac + l_ref[p].astype(F32)

            @pl.when(place == 0)
            def _():
                leave[p] = chip_sum.astype(BF)
                o_ref[p] = pair[p]

            @pl.when(place > 0)
            def _():
                onward(p).wait_recv()
                back(p).start()
                came = enter[p].astype(F32)
                leave[p] = (came * (fac * fac) + chip_sum).astype(BF)
                o_ref[p] = (came * fac + early).astype(BF)

            @pl.when(place < chips - 1)
            def _():
                onward(p).start()

        @pl.loop(0, pieces)
        def _(p):
            @pl.when(place > 0)
            def _():
                back(p).wait_send()

            @pl.when(place < chips - 1)
            def _():
                onward(p).wait_send()


def chain_seq(local, fac, flip, cid):
    shape = local.shape
    pieces = shape[0] * shape[1]
    chips = lax.axis_size("seq") // 2
    out = pl.pallas_call(
        functools.partial(chain_kernel, chips, shape[1], flip),
        out_shape=jax.ShapeDtypeStruct((pieces,) + shape[2:], BF),
        in_specs=[
            pl.BlockSpec(memory_space=pltpu.SMEM),
            pl.BlockSpec(memory_space=pltpu.VMEM),
        ],
        out_specs=pl.BlockSpec(memory_space=pltpu.VMEM),
        scratch_shapes=[pltpu.VMEM((pieces,) + shape[2:], BF)] * 3
        + [pltpu.SemaphoreType.DMA((pieces,))] * 6,
        compiler_params=params(cid),
        name=f"chain_{cid}",
    )(fac, local.astype(BF).reshape((pieces,) + shape[2:]))
    return out.reshape(shape)


def layer_norm(values, gain, bias):
    center = values - jnp.mean(values, -1, keepdims=True)
    spread = jnp.mean(center * center, -1, keepdims=True)
    return center * lax.rsqrt(spread + EPS) * gain + bias


def head_norm(values):
    center = values - jnp.mean(values, -1, keepdims=True)
    spread = jnp.mean(center * center, -1, keepdims=True)
    return center * lax.rsqrt(spread + EPS)


def rotation(values, angles):
    half_width = values.shape[-1] // 2
    cosine = jnp.cos(angles)
    sine = jnp.sin(angles)
    cosine = jnp.concatenate([cosine, cosine], -1)[:, None, :]
    sine = jnp.concatenate([sine, sine], -1)[:, None, :]
    turned = jnp.concatenate([-values[..., half_width:], values[..., :half_width]], -1)
    return values * cosine + turned * sine


def gated_mix(swish_pre, mixed):
    return jax.nn.silu(swish_pre) * head_norm(mixed)


def gated_mlp(gate, upper):
    return jax.nn.gelu(gate, approximate=True) * upper


def shards(
    inputs,
    query_weight,
    key_weight,
    value_weight,
    swish_weight,
    output_weight,
    gate_weight,
    up_weight,
    down_weight,
    attn_gain,
    attn_bias,
    mlp_gain,
    mlp_bias,
    output_grad,
):
    local_seqs, block_len, model_width = inputs.shape
    heads_local = query_weight.shape[1] // DK
    inputs_full = inputs.astype(jnp.float32)
    normed_one = layer_norm(inputs_full, attn_gain, attn_bias).astype(jnp.bfloat16)
    gathered_one = gather_tp(normed_one, 0)
    seq_count = gathered_one.shape[0]
    row_total = seq_count * block_len
    flat_one = gathered_one.reshape(row_total, model_width)
    query = jnp.dot(flat_one, query_weight, preferred_element_type=jnp.float32).reshape(
        seq_count, block_len, heads_local, DK
    )
    keys_pre = jnp.dot(flat_one, key_weight, preferred_element_type=jnp.float32).reshape(
        seq_count, block_len, heads_local, DK
    )
    value = (
        jnp.dot(flat_one, value_weight, preferred_element_type=jnp.float32)
        .astype(jnp.bfloat16)
        .reshape(seq_count, block_len, heads_local, DV)
    )
    swish_pre = jnp.dot(flat_one, swish_weight, preferred_element_type=jnp.float32).reshape(
        seq_count, block_len, heads_local, DV
    )
    half_width = DK // 2
    frequencies = jnp.power(10000.0, -jnp.arange(half_width, dtype=jnp.float32) / half_width)
    steps_in = jnp.arange(block_len, dtype=jnp.float32)
    positions = lax.axis_index("seq").astype(jnp.float32) * block_len + steps_in
    angles = positions[:, None] * frequencies[None, :]
    query_rot = rotation(query, angles).astype(jnp.bfloat16)
    key_rot = rotation(keys_pre, angles).astype(jnp.bfloat16)
    head_ids = (lax.axis_index("tp") * heads_local + jnp.arange(heads_local)).astype(jnp.float32)
    decays = 1.0 - jnp.exp2(-5.0 - head_ids)
    lag = steps_in[:, None] - steps_in[None, :]
    decay_mat = jnp.where(
        lag[None] >= 0, jnp.power(decays[:, None, None], jnp.maximum(lag, 0.0)[None]), 0.0
    )
    query_fac = jnp.power(decays[None, :], steps_in[:, None] + 1.0)
    key_fac = jnp.power(decays[None, :], block_len - 1.0 - steps_in[:, None])
    block_fac = jnp.power(decays, block_len * 1.0)
    raw = jnp.einsum("sthk,suhk->shtu", query_rot, key_rot, preferred_element_type=jnp.float32)
    scores = (raw * decay_mat[None]).astype(jnp.bfloat16)
    intra = jnp.einsum("shtu,suhv->sthv", scores, value, preferred_element_type=jnp.float32)
    key_dec = (key_rot * key_fac[None, :, :, None]).astype(jnp.bfloat16)
    local_state = jnp.einsum("suhk,suhv->shkv", key_dec, value, preferred_element_type=jnp.float32)
    prior_low = chain_seq(local_state, block_fac, False, 1)
    query_dec = (query_rot * query_fac[None, :, :, None]).astype(jnp.bfloat16)
    mixed = intra + jnp.einsum(
        "sthk,shkv->sthv", query_dec, prior_low, preferred_element_type=jnp.float32
    )
    gated = (
        gated_mix(swish_pre, mixed)
        .astype(jnp.bfloat16)
        .reshape(seq_count, block_len, heads_local * DV)
    )
    picked = gated
    attn_out = scatter_tp(
        jnp.dot(picked, output_weight, preferred_element_type=jnp.float32).astype(jnp.bfloat16), 2
    )
    hidden_res = inputs_full + attn_out
    normed_two = layer_norm(hidden_res, mlp_gain, mlp_bias).astype(jnp.bfloat16)
    gathered_two = gather_tp(normed_two, 3)
    flat_two = gathered_two.reshape(row_total, model_width)
    gate = jnp.dot(flat_two, gate_weight, preferred_element_type=jnp.float32)
    upper = jnp.dot(flat_two, up_weight, preferred_element_type=jnp.float32)
    hidden = gated_mlp(gate, upper).astype(jnp.bfloat16)
    hidden_seq = hidden.reshape(seq_count, block_len, hidden.shape[1])
    picked = hidden_seq
    mlp_out = scatter_tp(
        jnp.dot(picked, down_weight, preferred_element_type=jnp.float32).astype(jnp.bfloat16), 4
    )
    outputs = (hidden_res + mlp_out).astype(jnp.bfloat16)
    grad_all = gather_tp(output_grad, 5)
    grad_flat = grad_all.reshape(row_total, model_width)
    down_grad = jnp.einsum("nf,nd->fd", hidden, grad_flat, preferred_element_type=jnp.float32)
    hidden_grad = jnp.einsum(
        "nd,fd->nf", grad_flat, down_weight, preferred_element_type=jnp.float32
    )
    _, pull_mlp = jax.vjp(gated_mlp, gate, upper)
    gate_back, upper_back = pull_mlp(hidden_grad)
    gate_low = gate_back.astype(jnp.bfloat16)
    upper_low = upper_back.astype(jnp.bfloat16)
    gate_grad = jnp.einsum("nd,nf->df", flat_two, gate_low, preferred_element_type=jnp.float32)
    up_grad = jnp.einsum("nd,nf->df", flat_two, upper_low, preferred_element_type=jnp.float32)
    gate_seq = gate_low.reshape(seq_count, block_len, gate_low.shape[1])
    upper_seq = upper_low.reshape(seq_count, block_len, upper_low.shape[1])
    normed_two_grad = scatter_tp(
        (
            jnp.einsum("scf,df->scd", gate_seq, gate_weight, preferred_element_type=jnp.float32)
            + jnp.einsum("scf,df->scd", upper_seq, up_weight, preferred_element_type=jnp.float32)
        ).astype(jnp.bfloat16),
        6,
    )
    _, pull_two = jax.vjp(layer_norm, hidden_res, mlp_gain, mlp_bias)
    res_back, mlpgain_part, mlpbias_part = pull_two(normed_two_grad)
    res_grad = output_grad.astype(jnp.float32) + res_back
    res_all = gather_tp(res_grad.astype(jnp.bfloat16), 7)
    res_flat = res_all.reshape(row_total, model_width)
    gated_flat = gated.reshape(row_total, heads_local * DV)
    mixer_grad = jnp.einsum("ne,nd->ed", gated_flat, res_flat, preferred_element_type=jnp.float32)
    gated_back = jnp.einsum(
        "nd,ed->ne", res_flat, output_weight, preferred_element_type=jnp.float32
    ).reshape(seq_count, block_len, heads_local, DV)
    _, pull_mix = jax.vjp(gated_mix, swish_pre, mixed)
    swish_back, mixed_back = pull_mix(gated_back)
    swish_low = swish_back.astype(jnp.bfloat16)
    mixed_low = mixed_back.astype(jnp.bfloat16)
    scores_back = jnp.einsum(
        "sthv,suhv->shtu", mixed_low, value, preferred_element_type=jnp.float32
    )
    raw_low = (scores_back * decay_mat[None]).astype(jnp.bfloat16)
    prior_back = jnp.einsum(
        "sthk,sthv->shkv", query_dec, mixed_low, preferred_element_type=jnp.float32
    )
    later_low = chain_seq(prior_back, block_fac, True, 8)
    query_rot_back = (
        jnp.einsum("shtu,suhk->sthk", raw_low, key_rot, preferred_element_type=jnp.float32)
        + jnp.einsum("sthv,shkv->sthk", mixed_low, prior_low, preferred_element_type=jnp.float32)
        * query_fac[None, :, :, None]
    )
    key_rot_back = (
        jnp.einsum("shtu,sthk->suhk", raw_low, query_rot, preferred_element_type=jnp.float32)
        + jnp.einsum("suhv,shkv->suhk", value, later_low, preferred_element_type=jnp.float32)
        * key_fac[None, :, :, None]
    )
    value_low = (
        jnp.einsum("shtu,sthv->suhv", scores, mixed_low, preferred_element_type=jnp.float32)
        + jnp.einsum("suhk,shkv->suhv", key_dec, later_low, preferred_element_type=jnp.float32)
    ).astype(jnp.bfloat16)
    _, pull_rot = jax.vjp(lambda values: rotation(values, angles), query)
    query_low = (
        pull_rot(query_rot_back)[0]
        .astype(jnp.bfloat16)
        .reshape(seq_count, block_len, heads_local * DK)
    )
    key_low = (
        pull_rot(key_rot_back)[0]
        .astype(jnp.bfloat16)
        .reshape(seq_count, block_len, heads_local * DK)
    )
    value_seq = value_low.reshape(seq_count, block_len, heads_local * DV)
    swish_seq = swish_low.reshape(seq_count, block_len, heads_local * DV)
    query_grad = jnp.einsum(
        "nd,ne->de",
        flat_one,
        query_low.reshape(row_total, heads_local * DK),
        preferred_element_type=jnp.float32,
    )
    key_grad = jnp.einsum(
        "nd,ne->de",
        flat_one,
        key_low.reshape(row_total, heads_local * DK),
        preferred_element_type=jnp.float32,
    )
    value_grad = jnp.einsum(
        "nd,ne->de",
        flat_one,
        value_seq.reshape(row_total, heads_local * DV),
        preferred_element_type=jnp.float32,
    )
    swish_grad = jnp.einsum(
        "nd,ne->de",
        flat_one,
        swish_seq.reshape(row_total, heads_local * DV),
        preferred_element_type=jnp.float32,
    )
    total = jnp.zeros((local_seqs * lax.axis_size("tp"), block_len, model_width), jnp.float32)
    for source, weight in (
        (query_low, query_weight),
        (key_low, key_weight),
        (value_seq, value_weight),
        (swish_seq, swish_weight),
    ):
        picked = source
        total = total + jnp.einsum(
            "sce,de->scd", picked, weight, preferred_element_type=jnp.float32
        )
    normed_one_grad = scatter_tp(total.astype(jnp.bfloat16), 9)
    _, pull_one = jax.vjp(layer_norm, inputs_full, attn_gain, attn_bias)
    input_back, attngain_part, attnbias_part = pull_one(normed_one_grad)
    input_grad = (res_grad + input_back).astype(jnp.bfloat16)
    attngain_grad, attnbias_grad, mlpgain_grad, mlpbias_grad = (
        lax.psum_scatter(attngain_part, ("seq", "tp"), scatter_dimension=0, tiled=True),
        lax.psum_scatter(attnbias_part, ("seq", "tp"), scatter_dimension=0, tiled=True),
        lax.psum_scatter(mlpgain_part, ("seq", "tp"), scatter_dimension=0, tiled=True),
        lax.psum_scatter(mlpbias_part, ("seq", "tp"), scatter_dimension=0, tiled=True),
    )
    query_grad, key_grad, value_grad, swish_grad, mixer_grad, gate_grad, up_grad, down_grad = (
        lax.psum_scatter(
            query_grad.astype(jnp.bfloat16), "seq", scatter_dimension=0, tiled=True
        ).astype(jnp.float32),
        lax.psum_scatter(
            key_grad.astype(jnp.bfloat16), "seq", scatter_dimension=0, tiled=True
        ).astype(jnp.float32),
        lax.psum_scatter(
            value_grad.astype(jnp.bfloat16), "seq", scatter_dimension=0, tiled=True
        ).astype(jnp.float32),
        lax.psum_scatter(
            swish_grad.astype(jnp.bfloat16), "seq", scatter_dimension=0, tiled=True
        ).astype(jnp.float32),
        lax.psum_scatter(
            mixer_grad.astype(jnp.bfloat16), "seq", scatter_dimension=1, tiled=True
        ).astype(jnp.float32),
        lax.psum_scatter(
            gate_grad.astype(jnp.bfloat16), "seq", scatter_dimension=0, tiled=True
        ).astype(jnp.float32),
        lax.psum_scatter(
            up_grad.astype(jnp.bfloat16), "seq", scatter_dimension=0, tiled=True
        ).astype(jnp.float32),
        lax.psum_scatter(
            down_grad.astype(jnp.bfloat16), "seq", scatter_dimension=1, tiled=True
        ).astype(jnp.float32),
    )
    return (
        outputs,
        input_grad,
        query_grad,
        key_grad,
        value_grad,
        swish_grad,
        mixer_grad,
        gate_grad,
        up_grad,
        down_grad,
        attngain_grad,
        attnbias_grad,
        mlpgain_grad,
        mlpbias_grad,
    )


def solution(mesh):
    return jax.shard_map(
        shards,
        mesh=mesh,
        in_specs=(
            P("tp", "seq", None),
            P(None, "tp"),
            P(None, "tp"),
            P(None, "tp"),
            P(None, "tp"),
            P("tp", None),
            P(None, "tp"),
            P(None, "tp"),
            P("tp", None),
            P(),
            P(),
            P(),
            P(),
            P("tp", "seq", None),
        ),
        out_specs=(
            P("tp", "seq", None),
            P("tp", "seq", None),
            P("seq", "tp"),
            P("seq", "tp"),
            P("seq", "tp"),
            P("seq", "tp"),
            P("tp", "seq"),
            P("seq", "tp"),
            P("seq", "tp"),
            P("tp", "seq"),
            P(("seq", "tp")),
            P(("seq", "tp")),
            P(("seq", "tp")),
            P(("seq", "tp")),
        ),
        check_vma=False,
    )
```

```python
import functools

import jax
import jax.numpy as jnp
from jax import lax
from jax.experimental import pallas as pl
from jax.experimental.pallas import tpu as pltpu
from jax.sharding import PartitionSpec as P

DK = 256
DV = 512


EPS = 1e-05
MESH = pl.DeviceIdType.MESH
BF = jnp.bfloat16
F32 = jnp.float32
VMEM_LIMIT = 60 * 1024 * 1024


def remote(src, dst, ssem, rsem, slot, dev):
    return pltpu.make_async_remote_copy(
        src_ref=src,
        dst_ref=dst,
        send_sem=ssem.at[slot],
        recv_sem=rsem.at[slot],
        device_id=dev,
        device_id_type=MESH,
    )


def greet(devs):
    barrier = pltpu.get_barrier_semaphore()
    for dev in devs:
        pl.semaphore_signal(barrier, inc=1, device_id=dev, device_id_type=MESH)
    pl.semaphore_wait(barrier, len(devs))


def params(cid):
    return pltpu.CompilerParams(
        collective_id=cid, has_side_effects=True, vmem_limit_bytes=VMEM_LIMIT
    )


class Gather:
    def __init__(self, n, x, o, ssem, rsem):
        s, t = lax.axis_index("seq"), lax.axis_index("tp")
        self.n, self.t = n, t
        rows = x.shape[0]
        if n == 4:
            px, py = t + 1 - 2 * (t % 2), (t + 2) % 4
            dx, dy = (s, px), (s, py)
            self.peers = [dx, dy]
            half = rows // 2
            lo, hi = pl.ds(0, half), pl.ds(half, half)
            self.first = [
                remote(x.at[lo], o.at[t, lo], ssem, rsem, 0, dx),
                remote(x.at[hi], o.at[t, hi], ssem, rsem, 1, dy),
                remote(x.at[hi], o.at[t, hi], ssem, rsem, 2, dx),
                remote(x.at[lo], o.at[t, lo], ssem, rsem, 3, dy),
            ]
            self.relay = [
                remote(o.at[px, lo], o.at[px, lo], ssem, rsem, 4, dy),
                remote(o.at[py, hi], o.at[py, hi], ssem, rsem, 5, dx),
            ]
        else:
            self.peers = [(s, (t + k) % n) for k in range(1, n)]
            self.first = [
                remote(x, o.at[t], ssem, rsem, k, dev) for k, dev in enumerate(self.peers)
            ]
            self.relay = []

    def source(self, i):
        t = self.t
        if self.n == 4:
            near = jnp.where(i == 1, t + 1 - 2 * (t % 2), (t + 2) % 4)
            return jnp.where(i == 0, t, jnp.where(i == 3, 3 - t, near))
        return (t - i + self.n) % self.n

    def start(self):
        for copy in self.first:
            copy.start()

    def arrive(self, i):
        if self.n == 4:

            @pl.when(i == 1)
            def _():
                self.first[0].wait_recv()
                self.relay[0].start()
                self.first[1].wait_recv()
                self.relay[1].start()
                self.first[2].wait_recv()

            @pl.when(i == 2)
            def _():
                self.first[3].wait_recv()

            @pl.when(i == 3)
            def _():
                self.relay[0].wait_recv()
                self.relay[1].wait_recv()

        else:
            for k, copy in enumerate(self.first):

                @pl.when(i == k + 1)
                def _(copy=copy):
                    copy.wait_recv()

    def drain(self):
        for copy in self.first + self.relay:
            copy.wait_send()


class Scatter:
    def __init__(self, n, parts, near, far, hold, ssem, rsem):
        s, t = lax.axis_index("seq"), lax.axis_index("tp")
        self.n, self.t = n, t
        self.parts, self.near, self.far, self.hold = parts, near, far, hold
        if n == 4:
            self.px, self.py, pd = t + 1 - 2 * (t % 2), (t + 2) % 4, 3 - t
            dx, dy = (s, self.px), (s, self.py)
            self.peers = [dx, dy]
            half = parts.shape[-1] // 2
            self.cols = a, b = pl.ds(0, half), pl.ds(half, half)
            self.far_a = remote(parts.at[pd, :, a], near.at[0, 1], ssem, rsem, 0, dx)
            self.far_b = remote(parts.at[pd, :, b], near.at[1, 1], ssem, rsem, 1, dy)
            self.near_a = remote(parts.at[self.px, :, a], near.at[0, 0], ssem, rsem, 2, dx)
            self.near_b = remote(parts.at[self.py, :, b], near.at[1, 0], ssem, rsem, 3, dy)
            self.sum_a = remote(hold.at[0], far.at[0], ssem, rsem, 4, dy)
            self.sum_b = remote(hold.at[1], far.at[1], ssem, rsem, 5, dx)
            self.copies = [self.far_a, self.far_b, self.near_a, self.near_b, self.sum_a, self.sum_b]
        else:
            self.peers = [(s, (t + k) % n) for k in range(1, n)]
            self.copies = [
                remote(parts.at[(t - k + n) % n], near.at[k - 1], ssem, rsem, k - 1, (s, (t - k + n) % n))
                for k in range(1, n)
            ]

    def send(self, i):
        if self.n == 4:

            @pl.when(i == 1)
            def _():
                self.near_a.start()

            @pl.when(i == 2)
            def _():
                self.near_b.start()

            @pl.when(i == 3)
            def _():
                self.far_a.start()
                self.far_b.start()

        else:
            for k, copy in enumerate(self.copies):

                @pl.when(i == k + 1)
                def _(copy=copy):
                    copy.start()

    def relay(self):
        if self.n == 4:
            a, b = self.cols
            self.far_a.wait_recv()
            self.hold[0] = (
                self.parts[self.py, :, a].astype(F32) + self.near[0, 1].astype(F32)
            ).astype(BF)
            self.sum_a.start()
            self.far_b.wait_recv()
            self.hold[1] = (
                self.parts[self.px, :, b].astype(F32) + self.near[1, 1].astype(F32)
            ).astype(BF)
            self.sum_b.start()

    def finish(self, write):
        if self.n == 4:
            for side, (one, two) in enumerate(
                ((self.near_a, self.sum_a), (self.near_b, self.sum_b))
            ):
                one.wait_recv()
                two.wait_recv()
                write(
                    self.cols[side],
                    self.parts[self.t, :, self.cols[side]].astype(F32)
                    + self.near[side, 0].astype(F32)
                    + self.far[side].astype(F32),
                )
        else:
            total = self.parts[self.t].astype(F32)
            for k, copy in enumerate(self.copies):
                copy.wait_recv()
                total = total + self.near[k].astype(F32)
            write(slice(None), total)

    def drain(self):
        for copy in self.copies:
            copy.wait_send()


def scatter_scratch(n, rows, width):
    if n == 4:
        near, far = (2, 2, rows, width // 2), (2, rows, width // 2)
    else:
        near, far = (n - 1, rows, width), (1, 16, 128)
    return [pltpu.VMEM(near, BF), pltpu.VMEM(far, BF), pltpu.VMEM(far, BF)]


class Chain:
    def __init__(self, chips, heads, flip, fac, local, out, pair, enter, leave, ps, pr, zs, zr, bs, br):
        s, t = lax.axis_index("seq"), lax.axis_index("tp")
        core, chip, span = s % 2, s // 2, 2 * chips
        self.chips, self.heads, self.fac = chips, heads, fac
        self.local, self.out, self.pair, self.enter, self.leave = local, out, pair, enter, leave
        self.sems = ps, pr, zs, zr, bs, br
        self.partner = (s + 1 - 2 * core, t)
        above, below = ((s + 2) % span, t), ((s - 2 + span) % span, t)
        self.peers = [self.partner, above, below]
        if flip:
            self.first, self.place, self.ahead = core == 1, chips - 1 - chip, below
        else:
            self.first, self.place, self.ahead = core == 0, chip, above
        self.last = jnp.logical_not(self.first)

    def give(self, p):
        return remote(self.local.at[p], self.pair.at[p], self.sems[0], self.sems[1], p, self.partner)

    def back(self, p):
        return remote(self.enter.at[p], self.out.at[p], self.sems[4], self.sems[5], p, self.partner)

    def onward(self, p):
        return remote(self.leave.at[p], self.enter.at[p], self.sems[2], self.sems[3], p, self.ahead)

    def begin(self, p):
        @pl.when(self.first)
        def _():
            self.give(p).start()

            @pl.when(self.place == 0)
            def _():
                self.out[p] = jnp.zeros(self.out.shape[1:], BF)

    def step(self, p):
        @pl.when(self.first)
        def _():
            @pl.when(self.place > 0)
            def _():
                self.back(p).wait_recv()

        @pl.when(self.last)
        def _():
            fac = self.fac[p % self.heads]
            self.give(p).wait_recv()
            early = self.pair[p].astype(F32)
            chip_sum = early * fac + self.local[p].astype(F32)

            @pl.when(self.place == 0)
            def _():
                self.leave[p] = chip_sum.astype(BF)
                self.out[p] = self.pair[p]

            @pl.when(self.place > 0)
            def _():
                self.onward(p).wait_recv()
                self.back(p).start()
                came = self.enter[p].astype(F32)
                self.leave[p] = (came * (fac * fac) + chip_sum).astype(BF)
                self.out[p] = (came * fac + early).astype(BF)

            @pl.when(self.place < self.chips - 1)
            def _():
                self.onward(p).start()

    def drain(self, p):
        @pl.when(self.first)
        def _():
            self.give(p).wait_send()

        @pl.when(self.last)
        def _():
            @pl.when(self.place > 0)
            def _():
                self.back(p).wait_send()

            @pl.when(self.place < self.chips - 1)
            def _():
                self.onward(p).wait_send()


def chain_scratch(pieces):
    dma = pltpu.SemaphoreType.DMA
    return [pltpu.VMEM((pieces, DK, DV), BF)] * 3 + [dma((pieces,))] * 6


def dot(a, b, ca=1, cb=0):
    return lax.dot_general(a, b, (((ca,), (cb,)), ((), ())), preferred_element_type=F32)


def turn(v, cos, sin):
    lo, hi = v[:, : DK // 2], v[:, DK // 2 :]
    return jnp.concatenate([lo * cos - hi * sin, hi * cos + lo * sin], 1)


def turn_back(g, cos, sin):
    lo, hi = g[:, : DK // 2], g[:, DK // 2 :]
    return jnp.concatenate([lo * cos + hi * sin, hi * cos - lo * sin], 1)


def norm_of(m):
    center = m - jnp.mean(m, -1, keepdims=True)
    inv = lax.rsqrt(jnp.mean(center * center, -1, keepdims=True) + EPS)
    return center * inv, inv


def mixer_kernel(n, chips, heads, *refs):
    (
        fac, x, og, wk_h, wv_h, wq_h, ws_h, wo_h, decay, qfac, kfac, cos, sin,
        x_all, og_all, q, k, v, sp, mx, prior, gated, attn,
        wk, wv, wq, ws, wo, acc, parts, local,
    ) = refs[:31]
    near, far, hold = refs[31:34]
    chain_refs = refs[34:43]
    wsem, gs, gr, os, orr, ss, sr = refs[43:]
    rows = x.shape[0]
    gather = Gather(n, x, x_all, gs, gr)
    gather_og = Gather(n, og, og_all, os, orr)
    scatter = Scatter(n, parts, near, far, hold, ss, sr)
    chain = Chain(chips, heads, False, fac, local, prior, *chain_refs)
    loads = [
        pltpu.make_async_copy(a, w, wsem.at[i])
        for i, (a, w) in enumerate(((wk_h, wk), (wv_h, wv), (wq_h, wq), (ws_h, ws), (wo_h, wo)))
    ]
    for load in loads:
        load.start()
    greet(gather.peers + chain.peers)
    gather.start()
    gather_og.start()
    me = gather.source(0)
    x_all[me] = x[...]
    og_all[me] = og[...]
    for load in loads[:4]:
        load.wait()

    @pl.loop(0, n)
    def _(i):
        j = gather.source(i)
        gather.arrive(i)
        at = pl.ds(pl.multiple_of(j * rows, rows), rows)
        acc[:, : heads * DK] = dot(x_all[j], wk[...])
        v[at] = dot(x_all[j], wv[...]).astype(BF)
        for h in range(heads):
            vc = slice(h * DV, (h + 1) * DV)
            kc = slice(h * DK, (h + 1) * DK)
            key = turn(acc[:, kc], cos[...], sin[...]).astype(BF)
            k[at, kc] = key
            key_dec = (key.astype(F32) * kfac[h]).astype(BF)
            p = j * heads + h
            local[p] = dot(key_dec, v[at, vc], 0, 0).astype(BF)
            chain.begin(p)
        acc[:, : heads * DK] = dot(x_all[j], wq[...])
        for h in range(heads):
            kc = slice(h * DK, (h + 1) * DK)
            q[at, kc] = turn(acc[:, kc], cos[...], sin[...]).astype(BF)
        sp[at] = dot(x_all[j], ws[...])

    loads[4].wait()

    @pl.loop(0, n)
    def _(step):
        i = (step + 1) % n
        j = gather.source(i)
        gather_og.arrive(i)
        at = pl.ds(pl.multiple_of(j * rows, rows), rows)
        for h in range(heads):
            vc = slice(h * DV, (h + 1) * DV)
            kc = slice(h * DK, (h + 1) * DK)
            p = j * heads + h
            query = q[at, kc]
            scores = (dot(query, k[at, kc], 1, 1) * decay[h]).astype(BF)
            mx[at, vc] = dot(scores, v[at, vc])
            query_dec = (query.astype(F32) * qfac[h]).astype(BF)
            chain.step(p)
            mx[at, vc] += dot(query_dec, prior[p])
            pre = sp[at, vc]
            gated[at, vc] = (pre * jax.nn.sigmoid(pre) * norm_of(mx[at, vc])[0]).astype(BF)
        parts[j] = dot(gated[at], wo[...]).astype(BF)
        scatter.send(i)

    scatter.relay()

    def write(cols, total):
        attn[:, cols] = total

    scatter.finish(write)
    gather.drain()
    gather_og.drain()
    scatter.drain()

    @pl.loop(0, n * heads)
    def _(p):
        chain.drain(p)


def mixer(fac, x, og, wk, wv, wq, ws, wo, decay, qfac, kfac, cos, sin, cid):
    n = lax.axis_size("tp")
    chips = lax.axis_size("seq") // 2
    rows, model = x.shape
    heads = wk.shape[1] // DK
    pieces = n * heads
    total = n * rows
    dma = pltpu.SemaphoreType.DMA
    sems = max(6, n - 1)
    vmem = pl.BlockSpec(memory_space=pltpu.VMEM)
    hbm = pl.BlockSpec(memory_space=pl.ANY)
    shape = jax.ShapeDtypeStruct
    return pl.pallas_call(
        functools.partial(mixer_kernel, n, chips, heads),
        out_shape=(
            shape((n, rows, model), BF),
            shape((n, rows, model), BF),
            shape((total, heads * DK), BF),
            shape((total, heads * DK), BF),
            shape((total, heads * DV), BF),
            shape((total, heads * DV), F32),
            shape((total, heads * DV), F32),
            shape((pieces, DK, DV), BF),
            shape((total, heads * DV), BF),
            shape((rows, model), F32),
        ),
        in_specs=[pl.BlockSpec(memory_space=pltpu.SMEM), vmem, vmem] + [hbm] * 5 + [vmem] * 5,
        out_specs=(vmem,) * 10,
        scratch_shapes=[pltpu.VMEM(w.shape, BF) for w in (wk, wv, wq, ws, wo)]
        + [
            pltpu.VMEM((rows, heads * DK), F32),
            pltpu.VMEM((n, rows, model), BF),
            pltpu.VMEM((pieces, DK, DV), BF),
        ]
        + scatter_scratch(n, rows, model)
        + chain_scratch(pieces)
        + [dma((5,))] + [dma((sems,))] * 6,
        compiler_params=params(cid),
        name="mixer",
    )(fac, x, og, wk, wv, wq, ws, wo, decay, qfac, kfac, cos, sin)


GELU_C = 0.7978845608028654
GELU_A = 0.044715


def mlp_kernel(n, *refs):
    (
        x, og_all, wg_h, wu_h, wd_h,
        x_all, hidden, gate_low, upper_low, mlp_parts, grad_two,
        wg, wu, wd, hg, acc_g, acc_u, acc, parts, near, far, hold,
        wsem, gs, gr, ss, sr,
    ) = refs
    rows = x.shape[0]
    gather = Gather(n, x, x_all, gs, gr)
    scatter = Scatter(n, parts, near, far, hold, ss, sr)
    loads = [
        pltpu.make_async_copy(a, w, wsem.at[i])
        for i, (a, w) in enumerate(((wd_h, wd), (wg_h, wg), (wu_h, wu)))
    ]
    for load in loads:
        load.start()
    greet(gather.peers)
    gather.start()
    me = gather.source(0)
    x_all[me] = x[...]
    loads[0].wait()

    @pl.loop(0, n)
    def _(j):
        at = pl.ds(pl.multiple_of(j * rows, rows), rows)
        hg[at] = dot(og_all[j], wd[...], 1, 1)

    loads[1].wait()
    loads[2].wait()
    slab = 16

    @pl.loop(0, n)
    def _(i):
        j = gather.source(i)
        gather.arrive(i)
        start = pl.multiple_of(j * rows, rows)
        at = pl.ds(start, rows)
        acc_g[...] = dot(x_all[j], wg[...])
        acc_u[...] = dot(x_all[j], wu[...])

        @pl.loop(0, rows // slab)
        def _(r):
            here = pl.ds(pl.multiple_of(r * slab, slab), slab)
            there = pl.ds(pl.multiple_of(start + r * slab, slab), slab)
            g, u, back = acc_g[here], acc_u[here], hg[there]
            square = g * g
            th = jnp.tanh(GELU_C * (g + GELU_A * (square * g)))
            half = 0.5 * (1.0 + th)
            gelu = g * half
            slope = half + 0.5 * g * (1.0 - th * th) * (GELU_C * (1.0 + 3.0 * GELU_A * square))
            hidden[there] = (gelu * u).astype(BF)
            gate_low[there] = (back * u * slope).astype(BF)
            upper_low[there] = (back * gelu).astype(BF)

        acc[...] = dot(gate_low[at], wg[...], 1, 1)
        parts[j] = (acc[...] + dot(upper_low[at], wu[...], 1, 1)).astype(BF)
        scatter.send(i)

    @pl.loop(0, n)
    def _(j):
        at = pl.ds(pl.multiple_of(j * rows, rows), rows)
        mlp_parts[j] = dot(hidden[at], wd[...]).astype(BF)

    scatter.relay()

    def write(cols, total):
        grad_two[:, cols] = total

    scatter.finish(write)
    gather.drain()
    scatter.drain()


def mlp(x, og_all, wg, wu, wd, cid):
    n = lax.axis_size("tp")
    rows, model = x.shape
    width = wg.shape[1]
    total = n * rows
    dma = pltpu.SemaphoreType.DMA
    sems = max(6, n - 1)
    vmem = pl.BlockSpec(memory_space=pltpu.VMEM)
    hbm = pl.BlockSpec(memory_space=pl.ANY)
    shape = jax.ShapeDtypeStruct
    return pl.pallas_call(
        functools.partial(mlp_kernel, n),
        out_shape=(
            shape((n, rows, model), BF),
            shape((total, width), BF),
            shape((total, width), BF),
            shape((total, width), BF),
            shape((n, rows, model), BF),
            shape((rows, model), F32),
        ),
        in_specs=[vmem, vmem] + [hbm] * 3,
        out_specs=(vmem,) * 6,
        scratch_shapes=[pltpu.VMEM(w.shape, BF) for w in (wg, wu, wd)]
        + [
            pltpu.VMEM((total, width), F32),
            pltpu.VMEM((rows, width), F32),
            pltpu.VMEM((rows, width), F32),
            pltpu.VMEM((rows, model), F32),
            pltpu.VMEM((n, rows, model), BF),
        ]
        + scatter_scratch(n, rows, model)
        + [dma((3,))] + [dma((sems,))] * 4,
        compiler_params=params(cid),
        name="mlp",
    )(x, og_all, wg, wu, wd)


def mixer_back_kernel(n, chips, heads, *refs):
    (
        fac, res, wo_h, wq_h, wk_h, wv_h, ws_h, q, k, v, sp, mx, prior, mlp_parts, decay, qfac, kfac, cos, sin,
        res_all, swish_low, value_low, qk_low, grad_one, mlp_out,
        wo, wq, wk, wv, ws, mixed_low, acc, parts, local, later,
    ) = refs[:35]
    near, far, hold, mlp_near, mlp_far, mlp_hold = refs[35:41]
    chain_refs = refs[41:50]
    wsem, gs, gr, ss, sr, ms, mr = refs[50:]
    rows = res.shape[0]
    gather = Gather(n, res, res_all, gs, gr)
    scatter = Scatter(n, parts, near, far, hold, ss, sr)
    scatter_mlp = Scatter(n, mlp_parts, mlp_near, mlp_far, mlp_hold, ms, mr)
    chain = Chain(chips, heads, True, fac, local, later, *chain_refs)
    loads = [
        pltpu.make_async_copy(a, w, wsem.at[i])
        for i, (a, w) in enumerate(((wo_h, wo), (ws_h, ws), (wq_h, wq), (wk_h, wk), (wv_h, wv)))
    ]
    for load in loads:
        load.start()
    greet(gather.peers + chain.peers)
    gather.start()
    me = gather.source(0)
    res_all[me] = res[...]
    loads[0].wait()

    @pl.loop(0, n)
    def _(i):
        j = gather.source(i)
        gather.arrive(i)
        at = pl.ds(pl.multiple_of(j * rows, rows), rows)
        acc[:, : heads * DV] = dot(res_all[j], wo[...], 1, 1)
        for h in range(heads):
            vc = slice(h * DV, (h + 1) * DV)
            kc = slice(h * DK, (h + 1) * DK)
            back = acc[:, vc]
            normed, inv = norm_of(mx[at, vc])
            pre = sp[at, vc]
            sig = jax.nn.sigmoid(pre)
            swish_low[at, vc] = (back * normed * (sig * (1.0 + pre * (1.0 - sig)))).astype(BF)
            g = back * (pre * sig)
            g = inv * (
                g
                - jnp.mean(g, -1, keepdims=True)
                - normed * jnp.mean(g * normed, -1, keepdims=True)
            )
            g = g.astype(BF)
            mixed_low[at, vc] = g
            query_dec = (q[at, kc].astype(F32) * qfac[h]).astype(BF)
            p = j * heads + h
            local[p] = dot(query_dec, g, 0, 0).astype(BF)
            chain.begin(p)

    for load in loads[1:]:
        load.wait()
    for i in range(1, n):
        scatter_mlp.send(i)

    @pl.loop(0, n)
    def _(step):
        i = (step + 1) % n
        j = gather.source(i)
        at = pl.ds(pl.multiple_of(j * rows, rows), rows)
        for h in range(heads):
            vc = slice(h * DV, (h + 1) * DV)
            kc = slice(h * DK, (h + 1) * DK)
            p = j * heads + h
            g, value, query, key = mixed_low[at, vc], v[at, vc], q[at, kc], k[at, kc]
            raw_low = (dot(g, value, 1, 1) * decay[h]).astype(BF)
            query_back = dot(raw_low, key) + dot(g, prior[p], 1, 1) * qfac[h]
            qk_low[at, kc] = turn_back(query_back, cos[...], sin[...]).astype(BF)
            scores = (dot(query, key, 1, 1) * decay[h]).astype(BF)
            key_part = dot(raw_low, query, 0, 0)
            value_part = dot(scores, g, 0, 0)
            key_dec = (key.astype(F32) * kfac[h]).astype(BF)
            chain.step(p)
            after = later[p]
            key_back = key_part + dot(value, after, 1, 1) * kfac[h]
            qk_low[at, slice((heads + h) * DK, (heads + h + 1) * DK)] = turn_back(
                key_back, cos[...], sin[...]
            ).astype(BF)
            value_low[at, vc] = (value_part + dot(key_dec, after)).astype(BF)
        acc[...] = dot(swish_low[at], ws[...], 1, 1)
        acc[...] += dot(value_low[at], wv[...], 1, 1)
        acc[...] += dot(qk_low[at, : heads * DK], wq[...], 1, 1)
        parts[j] = (acc[...] + dot(qk_low[at, heads * DK :], wk[...], 1, 1)).astype(BF)
        scatter.send(i)

        @pl.when(step == n - 2)
        def _():
            scatter_mlp.relay()

    scatter.relay()

    def write(cols, total):
        grad_one[:, cols] = total

    scatter.finish(write)

    def write_mlp(cols, total):
        mlp_out[:, cols] = total

    scatter_mlp.finish(write_mlp)
    gather.drain()
    scatter.drain()
    scatter_mlp.drain()

    @pl.loop(0, n * heads)
    def _(p):
        chain.drain(p)


def mixer_back(fac, res, wo, wq, wk, wv, ws, q, k, v, sp, mx, prior, mlp_parts, decay, qfac, kfac, cos, sin, cid):
    n = lax.axis_size("tp")
    chips = lax.axis_size("seq") // 2
    rows, model = res.shape
    heads = q.shape[1] // DK
    pieces = n * heads
    total = n * rows
    dma = pltpu.SemaphoreType.DMA
    sems = max(6, n - 1)
    vmem = pl.BlockSpec(memory_space=pltpu.VMEM)
    hbm = pl.BlockSpec(memory_space=pl.ANY)
    shape = jax.ShapeDtypeStruct
    return pl.pallas_call(
        functools.partial(mixer_back_kernel, n, chips, heads),
        out_shape=(
            shape((n, rows, model), BF),
            shape((total, heads * DV), BF),
            shape((total, heads * DV), BF),
            shape((total, 2 * heads * DK), BF),
            shape((rows, model), F32),
            shape((rows, model), F32),
        ),
        in_specs=[pl.BlockSpec(memory_space=pltpu.SMEM), vmem] + [hbm] * 5 + [vmem] * 12,
        out_specs=(vmem,) * 6,
        scratch_shapes=[pltpu.VMEM(w.shape, BF) for w in (wo, wq, wk, wv, ws)]
        + [
            pltpu.VMEM((total, heads * DV), BF),
            pltpu.VMEM((rows, model), F32),
            pltpu.VMEM((n, rows, model), BF),
            pltpu.VMEM((pieces, DK, DV), BF),
            pltpu.VMEM((pieces, DK, DV), BF),
        ]
        + scatter_scratch(n, rows, model)
        + scatter_scratch(n, rows, model)
        + chain_scratch(pieces)
        + [dma((5,))]
        + [dma((sems,))] * 6,
        compiler_params=params(cid),
        name="mixer_back",
    )(fac, res, wo, wq, wk, wv, ws, q, k, v, sp, mx, prior, mlp_parts, decay, qfac, kfac, cos, sin)


def weights_kernel(
    chips, units, kinds, *refs
):
    kind_count = max(kinds) + 1
    wide = refs[:kind_count]
    deep = refs[kind_count : kind_count + units]
    vec = refs[kind_count + units]
    rest = refs[kind_count + units + 1 :]
    vec_near, vec_sum, vec_far, vs, vr, us, ur = rest[-7:]
    rest = rest[:-7]
    o_ref, vec_out, xs, ys, from_low, from_high, out, xsem, ysem, psx, prx, psy, pry, ssem, lsem, hsem = rest
    s = lax.axis_index("seq")
    t = lax.axis_index("tp")
    core = s % 2
    chip = s // 2
    tokens = ys.shape[1] // 2
    cut = xs.shape[3]
    span = 2 * chips
    partner = (s + 1 - 2 * core, t)
    above = ((s + 2) % span, t)
    below = ((s - 2 + span) % span, t)
    tp = vec.shape[0]
    ring = [((s + d) % span, t) for d in range(1, span)]
    cross = [(s, (t + d) % tp) for d in range(1, tp)]
    greet(ring + cross)
    vec_first = [
        remote(vec.at[(t + d) % tp], vec_near.at[d - 1], vs, vr, d - 1, cross[d - 1])
        for d in range(1, tp)
    ]
    vec_last = [
        remote(vec_sum.at[(s + d) % span], vec_far.at[d - 1], us, ur, d - 1, ring[d - 1])
        for d in range(1, span)
    ]
    for copy in vec_first:
        copy.start()

    def wide_own(kind, j):
        cols = pl.ds(pl.multiple_of((2 * j + core) * cut, cut), cut)
        return pltpu.make_async_copy(
            wide[kind].at[:, cols], xs.at[kind, j, pl.ds(0, tokens)], xsem.at[kind, j]
        )

    def wide_give(kind, j):
        cols = pl.ds(pl.multiple_of((2 * j + 1 - core) * cut, cut), cut)
        return pltpu.make_async_remote_copy(
            src_ref=wide[kind].at[:, cols],
            dst_ref=xs.at[kind, j, pl.ds(tokens, tokens)],
            send_sem=psx.at[kind, j],
            recv_sem=prx.at[kind, j],
            device_id=partner,
            device_id_type=MESH,
        )

    def deep_own(u):
        return pltpu.make_async_copy(deep[u], ys.at[u, pl.ds(0, tokens)], ysem.at[u])

    def deep_give(u):
        return pltpu.make_async_remote_copy(
            src_ref=deep[u],
            dst_ref=ys.at[u, pl.ds(tokens, tokens)],
            send_sem=psy.at[u],
            recv_sem=pry.at[u],
            device_id=partner,
            device_id_type=MESH,
        )

    seen = set()
    for u in range(units):
        deep_give(u).start()
        deep_own(u).start()
        if kinds[u] not in seen:
            seen.add(kinds[u])
            for j in range(chips):
                wide_give(kinds[u], j).start()
                wide_own(kinds[u], j).start()

    def ready(u):
        deep_own(u).wait()
        deep_give(u).wait_recv()
        if kinds[u] not in kinds[:u]:
            for j in range(chips):
                wide_own(kinds[u], j).wait()
                wide_give(kinds[u], j).wait_recv()

    def up(u, j):
        return pltpu.make_async_remote_copy(
            src_ref=out.at[u, j],
            dst_ref=from_low.at[u, j],
            send_sem=ssem.at[u, j],
            recv_sem=lsem.at[u, j],
            device_id=above,
            device_id_type=MESH,
        )

    def down(u, j):
        return pltpu.make_async_remote_copy(
            src_ref=out.at[u, j],
            dst_ref=from_high.at[u, j],
            send_sem=ssem.at[u, j],
            recv_sem=hsem.at[u, j],
            device_id=below,
            device_id_type=MESH,
        )

    def kind_of(u):
        kind = 0
        for w in range(units):
            if kinds[w]:
                kind = kind + jnp.where(u == w, kinds[w], 0)
        return kind

    def product(u, j):
        return lax.dot_general(
            xs[kind_of(u), j], ys[u], (((0,), (0,)), ((), ())), preferred_element_type=F32
        )

    low_half = chip < chips // 2
    rights = chips - 1 - chip

    def finish(u):
        total = product(u, chip)
        o_ref[u] = total

        @pl.when(chip > 0)
        def _():
            up(u, chip).wait_recv()
            o_ref[u] = o_ref[u] + from_low[u, chip].astype(F32)

        @pl.when(chip < chips - 1)
        def _():
            down(u, chip).wait_recv()
            o_ref[u] = o_ref[u] + from_high[u, chip].astype(F32)

    @pl.loop(0, units)
    def _(u):
        for w in range(units):

            @pl.when(u == w)
            def _(w=w):
                ready(w)

        @pl.loop(0, chips - 1)
        def _(k):
            j = jnp.where(
                low_half,
                jnp.where(k < rights, chips - 1 - k, k - rights),
                jnp.where(k < chip, k, chips - 1 - (k - chip)),
            )
            total = product(u, j)

            @pl.when(j > chip)
            def _():
                @pl.when(chip == 0)
                def _():
                    out[u, j] = total.astype(BF)

                @pl.when(chip > 0)
                def _():
                    up(u, j).wait_recv()
                    out[u, j] = (total + from_low[u, j].astype(F32)).astype(BF)

                up(u, j).start()

            @pl.when(j < chip)
            def _():
                @pl.when(chip == chips - 1)
                def _():
                    out[u, j] = total.astype(BF)

                @pl.when(chip < chips - 1)
                def _():
                    down(u, j).wait_recv()
                    out[u, j] = (total + from_high[u, j].astype(F32)).astype(BF)

                down(u, j).start()

        @pl.when(u == 0)
        def _():
            total = vec[t]
            for copy in vec_first:
                copy.wait_recv()
            vec_sum[...] = total + jnp.sum(vec_near[...], 0)
            for copy in vec_last:
                copy.start()

        @pl.when(u > 0)
        def _():
            finish(u - 1)

    vec_total = vec_sum[s]
    for copy in vec_last:
        copy.wait_recv()
    vec_out[...] = vec_total + jnp.sum(vec_far[...], 0)
    finish(units - 1)

    @pl.loop(0, units)
    def _(u):
        @pl.loop(0, chips)
        def _(j):
            @pl.when(j > chip)
            def _():
                up(u, j).wait_send()

            @pl.when(j < chip)
            def _():
                down(u, j).wait_send()

    for copy in vec_first + vec_last:
        copy.wait_send()
    for u in range(units):
        deep_give(u).wait_send()
    for kind in range(kind_count):
        for j in range(chips):
            wide_give(kind, j).wait_send()


def weight_sums(wide, deep, vec, kinds, cid):
    chips = lax.axis_size("seq") // 2
    tokens, model = wide[0].shape
    width = deep[0].shape[1]
    units = len(deep)
    cut = model // (2 * chips)
    block = (units, chips, cut, width)
    dma = pltpu.SemaphoreType.DMA
    return pl.pallas_call(
        functools.partial(weights_kernel, chips, units, kinds),
        out_shape=(
            jax.ShapeDtypeStruct((units, cut, width), F32),
            jax.ShapeDtypeStruct(vec.shape[2:], F32),
        ),
        in_specs=[pl.BlockSpec(memory_space=pl.ANY)] * (len(wide) + units)
        + [pl.BlockSpec(memory_space=pltpu.VMEM)],
        out_specs=(pl.BlockSpec(memory_space=pltpu.VMEM),) * 2,
        scratch_shapes=[
            pltpu.VMEM((len(wide), chips, 2 * tokens, cut), BF),
            pltpu.VMEM((units, 2 * tokens, width), BF),
            pltpu.VMEM(block, BF),
            pltpu.VMEM(block, BF),
            pltpu.VMEM(block, BF),
            dma((len(wide), chips)),
            dma((units,)),
            dma((len(wide), chips)),
            dma((len(wide), chips)),
            dma((units,)),
            dma((units,)),
            dma((units, chips)),
            dma((units, chips)),
            dma((units, chips)),
            pltpu.VMEM((vec.shape[0] - 1,) + vec.shape[1:], F32),
            pltpu.VMEM(vec.shape[1:], F32),
            pltpu.VMEM((2 * chips - 1,) + vec.shape[2:], F32),
            dma((vec.shape[0] - 1,)),
            dma((vec.shape[0] - 1,)),
            dma((2 * chips - 1,)),
            dma((2 * chips - 1,)),
        ],
        compiler_params=params(cid),
        name=f"weights_{cid}",
    )(*wide, *deep, vec)


def layer_norm(values, gain, bias):
    center = values - jnp.mean(values, -1, keepdims=True)
    spread = jnp.mean(center * center, -1, keepdims=True)
    return center * lax.rsqrt(spread + EPS) * gain + bias


def shards(
    inputs,
    query_weight,
    key_weight,
    value_weight,
    swish_weight,
    output_weight,
    gate_weight,
    up_weight,
    down_weight,
    attn_gain,
    attn_bias,
    mlp_gain,
    mlp_bias,
    output_grad,
):
    _, rows, model = inputs.shape
    heads = query_weight.shape[1] // DK
    inputs_full = inputs[0].astype(F32)
    cotangent = output_grad[0]

    half_width = DK // 2
    frequencies = jnp.power(10000.0, -jnp.arange(half_width, dtype=F32) / half_width)
    steps_in = jnp.arange(rows, dtype=F32)
    positions = lax.axis_index("seq").astype(F32) * rows + steps_in
    angles = positions[:, None] * frequencies[None, :]
    cosine, sine = jnp.cos(angles), jnp.sin(angles)
    head_ids = (lax.axis_index("tp") * heads + jnp.arange(heads)).astype(F32)
    decays = 1.0 - jnp.exp2(-5.0 - head_ids)
    lag = steps_in[:, None] - steps_in[None, :]
    decay_mat = jnp.where(
        lag[None] >= 0, jnp.power(decays[:, None, None], jnp.maximum(lag, 0.0)[None]), 0.0
    )
    query_fac = jnp.power(decays[:, None], steps_in[None, :] + 1.0)[:, :, None]
    key_fac = jnp.power(decays[:, None], rows - 1.0 - steps_in[None, :])[:, :, None]
    block_fac = jnp.power(decays, rows * 1.0)

    normed_one = layer_norm(inputs_full, attn_gain, attn_bias).astype(BF)
    one_all, grad_all, query, key, value, swish_pre, mixed, prior, gated, attn_out = mixer(
        block_fac, normed_one, cotangent, key_weight, value_weight, query_weight, swish_weight,
        output_weight, decay_mat, query_fac, key_fac, cosine, sine, 0,
    )
    hidden_res = inputs_full + attn_out
    normed_two = layer_norm(hidden_res, mlp_gain, mlp_bias).astype(BF)
    two_all, hidden, gate_low, upper_low, mlp_parts, normed_two_grad = mlp(
        normed_two, grad_all, gate_weight, up_weight, down_weight, 1
    )
    flat = lambda a: a.reshape(-1, model)
    product = lambda a, b: jnp.einsum("na,nb->ab", a, b, preferred_element_type=F32).astype(BF)
    _, pull_two = jax.vjp(layer_norm, hidden_res, mlp_gain, mlp_bias)
    res_back, mlpgain_part, mlpbias_part = pull_two(normed_two_grad)
    res_grad = cotangent.astype(F32) + res_back
    down_low = product(hidden, flat(grad_all))
    gatew_low = product(flat(two_all), gate_low)
    upw_low = product(flat(two_all), upper_low)
    down_low, gatew_low, upw_low, res_low = lax.optimization_barrier(
        (down_low, gatew_low, upw_low, res_grad.astype(BF))
    )
    scatter = functools.partial(lax.psum_scatter, axis_name="seq", tiled=True)
    gate_grad = scatter(gatew_low, scatter_dimension=0).astype(F32)
    up_grad = scatter(upw_low, scatter_dimension=0).astype(F32)
    down_grad = scatter(down_low, scatter_dimension=1).astype(F32)

    res_all, swish_low, value_low, qk_low, normed_one_grad, mlp_out = mixer_back(
        block_fac, res_low, output_weight, query_weight, key_weight, value_weight, swish_weight,
        query, key, value, swish_pre, mixed, prior, mlp_parts, decay_mat, query_fac, key_fac,
        cosine, sine, 2,
    )
    outputs = (hidden_res + mlp_out).astype(BF)
    _, pull_one = jax.vjp(layer_norm, inputs_full, attn_gain, attn_bias)
    input_back, attngain_part, attnbias_part = pull_one(normed_one_grad)
    input_grad = (res_grad + input_back).astype(BF)

    seqs, tps = lax.axis_size("seq"), lax.axis_size("tp")
    each = model // (seqs * tps)
    vectors = jnp.stack([attngain_part, attnbias_part, mlpgain_part, mlpbias_part])
    vectors = vectors.reshape(4, seqs, tps, each).transpose(2, 1, 0, 3).reshape(tps, seqs, 4 * each)
    vectors = jnp.pad(vectors, ((0, 0), (0, 0), (0, 1024 - 4 * each))).reshape(tps, seqs, 8, 128)
    sums, vector_sums = weight_sums(
        (flat(one_all), flat(res_all)), (swish_low, gated, value_low, qk_low), vectors, (0, 1, 0, 0), 3
    )
    vector_sums = vector_sums.reshape(-1)[: 4 * each].reshape(4, each)
    return (
        outputs[None],
        input_grad[None],
        sums[3, :, : heads * DK],
        sums[3, :, heads * DK :],
        sums[2],
        sums[0],
        sums[1].T,
        gate_grad,
        up_grad,
        down_grad,
        vector_sums[0],
        vector_sums[1],
        vector_sums[2],
        vector_sums[3],
    )


def solution(mesh):
    return jax.shard_map(
        shards,
        mesh=mesh,
        in_specs=(
            P("tp", "seq", None),
            P(None, "tp"),
            P(None, "tp"),
            P(None, "tp"),
            P(None, "tp"),
            P("tp", None),
            P(None, "tp"),
            P(None, "tp"),
            P("tp", None),
            P(),
            P(),
            P(),
            P(),
            P("tp", "seq", None),
        ),
        out_specs=(
            P("tp", "seq", None),
            P("tp", "seq", None),
            P("seq", "tp"),
            P("seq", "tp"),
            P("seq", "tp"),
            P("seq", "tp"),
            P("tp", "seq"),
            P("seq", "tp"),
            P("seq", "tp"),
            P("tp", "seq"),
            P(("seq", "tp")),
            P(("seq", "tp")),
            P(("seq", "tp")),
            P(("seq", "tp")),
        ),
        check_vma=False,
    )
```

```python
import functools

import jax
import jax.numpy as jnp
from jax import lax
from jax.experimental import pallas as pl
from jax.experimental.pallas import tpu as pltpu
from jax.sharding import PartitionSpec as P

DK = 256
DV = 512


EPS = 1e-05
MESH = pl.DeviceIdType.MESH
BF = jnp.bfloat16
F32 = jnp.float32
VMEM_LIMIT = 60 * 1024 * 1024


def remote(src, dst, ssem, rsem, slot, dev):
    return pltpu.make_async_remote_copy(
        src_ref=src,
        dst_ref=dst,
        send_sem=ssem.at[slot],
        recv_sem=rsem.at[slot],
        device_id=dev,
        device_id_type=MESH,
    )


def greet(devs):
    barrier = pltpu.get_barrier_semaphore()
    for dev in devs:
        pl.semaphore_signal(barrier, inc=1, device_id=dev, device_id_type=MESH)
    pl.semaphore_wait(barrier, len(devs))


def params(cid):
    return pltpu.CompilerParams(
        collective_id=cid, has_side_effects=True, vmem_limit_bytes=VMEM_LIMIT
    )


class Gather:
    def __init__(self, n, x, o, ssem, rsem, base=0):
        s, t = lax.axis_index("seq"), lax.axis_index("tp")
        self.n, self.t = n, t
        rows = x.shape[0]
        if n == 4:
            px, py = t + 1 - 2 * (t % 2), (t + 2) % 4
            dx, dy = (s, px), (s, py)
            self.peers = [dx, dy]
            half = rows // 2
            lo, hi = pl.ds(0, half), pl.ds(half, half)
            self.first = [
                remote(x.at[lo], o.at[base + t, lo], ssem, rsem, 0, dx),
                remote(x.at[hi], o.at[base + t, hi], ssem, rsem, 1, dy),
                remote(x.at[hi], o.at[base + t, hi], ssem, rsem, 2, dx),
                remote(x.at[lo], o.at[base + t, lo], ssem, rsem, 3, dy),
            ]
            self.relay = [
                remote(o.at[base + px, lo], o.at[base + px, lo], ssem, rsem, 4, dy),
                remote(o.at[base + py, hi], o.at[base + py, hi], ssem, rsem, 5, dx),
            ]
        else:
            self.peers = [(s, (t + k) % n) for k in range(1, n)]
            self.first = [
                remote(x, o.at[base + t], ssem, rsem, k, dev) for k, dev in enumerate(self.peers)
            ]
            self.relay = []

    def source(self, i):
        t = self.t
        if self.n == 4:
            near = jnp.where(i == 1, t + 1 - 2 * (t % 2), (t + 2) % 4)
            return jnp.where(i == 0, t, jnp.where(i == 3, 3 - t, near))
        return (t - i + self.n) % self.n

    def start(self):
        for copy in self.first:
            copy.start()

    def arrive(self, i):
        if self.n == 4:

            @pl.when(i == 1)
            def _():
                self.first[0].wait_recv()
                self.relay[0].start()
                self.first[1].wait_recv()
                self.relay[1].start()
                self.first[2].wait_recv()

            @pl.when(i == 2)
            def _():
                self.first[3].wait_recv()

            @pl.when(i == 3)
            def _():
                self.relay[0].wait_recv()
                self.relay[1].wait_recv()

        else:
            for k, copy in enumerate(self.first):

                @pl.when(i == k + 1)
                def _(copy=copy):
                    copy.wait_recv()

    def drain(self):
        for copy in self.first + self.relay:
            copy.wait_send()


class Scatter:
    def __init__(self, n, parts, near, far, hold, ssem, rsem):
        s, t = lax.axis_index("seq"), lax.axis_index("tp")
        self.n, self.t = n, t
        self.parts, self.near, self.far, self.hold = parts, near, far, hold
        if n == 4:
            self.px, self.py, pd = t + 1 - 2 * (t % 2), (t + 2) % 4, 3 - t
            dx, dy = (s, self.px), (s, self.py)
            self.peers = [dx, dy]
            half = parts.shape[-1] // 2
            self.cols = a, b = pl.ds(0, half), pl.ds(half, half)
            self.far_a = remote(parts.at[pd, :, a], near.at[0, 1], ssem, rsem, 0, dx)
            self.far_b = remote(parts.at[pd, :, b], near.at[1, 1], ssem, rsem, 1, dy)
            self.near_a = remote(parts.at[self.px, :, a], near.at[0, 0], ssem, rsem, 2, dx)
            self.near_b = remote(parts.at[self.py, :, b], near.at[1, 0], ssem, rsem, 3, dy)
            self.sum_a = remote(hold.at[0], far.at[0], ssem, rsem, 4, dy)
            self.sum_b = remote(hold.at[1], far.at[1], ssem, rsem, 5, dx)
            self.copies = [self.far_a, self.far_b, self.near_a, self.near_b, self.sum_a, self.sum_b]
        else:
            self.peers = [(s, (t + k) % n) for k in range(1, n)]
            self.copies = [
                remote(parts.at[(t - k + n) % n], near.at[k - 1], ssem, rsem, k - 1, (s, (t - k + n) % n))
                for k in range(1, n)
            ]

    def send(self, i):
        if self.n == 4:

            @pl.when(i == 1)
            def _():
                self.near_a.start()

            @pl.when(i == 2)
            def _():
                self.near_b.start()

            @pl.when(i == 3)
            def _():
                self.far_a.start()
                self.far_b.start()

        else:
            for k, copy in enumerate(self.copies):

                @pl.when(i == k + 1)
                def _(copy=copy):
                    copy.start()

    def relay(self):
        if self.n == 4:
            a, b = self.cols
            self.far_a.wait_recv()
            self.hold[0] = (
                self.parts[self.py, :, a].astype(F32) + self.near[0, 1].astype(F32)
            ).astype(BF)
            self.sum_a.start()
            self.far_b.wait_recv()
            self.hold[1] = (
                self.parts[self.px, :, b].astype(F32) + self.near[1, 1].astype(F32)
            ).astype(BF)
            self.sum_b.start()

    def finish(self, write):
        if self.n == 4:
            for side, (one, two) in enumerate(
                ((self.near_a, self.sum_a), (self.near_b, self.sum_b))
            ):
                one.wait_recv()
                two.wait_recv()
                write(
                    self.cols[side],
                    self.parts[self.t, :, self.cols[side]].astype(F32)
                    + self.near[side, 0].astype(F32)
                    + self.far[side].astype(F32),
                )
        else:
            total = self.parts[self.t].astype(F32)
            for k, copy in enumerate(self.copies):
                copy.wait_recv()
                total = total + self.near[k].astype(F32)
            write(slice(None), total)

    def drain(self):
        for copy in self.copies:
            copy.wait_send()


def scatter_scratch(n, rows, width):
    if n == 4:
        near, far = (2, 2, rows, width // 2), (2, rows, width // 2)
    else:
        near, far = (n - 1, rows, width), (1, 16, 128)
    return [pltpu.VMEM(near, BF), pltpu.VMEM(far, BF), pltpu.VMEM(far, BF)]


class Ends:
    def __init__(self, chips):
        s, t = lax.axis_index("seq"), lax.axis_index("tp")
        chip, span = s // 2, 2 * chips
        self.gives = (chip == 0) | (chip == chips - 1)
        self.takes = (chip == 1) | (chip == chips - 2)
        self.peers = [((s + 2) % span, t), ((s - 2 + span) % span, t)]
        step = jnp.where(chip == 0, 2, jnp.where(chip == chips - 1, span - 2, 0))
        self.mate = ((s + step) % span, t)


class Chain:
    def __init__(self, chips, heads, flip, fac, local, out, pair, enter, ps, pr, zs, zr, bs, br):
        s, t = lax.axis_index("seq"), lax.axis_index("tp")
        core, chip, span = s % 2, s // 2, 2 * chips
        self.chips, self.heads, self.fac = chips, heads, fac
        self.local, self.out, self.pair, self.enter, self.leave = local, out, pair, enter, local
        self.sems = ps, pr, zs, zr, bs, br
        self.partner = (s + 1 - 2 * core, t)
        above, below = ((s + 2) % span, t), ((s - 2 + span) % span, t)
        self.peers = [self.partner, above, below]
        if flip:
            self.first, self.place, self.ahead = core == 1, chips - 1 - chip, below
        else:
            self.first, self.place, self.ahead = core == 0, chip, above
        self.last = jnp.logical_not(self.first)

    def give(self, p):
        return remote(self.local.at[p], self.pair.at[p], self.sems[0], self.sems[1], p, self.partner)

    def back(self, p):
        return remote(self.enter.at[p], self.out.at[p], self.sems[4], self.sems[5], p, self.partner)

    def onward(self, p):
        return remote(self.leave.at[p], self.enter.at[p], self.sems[2], self.sems[3], p, self.ahead)

    def begin(self, p):
        @pl.when(self.first)
        def _():
            self.give(p).start()

            @pl.when(self.place == 0)
            def _():
                self.out[p] = jnp.zeros(self.out.shape[1:], BF)

    def step(self, p):
        @pl.when(self.first)
        def _():
            @pl.when(self.place > 0)
            def _():
                self.back(p).wait_recv()

        @pl.when(self.last)
        def _():
            fac = self.fac[p % self.heads]
            self.give(p).wait_recv()
            early = self.pair[p].astype(F32)
            chip_sum = early * fac + self.local[p].astype(F32)

            @pl.when(self.place == 0)
            def _():
                self.leave[p] = chip_sum.astype(BF)
                self.out[p] = self.pair[p]

            @pl.when(self.place > 0)
            def _():
                self.onward(p).wait_recv()
                self.back(p).start()
                came = self.enter[p].astype(F32)
                self.leave[p] = (came * (fac * fac) + chip_sum).astype(BF)
                self.out[p] = (came * fac + early).astype(BF)

            @pl.when(self.place < self.chips - 1)
            def _():
                self.onward(p).start()

    def drain(self, p):
        @pl.when(self.first)
        def _():
            self.give(p).wait_send()

        @pl.when(self.last)
        def _():
            @pl.when(self.place > 0)
            def _():
                self.back(p).wait_send()

            @pl.when(self.place < self.chips - 1)
            def _():
                self.onward(p).wait_send()


def chain_scratch(pieces):
    dma = pltpu.SemaphoreType.DMA
    return [pltpu.VMEM((pieces, DK, DV), BF)] * 2 + [dma((pieces,))] * 6


def dot(a, b, ca=1, cb=0):
    return lax.dot_general(a, b, (((ca,), (cb,)), ((), ())), preferred_element_type=F32)


def turn(v, cos, sin):
    lo, hi = v[:, : DK // 2], v[:, DK // 2 :]
    return jnp.concatenate([lo * cos - hi * sin, hi * cos + lo * sin], 1)


def turn_back(g, cos, sin):
    lo, hi = g[:, : DK // 2], g[:, DK // 2 :]
    return jnp.concatenate([lo * cos + hi * sin, hi * cos - lo * sin], 1)


def norm_of(m):
    center = m - jnp.mean(m, -1, keepdims=True)
    inv = lax.rsqrt(jnp.mean(center * center, -1, keepdims=True) + EPS)
    return center * inv, inv


class LineSums:
    def __init__(self, chips, lo, hi, wide, deep, kinds, refs, swap=False):
        s, t = lax.axis_index("seq"), lax.axis_index("tp")
        self.core, self.chip, self.chips, self.lo, self.hi = s % 2, s // 2, chips, lo, hi
        self.wide, self.deep, self.kinds = wide, deep, kinds
        (
            self.xs, self.ys, self.buf, self.out,
            self.xsem, self.ysem, self.psx, self.prx, self.psy, self.pry, self.ssem, self.rsem,
        ) = refs
        self.units = len(deep)
        self.swap = swap
        self.tokens = self.ys.shape[1] // 2
        self.cut = self.xs.shape[3]
        span = 2 * chips
        self.partner = (s + 1 - 2 * self.core, t)
        self.above = ((s + 2) % span, t)
        self.below = ((s - 2 + span) % span, t)
        self.peers = [self.partner, self.above, self.below]

    def cols(self, j, core):
        return pl.ds(pl.multiple_of((2 * j + core) * self.cut, self.cut), self.cut)

    def wide_own(self, kind, j):
        return pltpu.make_async_copy(
            self.wide[kind].at[:, self.cols(j, self.core)],
            self.xs.at[kind, j, pl.ds(0, self.tokens)],
            self.xsem.at[kind, j],
        )

    def wide_give(self, kind, j):
        return pltpu.make_async_remote_copy(
            src_ref=self.wide[kind].at[:, self.cols(j, 1 - self.core)],
            dst_ref=self.xs.at[kind, j, pl.ds(self.tokens, self.tokens)],
            send_sem=self.psx.at[kind, j],
            recv_sem=self.prx.at[kind, j],
            device_id=self.partner,
            device_id_type=MESH,
        )

    def deep_own(self, u):
        return pltpu.make_async_copy(
            self.deep[u], self.ys.at[u, pl.ds(0, self.tokens)], self.ysem.at[u]
        )

    def deep_give(self, u):
        return remote(
            self.deep[u], self.ys.at[u, pl.ds(self.tokens, self.tokens)], self.psy, self.pry, u,
            self.partner,
        )

    def adds(self):
        return (self.chip >= self.lo) & (self.chip <= self.hi)

    def share(self, u):
        @pl.when(self.adds())
        def _():
            if self.kinds[u] not in self.kinds[:u]:
                for j in range(self.chips):
                    self.wide_give(self.kinds[u], j).start()
                    self.wide_own(self.kinds[u], j).start()
            self.deep_give(u).start()
            self.deep_own(u).start()

    def ready(self, u):
        @pl.when(self.adds())
        def _():
            self.deep_own(u).wait()
            self.deep_give(u).wait_recv()
            if self.kinds[u] not in self.kinds[:u]:
                for j in range(self.chips):
                    self.wide_own(self.kinds[u], j).wait()
                    self.wide_give(self.kinds[u], j).wait_recv()

    def up(self, u, j):
        return remote(
            self.buf.at[u, j], self.buf.at[u, j], self.ssem.at[u], self.rsem.at[u], j, self.above
        )

    def down(self, u, j):
        slot = jnp.where(j == self.chip - 1, self.chips, j)
        return pltpu.make_async_remote_copy(
            src_ref=self.buf.at[u, j],
            dst_ref=self.buf.at[u, slot],
            send_sem=self.ssem.at[u, j],
            recv_sem=self.rsem.at[u, slot],
            device_id=self.below,
            device_id_type=MESH,
        )

    def arrived(self, u, slot):
        remote(
            self.buf.at[u, slot], self.buf.at[u, slot], self.ssem.at[u], self.rsem.at[u], slot,
            self.above,
        ).wait_recv()
        return self.buf[u, slot].astype(F32)

    def product(self, u, j):
        kind = 0
        for w in range(self.units):
            if self.kinds[w]:
                kind = kind + jnp.where(u == w, self.kinds[w], 0)
        if self.swap:
            return dot(self.ys[u], self.xs[kind, j], 0, 0)
        return dot(self.xs[kind, j], self.ys[u], 0, 0)

    def order(self, k):
        rights = self.chips - 1 - self.chip
        return jnp.where(
            self.chip < self.chips // 2,
            jnp.where(k < rights, self.chips - 1 - k, k - rights),
            jnp.where(k < self.chip, k, self.chips - 1 - (k - self.chip)),
        )

    def step(self, u, k):
        chip = self.chip
        j = self.order(k)

        @pl.when(self.adds())
        def _():
            total = self.product(u, j)

            @pl.when(((j > chip) & (chip == self.lo)) | ((j < chip) & (chip == self.hi)))
            def _():
                self.buf[u, j] = total.astype(BF)

            @pl.when(((j > chip) & (chip > self.lo)) | ((j < chip) & (chip < self.hi)))
            def _():
                self.buf[u, j] = (total + self.arrived(u, j)).astype(BF)

            @pl.when(j > chip)
            def _():
                self.up(u, j).start()

            @pl.when(j < chip)
            def _():
                self.down(u, j).start()

    def finish(self, u):
        chip = self.chip

        @pl.when(self.adds())
        def _():
            self.out[u] = self.product(u, chip)

        @pl.when((chip < self.lo) | (chip > self.hi))
        def _():
            self.out[u] = jnp.zeros(self.out.shape[1:], F32)

        @pl.when(chip > self.lo)
        def _():
            self.out[u] += self.arrived(u, chip)

        @pl.when(chip < self.hi)
        def _():
            self.out[u] += self.arrived(u, self.chips)

    def drain(self):
        @pl.when(self.adds())
        def _():
            @pl.loop(0, self.units)
            def _(u):
                @pl.loop(0, self.chips)
                def _(j):
                    @pl.when(j > self.chip)
                    def _():
                        self.up(u, j).wait_send()

                    @pl.when(j < self.chip)
                    def _():
                        self.down(u, j).wait_send()

            for u in range(self.units):
                self.deep_give(u).wait_send()
            for kind in range(max(self.kinds) + 1):
                for j in range(self.chips):
                    self.wide_give(kind, j).wait_send()


def line_scratch(chips, units, kinds, tokens, cut, width, swap=False):
    dma = pltpu.SemaphoreType.DMA
    block = (width, cut) if swap else (cut, width)
    return [
        pltpu.VMEM((kinds, chips, 2 * tokens, cut), BF),
        pltpu.VMEM((units, 2 * tokens, width), BF),
        pltpu.VMEM((units, chips + 1) + block, BF),
        pltpu.VMEM((units,) + block, F32),
        dma((kinds, chips)),
        dma((units,)),
        dma((kinds, chips)),
        dma((kinds, chips)),
        dma((units,)),
        dma((units,)),
        dma((units, chips + 1)),
        dma((units, chips + 1)),
    ]


def mixer_kernel(n, chips, heads, *refs):
    (
        fac, x, og, wk_h, wv_h, wq_h, ws_h, wo_h, decay, qfac, kfac, cos, sin,
        x_all, og_all, q, k, v, sp, mx, prior, gated, attn,
        wk, wv, wq, ws, wo, acc, parts, local,
    ) = refs[:31]
    near, far, hold = refs[31:34]
    chain_refs = refs[34:42]
    wsem, gs, gr, os, orr, ss, sr, og_near, es, er, ns, nr = refs[42:]
    rows = x.shape[0]
    gather = Gather(n, x, x_all, gs, gr)
    gather_og = Gather(n, og, og_all, os, orr)
    ends = Ends(chips)
    gather_near = Gather(n, og_near, og_all, ns, nr, n)
    hand = remote(og, og_near, es, er, 0, ends.mate)
    scatter = Scatter(n, parts, near, far, hold, ss, sr)
    chain = Chain(chips, heads, False, fac, local, prior, *chain_refs)
    loads = [
        pltpu.make_async_copy(a, w, wsem.at[i])
        for i, (a, w) in enumerate(((wk_h, wk), (wv_h, wv), (wq_h, wq), (ws_h, ws), (wo_h, wo)))
    ]
    for load in loads:
        load.start()
    greet(gather.peers + chain.peers)
    gather.start()
    gather_og.start()

    @pl.when(ends.gives)
    def _():
        hand.start()

    me = gather.source(0)
    x_all[me] = x[...]
    og_all[me] = og[...]
    for load in loads[:4]:
        load.wait()

    @pl.loop(0, n)
    def _(i):
        j = gather.source(i)
        gather.arrive(i)
        at = pl.ds(pl.multiple_of(j * rows, rows), rows)
        acc[:, : heads * DK] = dot(x_all[j], wk[...])
        v[at] = dot(x_all[j], wv[...]).astype(BF)
        for h in range(heads):
            vc = slice(h * DV, (h + 1) * DV)
            kc = slice(h * DK, (h + 1) * DK)
            key = turn(acc[:, kc], cos[...], sin[...]).astype(BF)
            k[at, kc] = key
            key_dec = (key.astype(F32) * kfac[h]).astype(BF)
            p = j * heads + h
            local[p] = dot(key_dec, v[at, vc], 0, 0).astype(BF)
            chain.begin(p)
        acc[:, : heads * DK] = dot(x_all[j], wq[...])
        for h in range(heads):
            kc = slice(h * DK, (h + 1) * DK)
            q[at, kc] = turn(acc[:, kc], cos[...], sin[...]).astype(BF)
        sp[at] = dot(x_all[j], ws[...])

    loads[4].wait()

    @pl.when(ends.takes)
    def _():
        hand.wait_recv()
        gather_near.start()
        og_all[n + me] = og_near[...]

    @pl.loop(0, n)
    def _(step):
        i = (step + 1) % n
        j = gather.source(i)
        gather_og.arrive(i)

        @pl.when(ends.takes & (step > 0))
        def _():
            gather_near.arrive(step)

        at = pl.ds(pl.multiple_of(j * rows, rows), rows)
        for h in range(heads):
            vc = slice(h * DV, (h + 1) * DV)
            kc = slice(h * DK, (h + 1) * DK)
            p = j * heads + h
            query = q[at, kc]
            scores = (dot(query, k[at, kc], 1, 1) * decay[h]).astype(BF)
            mx[at, vc] = dot(scores, v[at, vc])
            query_dec = (query.astype(F32) * qfac[h]).astype(BF)
            chain.step(p)
            mx[at, vc] += dot(query_dec, prior[p])
            pre = sp[at, vc]
            gated[at, vc] = (pre * jax.nn.sigmoid(pre) * norm_of(mx[at, vc])[0]).astype(BF)
        parts[j] = dot(gated[at], wo[...]).astype(BF)
        scatter.send(i)

    scatter.relay()

    def write(cols, total):
        attn[:, cols] = total

    scatter.finish(write)
    gather.drain()
    gather_og.drain()

    @pl.when(ends.gives)
    def _():
        hand.wait_send()

    @pl.when(ends.takes)
    def _():
        gather_near.drain()

    scatter.drain()

    @pl.loop(0, n * heads)
    def _(p):
        chain.drain(p)


def mixer(fac, x, og, wk, wv, wq, ws, wo, decay, qfac, kfac, cos, sin, cid):
    n = lax.axis_size("tp")
    chips = lax.axis_size("seq") // 2
    rows, model = x.shape
    heads = wk.shape[1] // DK
    pieces = n * heads
    total = n * rows
    dma = pltpu.SemaphoreType.DMA
    sems = max(6, n - 1)
    vmem = pl.BlockSpec(memory_space=pltpu.VMEM)
    hbm = pl.BlockSpec(memory_space=pl.ANY)
    shape = jax.ShapeDtypeStruct
    return pl.pallas_call(
        functools.partial(mixer_kernel, n, chips, heads),
        out_shape=(
            shape((n, rows, model), BF),
            shape((2 * n, rows, model), BF),
            shape((total, heads * DK), BF),
            shape((total, heads * DK), BF),
            shape((total, heads * DV), BF),
            shape((total, heads * DV), F32),
            shape((total, heads * DV), F32),
            shape((pieces, DK, DV), BF),
            shape((total, heads * DV), BF),
            shape((rows, model), F32),
        ),
        in_specs=[pl.BlockSpec(memory_space=pltpu.SMEM), vmem, vmem] + [hbm] * 5 + [vmem] * 5,
        out_specs=(vmem,) * 10,
        scratch_shapes=[pltpu.VMEM(w.shape, BF) for w in (wk, wv, wq, ws, wo)]
        + [
            pltpu.VMEM((rows, heads * DK), F32),
            pltpu.VMEM((n, rows, model), BF),
            pltpu.VMEM((pieces, DK, DV), BF),
        ]
        + scatter_scratch(n, rows, model)
        + chain_scratch(pieces)
        + [dma((5,))]
        + [dma((sems,))] * 6
        + [pltpu.VMEM((rows, model), BF), dma((1,)), dma((1,)), dma((sems,)), dma((sems,))],
        compiler_params=params(cid),
        name="mixer",
    )(fac, x, og, wk, wv, wq, ws, wo, decay, qfac, kfac, cos, sin)


GELU_C = 0.7978845608028654
GELU_A = 0.044715


def mlp_kernel(n, chips, *refs):
    (
        x, og_all, wg_h, wu_h, wd_h,
        x_all, hidden, gate_low, upper_low, mlp_parts, grad_two,
        wg, wu, wd, hg, acc_g, acc_u, acc, parts, near, far, hold,
        wsem, gs, gr, ss, sr, es, er,
    ) = refs
    rows = x.shape[0]
    gather = Gather(n, x, x_all, gs, gr)
    scatter = Scatter(n, parts, near, far, hold, ss, sr)
    ends = Ends(chips)
    loads = [
        pltpu.make_async_copy(a, w, wsem.at[i])
        for i, (a, w) in enumerate(((wd_h, wd), (wg_h, wg), (wu_h, wu)))
    ]
    for load in loads:
        load.start()
    greet(gather.peers + ends.peers)
    gather.start()
    me = gather.source(0)
    x_all[me] = x[...]
    loads[0].wait()

    def hand(i):
        j = gather.source(i)
        return remote(x_all.at[j], x_all.at[n + j], es, er, i, ends.mate)

    @pl.loop(0, n)
    def _(j):
        at = pl.ds(pl.multiple_of(j * rows, rows), rows)
        hg[at] = dot(og_all[j], wd[...], 1, 1)

    loads[1].wait()
    loads[2].wait()
    slab = 16

    def units(block, back_at):
        start = pl.multiple_of(block * rows, rows)
        acc_g[...] = dot(x_all[block], wg[...])
        acc_u[...] = dot(x_all[block], wu[...])

        @pl.loop(0, rows // slab)
        def _(r):
            here = pl.ds(pl.multiple_of(r * slab, slab), slab)
            there = pl.ds(pl.multiple_of(start + r * slab, slab), slab)
            g, u = acc_g[here], acc_u[here]
            back = hg[pl.ds(pl.multiple_of(back_at + r * slab, slab), slab)]
            square = g * g
            th = jnp.tanh(GELU_C * (g + GELU_A * (square * g)))
            half = 0.5 * (1.0 + th)
            gelu = g * half
            slope = half + 0.5 * g * (1.0 - th * th) * (GELU_C * (1.0 + 3.0 * GELU_A * square))
            hidden[there] = (gelu * u).astype(BF)
            gate_low[there] = (back * u * slope).astype(BF)
            upper_low[there] = (back * gelu).astype(BF)

    @pl.loop(0, n)
    def _(i):
        j = gather.source(i)
        gather.arrive(i)

        @pl.when(ends.gives)
        def _():
            hand(i).start()

        units(j, j * rows)
        at = pl.ds(pl.multiple_of(j * rows, rows), rows)
        acc[...] = dot(gate_low[at], wg[...], 1, 1)
        parts[j] = (acc[...] + dot(upper_low[at], wu[...], 1, 1)).astype(BF)
        scatter.send(i)

    def extra(i):
        @pl.when(ends.takes)
        def _():
            j = gather.source(i)
            hg[pl.ds(0, rows)] = dot(og_all[n + j], wd[...], 1, 1)
            hand(i).wait_recv()
            units(n + j, 0)

    @pl.loop(0, n // 2)
    def _(i):
        extra(i)

    scatter.relay()

    @pl.loop(0, n)
    def _(j):
        at = pl.ds(pl.multiple_of(j * rows, rows), rows)
        mlp_parts[j] = dot(hidden[at], wd[...]).astype(BF)

    def write(cols, total):
        grad_two[:, cols] = total

    scatter.finish(write)

    @pl.loop(n // 2, n)
    def _(i):
        extra(i)

    gather.drain()
    scatter.drain()

    @pl.when(ends.gives)
    def _():
        @pl.loop(0, n)
        def _(i):
            hand(i).wait_send()


def mlp(x, og_all, wg, wu, wd, cid):
    n = lax.axis_size("tp")
    chips = lax.axis_size("seq") // 2
    rows, model = x.shape
    width = wg.shape[1]
    total = n * rows
    dma = pltpu.SemaphoreType.DMA
    sems = max(6, n - 1)
    vmem = pl.BlockSpec(memory_space=pltpu.VMEM)
    hbm = pl.BlockSpec(memory_space=pl.ANY)
    shape = jax.ShapeDtypeStruct
    return pl.pallas_call(
        functools.partial(mlp_kernel, n, chips),
        out_shape=(
            shape((2 * n, rows, model), BF),
            shape((2 * total, width), BF),
            shape((2 * total, width), BF),
            shape((2 * total, width), BF),
            shape((n, rows, model), BF),
            shape((rows, model), F32),
        ),
        in_specs=[vmem, vmem] + [hbm] * 3,
        out_specs=(vmem,) * 6,
        scratch_shapes=[pltpu.VMEM(w.shape, BF) for w in (wg, wu, wd)]
        + [
            pltpu.VMEM((total, width), F32),
            pltpu.VMEM((rows, width), F32),
            pltpu.VMEM((rows, width), F32),
            pltpu.VMEM((rows, model), F32),
            pltpu.VMEM((n, rows, model), BF),
        ]
        + scatter_scratch(n, rows, model)
        + [dma((3,))]
        + [dma((sems,))] * 4
        + [dma((n,)), dma((n,))],
        compiler_params=params(cid),
        name="mlp",
    )(x, og_all, wg, wu, wd)


def mixer_back_kernel(n, chips, heads, *refs):
    (
        fac, res, wo_h, wq_h, wk_h, wv_h, ws_h, q, k, v, sp, mx, prior, mlp_parts, decay, qfac, kfac, cos, sin,
        res_all, swish_low, value_low, qk_low, grad_one, mlp_out,
        wo, wq, wk, wv, ws, mixed_low, acc, parts, local, later,
    ) = refs[:35]
    near, far, hold, mlp_near, mlp_far, mlp_hold = refs[35:41]
    chain_refs = refs[41:49]
    wsem, gs, gr, ss, sr, ms, mr = refs[49:]
    rows = res.shape[0]
    gather = Gather(n, res, res_all, gs, gr)
    scatter = Scatter(n, parts, near, far, hold, ss, sr)
    scatter_mlp = Scatter(n, mlp_parts, mlp_near, mlp_far, mlp_hold, ms, mr)
    chain = Chain(chips, heads, True, fac, local, later, *chain_refs)
    loads = [
        pltpu.make_async_copy(a, w, wsem.at[i])
        for i, (a, w) in enumerate(((wo_h, wo), (ws_h, ws), (wq_h, wq), (wk_h, wk), (wv_h, wv)))
    ]
    for load in loads:
        load.start()
    greet(gather.peers + chain.peers)
    gather.start()
    me = gather.source(0)
    res_all[me] = res[...]
    loads[0].wait()

    @pl.loop(0, n)
    def _(i):
        j = gather.source(i)
        gather.arrive(i)
        at = pl.ds(pl.multiple_of(j * rows, rows), rows)
        acc[:, : heads * DV] = dot(res_all[j], wo[...], 1, 1)
        for h in range(heads):
            vc = slice(h * DV, (h + 1) * DV)
            kc = slice(h * DK, (h + 1) * DK)
            back = acc[:, vc]
            normed, inv = norm_of(mx[at, vc])
            pre = sp[at, vc]
            sig = jax.nn.sigmoid(pre)
            swish_low[at, vc] = (back * normed * (sig * (1.0 + pre * (1.0 - sig)))).astype(BF)
            g = back * (pre * sig)
            g = inv * (
                g
                - jnp.mean(g, -1, keepdims=True)
                - normed * jnp.mean(g * normed, -1, keepdims=True)
            )
            g = g.astype(BF)
            mixed_low[at, vc] = g
            query_dec = (q[at, kc].astype(F32) * qfac[h]).astype(BF)
            p = j * heads + h
            local[p] = dot(query_dec, g, 0, 0).astype(BF)
            chain.begin(p)

    for load in loads[1:]:
        load.wait()
    for i in range(1, n):
        scatter_mlp.send(i)

    @pl.loop(0, n)
    def _(step):
        i = (step + 1) % n
        j = gather.source(i)
        at = pl.ds(pl.multiple_of(j * rows, rows), rows)
        for h in range(heads):
            vc = slice(h * DV, (h + 1) * DV)
            kc = slice(h * DK, (h + 1) * DK)
            p = j * heads + h
            g, value, query, key = mixed_low[at, vc], v[at, vc], q[at, kc], k[at, kc]
            raw_low = (dot(g, value, 1, 1) * decay[h]).astype(BF)
            query_back = dot(raw_low, key) + dot(g, prior[p], 1, 1) * qfac[h]
            qk_low[at, kc] = turn_back(query_back, cos[...], sin[...]).astype(BF)
            scores = (dot(query, key, 1, 1) * decay[h]).astype(BF)
            key_part = dot(raw_low, query, 0, 0)
            value_part = dot(scores, g, 0, 0)
            key_dec = (key.astype(F32) * kfac[h]).astype(BF)
            chain.step(p)
            after = later[p]
            key_back = key_part + dot(value, after, 1, 1) * kfac[h]
            qk_low[at, slice((heads + h) * DK, (heads + h + 1) * DK)] = turn_back(
                key_back, cos[...], sin[...]
            ).astype(BF)
            value_low[at, vc] = (value_part + dot(key_dec, after)).astype(BF)
        acc[...] = dot(swish_low[at], ws[...], 1, 1)
        acc[...] += dot(value_low[at], wv[...], 1, 1)
        acc[...] += dot(qk_low[at, : heads * DK], wq[...], 1, 1)
        parts[j] = (acc[...] + dot(qk_low[at, heads * DK :], wk[...], 1, 1)).astype(BF)
        scatter.send(i)

        @pl.when(step == n - 2)
        def _():
            scatter_mlp.relay()

    scatter.relay()

    def write(cols, total):
        grad_one[:, cols] = total

    scatter.finish(write)

    def write_mlp(cols, total):
        mlp_out[:, cols] = total

    scatter_mlp.finish(write_mlp)
    gather.drain()
    scatter.drain()
    scatter_mlp.drain()

    @pl.loop(0, n * heads)
    def _(p):
        chain.drain(p)


def mixer_back(fac, res, wo, wq, wk, wv, ws, q, k, v, sp, mx, prior, mlp_parts, decay, qfac, kfac, cos, sin, cid):
    n = lax.axis_size("tp")
    chips = lax.axis_size("seq") // 2
    rows, model = res.shape
    heads = q.shape[1] // DK
    pieces = n * heads
    total = n * rows
    dma = pltpu.SemaphoreType.DMA
    sems = max(6, n - 1)
    vmem = pl.BlockSpec(memory_space=pltpu.VMEM)
    hbm = pl.BlockSpec(memory_space=pl.ANY)
    shape = jax.ShapeDtypeStruct
    return pl.pallas_call(
        functools.partial(mixer_back_kernel, n, chips, heads),
        out_shape=(
            shape((n, rows, model), BF),
            shape((total, heads * DV), BF),
            shape((total, heads * DV), BF),
            shape((total, 2 * heads * DK), BF),
            shape((rows, model), F32),
            shape((rows, model), F32),
        ),
        in_specs=[pl.BlockSpec(memory_space=pltpu.SMEM), vmem] + [hbm] * 5 + [vmem] * 12,
        out_specs=(vmem,) * 6,
        scratch_shapes=[pltpu.VMEM(w.shape, BF) for w in (wo, wq, wk, wv, ws)]
        + [
            pltpu.VMEM((total, heads * DV), BF),
            pltpu.VMEM((rows, model), F32),
            pltpu.VMEM((n, rows, model), BF),
            pltpu.VMEM((pieces, DK, DV), BF),
            pltpu.VMEM((pieces, DK, DV), BF),
        ]
        + scatter_scratch(n, rows, model)
        + scatter_scratch(n, rows, model)
        + chain_scratch(pieces)
        + [dma((5,))]
        + [dma((sems,))] * 6,
        compiler_params=params(cid),
        name="mixer_back",
    )(fac, res, wo, wq, wk, wv, ws, q, k, v, sp, mx, prior, mlp_parts, decay, qfac, kfac, cos, sin)


def weights_kernel(chips, *refs):
    (
        two, og, hidden, gate_low, up_low, one, res, swish_low, gated, value_low, qk_low, vec,
        down_o, gate_o, up_o, swish_o, mixer_o, value_o, query_o, key_o, vec_out,
    ) = refs[:21]
    mlp = LineSums(
        chips, 1, chips - 2, (two, og), (gate_low, up_low, hidden), (0, 0, 1), refs[21:33]
    )
    mix = LineSums(
        chips, 0, chips - 1, (one, res), (swish_low, gated, value_low, qk_low), (0, 1, 0, 0),
        refs[33:45],
    )
    turned, osem, vec_near, vec_sum, vec_far, vs, vr, us, ur = refs[45:]
    s, t = lax.axis_index("seq"), lax.axis_index("tp")
    span, tp = 2 * chips, vec.shape[0]
    ring = [((s + d) % span, t) for d in range(1, span)]
    cross = [(s, (t + d) % tp) for d in range(1, tp)]
    greet(ring + cross)
    vec_first = [
        remote(vec.at[(t + d) % tp], vec_near.at[d - 1], vs, vr, d - 1, cross[d - 1])
        for d in range(1, tp)
    ]
    vec_last = [
        remote(vec_sum.at[(s + d) % span], vec_far.at[d - 1], us, ur, d - 1, ring[d - 1])
        for d in range(1, span)
    ]
    for copy in vec_first:
        copy.start()
    for u in range(mix.units):
        if u < mlp.units:
            mlp.share(u)
        mix.share(u)

    @pl.loop(0, mix.units)
    def _(u):
        for w in range(mix.units):

            @pl.when(u == w)
            def _(w=w):
                if w < mlp.units:
                    mlp.ready(w)
                mix.ready(w)

        @pl.loop(0, chips - 1)
        def _(k):
            @pl.when(u < mlp.units)
            def _():
                mlp.step(u, k)

            mix.step(u, k)

        @pl.when(u == 0)
        def _():
            total = vec[t]
            for copy in vec_first:
                copy.wait_recv()
            vec_sum[...] = total + jnp.sum(vec_near[...], 0)
            for copy in vec_last:
                copy.start()

        @pl.when(u > 0)
        def _():
            mlp.finish(u - 1)
            mix.finish(u - 1)

    half = mix.out.shape[2] // 2
    lo, hi = pl.ds(0, half), pl.ds(half, half)
    turned[...] = mlp.out[2].T
    pairs = [
        (mlp.out.at[0], gate_o),
        (mlp.out.at[1], up_o),
        (mix.out.at[0], swish_o),
        (turned, down_o),
        (turned, mixer_o),
        (mix.out.at[2], value_o),
        (mix.out.at[3, :, lo], query_o),
        (mix.out.at[3, :, hi], key_o),
    ]
    copies = [pltpu.make_async_copy(a, b, osem.at[i]) for i, (a, b) in enumerate(pairs)]
    for i in (3, 0, 1, 2, 5):
        copies[i].start()
    copies[3].wait()
    turned[...] = mix.out[1].T
    copies[4].start()
    mix.finish(mix.units - 1)
    for copy in copies[6:]:
        copy.start()
    vec_total = vec_sum[s]
    for copy in vec_last:
        copy.wait_recv()
    vec_out[...] = vec_total + jnp.sum(vec_far[...], 0)
    for copy in vec_first + vec_last:
        copy.wait_send()
    mlp.drain()
    mix.drain()
    for i, copy in enumerate(copies):
        if i != 3:
            copy.wait()


def weight_sums(two, og, hidden, gate_low, up_low, one, res, swish_low, gated, value_low, qk_low, vec, cid):
    chips = lax.axis_size("seq") // 2
    tokens, model = one.shape
    width = gated.shape[1]
    mlp_tokens, mlp_width = gate_low.shape
    keys = qk_low.shape[1] // 2
    cut = model // (2 * chips)
    dma = pltpu.SemaphoreType.DMA
    vmem = pl.BlockSpec(memory_space=pltpu.VMEM)
    hbm = pl.BlockSpec(memory_space=pl.ANY)
    shape = lambda *a: jax.ShapeDtypeStruct(a, F32)
    ring, cross = 2 * chips - 1, vec.shape[0] - 1
    return pl.pallas_call(
        functools.partial(weights_kernel, chips),
        out_shape=(
            shape(mlp_width, cut),
            shape(cut, mlp_width),
            shape(cut, mlp_width),
            shape(cut, width),
            shape(width, cut),
            shape(cut, width),
            shape(cut, keys),
            shape(cut, keys),
            shape(*vec.shape[2:]),
        ),
        in_specs=[hbm] * 11 + [vmem],
        out_specs=(hbm,) * 8 + (vmem,),
        scratch_shapes=line_scratch(chips, 3, 2, mlp_tokens, cut, mlp_width)
        + line_scratch(chips, 4, 2, tokens, cut, width)
        + [
            pltpu.VMEM((width, cut), F32),
            dma((8,)),
            pltpu.VMEM((cross,) + vec.shape[1:], F32),
            pltpu.VMEM(vec.shape[1:], F32),
            pltpu.VMEM((ring,) + vec.shape[2:], F32),
            dma((cross,)),
            dma((cross,)),
            dma((ring,)),
            dma((ring,)),
        ],
        compiler_params=params(cid),
        name="weights",
    )(two, og, hidden, gate_low, up_low, one, res, swish_low, gated, value_low, qk_low, vec)


def layer_norm(values, gain, bias):
    center = values - jnp.mean(values, -1, keepdims=True)
    spread = jnp.mean(center * center, -1, keepdims=True)
    return center * lax.rsqrt(spread + EPS) * gain + bias


def shards(
    inputs,
    query_weight,
    key_weight,
    value_weight,
    swish_weight,
    output_weight,
    gate_weight,
    up_weight,
    down_weight,
    attn_gain,
    attn_bias,
    mlp_gain,
    mlp_bias,
    output_grad,
):
    _, rows, model = inputs.shape
    heads = query_weight.shape[1] // DK
    inputs_full = inputs[0].astype(F32)
    cotangent = output_grad[0]

    half_width = DK // 2
    frequencies = jnp.power(10000.0, -jnp.arange(half_width, dtype=F32) / half_width)
    steps_in = jnp.arange(rows, dtype=F32)
    positions = lax.axis_index("seq").astype(F32) * rows + steps_in
    angles = positions[:, None] * frequencies[None, :]
    cosine, sine = jnp.cos(angles), jnp.sin(angles)
    head_ids = (lax.axis_index("tp") * heads + jnp.arange(heads)).astype(F32)
    decays = 1.0 - jnp.exp2(-5.0 - head_ids)
    lag = steps_in[:, None] - steps_in[None, :]
    decay_mat = jnp.where(
        lag[None] >= 0, jnp.power(decays[:, None, None], jnp.maximum(lag, 0.0)[None]), 0.0
    )
    query_fac = jnp.power(decays[:, None], steps_in[None, :] + 1.0)[:, :, None]
    key_fac = jnp.power(decays[:, None], rows - 1.0 - steps_in[None, :])[:, :, None]
    block_fac = jnp.power(decays, rows * 1.0)

    normed_one = layer_norm(inputs_full, attn_gain, attn_bias).astype(BF)
    one_all, grad_all, query, key, value, swish_pre, mixed, prior, gated, attn_out = mixer(
        block_fac, normed_one, cotangent, key_weight, value_weight, query_weight, swish_weight,
        output_weight, decay_mat, query_fac, key_fac, cosine, sine, 0,
    )
    hidden_res = inputs_full + attn_out
    normed_two = layer_norm(hidden_res, mlp_gain, mlp_bias).astype(BF)
    two_all, hidden, gate_low, upper_low, mlp_parts, normed_two_grad = mlp(
        normed_two, grad_all, gate_weight, up_weight, down_weight, 1
    )
    flat = lambda a: a.reshape(-1, model)
    _, pull_two = jax.vjp(layer_norm, hidden_res, mlp_gain, mlp_bias)
    res_back, mlpgain_part, mlpbias_part = pull_two(normed_two_grad)
    res_grad = cotangent.astype(F32) + res_back
    res_all, swish_low, value_low, qk_low, normed_one_grad, mlp_out = mixer_back(
        block_fac, res_grad.astype(BF), output_weight, query_weight, key_weight, value_weight, swish_weight,
        query, key, value, swish_pre, mixed, prior, mlp_parts, decay_mat, query_fac, key_fac,
        cosine, sine, 2,
    )
    outputs = (hidden_res + mlp_out).astype(BF)
    _, pull_one = jax.vjp(layer_norm, inputs_full, attn_gain, attn_bias)
    input_back, attngain_part, attnbias_part = pull_one(normed_one_grad)
    input_grad = (res_grad + input_back).astype(BF)

    seqs, tps = lax.axis_size("seq"), lax.axis_size("tp")
    each = model // (seqs * tps)
    vectors = jnp.stack([attngain_part, attnbias_part, mlpgain_part, mlpbias_part])
    vectors = vectors.reshape(4, seqs, tps, each).transpose(2, 1, 0, 3).reshape(tps, seqs, 4 * each)
    vectors = jnp.pad(vectors, ((0, 0), (0, 0), (0, 1024 - 4 * each))).reshape(tps, seqs, 8, 128)
    down_grad, gate_grad, up_grad, swish_grad, mixer_grad, value_grad, query_grad, key_grad, vector_sums = (
        weight_sums(
            flat(two_all), flat(grad_all), hidden, gate_low, upper_low, flat(one_all), flat(res_all), swish_low, gated,
            value_low, qk_low, vectors, 3,
        )
    )
    vector_sums = vector_sums.reshape(-1)[: 4 * each].reshape(4, each)
    return (
        outputs[None],
        input_grad[None],
        query_grad,
        key_grad,
        value_grad,
        swish_grad,
        mixer_grad,
        gate_grad,
        up_grad,
        down_grad,
        vector_sums[0],
        vector_sums[1],
        vector_sums[2],
        vector_sums[3],
    )


def solution(mesh):
    return jax.shard_map(
        shards,
        mesh=mesh,
        in_specs=(
            P("tp", "seq", None),
            P(None, "tp"),
            P(None, "tp"),
            P(None, "tp"),
            P(None, "tp"),
            P("tp", None),
            P(None, "tp"),
            P(None, "tp"),
            P("tp", None),
            P(),
            P(),
            P(),
            P(),
            P("tp", "seq", None),
        ),
        out_specs=(
            P("tp", "seq", None),
            P("tp", "seq", None),
            P("seq", "tp"),
            P("seq", "tp"),
            P("seq", "tp"),
            P("seq", "tp"),
            P("tp", "seq"),
            P("seq", "tp"),
            P("seq", "tp"),
            P("tp", "seq"),
            P(("seq", "tp")),
            P(("seq", "tp")),
            P(("seq", "tp")),
            P(("seq", "tp")),
        ),
        check_vma=False,
    )
```

```python
import functools

import jax
import jax.numpy as jnp
from jax import lax
from jax.experimental import pallas as pl
from jax.experimental.pallas import tpu as pltpu
from jax.sharding import PartitionSpec as P

DK = 256
DV = 512


EPS = 1e-05
MESH = pl.DeviceIdType.MESH
BF = jnp.bfloat16
F32 = jnp.float32
VMEM_LIMIT = 61 * 1024 * 1024


def remote(src, dst, ssem, rsem, slot, dev):
    return pltpu.make_async_remote_copy(
        src_ref=src,
        dst_ref=dst,
        send_sem=ssem.at[slot],
        recv_sem=rsem.at[slot],
        device_id=dev,
        device_id_type=MESH,
    )


def greet(devs):
    barrier = pltpu.get_barrier_semaphore()
    for dev in devs:
        pl.semaphore_signal(barrier, inc=1, device_id=dev, device_id_type=MESH)
    pl.semaphore_wait(barrier, len(devs))


def params(cid):
    return pltpu.CompilerParams(
        collective_id=cid, has_side_effects=True, vmem_limit_bytes=VMEM_LIMIT
    )


class Gather:
    def __init__(self, n, x, o, ssem, rsem, base=0):
        s, t = lax.axis_index("seq"), lax.axis_index("tp")
        self.n, self.t = n, t
        rows = x.shape[0]
        if n == 4:
            px, py = t + 1 - 2 * (t % 2), (t + 2) % 4
            dx, dy = (s, px), (s, py)
            self.peers = [dx, dy]
            half = rows // 2
            lo, hi = pl.ds(0, half), pl.ds(half, half)
            self.first = [
                remote(x.at[lo], o.at[base + t, lo], ssem, rsem, 0, dx),
                remote(x.at[hi], o.at[base + t, hi], ssem, rsem, 1, dy),
                remote(x.at[hi], o.at[base + t, hi], ssem, rsem, 2, dx),
                remote(x.at[lo], o.at[base + t, lo], ssem, rsem, 3, dy),
            ]
            self.relay = [
                remote(o.at[base + px, lo], o.at[base + px, lo], ssem, rsem, 4, dy),
                remote(o.at[base + py, hi], o.at[base + py, hi], ssem, rsem, 5, dx),
            ]
        else:
            self.peers = [(s, (t + k) % n) for k in range(1, n)]
            self.first = [
                remote(x, o.at[base + t], ssem, rsem, k, dev) for k, dev in enumerate(self.peers)
            ]
            self.relay = []

    def source(self, i):
        t = self.t
        if self.n == 4:
            near = jnp.where(i == 1, t + 1 - 2 * (t % 2), (t + 2) % 4)
            return jnp.where(i == 0, t, jnp.where(i == 3, 3 - t, near))
        return (t - i + self.n) % self.n

    def start(self):
        for copy in self.first:
            copy.start()

    def relays(self):
        for copy, onward in zip(self.first, self.relay):
            copy.wait_recv()
            onward.start()

    def arrive(self, i):
        if self.n == 4:

            @pl.when(i == 1)
            def _():
                self.first[2].wait_recv()

            @pl.when(i == 2)
            def _():
                self.first[3].wait_recv()

            @pl.when(i == 3)
            def _():
                self.relay[0].wait_recv()
                self.relay[1].wait_recv()

        else:
            for k, copy in enumerate(self.first):

                @pl.when(i == k + 1)
                def _(copy=copy):
                    copy.wait_recv()

    def drain(self):
        for copy in self.first + self.relay:
            copy.wait_send()


class Scatter:
    def __init__(self, n, parts, near, far, hold, ssem, rsem):
        s, t = lax.axis_index("seq"), lax.axis_index("tp")
        self.n, self.t = n, t
        self.parts, self.near, self.far, self.hold = parts, near, far, hold
        if n == 4:
            self.px, self.py, pd = t + 1 - 2 * (t % 2), (t + 2) % 4, 3 - t
            dx, dy = (s, self.px), (s, self.py)
            self.peers = [dx, dy]
            half = parts.shape[-1] // 2
            self.cols = a, b = pl.ds(0, half), pl.ds(half, half)
            rows = parts.shape[1] // 2
            self.halves = (pl.ds(0, rows), pl.ds(rows, rows))
            self.far_a = [
                remote(parts.at[pd, r, a], near.at[0, 1, r], ssem, rsem, i, dx)
                for i, r in enumerate(self.halves)
            ]
            self.far_b = [
                remote(parts.at[pd, r, b], near.at[1, 1, r], ssem, rsem, 6 + i, dy)
                for i, r in enumerate(self.halves)
            ]
            self.near_a = remote(parts.at[self.px, :, a], near.at[0, 0], ssem, rsem, 2, dx)
            self.near_b = remote(parts.at[self.py, :, b], near.at[1, 0], ssem, rsem, 3, dy)
            self.sum_a = [
                remote(hold.at[0, r], far.at[0, r], ssem, rsem, 4 + i, dy)
                for i, r in enumerate(self.halves)
            ]
            self.sum_b = [
                remote(hold.at[1, r], far.at[1, r], ssem, rsem, 8 + i, dx)
                for i, r in enumerate(self.halves)
            ]
            self.copies = self.far_a + self.far_b + [self.near_a, self.near_b]
            self.copies += self.sum_a + self.sum_b
        else:
            self.peers = [(s, (t + k) % n) for k in range(1, n)]
            self.copies = [
                remote(parts.at[(t - k + n) % n], near.at[k - 1], ssem, rsem, k - 1, (s, (t - k + n) % n))
                for k in range(1, n)
            ]

    def send(self, i):
        if self.n == 4:

            @pl.when(i == 1)
            def _():
                self.near_a.start()

            @pl.when(i == 2)
            def _():
                self.near_b.start()

            @pl.when(i == 3)
            def _():
                for copy_a, copy_b in zip(self.far_a, self.far_b):
                    copy_a.start()
                    copy_b.start()

        else:
            for k, copy in enumerate(self.copies):

                @pl.when(i == k + 1)
                def _(copy=copy):
                    copy.start()

    def relay(self):
        if self.n == 4:
            sides = (self.cols[0], self.py, self.far_a, self.sum_a), (
                self.cols[1], self.px, self.far_b, self.sum_b
            )
            for i, r in enumerate(self.halves):
                for side, (cols, who, came, onward) in enumerate(sides):
                    came[i].wait_recv()
                    self.hold[side, r] = (
                        self.parts[who, r, cols].astype(F32) + self.near[side, 1, r].astype(F32)
                    ).astype(BF)
                    onward[i].start()

    def finish(self, write):
        if self.n == 4:
            for side, (one, two) in enumerate(
                ((self.near_a, self.sum_a), (self.near_b, self.sum_b))
            ):
                one.wait_recv()
                for copy in two:
                    copy.wait_recv()
                write(
                    self.cols[side],
                    self.parts[self.t, :, self.cols[side]].astype(F32)
                    + self.near[side, 0].astype(F32)
                    + self.far[side].astype(F32),
                )
        else:
            total = self.parts[self.t].astype(F32)
            for k, copy in enumerate(self.copies):
                copy.wait_recv()
                total = total + self.near[k].astype(F32)
            write(slice(None), total)

    def drain(self):
        for copy in self.copies:
            copy.wait_send()


def scatter_scratch(n, rows, width):
    if n == 4:
        near, far = (2, 2, rows, width // 2), (2, rows, width // 2)
    else:
        near, far = (n - 1, rows, width), (1, 16, 128)
    return [pltpu.VMEM(near, BF), pltpu.VMEM(far, BF), pltpu.VMEM(far, BF)]


class Ends:
    def __init__(self, chips):
        s, t = lax.axis_index("seq"), lax.axis_index("tp")
        chip, span = s // 2, 2 * chips
        self.gives = (chip == 0) | (chip == chips - 1)
        self.takes = (chip == 1) | (chip == chips - 2)
        self.peers = [((s + 2) % span, t), ((s - 2 + span) % span, t)]
        step = jnp.where(chip == 0, 2, jnp.where(chip == chips - 1, span - 2, 0))
        self.mate = ((s + step) % span, t)


class Chain:
    def __init__(self, chips, heads, flip, fac, local, out, pair, enter, ps, pr, zs, zr, bs, br):
        s, t = lax.axis_index("seq"), lax.axis_index("tp")
        core, chip, span = s % 2, s // 2, 2 * chips
        self.chips, self.heads, self.fac = chips, heads, fac
        self.local, self.out, self.pair, self.enter, self.leave = local, out, pair, enter, local
        self.sems = ps, pr, zs, zr, bs, br
        self.partner = (s + 1 - 2 * core, t)
        above, below = ((s + 2) % span, t), ((s - 2 + span) % span, t)
        self.peers = [self.partner, above, below]
        if flip:
            self.first, self.place, self.ahead = core == 1, chips - 1 - chip, below
        else:
            self.first, self.place, self.ahead = core == 0, chip, above
        self.last = jnp.logical_not(self.first)

    def give(self, p):
        return remote(self.local.at[p], self.pair.at[p], self.sems[0], self.sems[1], p, self.partner)

    def back(self, p):
        return remote(self.enter.at[p], self.out.at[p], self.sems[4], self.sems[5], p, self.partner)

    def onward(self, p):
        return remote(self.leave.at[p], self.enter.at[p], self.sems[2], self.sems[3], p, self.ahead)

    def piece(self, gather, index):
        return gather.source(index // self.heads) * self.heads + index % self.heads

    def open(self, gather, i):
        @pl.when(self.place == 0)
        def _():
            @pl.loop(0, self.heads)
            def _(h):
                self.step(self.piece(gather, i * self.heads + h))

    def tick(self, gather, now):
        total = self.local.shape[0]
        ends = self.place == self.chips - 1
        lag = jnp.minimum(3 * (self.place - 1), total - self.heads)
        index = jnp.where(ends, (self.heads + now) % total, now - lag)
        due = (self.place > 0) & (index >= 0) & (index < total)

        @pl.when(due & (jnp.logical_not(ends) | (now >= total)))
        def _():
            self.step(self.piece(gather, jnp.maximum(index, 0)))

    def begin(self, p):
        @pl.when(self.first)
        def _():
            self.give(p).start()

            @pl.when(self.place == 0)
            def _():
                self.out[p] = jnp.zeros(self.out.shape[1:], BF)

    def step(self, p):
        @pl.when(self.first)
        def _():
            @pl.when(self.place > 0)
            def _():
                self.back(p).wait_recv()

        @pl.when(self.last)
        def _():
            fac = self.fac[p % self.heads]
            self.give(p).wait_recv()
            early = self.pair[p].astype(F32)
            chip_sum = early * fac + self.local[p].astype(F32)

            @pl.when(self.place == 0)
            def _():
                self.leave[p] = chip_sum.astype(BF)
                self.out[p] = self.pair[p]

            @pl.when(self.place > 0)
            def _():
                self.onward(p).wait_recv()
                self.back(p).start()
                came = self.enter[p].astype(F32)
                self.leave[p] = (came * (fac * fac) + chip_sum).astype(BF)
                self.out[p] = (came * fac + early).astype(BF)

            @pl.when(self.place < self.chips - 1)
            def _():
                self.onward(p).start()

    def drain(self, p):
        @pl.when(self.first)
        def _():
            self.give(p).wait_send()

        @pl.when(self.last)
        def _():
            @pl.when(self.place > 0)
            def _():
                self.back(p).wait_send()

            @pl.when(self.place < self.chips - 1)
            def _():
                self.onward(p).wait_send()


def chain_scratch(pieces):
    dma = pltpu.SemaphoreType.DMA
    return [pltpu.VMEM((pieces, DK, DV), BF)] * 2 + [dma((pieces,))] * 6


def dot(a, b, ca=1, cb=0):
    return lax.dot_general(a, b, (((ca,), (cb,)), ((), ())), preferred_element_type=F32)


def turn(v, cos, sin):
    lo, hi = v[:, : DK // 2], v[:, DK // 2 :]
    return jnp.concatenate([lo * cos - hi * sin, hi * cos + lo * sin], 1)


def turn_back(g, cos, sin):
    lo, hi = g[:, : DK // 2], g[:, DK // 2 :]
    return jnp.concatenate([lo * cos + hi * sin, hi * cos - lo * sin], 1)


def norm_of(m):
    center = m - jnp.mean(m, -1, keepdims=True)
    inv = lax.rsqrt(jnp.mean(center * center, -1, keepdims=True) + EPS)
    return center * inv, inv


class LineSums:
    def __init__(self, chips, lo, hi, wide, deep, kinds, refs, swap=False):
        s, t = lax.axis_index("seq"), lax.axis_index("tp")
        self.core, self.chip, self.chips, self.lo, self.hi = s % 2, s // 2, chips, lo, hi
        self.wide, self.deep, self.kinds = wide, deep, kinds
        (
            self.xs, self.ys, self.buf, self.out,
            self.xsem, self.ysem, self.psx, self.prx, self.psy, self.pry, self.ssem, self.rsem,
        ) = refs
        self.units = len(deep)
        self.swap = swap
        self.tokens = self.ys.shape[1] // 2
        self.cut = self.xs.shape[3]
        self.spans = [self.places(parts) for parts in wide], [self.places(parts) for parts in deep]
        span = 2 * chips
        self.partner = (s + 1 - 2 * self.core, t)
        self.above = ((s + 2) % span, t)
        self.below = ((s - 2 + span) % span, t)
        self.peers = [self.partner, self.above, self.below]

    def cols(self, j, core):
        return pl.ds(pl.multiple_of((2 * j + core) * self.cut, self.cut), self.cut)

    def places(self, parts):
        found, start = [], 0
        for part in parts:
            found.append((start, part.shape[0]))
            start += part.shape[0]
        assert start == self.tokens
        return found

    def wide_own(self, kind, j):
        return [
            pltpu.make_async_copy(
                part.at[:, self.cols(j, self.core)],
                self.xs.at[kind, j, pl.ds(start, size)],
                self.xsem.at[kind, j, i],
            )
            for i, (part, (start, size)) in enumerate(zip(self.wide[kind], self.spans[0][kind]))
        ]

    def wide_give(self, kind, j):
        return [
            remote(
                part.at[:, self.cols(j, 1 - self.core)],
                self.xs.at[kind, j, pl.ds(self.tokens + start, size)],
                self.psx.at[kind, j],
                self.prx.at[kind, j],
                i,
                self.partner,
            )
            for i, (part, (start, size)) in enumerate(zip(self.wide[kind], self.spans[0][kind]))
        ]

    def deep_own(self, u):
        return [
            pltpu.make_async_copy(
                part, self.ys.at[u, pl.ds(start, size)], self.ysem.at[u, i]
            )
            for i, (part, (start, size)) in enumerate(zip(self.deep[u], self.spans[1][u]))
        ]

    def deep_give(self, u):
        return [
            remote(
                part,
                self.ys.at[u, pl.ds(self.tokens + start, size)],
                self.psy.at[u],
                self.pry.at[u],
                i,
                self.partner,
            )
            for i, (part, (start, size)) in enumerate(zip(self.deep[u], self.spans[1][u]))
        ]

    def adds(self):
        return (self.chip >= self.lo) & (self.chip <= self.hi)

    def share(self, u):
        @pl.when(self.adds())
        def _():
            if self.kinds[u] not in self.kinds[:u]:
                for j in range(self.chips):
                    for copy in self.wide_give(self.kinds[u], j) + self.wide_own(self.kinds[u], j):
                        copy.start()
            for copy in self.deep_give(u) + self.deep_own(u):
                copy.start()

    def ready(self, u):
        @pl.when(self.adds())
        def _():
            own, given = self.deep_own(u), self.deep_give(u)
            if self.kinds[u] not in self.kinds[:u]:
                for j in range(self.chips):
                    own += self.wide_own(self.kinds[u], j)
                    given += self.wide_give(self.kinds[u], j)
            for copy in own:
                copy.wait()
            for copy in given:
                copy.wait_recv()

    def up(self, u, j):
        return remote(
            self.buf.at[u, j], self.buf.at[u, j], self.ssem.at[u], self.rsem.at[u], j, self.above
        )

    def down(self, u, j):
        slot = jnp.where(j == self.chip - 1, self.chips, j)
        return pltpu.make_async_remote_copy(
            src_ref=self.buf.at[u, j],
            dst_ref=self.buf.at[u, slot],
            send_sem=self.ssem.at[u, j],
            recv_sem=self.rsem.at[u, slot],
            device_id=self.below,
            device_id_type=MESH,
        )

    def arrived(self, u, slot):
        remote(
            self.buf.at[u, slot], self.buf.at[u, slot], self.ssem.at[u], self.rsem.at[u], slot,
            self.above,
        ).wait_recv()
        return self.buf[u, slot].astype(F32)

    def product(self, u, j):
        kind = 0
        for w in range(self.units):
            if self.kinds[w]:
                kind = kind + jnp.where(u == w, self.kinds[w], 0)
        if self.swap:
            return dot(self.ys[u], self.xs[kind, j], 0, 0)
        return dot(self.xs[kind, j], self.ys[u], 0, 0)

    def order(self, k):
        rights = self.chips - 1 - self.chip
        return jnp.where(
            self.chip < self.chips // 2,
            jnp.where(k < rights, self.chips - 1 - k, k - rights),
            jnp.where(k < self.chip, k, self.chips - 1 - (k - self.chip)),
        )

    def step(self, u, k):
        chip = self.chip
        j = self.order(k)

        @pl.when(self.adds())
        def _():
            total = self.product(u, j)

            @pl.when(((j > chip) & (chip == self.lo)) | ((j < chip) & (chip == self.hi)))
            def _():
                self.buf[u, j] = total.astype(BF)

            @pl.when(((j > chip) & (chip > self.lo)) | ((j < chip) & (chip < self.hi)))
            def _():
                self.buf[u, j] = (total + self.arrived(u, j)).astype(BF)

            @pl.when(j > chip)
            def _():
                self.up(u, j).start()

            @pl.when(j < chip)
            def _():
                self.down(u, j).start()

    def finish(self, u):
        chip = self.chip

        @pl.when(self.adds())
        def _():
            self.out[u] = self.product(u, chip)

        @pl.when((chip < self.lo) | (chip > self.hi))
        def _():
            self.out[u] = jnp.zeros(self.out.shape[1:], F32)

        @pl.when(chip > self.lo)
        def _():
            self.out[u] += self.arrived(u, chip)

        @pl.when(chip < self.hi)
        def _():
            self.out[u] += self.arrived(u, self.chips)

    def drain(self):
        @pl.when(self.adds())
        def _():
            @pl.loop(0, self.units)
            def _(u):
                @pl.loop(0, self.chips)
                def _(j):
                    @pl.when(j > self.chip)
                    def _():
                        self.up(u, j).wait_send()

                    @pl.when(j < self.chip)
                    def _():
                        self.down(u, j).wait_send()

            for u in range(self.units):
                for copy in self.deep_give(u):
                    copy.wait_send()
            for kind in range(max(self.kinds) + 1):
                for j in range(self.chips):
                    for copy in self.wide_give(kind, j):
                        copy.wait_send()


def line_scratch(chips, units, kinds, tokens, cut, width, swap=False):
    dma = pltpu.SemaphoreType.DMA
    block = (width, cut) if swap else (cut, width)
    return [
        pltpu.VMEM((kinds, chips, 2 * tokens, cut), BF),
        pltpu.VMEM((units, 2 * tokens, width), BF),
        pltpu.VMEM((units, chips + 1) + block, BF),
        pltpu.VMEM((units,) + block, F32),
        dma((kinds, chips, 2)),
        dma((units, 2)),
        dma((kinds, chips, 2)),
        dma((kinds, chips, 2)),
        dma((units, 2)),
        dma((units, 2)),
        dma((units, chips + 1)),
        dma((units, chips + 1)),
    ]


def mixer_kernel(n, chips, heads, *refs):
    (
        fac, x, og, wk_h, wv_h, wq_h, ws_h, wo_h, decay, qfac, kfac, cos, sin,
        x_o, og_o, q_o, k_o, v_o, sp_o, mx_o, prior_o, gated_o, attn,
        x_all, og_all, q, k, v, sp, mx, prior, gated, wk, wv, wq, ws, wo, acc, parts, local,
    ) = refs[:40]
    near, far, hold = refs[40:43]
    chain_refs = refs[43:51]
    wsem, gs, gr, os, orr, ss, sr, es, er, osem, bsem = refs[51:]
    rows = x.shape[0]
    gather = Gather(n, x, x_all, gs, gr)
    gather_og = Gather(n, og, og_all, os, orr)
    ends = Ends(chips)
    hand_own = remote(og, og_o.at[n], es, er, 0, ends.mate)

    def hand(i):
        return remote(og_all.at[gather.source(i)], og_o.at[n + i], es, er, i, ends.mate)

    scatter = Scatter(n, parts, near, far, hold, ss, sr)
    chain = Chain(chips, heads, False, fac, local, prior, *chain_refs)
    loads = [
        pltpu.make_async_copy(a, w, wsem.at[i])
        for i, (a, w) in enumerate(((wk_h, wk), (wv_h, wv), (wq_h, wq), (ws_h, ws), (wo_h, wo)))
    ]
    for load in loads:
        load.start()
    greet(gather.peers + chain.peers)
    gather.start()

    @pl.when(ends.gives)
    def _():
        hand_own.start()

    me = gather.source(0)
    x_all[me] = x[...]
    og_all[me] = og[...]
    for load in loads[:2]:
        load.wait()

    @pl.loop(0, n)
    def _(i):
        j = gather.source(i)
        gather.arrive(i)
        at = pl.ds(pl.multiple_of(j * rows, rows), rows)
        acc[:, : heads * DK] = dot(x_all[j], wk[...])

        v[at] = dot(x_all[j], wv[...]).astype(BF)
        for h in range(heads):
            vc = slice(h * DV, (h + 1) * DV)
            kc = slice(h * DK, (h + 1) * DK)
            key = turn(acc[:, kc], cos[...], sin[...]).astype(BF)
            k[at, kc] = key
            key_dec = (key.astype(F32) * kfac[h]).astype(BF)
            p = j * heads + h
            local[p] = dot(key_dec, v[at, vc], 0, 0).astype(BF)
            chain.begin(p)

        chain.open(gather, i)

        @pl.when(i == 0)
        def _():
            gather.relays()
            gather_og.start()

    puts = [
        pltpu.make_async_copy(a, b, osem.at[i])
        for i, (a, b) in enumerate(
            ((x_all, x_o), (k, k_o), (v, v_o), (q, q_o), (sp, sp_o), (og_all, og_o.at[pl.ds(0, n)]))
        )
    ]
    for put in puts[:3]:
        put.start()
    for load in loads[2:]:
        load.wait()

    @pl.loop(0, n)
    def _(i):
        j = gather.source(i)
        at = pl.ds(pl.multiple_of(j * rows, rows), rows)
        acc[:, : heads * DK] = dot(x_all[j], wq[...])
        for h in range(heads):
            kc = slice(h * DK, (h + 1) * DK)
            vc = slice(h * DV, (h + 1) * DV)
            query = turn(acc[:, kc], cos[...], sin[...]).astype(BF)
            q[at, kc] = query
            scores = (dot(query, k[at, kc], 1, 1) * decay[h]).astype(BF)
            mx[at, vc] = dot(scores, v[at, vc])
            sp[at, vc] = dot(x_all[j], ws[:, vc])
            chain.tick(gather, i * heads + h)

    for put in puts[3:5]:
        put.start()
    gather_og.relays()

    def blocks(j):
        at = pl.ds(pl.multiple_of(j * rows, rows), rows)
        of = pl.ds(j * heads, heads)
        return [
            pltpu.make_async_copy(mx.at[at], mx_o.at[at], bsem.at[0, j]),
            pltpu.make_async_copy(gated.at[at], gated_o.at[at], bsem.at[1, j]),
            pltpu.make_async_copy(prior.at[of], prior_o.at[of], bsem.at[2, j]),
        ]


    @pl.loop(0, n)
    def _(step):
        i = (step + 1) % n
        j = gather.source(i)
        gather_og.arrive(i)

        @pl.when(ends.gives & (i > 0) & (i < n - 1))
        def _():
            hand(i).start()

        at = pl.ds(pl.multiple_of(j * rows, rows), rows)
        for h in range(heads):
            vc = slice(h * DV, (h + 1) * DV)
            kc = slice(h * DK, (h + 1) * DK)
            p = j * heads + h
            chain.tick(gather, (n + step) * heads + h)
            query_dec = (q[at, kc].astype(F32) * qfac[h]).astype(BF)
            mx[at, vc] += dot(query_dec, prior[p])
            pre = sp[at, vc]
            gated[at, vc] = (pre * jax.nn.sigmoid(pre) * norm_of(mx[at, vc])[0]).astype(BF)
        parts[j] = dot(gated[at], wo[...]).astype(BF)
        scatter.send(i)
        for put in blocks(j):
            put.start()

    puts[5].start()
    scatter.relay()

    def write(cols, total):
        attn[:, cols] = total

    scatter.finish(write)
    gather.drain()
    gather_og.drain()
    for put in puts:
        put.wait()

    @pl.loop(0, n)
    def _(j):
        for put in blocks(j):
            put.wait()

    @pl.when(ends.gives)
    def _():
        hand_own.wait_send()

        @pl.loop(1, n - 1)
        def _(i):
            hand(i).wait_send()

    @pl.when(ends.takes)
    def _():
        @pl.loop(0, n - 1)
        def _(i):
            hand(i).wait_recv()

    scatter.drain()

    @pl.loop(0, n * heads)
    def _(p):
        chain.drain(p)


def mixer(fac, x, og, wk, wv, wq, ws, wo, decay, qfac, kfac, cos, sin, cid):
    n = lax.axis_size("tp")
    chips = lax.axis_size("seq") // 2
    rows, model = x.shape
    heads = wk.shape[1] // DK
    pieces = n * heads
    total = n * rows
    dma = pltpu.SemaphoreType.DMA
    sems = max(10, n - 1)
    vmem = pl.BlockSpec(memory_space=pltpu.VMEM)
    hbm = pl.BlockSpec(memory_space=pl.ANY)
    shape = jax.ShapeDtypeStruct
    return pl.pallas_call(
        functools.partial(mixer_kernel, n, chips, heads),
        out_shape=(
            shape((n, rows, model), BF),
            shape((2 * n - 1, rows, model), BF),
            shape((total, heads * DK), BF),
            shape((total, heads * DK), BF),
            shape((total, heads * DV), BF),
            shape((total, heads * DV), F32),
            shape((total, heads * DV), F32),
            shape((pieces, DK, DV), BF),
            shape((total, heads * DV), BF),
            shape((rows, model), F32),
        ),
        in_specs=[pl.BlockSpec(memory_space=pltpu.SMEM), vmem, vmem] + [hbm] * 5 + [vmem] * 5,
        out_specs=(hbm,) * 9 + (vmem,),
        scratch_shapes=[
            pltpu.VMEM((n, rows, model), BF),
            pltpu.VMEM((n, rows, model), BF),
            pltpu.VMEM((total, heads * DK), BF),
            pltpu.VMEM((total, heads * DK), BF),
            pltpu.VMEM((total, heads * DV), BF),
            pltpu.VMEM((total, heads * DV), F32),
            pltpu.VMEM((total, heads * DV), F32),
            pltpu.VMEM((pieces, DK, DV), BF),
            pltpu.VMEM((total, heads * DV), BF),
        ]
        + [pltpu.VMEM(w.shape, BF) for w in (wk, wv, wq, ws, wo)]
        + [
            pltpu.VMEM((rows, heads * DK), F32),
            pltpu.VMEM((n, rows, model), BF),
            pltpu.VMEM((pieces, DK, DV), BF),
        ]
        + scatter_scratch(n, rows, model)
        + chain_scratch(pieces)
        + [dma((5,))]
        + [dma((sems,))] * 6
        + [dma((n - 1,)), dma((n - 1,)), dma((6,)), dma((3, n))],
        compiler_params=params(cid),
        name="mixer",
    )(fac, x, og, wk, wv, wq, ws, wo, decay, qfac, kfac, cos, sin)


GELU_C = 0.7978845608028654
GELU_A = 0.044715


def gelu_of(g):
    square = g * g
    th = jnp.tanh(GELU_C * (g + GELU_A * (square * g)))
    half = 0.5 * (1.0 + th)
    slope = half + 0.5 * g * (1.0 - th * th) * (GELU_C * (1.0 + 3.0 * GELU_A * square))
    return g * half, slope


def mlp_kernel(n, chips, *refs):
    (
        x, og_h, wg_h, wu_h, wd_h,
        x_o, hidden_o, gate_o, upper_o, mlp_o, grad_two, gate_late, up_late,
        og_all, x_all, hidden, gate_low, upper_low, mlp_parts, wg, wu, wd, hg, acc_g, acc_u, acc, parts, near, far, hold,
        wsem, gs, gr, ss, sr, es, er, osem, bsem,
    ) = refs
    rows = x.shape[0]
    gather = Gather(n, x, x_all, gs, gr)
    scatter = Scatter(n, parts, near, far, hold, ss, sr)
    ends = Ends(chips)
    loads = [
        pltpu.make_async_copy(a, w, wsem.at[i])
        for i, (a, w) in enumerate(((wd_h, wd), (wg_h, wg), (wu_h, wu)))
    ]
    loads.append(pltpu.make_async_copy(og_h, og_all, wsem.at[3]))
    for load in [loads[0], loads[3], loads[1], loads[2]]:
        load.start()
    greet(gather.peers + ends.peers)
    gather.start()
    me = gather.source(0)

    def hand(i):
        j = gather.source(i)
        return remote(x_all.at[j], x_all.at[n + i], es, er, i, ends.mate)

    first = remote(x, x_all.at[n], es, er, 0, ends.mate)

    @pl.when(ends.gives)
    def _():
        first.start()

    x_all[me] = x[...]
    loads[0].wait()
    loads[3].wait()
    pair = 2 * rows

    @pl.loop(0, n // 2)
    def _(c):
        two = pl.ds(pl.multiple_of(2 * c, 2), 2)
        at = pl.ds(pl.multiple_of(c * pair, pair), pair)
        hg[at] = dot(og_all[two].reshape(pair, x.shape[1]), wd[...], 1, 1)

    gather.relays()
    loads[1].wait()
    loads[2].wait()
    slab = 16

    def units(block, back_at, extra):
        start = pl.multiple_of(block * rows, rows)
        acc_g[...] = dot(x_all[block], wg[...])
        acc_u[...] = dot(x_all[block], wu[...])
        if extra:
            gate_late[...] = acc_g[...]
            up_late[...] = acc_u[...]

        @pl.loop(0, rows // slab)
        def _(r):
            here = pl.ds(pl.multiple_of(r * slab, slab), slab)
            there = pl.ds(pl.multiple_of(start + r * slab, slab), slab)
            g, u = acc_g[here], acc_u[here]
            gelu, slope = gelu_of(g)
            hidden[there] = (gelu * u).astype(BF)
            back = hg[pl.ds(pl.multiple_of(back_at + r * slab, slab), slab)]
            gate_low[there] = (back * u * slope).astype(BF)
            upper_low[there] = (back * gelu).astype(BF)

    @pl.loop(0, n)
    def _(turn):
        i = jnp.where(turn == 2, 3, jnp.where(turn == 3, 2, turn)) if n == 4 else turn
        j = gather.source(i)
        gather.arrive(i)

        @pl.when(ends.gives & (i > 0))
        def _():
            hand(i).start()

        units(j, j * rows, False)
        at = pl.ds(pl.multiple_of(j * rows, rows), rows)
        acc[...] = dot(gate_low[at], wg[...], 1, 1)
        parts[j] = (acc[...] + dot(upper_low[at], wu[...], 1, 1)).astype(BF)
        scatter.send(i)

    whole = pl.ds(0, n * rows)
    puts = [
        pltpu.make_async_copy(a, b, osem.at[i])
        for i, (a, b) in enumerate(
            (
                (x_all.at[pl.ds(0, n)], x_o.at[pl.ds(0, n)]),
                (hidden.at[whole], hidden_o.at[whole]),
                (gate_low.at[whole], gate_o.at[whole]),
                (upper_low.at[whole], upper_o.at[whole]),
                (mlp_parts, mlp_o),
            )
        )
    ]
    for put in puts[:4]:
        put.start()

    def blocks(i):
        at = pl.ds(pl.multiple_of((n + i) * rows, rows), rows)
        return [
            pltpu.make_async_copy(x_all.at[n + i], x_o.at[n + i], bsem.at[0, i]),
            pltpu.make_async_copy(hidden.at[at], hidden_o.at[at], bsem.at[1, i]),
        ]

    def late_blocks(i):
        at = pl.ds(pl.multiple_of((n + i) * rows, rows), rows)
        return [
            pltpu.make_async_copy(gate_low.at[at], gate_o.at[at], bsem.at[2, i]),
            pltpu.make_async_copy(upper_low.at[at], upper_o.at[at], bsem.at[3, i]),
        ]

    def extra(i):
        @pl.when(ends.takes)
        def _():
            hg[pl.ds(0, rows)] = dot(og_all[n + jnp.minimum(i, n - 2)], wd[...], 1, 1)
            hand(i).wait_recv()
            units(n + i, 0, True)
            for put in blocks(i):
                put.start()

            @pl.when(i < n - 1)
            def _():
                for put in late_blocks(i):
                    put.start()

    @pl.loop(0, n // 2)
    def _(i):
        extra(i)

    scatter.relay()

    @pl.loop(0, n // 2)
    def _(c):
        two = pl.ds(pl.multiple_of(2 * c, 2), 2)
        at = pl.ds(pl.multiple_of(c * pair, pair), pair)
        mlp_parts[two] = dot(hidden[at], wd[...]).astype(BF).reshape(2, rows, x.shape[1])

    puts[4].start()

    def write(cols, total):
        grad_two[:, cols] = total

    scatter.finish(write)

    @pl.loop(n // 2, n)
    def _(i):
        extra(i)

    @pl.when(ends.takes)
    def _():
        @pl.loop(0, n)
        def _(i):
            for put in blocks(i):
                put.wait()

        @pl.loop(0, n - 1)
        def _(i):
            for put in late_blocks(i):
                put.wait()

    for put in puts:
        put.wait()

    gather.drain()
    scatter.drain()

    @pl.when(ends.gives)
    def _():
        first.wait_send()

        @pl.loop(1, n)
        def _(i):
            hand(i).wait_send()


def mlp(x, og_all, wg, wu, wd, cid):
    n = lax.axis_size("tp")
    chips = lax.axis_size("seq") // 2
    rows, model = x.shape
    width = wg.shape[1]
    total = n * rows
    dma = pltpu.SemaphoreType.DMA
    sems = max(10, n - 1)
    vmem = pl.BlockSpec(memory_space=pltpu.VMEM)
    hbm = pl.BlockSpec(memory_space=pl.ANY)
    shape = jax.ShapeDtypeStruct
    return pl.pallas_call(
        functools.partial(mlp_kernel, n, chips),
        out_shape=(
            shape((2 * n, rows, model), BF),
            shape((2 * total, width), BF),
            shape((2 * total - rows, width), BF),
            shape((2 * total - rows, width), BF),
            shape((n, rows, model), BF),
            shape((rows, model), F32),
            shape((rows, width), F32),
            shape((rows, width), F32),
        ),
        in_specs=[vmem] + [hbm] * 4,
        out_specs=(hbm,) * 5 + (vmem,) * 3,
        scratch_shapes=[
            pltpu.VMEM(og_all.shape, BF),
            pltpu.VMEM((2 * n, rows, model), BF),
            pltpu.VMEM((2 * total, width), BF),
            pltpu.VMEM((2 * total, width), BF),
            pltpu.VMEM((2 * total, width), BF),
            pltpu.VMEM((n, rows, model), BF),
        ]
        + [pltpu.VMEM(w.shape, BF) for w in (wg, wu, wd)]
        + [
            pltpu.VMEM((total, width), F32),
            pltpu.VMEM((rows, width), F32),
            pltpu.VMEM((rows, width), F32),
            pltpu.VMEM((rows, model), F32),
            pltpu.VMEM((n, rows, model), BF),
        ]
        + scatter_scratch(n, rows, model)
        + [dma((4,))]
        + [dma((sems,))] * 4
        + [dma((n,)), dma((n,)), dma((5,)), dma((4, n))],
        compiler_params=params(cid),
        name="mlp",
    )(x, og_all, wg, wu, wd)


def mixer_back_kernel(n, chips, heads, *refs):
    (
        fac, res, wo_h, wq_h, wk_h, wv_h, ws_h, q_h, k_h, v_h, sp_h, mx_h, prior_h, mlp_h, decay, qfac, kfac, cos, sin, og_h, wd_h, gate_late, up_late,
        res_o, swish_o, value_o, qk_o, grad_one, mlp_out, og_late, gate_low, upper_low,
        q, k, v, sp, mx, prior, mlp_parts, res_all, swish_low, value_low, qk_low, wo, wq, wk, wv, ws, mixed_low, sums, parts, local, later, key_part, value_part,
    ) = refs[:55]
    near, far, hold, mlp_near, mlp_far, mlp_hold = refs[55:61]
    chain_refs = refs[61:69]
    wsem, gs, gr, ss, sr, ms, mr, es, er, isem, lsem, osem, bsem = refs[69:]
    rows = res.shape[0]
    gather = Gather(n, res, res_all, gs, gr)
    scatter = Scatter(n, parts, near, far, hold, ss, sr)
    scatter_mlp = Scatter(n, mlp_parts, mlp_near, mlp_far, mlp_hold, ms, mr)
    chain = Chain(chips, heads, True, fac, local, later, *chain_refs)
    ends = Ends(chips)
    late = remote(og_h.at[gather.source(n - 1)], og_late, es, er, 0, ends.mate)
    load_late = pltpu.make_async_copy(wd_h, wo, wsem.at[5])
    loads = [
        pltpu.make_async_copy(a, w, wsem.at[i])
        for i, (a, w) in enumerate(((wo_h, wo), (ws_h, ws), (wq_h, wq), (wk_h, wk), (wv_h, wv)))
    ]
    def entering(i):
        j = gather.source(i)
        at = pl.ds(pl.multiple_of(j * rows, rows), rows)
        return [
            pltpu.make_async_copy(a.at[at], b.at[at], isem.at[w, j])
            for w, (a, b) in enumerate(((mx_h, mx), (sp_h, sp), (q_h, q)))
        ]

    loads += [
        pltpu.make_async_copy(a, b, lsem.at[i])
        for i, (a, b) in enumerate(((k_h, k), (v_h, v), (prior_h, prior), (mlp_h, mlp_parts)))
    ]
    loads[0].start()
    for i in range(n):
        for load in entering(i):
            load.start()
    for load in loads[1:]:
        load.start()
    greet(gather.peers + chain.peers)
    gather.start()
    me = gather.source(0)
    res_all[me] = res[...]
    loads[0].wait()

    @pl.loop(0, n)
    def _(i):
        j = gather.source(i)
        gather.arrive(i)
        at = pl.ds(pl.multiple_of(j * rows, rows), rows)
        for load in entering(i):
            load.wait()
        sums[j, :, : heads * DV] = dot(res_all[j], wo[...], 1, 1).astype(sums.dtype)

        for h in range(heads):
            vc = slice(h * DV, (h + 1) * DV)
            kc = slice(h * DK, (h + 1) * DK)
            back = sums[j, :, vc].astype(F32)
            normed, inv = norm_of(mx[at, vc])
            pre = sp[at, vc]
            sig = jax.nn.sigmoid(pre)
            swish_low[at, vc] = (back * normed * (sig * (1.0 + pre * (1.0 - sig)))).astype(BF)
            g = back * (pre * sig)
            g = inv * (
                g
                - jnp.mean(g, -1, keepdims=True)
                - normed * jnp.mean(g * normed, -1, keepdims=True)
            )
            g = g.astype(BF)
            mixed_low[at, vc] = g
            query_dec = (q[at, kc].astype(F32) * qfac[h]).astype(BF)
            p = j * heads + h
            local[p] = dot(query_dec, g, 0, 0).astype(BF)
            chain.begin(p)

        chain.open(gather, i)

        @pl.when(i == 0)
        def _():
            gather.relays()

    puts = [
        pltpu.make_async_copy(res_all, res_o, osem.at[0]),
        pltpu.make_async_copy(swish_low, swish_o, osem.at[1]),
    ]
    for put in puts:
        put.start()

    def leaving(j):
        at = pl.ds(pl.multiple_of(j * rows, rows), rows)
        return [
            pltpu.make_async_copy(value_low.at[at], value_o.at[at], bsem.at[0, j]),
            pltpu.make_async_copy(qk_low.at[at], qk_o.at[at], bsem.at[1, j]),
        ]

    for load in loads[1:]:
        load.wait()
    for i in range(1, n):
        scatter_mlp.send(i)

    @pl.when(ends.gives)
    def _():
        late.start()

    @pl.when(ends.takes)
    def _():
        load_late.start()

    @pl.loop(0, n)
    def _(i):
        j = gather.source(i)
        at = pl.ds(pl.multiple_of(j * rows, rows), rows)
        for h in range(heads):
            vc = slice(h * DV, (h + 1) * DV)
            kc = slice(h * DK, (h + 1) * DK)
            g, query, key = mixed_low[at, vc], q[at, kc], k[at, kc]
            chain.tick(gather, i * heads + h)
            raw_low = (dot(g, v[at, vc], 1, 1) * decay[h]).astype(BF)
            query_back = dot(raw_low, key) + dot(g, prior[j * heads + h], 1, 1) * qfac[h]
            qk_low[at, kc] = turn_back(query_back, cos[...], sin[...]).astype(BF)
            scores = (dot(query, key, 1, 1) * decay[h]).astype(BF)
            key_part[at, kc] = dot(raw_low, query, 0, 0).astype(key_part.dtype)
            value_part[at, vc] = dot(scores, g, 0, 0).astype(value_part.dtype)
        sums[j] = dot(swish_low[at], ws[...], 1, 1).astype(sums.dtype)
        sums[j] += dot(qk_low[at, : heads * DK], wq[...], 1, 1).astype(sums.dtype)

    scatter_mlp.relay()

    @pl.loop(0, n)
    def _(step):
        i = (step + 1) % n
        j = gather.source(i)
        at = pl.ds(pl.multiple_of(j * rows, rows), rows)
        for h in range(heads):
            vc = slice(h * DV, (h + 1) * DV)
            kc = slice(h * DK, (h + 1) * DK)
            chain.tick(gather, (n + step) * heads + h)
            after = later[j * heads + h]
            key_dec = (k[at, kc].astype(F32) * kfac[h]).astype(BF)
            key_back = key_part[at, kc].astype(F32) + dot(v[at, vc], after, 1, 1) * kfac[h]
            qk_low[at, slice((heads + h) * DK, (heads + h + 1) * DK)] = turn_back(
                key_back, cos[...], sin[...]
            ).astype(BF)
            value_low[at, vc] = (value_part[at, vc] + dot(key_dec, after)).astype(BF)
        sums[j] += dot(value_low[at], wv[...], 1, 1).astype(sums.dtype)
        parts[j] = (sums[j].astype(F32) + dot(qk_low[at, heads * DK :], wk[...], 1, 1)).astype(BF)
        scatter.send(i)
        for put in leaving(j):
            put.start()

    scatter.relay()

    @pl.when(ends.takes)
    def _():
        width = gate_late.shape[1]
        load_late.wait()
        late.wait_recv()
        sums[0, :, :width] = dot(og_late[...], wo[...], 1, 1).astype(sums.dtype)
        slab = 16

        @pl.loop(0, rows // slab)
        def _(r):
            here = pl.ds(pl.multiple_of(r * slab, slab), slab)
            gelu, slope = gelu_of(gate_late[here])
            back = sums[0, here, :width].astype(F32)
            gate_low[here] = (back * up_late[here] * slope).astype(BF)
            upper_low[here] = (back * gelu).astype(BF)

    def write(cols, total):
        grad_one[:, cols] = total

    scatter.finish(write)

    def write_mlp(cols, total):
        mlp_out[:, cols] = total

    scatter_mlp.finish(write_mlp)
    gather.drain()
    scatter.drain()
    scatter_mlp.drain()

    @pl.when(ends.gives)
    def _():
        late.wait_send()

    for put in puts:
        put.wait()

    @pl.loop(0, n)
    def _(j):
        for put in leaving(j):
            put.wait()

    @pl.loop(0, n * heads)
    def _(p):
        chain.drain(p)


def mixer_back(fac, res, wo, wq, wk, wv, ws, q, k, v, sp, mx, prior, mlp_parts, decay, qfac, kfac, cos, sin, og_all, wd, gate_late, up_late, cid):
    n = lax.axis_size("tp")
    chips = lax.axis_size("seq") // 2
    rows, model = res.shape
    heads = q.shape[1] // DK
    pieces = n * heads
    total = n * rows
    keep = F32 if n <= 4 else BF
    dma = pltpu.SemaphoreType.DMA
    sems = max(10, n - 1)
    vmem = pl.BlockSpec(memory_space=pltpu.VMEM)
    hbm = pl.BlockSpec(memory_space=pl.ANY)
    shape = jax.ShapeDtypeStruct
    return pl.pallas_call(
        functools.partial(mixer_back_kernel, n, chips, heads),
        out_shape=(
            shape((n, rows, model), BF),
            shape((total, heads * DV), BF),
            shape((total, heads * DV), BF),
            shape((total, 2 * heads * DK), BF),
            shape((rows, model), F32),
            shape((rows, model), F32),
            shape((rows, model), BF),
            shape(gate_late.shape, BF),
            shape(gate_late.shape, BF),
        ),
        in_specs=[pl.BlockSpec(memory_space=pltpu.SMEM), vmem] + [hbm] * 12 + [vmem] * 5 + [hbm, hbm, vmem, vmem],
        out_specs=(hbm,) * 4 + (vmem,) * 5,
        scratch_shapes=[pltpu.VMEM(a.shape, a.dtype) for a in (q, k, v, sp, mx, prior, mlp_parts)]
        + [
            pltpu.VMEM((n, rows, model), BF),
            pltpu.VMEM((total, heads * DV), BF),
            pltpu.VMEM((total, heads * DV), BF),
            pltpu.VMEM((total, 2 * heads * DK), BF),
        ]
        + [pltpu.VMEM(w.shape, BF) for w in (wo, wq, wk, wv, ws)]
        + [
            pltpu.VMEM((total, heads * DV), BF),
            pltpu.VMEM((n, rows, model), keep),
            pltpu.VMEM((n, rows, model), BF),
            pltpu.VMEM((pieces, DK, DV), BF),
            pltpu.VMEM((pieces, DK, DV), BF),
            pltpu.VMEM((total, heads * DK), keep),
            pltpu.VMEM((total, heads * DV), BF),
        ]
        + scatter_scratch(n, rows, model)
        + scatter_scratch(n, rows, model)
        + chain_scratch(pieces)
        + [dma((6,))]
        + [dma((sems,))] * 6
        + [dma((1,)), dma((1,)), dma((3, n)), dma((4,)), dma((2,)), dma((2, n))],
        compiler_params=params(cid),
        name="mixer_back",
    )(fac, res, wo, wq, wk, wv, ws, q, k, v, sp, mx, prior, mlp_parts, decay, qfac, kfac, cos, sin, og_all, wd, gate_late, up_late)


def weights_kernel(chips, *refs):
    (
        two, og, og_late, hidden, gate_low, gate_late, up_low, up_late,
        one, res, swish_low, gated, value_low, qk_low, vec,
        down_o, gate_o, up_o, swish_o, mixer_o, value_o, query_o, key_o, vec_out,
    ) = refs[:24]
    mlp = LineSums(
        chips, 1, chips - 2, ((two,), (og, og_late)),
        ((gate_low, gate_late), (up_low, up_late), (hidden,)), (0, 0, 1), refs[24:36],
    )
    mix = LineSums(
        chips, 0, chips - 1, ((one,), (res,)), ((swish_low,), (gated,), (value_low,), (qk_low,)),
        (0, 1, 0, 0), refs[36:48],
    )
    turned, osem, vec_near, vec_sum, vec_far, vs, vr, us, ur = refs[48:]
    s, t = lax.axis_index("seq"), lax.axis_index("tp")
    span, tp = 2 * chips, vec.shape[0]
    ring = [((s + d) % span, t) for d in range(1, span)]
    cross = [(s, (t + d) % tp) for d in range(1, tp)]
    greet(ring + cross)
    vec_first = [
        remote(vec.at[(t + d) % tp], vec_near.at[d - 1], vs, vr, d - 1, cross[d - 1])
        for d in range(1, tp)
    ]
    vec_last = [
        remote(vec_sum.at[(s + d) % span], vec_far.at[d - 1], us, ur, d - 1, ring[d - 1])
        for d in range(1, span)
    ]
    for copy in vec_first:
        copy.start()
    for u in range(mix.units):
        if u < mlp.units:
            mlp.share(u)
        mix.share(u)

    @pl.loop(0, mix.units)
    def _(u):
        for w in range(mix.units):

            @pl.when(u == w)
            def _(w=w):
                if w < mlp.units:
                    mlp.ready(w)

        @pl.when(u < mlp.units)
        def _():
            mlp.step(u, 0)

        for w in range(mix.units):

            @pl.when(u == w)
            def _(w=w):
                mix.ready(w)

        @pl.loop(0, chips - 1)
        def _(k):
            @pl.when((u < mlp.units) & (k > 0))
            def _():
                mlp.step(u, k)

            mix.step(u, k)

        @pl.when(u == 0)
        def _():
            total = vec[t]
            for copy in vec_first:
                copy.wait_recv()
            vec_sum[...] = total + jnp.sum(vec_near[...], 0)
            for copy in vec_last:
                copy.start()

        @pl.when(u > 0)
        def _():
            mlp.finish(u - 1)
            mix.finish(u - 1)

    half = mix.out.shape[2] // 2
    lo, hi = pl.ds(0, half), pl.ds(half, half)
    turned[...] = mlp.out[2].T
    pairs = [
        (mlp.out.at[0], gate_o),
        (mlp.out.at[1], up_o),
        (mix.out.at[0], swish_o),
        (turned, down_o),
        (turned, mixer_o),
        (mix.out.at[2], value_o),
        (mix.out.at[3, :, lo], query_o),
        (mix.out.at[3, :, hi], key_o),
    ]
    copies = [pltpu.make_async_copy(a, b, osem.at[i]) for i, (a, b) in enumerate(pairs)]
    for i in (3, 0, 1, 2, 5):
        copies[i].start()
    copies[3].wait()
    turned[...] = mix.out[1].T
    copies[4].start()
    mix.finish(mix.units - 1)
    for copy in copies[6:]:
        copy.start()
    vec_total = vec_sum[s]
    for copy in vec_last:
        copy.wait_recv()
    vec_out[...] = vec_total + jnp.sum(vec_far[...], 0)
    for copy in vec_first + vec_last:
        copy.wait_send()
    mlp.drain()
    mix.drain()
    for i, copy in enumerate(copies):
        if i != 3:
            copy.wait()


def weight_sums(
    two, og, og_late, hidden, gate_low, gate_late, up_low, up_late, one, res, swish_low, gated, value_low,
    qk_low, vec, cid,
):
    chips = lax.axis_size("seq") // 2
    tokens, model = one.shape
    width = gated.shape[1]
    mlp_tokens, mlp_width = hidden.shape
    keys = qk_low.shape[1] // 2
    cut = model // (2 * chips)
    dma = pltpu.SemaphoreType.DMA
    vmem = pl.BlockSpec(memory_space=pltpu.VMEM)
    hbm = pl.BlockSpec(memory_space=pl.ANY)
    shape = lambda *a: jax.ShapeDtypeStruct(a, F32)
    ring, cross = 2 * chips - 1, vec.shape[0] - 1
    return pl.pallas_call(
        functools.partial(weights_kernel, chips),
        out_shape=(
            shape(mlp_width, cut),
            shape(cut, mlp_width),
            shape(cut, mlp_width),
            shape(cut, width),
            shape(width, cut),
            shape(cut, width),
            shape(cut, keys),
            shape(cut, keys),
            shape(*vec.shape[2:]),
        ),
        in_specs=[hbm] * 14 + [vmem],
        out_specs=(hbm,) * 8 + (vmem,),
        scratch_shapes=line_scratch(chips, 3, 2, mlp_tokens, cut, mlp_width)
        + line_scratch(chips, 4, 2, tokens, cut, width)
        + [
            pltpu.VMEM((width, cut), F32),
            dma((8,)),
            pltpu.VMEM((cross,) + vec.shape[1:], F32),
            pltpu.VMEM(vec.shape[1:], F32),
            pltpu.VMEM((ring,) + vec.shape[2:], F32),
            dma((cross,)),
            dma((cross,)),
            dma((ring,)),
            dma((ring,)),
        ],
        compiler_params=params(cid),
        name="weights",
    )(two, og, og_late, hidden, gate_low, gate_late, up_low, up_late, one, res, swish_low, gated, value_low, qk_low, vec)


def layer_norm(values, gain, bias):
    center = values - jnp.mean(values, -1, keepdims=True)
    spread = jnp.mean(center * center, -1, keepdims=True)
    return center * lax.rsqrt(spread + EPS) * gain + bias


def shards(
    inputs,
    query_weight,
    key_weight,
    value_weight,
    swish_weight,
    output_weight,
    gate_weight,
    up_weight,
    down_weight,
    attn_gain,
    attn_bias,
    mlp_gain,
    mlp_bias,
    output_grad,
):
    _, rows, model = inputs.shape
    heads = query_weight.shape[1] // DK
    inputs_full = inputs[0].astype(F32)
    cotangent = output_grad[0]

    half_width = DK // 2
    frequencies = jnp.power(10000.0, -jnp.arange(half_width, dtype=F32) / half_width)
    steps_in = jnp.arange(rows, dtype=F32)
    positions = lax.axis_index("seq").astype(F32) * rows + steps_in
    angles = positions[:, None] * frequencies[None, :]
    cosine, sine = jnp.cos(angles), jnp.sin(angles)
    head_ids = (lax.axis_index("tp") * heads + jnp.arange(heads)).astype(F32)
    decays = 1.0 - jnp.exp2(-5.0 - head_ids)
    lag = steps_in[:, None] - steps_in[None, :]
    decay_mat = jnp.where(
        lag[None] >= 0, jnp.power(decays[:, None, None], jnp.maximum(lag, 0.0)[None]), 0.0
    )
    query_fac = jnp.power(decays[:, None], steps_in[None, :] + 1.0)[:, :, None]
    key_fac = jnp.power(decays[:, None], rows - 1.0 - steps_in[None, :])[:, :, None]
    block_fac = jnp.power(decays, rows * 1.0)

    normed_one = layer_norm(inputs_full, attn_gain, attn_bias).astype(BF)
    one_all, grad_all, query, key, value, swish_pre, mixed, prior, gated, attn_out = mixer(
        block_fac, normed_one, cotangent, key_weight, value_weight, query_weight, swish_weight,
        output_weight, decay_mat, query_fac, key_fac, cosine, sine, 0,
    )
    hidden_res = inputs_full + attn_out
    normed_two = layer_norm(hidden_res, mlp_gain, mlp_bias).astype(BF)
    two_all, hidden, gate_low, upper_low, mlp_parts, normed_two_grad, gate_pre, up_pre = mlp(
        normed_two, grad_all, gate_weight, up_weight, down_weight, 1
    )
    flat = lambda a: a.reshape(-1, model)
    _, pull_two = jax.vjp(layer_norm, hidden_res, mlp_gain, mlp_bias)
    res_back, mlpgain_part, mlpbias_part = pull_two(normed_two_grad)
    res_grad = cotangent.astype(F32) + res_back
    res_all, swish_low, value_low, qk_low, normed_one_grad, mlp_out, og_late, gate_late, up_late = mixer_back(
        block_fac, res_grad.astype(BF), output_weight, query_weight, key_weight, value_weight, swish_weight,
        query, key, value, swish_pre, mixed, prior, mlp_parts, decay_mat, query_fac, key_fac,
        cosine, sine, grad_all, down_weight, gate_pre, up_pre, 2,
    )
    outputs = (hidden_res + mlp_out).astype(BF)
    _, pull_one = jax.vjp(layer_norm, inputs_full, attn_gain, attn_bias)
    input_back, attngain_part, attnbias_part = pull_one(normed_one_grad)
    input_grad = (res_grad + input_back).astype(BF)

    seqs, tps = lax.axis_size("seq"), lax.axis_size("tp")
    each = model // (seqs * tps)
    vectors = jnp.stack([attngain_part, attnbias_part, mlpgain_part, mlpbias_part])
    vectors = vectors.reshape(4, seqs, tps, each).transpose(2, 1, 0, 3).reshape(tps, seqs, 4 * each)
    vectors = jnp.pad(vectors, ((0, 0), (0, 0), (0, 1024 - 4 * each))).reshape(tps, seqs, 8, 128)
    down_grad, gate_grad, up_grad, swish_grad, mixer_grad, value_grad, query_grad, key_grad, vector_sums = (
        weight_sums(
            flat(two_all), flat(grad_all), og_late, hidden, gate_low, gate_late, upper_low, up_late, flat(one_all), flat(res_all), swish_low, gated,
            value_low, qk_low, vectors, 3,
        )
    )
    vector_sums = vector_sums.reshape(-1)[: 4 * each].reshape(4, each)
    return (
        outputs[None],
        input_grad[None],
        query_grad,
        key_grad,
        value_grad,
        swish_grad,
        mixer_grad,
        gate_grad,
        up_grad,
        down_grad,
        vector_sums[0],
        vector_sums[1],
        vector_sums[2],
        vector_sums[3],
    )


def solution(mesh):
    return jax.shard_map(
        shards,
        mesh=mesh,
        in_specs=(
            P("tp", "seq", None),
            P(None, "tp"),
            P(None, "tp"),
            P(None, "tp"),
            P(None, "tp"),
            P("tp", None),
            P(None, "tp"),
            P(None, "tp"),
            P("tp", None),
            P(),
            P(),
            P(),
            P(),
            P("tp", "seq", None),
        ),
        out_specs=(
            P("tp", "seq", None),
            P("tp", "seq", None),
            P("seq", "tp"),
            P("seq", "tp"),
            P("seq", "tp"),
            P("seq", "tp"),
            P("tp", "seq"),
            P("seq", "tp"),
            P("seq", "tp"),
            P("tp", "seq"),
            P(("seq", "tp")),
            P(("seq", "tp")),
            P(("seq", "tp")),
            P(("seq", "tp")),
        ),
        check_vma=False,
    )
```

```python
import functools

import jax
import jax.numpy as jnp
import numpy as np
from jax import lax
from jax.experimental import pallas as pl
from jax.experimental.pallas import tpu as pltpu
from jax.sharding import PartitionSpec as P

DK = 256
DV = 512


EPS = 1e-05
MESH = pl.DeviceIdType.MESH
BF = jnp.bfloat16
F32 = jnp.float32
VMEM_LIMIT = 61 * 1024 * 1024


def remote(src, dst, ssem, rsem, slot, dev):
    return pltpu.make_async_remote_copy(
        src_ref=src,
        dst_ref=dst,
        send_sem=ssem.at[slot],
        recv_sem=rsem.at[slot],
        device_id=dev,
        device_id_type=MESH,
    )


def greet(devs):
    barrier = pltpu.get_barrier_semaphore()
    for dev in devs:
        pl.semaphore_signal(barrier, inc=1, device_id=dev, device_id_type=MESH)
    pl.semaphore_wait(barrier, len(devs))


def params(cid):
    return pltpu.CompilerParams(
        collective_id=cid, has_side_effects=True, vmem_limit_bytes=VMEM_LIMIT
    )


class Gather:
    def __init__(self, n, x, o, ssem, rsem, base=0):
        s, t = lax.axis_index("seq"), lax.axis_index("tp")
        self.n, self.t = n, t
        rows = x.shape[0]
        if n == 4:
            px, py = t + 1 - 2 * (t % 2), (t + 2) % 4
            dx, dy = (s, px), (s, py)
            self.peers = [dx, dy]
            half = rows // 2
            lo, hi = pl.ds(0, half), pl.ds(half, half)
            self.first = [
                remote(x.at[lo], o.at[base + t, lo], ssem, rsem, 0, dx),
                remote(x.at[hi], o.at[base + t, hi], ssem, rsem, 1, dy),
                remote(x.at[hi], o.at[base + t, hi], ssem, rsem, 2, dx),
                remote(x.at[lo], o.at[base + t, lo], ssem, rsem, 3, dy),
            ]
            self.relay = [
                remote(o.at[base + px, lo], o.at[base + px, lo], ssem, rsem, 4, dy),
                remote(o.at[base + py, hi], o.at[base + py, hi], ssem, rsem, 5, dx),
            ]
        else:
            self.peers = [(s, (t + k) % n) for k in range(1, n)]
            self.first = [
                remote(x, o.at[base + t], ssem, rsem, k, dev) for k, dev in enumerate(self.peers)
            ]
            self.relay = []

    def source(self, i):
        t = self.t
        if self.n == 4:
            near = jnp.where(i == 1, t + 1 - 2 * (t % 2), (t + 2) % 4)
            return jnp.where(i == 0, t, jnp.where(i == 3, 3 - t, near))
        return (t - i + self.n) % self.n

    def start(self):
        for copy in self.first:
            copy.start()

    def relays(self):
        for copy, onward in zip(self.first, self.relay):
            copy.wait_recv()
            onward.start()

    def arrive(self, i):
        if self.n == 4:

            @pl.when(i == 1)
            def _():
                self.first[2].wait_recv()

            @pl.when(i == 2)
            def _():
                self.first[3].wait_recv()

            @pl.when(i == 3)
            def _():
                self.relay[0].wait_recv()
                self.relay[1].wait_recv()

        else:
            for k, copy in enumerate(self.first):

                @pl.when(i == k + 1)
                def _(copy=copy):
                    copy.wait_recv()

    def drain(self):
        for copy in self.first + self.relay:
            copy.wait_send()


class Scatter:
    def __init__(self, n, parts, near, far, hold, ssem, rsem):
        s, t = lax.axis_index("seq"), lax.axis_index("tp")
        self.n, self.t = n, t
        self.parts, self.near, self.far, self.hold = parts, near, far, hold
        if n == 4:
            self.px, self.py, pd = t + 1 - 2 * (t % 2), (t + 2) % 4, 3 - t
            dx, dy = (s, self.px), (s, self.py)
            self.peers = [dx, dy]
            half = parts.shape[-1] // 2
            self.cols = a, b = pl.ds(0, half), pl.ds(half, half)
            rows = parts.shape[1] // 2
            self.halves = (pl.ds(0, rows), pl.ds(rows, rows))
            self.far_a = [
                remote(parts.at[pd, r, a], near.at[0, 1, r], ssem, rsem, i, dx)
                for i, r in enumerate(self.halves)
            ]
            self.far_b = [
                remote(parts.at[pd, r, b], near.at[1, 1, r], ssem, rsem, 6 + i, dy)
                for i, r in enumerate(self.halves)
            ]
            self.near_a = remote(parts.at[self.px, :, a], near.at[0, 0], ssem, rsem, 2, dx)
            self.near_b = remote(parts.at[self.py, :, b], near.at[1, 0], ssem, rsem, 3, dy)
            self.sum_a = [
                remote(hold.at[0, r], far.at[0, r], ssem, rsem, 4 + i, dy)
                for i, r in enumerate(self.halves)
            ]
            self.sum_b = [
                remote(hold.at[1, r], far.at[1, r], ssem, rsem, 8 + i, dx)
                for i, r in enumerate(self.halves)
            ]
            self.copies = self.far_a + self.far_b + [self.near_a, self.near_b]
            self.copies += self.sum_a + self.sum_b
        else:
            self.peers = [(s, (t + k) % n) for k in range(1, n)]
            self.copies = [
                remote(parts.at[(t - k + n) % n], near.at[k - 1], ssem, rsem, k - 1, (s, (t - k + n) % n))
                for k in range(1, n)
            ]

    def send(self, i):
        if self.n == 4:

            @pl.when(i == 1)
            def _():
                self.near_a.start()

            @pl.when(i == 2)
            def _():
                self.near_b.start()

            @pl.when(i == 3)
            def _():
                for copy_a, copy_b in zip(self.far_a, self.far_b):
                    copy_a.start()
                    copy_b.start()

        else:
            for k, copy in enumerate(self.copies):

                @pl.when(i == k + 1)
                def _(copy=copy):
                    copy.start()

    def relay(self):
        if self.n == 4:
            sides = (self.cols[0], self.py, self.far_a, self.sum_a), (
                self.cols[1], self.px, self.far_b, self.sum_b
            )
            for i, r in enumerate(self.halves):
                for side, (cols, who, came, onward) in enumerate(sides):
                    came[i].wait_recv()
                    self.hold[side, r] = (
                        self.parts[who, r, cols].astype(F32) + self.near[side, 1, r].astype(F32)
                    ).astype(BF)
                    onward[i].start()

    def finish(self, write):
        if self.n == 4:
            for side, (one, two) in enumerate(
                ((self.near_a, self.sum_a), (self.near_b, self.sum_b))
            ):
                one.wait_recv()
                for copy in two:
                    copy.wait_recv()
                write(
                    self.cols[side],
                    self.parts[self.t, :, self.cols[side]].astype(F32)
                    + self.near[side, 0].astype(F32)
                    + self.far[side].astype(F32),
                )
        else:
            total = self.parts[self.t].astype(F32)
            for k, copy in enumerate(self.copies):
                copy.wait_recv()
                total = total + self.near[k].astype(F32)
            write(slice(None), total)

    def drain(self):
        for copy in self.copies:
            copy.wait_send()


def scatter_scratch(n, rows, width):
    if n == 4:
        near, far = (2, 2, rows, width // 2), (2, rows, width // 2)
    else:
        near, far = (n - 1, rows, width), (1, 16, 128)
    return [pltpu.VMEM(near, BF), pltpu.VMEM(far, BF), pltpu.VMEM(far, BF)]


class Ends:
    def __init__(self, chips):
        s, t = lax.axis_index("seq"), lax.axis_index("tp")
        chip, span = s // 2, 2 * chips
        self.gives = (chip == 0) | (chip == chips - 1)
        self.takes = (chip == 1) | (chip == chips - 2)
        self.peers = [((s + 2) % span, t), ((s - 2 + span) % span, t)]
        step = jnp.where(chip == 0, 2, jnp.where(chip == chips - 1, span - 2, 0))
        self.mate = ((s + step) % span, t)


class Chain:
    def __init__(self, chips, heads, flip, fac, local, out, pair, enter, ps, pr, zs, zr, bs, br):
        s, t = lax.axis_index("seq"), lax.axis_index("tp")
        core, chip, span = s % 2, s // 2, 2 * chips
        self.chips, self.heads, self.fac = chips, heads, fac
        self.local, self.out, self.pair, self.enter, self.leave = local, out, pair, enter, local
        self.sems = ps, pr, zs, zr, bs, br
        self.partner = (s + 1 - 2 * core, t)
        above, below = ((s + 2) % span, t), ((s - 2 + span) % span, t)
        self.peers = [self.partner, above, below]
        if flip:
            self.first, self.place, self.ahead = core == 1, chips - 1 - chip, below
        else:
            self.first, self.place, self.ahead = core == 0, chip, above
        self.last = jnp.logical_not(self.first)

    def give(self, p):
        return remote(self.local.at[p], self.pair.at[p], self.sems[0], self.sems[1], p, self.partner)

    def back(self, p):
        return remote(self.enter.at[p], self.out.at[p], self.sems[4], self.sems[5], p, self.partner)

    def onward(self, p):
        return remote(self.leave.at[p], self.enter.at[p], self.sems[2], self.sems[3], p, self.ahead)

    def piece(self, gather, index):
        return gather.source(index // self.heads) * self.heads + index % self.heads

    def open(self, gather, i):
        @pl.when(self.place == 0)
        def _():
            @pl.loop(0, self.heads)
            def _(h):
                self.step(self.piece(gather, i * self.heads + h))

    def tick(self, gather, now):
        total = self.local.shape[0]
        ends = self.place == self.chips - 1
        lag = jnp.minimum(3 * (self.place - 1), total - self.heads)
        index = jnp.where(ends, (self.heads + now) % total, now - lag)
        due = (self.place > 0) & (index >= 0) & (index < total)

        @pl.when(due & (jnp.logical_not(ends) | (now >= total)))
        def _():
            self.step(self.piece(gather, jnp.maximum(index, 0)))

    def begin(self, p):
        @pl.when(self.first)
        def _():
            self.give(p).start()

            @pl.when(self.place == 0)
            def _():
                self.out[p] = jnp.zeros(self.out.shape[1:], BF)

    def step(self, p):
        @pl.when(self.first)
        def _():
            @pl.when(self.place > 0)
            def _():
                self.back(p).wait_recv()

        @pl.when(self.last)
        def _():
            fac = self.fac[0, lax.axis_index("tp") * self.heads + p % self.heads]
            self.give(p).wait_recv()
            early = self.pair[p].astype(F32)
            chip_sum = early * fac + self.local[p].astype(F32)

            @pl.when(self.place == 0)
            def _():
                self.leave[p] = chip_sum.astype(BF)
                self.out[p] = self.pair[p]

            @pl.when(self.place > 0)
            def _():
                self.onward(p).wait_recv()
                self.back(p).start()
                came = self.enter[p].astype(F32)
                self.leave[p] = (came * (fac * fac) + chip_sum).astype(BF)
                self.out[p] = (came * fac + early).astype(BF)

            @pl.when(self.place < self.chips - 1)
            def _():
                self.onward(p).start()

    def drain(self, p):
        @pl.when(self.first)
        def _():
            self.give(p).wait_send()

        @pl.when(self.last)
        def _():
            @pl.when(self.place > 0)
            def _():
                self.back(p).wait_send()

            @pl.when(self.place < self.chips - 1)
            def _():
                self.onward(p).wait_send()


def chain_scratch(pieces):
    dma = pltpu.SemaphoreType.DMA
    return [pltpu.VMEM((pieces, DK, DV), BF)] * 2 + [dma((pieces,))] * 6


def dot(a, b, ca=1, cb=0):
    return lax.dot_general(a, b, (((ca,), (cb,)), ((), ())), preferred_element_type=F32)


def turn(v, cos, sin):
    lo, hi = v[:, : DK // 2], v[:, DK // 2 :]
    return jnp.concatenate([lo * cos - hi * sin, hi * cos + lo * sin], 1)


def turn_back(g, cos, sin):
    lo, hi = g[:, : DK // 2], g[:, DK // 2 :]
    return jnp.concatenate([lo * cos + hi * sin, hi * cos - lo * sin], 1)


def row_stats(v):
    center = v - jnp.mean(v, -1, keepdims=True)
    return center, lax.rsqrt(jnp.mean(center * center, -1, keepdims=True) + EPS)


def norm_pull(grad, hat, inv, gain):
    g = grad * gain
    return (g - jnp.mean(g, -1, keepdims=True) - hat * jnp.mean(g * hat, -1, keepdims=True)) * inv


def norm_of(m):
    center = m - jnp.mean(m, -1, keepdims=True)
    inv = lax.rsqrt(jnp.mean(center * center, -1, keepdims=True) + EPS)
    return center * inv, inv


class LineSums:
    def __init__(self, chips, lo, hi, wide, deep, kinds, refs, swap=False):
        s, t = lax.axis_index("seq"), lax.axis_index("tp")
        self.core, self.chip, self.chips, self.lo, self.hi = s % 2, s // 2, chips, lo, hi
        self.wide, self.deep, self.kinds = wide, deep, kinds
        (
            self.xs, self.ys, self.buf, self.out,
            self.xsem, self.ysem, self.psx, self.prx, self.psy, self.pry, self.ssem, self.rsem,
        ) = refs
        self.units = len(deep)
        self.swap = swap
        self.tokens = self.ys.shape[1] // 2
        self.cut = self.xs.shape[3]
        self.spans = [self.places(parts) for parts in wide], [self.places(parts) for parts in deep]
        span = 2 * chips
        self.partner = (s + 1 - 2 * self.core, t)
        self.above = ((s + 2) % span, t)
        self.below = ((s - 2 + span) % span, t)
        self.peers = [self.partner, self.above, self.below]

    def cols(self, j, core):
        return pl.ds(pl.multiple_of((2 * j + core) * self.cut, self.cut), self.cut)

    def places(self, parts):
        found, start = [], 0
        for part in parts:
            found.append((start, part.shape[0]))
            start += part.shape[0]
        assert start == self.tokens
        return found

    def wide_own(self, kind, j):
        return [
            pltpu.make_async_copy(
                part.at[:, self.cols(j, self.core)],
                self.xs.at[kind, j, pl.ds(start, size)],
                self.xsem.at[kind, j, i],
            )
            for i, (part, (start, size)) in enumerate(zip(self.wide[kind], self.spans[0][kind]))
        ]

    def wide_give(self, kind, j):
        return [
            remote(
                part.at[:, self.cols(j, 1 - self.core)],
                self.xs.at[kind, j, pl.ds(self.tokens + start, size)],
                self.psx.at[kind, j],
                self.prx.at[kind, j],
                i,
                self.partner,
            )
            for i, (part, (start, size)) in enumerate(zip(self.wide[kind], self.spans[0][kind]))
        ]

    def deep_own(self, u):
        return [
            pltpu.make_async_copy(
                part, self.ys.at[u, pl.ds(start, size)], self.ysem.at[u, i]
            )
            for i, (part, (start, size)) in enumerate(zip(self.deep[u], self.spans[1][u]))
        ]

    def deep_give(self, u):
        return [
            remote(
                part,
                self.ys.at[u, pl.ds(self.tokens + start, size)],
                self.psy.at[u],
                self.pry.at[u],
                i,
                self.partner,
            )
            for i, (part, (start, size)) in enumerate(zip(self.deep[u], self.spans[1][u]))
        ]

    def adds(self):
        return (self.chip >= self.lo) & (self.chip <= self.hi)

    def share(self, u):
        @pl.when(self.adds())
        def _():
            if self.kinds[u] not in self.kinds[:u]:
                for j in range(self.chips):
                    for copy in self.wide_give(self.kinds[u], j) + self.wide_own(self.kinds[u], j):
                        copy.start()
            for copy in self.deep_give(u) + self.deep_own(u):
                copy.start()

    def ready(self, u):
        @pl.when(self.adds())
        def _():
            own, given = self.deep_own(u), self.deep_give(u)
            if self.kinds[u] not in self.kinds[:u]:
                for j in range(self.chips):
                    own += self.wide_own(self.kinds[u], j)
                    given += self.wide_give(self.kinds[u], j)
            for copy in own:
                copy.wait()
            for copy in given:
                copy.wait_recv()

    def up(self, u, j):
        return remote(
            self.buf.at[u, j], self.buf.at[u, j], self.ssem.at[u], self.rsem.at[u], j, self.above
        )

    def down(self, u, j):
        slot = jnp.where(j == self.chip - 1, self.chips, j)
        return pltpu.make_async_remote_copy(
            src_ref=self.buf.at[u, j],
            dst_ref=self.buf.at[u, slot],
            send_sem=self.ssem.at[u, j],
            recv_sem=self.rsem.at[u, slot],
            device_id=self.below,
            device_id_type=MESH,
        )

    def arrived(self, u, slot):
        remote(
            self.buf.at[u, slot], self.buf.at[u, slot], self.ssem.at[u], self.rsem.at[u], slot,
            self.above,
        ).wait_recv()
        return self.buf[u, slot].astype(F32)

    def product(self, u, j):
        kind = 0
        for w in range(self.units):
            if self.kinds[w]:
                kind = kind + jnp.where(u == w, self.kinds[w], 0)
        if self.swap:
            return dot(self.ys[u], self.xs[kind, j], 0, 0)
        return dot(self.xs[kind, j], self.ys[u], 0, 0)

    def order(self, k):
        rights = self.chips - 1 - self.chip
        return jnp.where(
            self.chip < self.chips // 2,
            jnp.where(k < rights, self.chips - 1 - k, k - rights),
            jnp.where(k < self.chip, k, self.chips - 1 - (k - self.chip)),
        )

    def step(self, u, k):
        chip = self.chip
        j = self.order(k)

        @pl.when(self.adds())
        def _():
            total = self.product(u, j)

            @pl.when(((j > chip) & (chip == self.lo)) | ((j < chip) & (chip == self.hi)))
            def _():
                self.buf[u, j] = total.astype(BF)

            @pl.when(((j > chip) & (chip > self.lo)) | ((j < chip) & (chip < self.hi)))
            def _():
                self.buf[u, j] = (total + self.arrived(u, j)).astype(BF)

            @pl.when(j > chip)
            def _():
                self.up(u, j).start()

            @pl.when(j < chip)
            def _():
                self.down(u, j).start()

    def finish(self, u):
        chip = self.chip

        @pl.when(self.adds())
        def _():
            self.out[u] = self.product(u, chip)

        @pl.when((chip < self.lo) | (chip > self.hi))
        def _():
            self.out[u] = jnp.zeros(self.out.shape[1:], F32)

        @pl.when(chip > self.lo)
        def _():
            self.out[u] += self.arrived(u, chip)

        @pl.when(chip < self.hi)
        def _():
            self.out[u] += self.arrived(u, self.chips)

    def drain(self):
        @pl.when(self.adds())
        def _():
            @pl.loop(0, self.units)
            def _(u):
                @pl.loop(0, self.chips)
                def _(j):
                    @pl.when(j > self.chip)
                    def _():
                        self.up(u, j).wait_send()

                    @pl.when(j < self.chip)
                    def _():
                        self.down(u, j).wait_send()

            for u in range(self.units):
                for copy in self.deep_give(u):
                    copy.wait_send()
            for kind in range(max(self.kinds) + 1):
                for j in range(self.chips):
                    for copy in self.wide_give(kind, j):
                        copy.wait_send()


def line_scratch(chips, units, kinds, tokens, cut, width, swap=False):
    dma = pltpu.SemaphoreType.DMA
    block = (width, cut) if swap else (cut, width)
    return [
        pltpu.VMEM((kinds, chips, 2 * tokens, cut), BF),
        pltpu.VMEM((units, 2 * tokens, width), BF),
        pltpu.VMEM((units, chips + 1) + block, BF),
        pltpu.VMEM((units,) + block, F32),
        dma((kinds, chips, 2)),
        dma((units, 2)),
        dma((kinds, chips, 2)),
        dma((kinds, chips, 2)),
        dma((units, 2)),
        dma((units, 2)),
        dma((units, chips + 1)),
        dma((units, chips + 1)),
    ]


def mixer_kernel(n, chips, heads, *refs):
    (
        fac, raw, og, wk_h, wv_h, wq_h, ws_h, wo_h, gain, bias, freq,
        x_o, og_o, q_o, k_o, v_o, sp_o, mx_o, prior_o, gated_o, attn, decay, qfac, kfac, cos, sin,
        x_all, og_all, q, k, v, sp, mx, prior, gated, x, wk, wv, wq, ws, wo, acc, parts, local,
    ) = refs[:44]
    near, far, hold = refs[44:47]
    chain_refs = refs[47:55]
    wsem, gs, gr, os, orr, ss, sr, es, er, osem, bsem = refs[55:]
    rows = raw.shape[0]
    gather = Gather(n, x, x_all, gs, gr)
    gather_og = Gather(n, og, og_all, os, orr)
    ends = Ends(chips)
    hand_own = remote(og, og_o.at[n], es, er, 0, ends.mate)

    def hand(i):
        return remote(og_all.at[gather.source(i)], og_o.at[n + i], es, er, i, ends.mate)

    scatter = Scatter(n, parts, near, far, hold, ss, sr)
    chain = Chain(chips, heads, False, fac, local, prior, *chain_refs)
    loads = [
        pltpu.make_async_copy(a, w, wsem.at[i])
        for i, (a, w) in enumerate(((wk_h, wk), (wv_h, wv), (wq_h, wq), (ws_h, ws), (wo_h, wo)))
    ]
    for load in loads:
        load.start()
    slab = 16

    @pl.loop(0, rows // slab)
    def _(r):
        here = pl.ds(pl.multiple_of(r * slab, slab), slab)
        center, inv = row_stats(raw[here].astype(F32))
        x[here] = (center * inv * gain[...] + bias[...]).astype(BF)

    greet(gather.peers + chain.peers)
    gather.start()
    place = lax.broadcasted_iota(jnp.int32, (rows, 1), 0).astype(F32)
    angles = (lax.axis_index("seq").astype(F32) * rows + place) * freq[...]
    cos[...] = jnp.cos(angles)
    sin[...] = jnp.sin(angles)
    lag = place - lax.broadcasted_iota(jnp.int32, (rows, rows), 1).astype(F32)
    for h in range(heads):
        rate = fac[1, lax.axis_index("tp") * heads + h]
        decay[h] = jnp.where(lag >= 0, jnp.exp(jnp.maximum(lag, 0.0) * rate), 0.0)
        qfac[h] = jnp.exp((place + 1.0) * rate)
        kfac[h] = jnp.exp((rows - 1.0 - place) * rate)

    @pl.when(ends.gives)
    def _():
        hand_own.start()

    me = gather.source(0)
    x_all[me] = x[...]
    og_all[me] = og[...]
    for load in loads[:2]:
        load.wait()

    @pl.loop(0, n)
    def _(i):
        j = gather.source(i)
        gather.arrive(i)
        at = pl.ds(pl.multiple_of(j * rows, rows), rows)
        acc[:, : heads * DK] = dot(x_all[j], wk[...])

        v[at] = dot(x_all[j], wv[...]).astype(BF)
        for h in range(heads):
            vc = slice(h * DV, (h + 1) * DV)
            kc = slice(h * DK, (h + 1) * DK)
            key = turn(acc[:, kc], cos[...], sin[...]).astype(BF)
            k[at, kc] = key
            key_dec = (key.astype(F32) * kfac[h]).astype(BF)
            p = j * heads + h
            local[p] = dot(key_dec, v[at, vc], 0, 0).astype(BF)
            chain.begin(p)

        chain.open(gather, i)

        @pl.when(i == 0)
        def _():
            gather.relays()
            gather_og.start()

    puts = [
        pltpu.make_async_copy(a, b, osem.at[i])
        for i, (a, b) in enumerate(
            ((x_all, x_o), (k, k_o), (v, v_o), (q, q_o), (sp, sp_o), (og_all, og_o.at[pl.ds(0, n)]))
        )
    ]
    for put in puts[:3]:
        put.start()
    for load in loads[2:]:
        load.wait()

    @pl.loop(0, n)
    def _(i):
        j = gather.source(i)
        at = pl.ds(pl.multiple_of(j * rows, rows), rows)
        acc[:, : heads * DK] = dot(x_all[j], wq[...])
        for h in range(heads):
            kc = slice(h * DK, (h + 1) * DK)
            vc = slice(h * DV, (h + 1) * DV)
            query = turn(acc[:, kc], cos[...], sin[...]).astype(BF)
            q[at, kc] = query
            scores = (dot(query, k[at, kc], 1, 1) * decay[h]).astype(BF)
            mx[at, vc] = dot(scores, v[at, vc])
            sp[at, vc] = dot(x_all[j], ws[:, vc])
            chain.tick(gather, i * heads + h)

    for put in puts[3:5]:
        put.start()
    gather_og.relays()

    def blocks(j):
        at = pl.ds(pl.multiple_of(j * rows, rows), rows)
        of = pl.ds(j * heads, heads)
        return [
            pltpu.make_async_copy(mx.at[at], mx_o.at[at], bsem.at[0, j]),
            pltpu.make_async_copy(gated.at[at], gated_o.at[at], bsem.at[1, j]),
            pltpu.make_async_copy(prior.at[of], prior_o.at[of], bsem.at[2, j]),
        ]


    @pl.loop(0, n)
    def _(step):
        i = (step + 1) % n
        j = gather.source(i)
        gather_og.arrive(i)

        @pl.when(ends.gives & (i > 0) & (i < n - 1))
        def _():
            hand(i).start()

        at = pl.ds(pl.multiple_of(j * rows, rows), rows)
        for h in range(heads):
            vc = slice(h * DV, (h + 1) * DV)
            kc = slice(h * DK, (h + 1) * DK)
            p = j * heads + h
            chain.tick(gather, (n + step) * heads + h)
            query_dec = (q[at, kc].astype(F32) * qfac[h]).astype(BF)
            mx[at, vc] += dot(query_dec, prior[p])
            pre = sp[at, vc]
            gated[at, vc] = (pre * jax.nn.sigmoid(pre) * norm_of(mx[at, vc])[0]).astype(BF)
        parts[j] = dot(gated[at], wo[...]).astype(BF)
        scatter.send(i)
        for put in blocks(j):
            put.start()

    puts[5].start()
    scatter.relay()

    def write(cols, total):
        attn[:, cols] = total

    scatter.finish(write)
    gather.drain()
    gather_og.drain()
    for put in puts:
        put.wait()

    @pl.loop(0, n)
    def _(j):
        for put in blocks(j):
            put.wait()

    @pl.when(ends.gives)
    def _():
        hand_own.wait_send()

        @pl.loop(1, n - 1)
        def _(i):
            hand(i).wait_send()

    @pl.when(ends.takes)
    def _():
        @pl.loop(0, n - 1)
        def _(i):
            hand(i).wait_recv()

    scatter.drain()

    @pl.loop(0, n * heads)
    def _(p):
        chain.drain(p)


def mixer(fac, x, og, wk, wv, wq, ws, wo, gain, bias, freq, cid):
    n = lax.axis_size("tp")
    chips = lax.axis_size("seq") // 2
    rows, model = x.shape
    heads = wk.shape[1] // DK
    pieces = n * heads
    total = n * rows
    dma = pltpu.SemaphoreType.DMA
    sems = max(10, n - 1)
    vmem = pl.BlockSpec(memory_space=pltpu.VMEM)
    hbm = pl.BlockSpec(memory_space=pl.ANY)
    shape = jax.ShapeDtypeStruct
    return pl.pallas_call(
        functools.partial(mixer_kernel, n, chips, heads),
        out_shape=(
            shape((n, rows, model), BF),
            shape((2 * n - 1, rows, model), BF),
            shape((total, heads * DK), BF),
            shape((total, heads * DK), BF),
            shape((total, heads * DV), BF),
            shape((total, heads * DV), F32),
            shape((total, heads * DV), F32),
            shape((pieces, DK, DV), BF),
            shape((total, heads * DV), BF),
            shape((rows, model), F32),
            shape((heads, rows, rows), F32),
            shape((heads, rows, 1), F32),
            shape((heads, rows, 1), F32),
            shape((rows, DK // 2), F32),
            shape((rows, DK // 2), F32),
        ),
        in_specs=[pl.BlockSpec(memory_space=pltpu.SMEM), vmem, vmem] + [hbm] * 5 + [vmem] * 3,
        out_specs=(hbm,) * 9 + (vmem,) * 6,
        scratch_shapes=[
            pltpu.VMEM((n, rows, model), BF),
            pltpu.VMEM((n, rows, model), BF),
            pltpu.VMEM((total, heads * DK), BF),
            pltpu.VMEM((total, heads * DK), BF),
            pltpu.VMEM((total, heads * DV), BF),
            pltpu.VMEM((total, heads * DV), F32),
            pltpu.VMEM((total, heads * DV), F32),
            pltpu.VMEM((pieces, DK, DV), BF),
            pltpu.VMEM((total, heads * DV), BF),
            pltpu.VMEM((rows, model), BF),
        ]
        + [pltpu.VMEM(w.shape, BF) for w in (wk, wv, wq, ws, wo)]
        + [
            pltpu.VMEM((rows, heads * DK), F32),
            pltpu.VMEM((n, rows, model), BF),
            pltpu.VMEM((pieces, DK, DV), BF),
        ]
        + scatter_scratch(n, rows, model)
        + chain_scratch(pieces)
        + [dma((5,))]
        + [dma((sems,))] * 6
        + [dma((n - 1,)), dma((n - 1,)), dma((6,)), dma((3, n))],
        compiler_params=params(cid),
        name="mixer",
    )(fac, x, og, wk, wv, wq, ws, wo, gain, bias, freq)


GELU_C = 0.7978845608028654
GELU_A = 0.044715


def gelu_of(g):
    square = g * g
    th = jnp.tanh(GELU_C * (g + GELU_A * (square * g)))
    half = 0.5 * (1.0 + th)
    slope = half + 0.5 * g * (1.0 - th * th) * (GELU_C * (1.0 + 3.0 * GELU_A * square))
    return g * half, slope


def mlp_kernel(n, chips, *refs):
    (
        raw, attn, cot, gain, bias, og_h, wg_h, wu_h, wd_h,
        x_o, hidden_o, gate_o, upper_o, mlp_o, res_grad, res_low, vec, gate_late, up_late,
        og_all, x, grad_two, x_all, hidden, gate_low, upper_low, mlp_parts, wg, wu, wd, hg, acc_g, acc_u, acc, parts, near, far, hold,
        wsem, gs, gr, ss, sr, es, er, osem, bsem,
    ) = refs
    rows = raw.shape[0]
    slab = 16
    gather = Gather(n, x, x_all, gs, gr)
    scatter = Scatter(n, parts, near, far, hold, ss, sr)
    ends = Ends(chips)
    loads = [
        pltpu.make_async_copy(a, w, wsem.at[i])
        for i, (a, w) in enumerate(((wd_h, wd), (wg_h, wg), (wu_h, wu)))
    ]
    loads.append(pltpu.make_async_copy(og_h, og_all, wsem.at[3]))
    for load in [loads[0], loads[3], loads[1], loads[2]]:
        load.start()
    @pl.loop(0, rows // slab)
    def _(r):
        here = pl.ds(pl.multiple_of(r * slab, slab), slab)
        center, inv = row_stats(raw[here].astype(F32) + attn[here])
        x[here] = (center * inv * gain[...] + bias[...]).astype(BF)

    greet(gather.peers + ends.peers)
    gather.start()
    me = gather.source(0)

    def hand(i):
        j = gather.source(i)
        return remote(x_all.at[j], x_all.at[n + i], es, er, i, ends.mate)

    first = remote(x, x_all.at[n], es, er, 0, ends.mate)

    @pl.when(ends.gives)
    def _():
        first.start()

    x_all[me] = x[...]
    loads[0].wait()
    loads[3].wait()
    pair = 2 * rows

    @pl.loop(0, n // 2)
    def _(c):
        two = pl.ds(pl.multiple_of(2 * c, 2), 2)
        at = pl.ds(pl.multiple_of(c * pair, pair), pair)
        hg[at] = dot(og_all[two].reshape(pair, x.shape[1]), wd[...], 1, 1)

    gather.relays()
    loads[1].wait()
    loads[2].wait()

    def units(block, back_at, extra):
        start = pl.multiple_of(block * rows, rows)
        acc_g[...] = dot(x_all[block], wg[...])
        acc_u[...] = dot(x_all[block], wu[...])
        if extra:
            gate_late[...] = acc_g[...]
            up_late[...] = acc_u[...]

        @pl.loop(0, rows // slab)
        def _(r):
            here = pl.ds(pl.multiple_of(r * slab, slab), slab)
            there = pl.ds(pl.multiple_of(start + r * slab, slab), slab)
            g, u = acc_g[here], acc_u[here]
            gelu, slope = gelu_of(g)
            hidden[there] = (gelu * u).astype(BF)
            back = hg[pl.ds(pl.multiple_of(back_at + r * slab, slab), slab)]
            gate_low[there] = (back * u * slope).astype(BF)
            upper_low[there] = (back * gelu).astype(BF)

    @pl.loop(0, n)
    def _(turn):
        i = jnp.where(turn == 2, 3, jnp.where(turn == 3, 2, turn)) if n == 4 else turn
        j = gather.source(i)
        gather.arrive(i)

        @pl.when(ends.gives & (i > 0))
        def _():
            hand(i).start()

        units(j, j * rows, False)
        at = pl.ds(pl.multiple_of(j * rows, rows), rows)
        acc[...] = dot(gate_low[at], wg[...], 1, 1)
        parts[j] = (acc[...] + dot(upper_low[at], wu[...], 1, 1)).astype(BF)
        scatter.send(i)

    whole = pl.ds(0, n * rows)
    puts = [
        pltpu.make_async_copy(a, b, osem.at[i])
        for i, (a, b) in enumerate(
            (
                (x_all.at[pl.ds(0, n)], x_o.at[pl.ds(0, n)]),
                (hidden.at[whole], hidden_o.at[whole]),
                (gate_low.at[whole], gate_o.at[whole]),
                (upper_low.at[whole], upper_o.at[whole]),
                (mlp_parts, mlp_o),
            )
        )
    ]
    for put in puts[:4]:
        put.start()

    def blocks(i):
        at = pl.ds(pl.multiple_of((n + i) * rows, rows), rows)
        return [
            pltpu.make_async_copy(x_all.at[n + i], x_o.at[n + i], bsem.at[0, i]),
            pltpu.make_async_copy(hidden.at[at], hidden_o.at[at], bsem.at[1, i]),
        ]

    def late_blocks(i):
        at = pl.ds(pl.multiple_of((n + i) * rows, rows), rows)
        return [
            pltpu.make_async_copy(gate_low.at[at], gate_o.at[at], bsem.at[2, i]),
            pltpu.make_async_copy(upper_low.at[at], upper_o.at[at], bsem.at[3, i]),
        ]

    def extra(i):
        @pl.when(ends.takes)
        def _():
            hg[pl.ds(0, rows)] = dot(og_all[n + jnp.minimum(i, n - 2)], wd[...], 1, 1)
            hand(i).wait_recv()
            units(n + i, 0, True)
            for put in blocks(i):
                put.start()

            @pl.when(i < n - 1)
            def _():
                for put in late_blocks(i):
                    put.start()

    @pl.loop(0, n // 2)
    def _(i):
        extra(i)

    scatter.relay()

    @pl.loop(0, n // 2)
    def _(c):
        two = pl.ds(pl.multiple_of(2 * c, 2), 2)
        at = pl.ds(pl.multiple_of(c * pair, pair), pair)
        mlp_parts[two] = dot(hidden[at], wd[...]).astype(BF).reshape(2, rows, x.shape[1])

    puts[4].start()

    def write(cols, total):
        grad_two[:, cols] = total

    scatter.finish(write)
    vec[...] = jnp.zeros_like(vec)

    @pl.loop(0, rows // slab)
    def _(r):
        here = pl.ds(pl.multiple_of(r * slab, slab), slab)
        center, inv = row_stats(raw[here].astype(F32) + attn[here])
        hat, grad = center * inv, grad_two[here]
        total = cot[here].astype(F32) + norm_pull(grad, hat, inv, gain[...])
        res_grad[here] = total
        res_low[here] = total.astype(BF)
        vec[2:3] += jnp.sum(grad * hat, 0, keepdims=True)
        vec[3:4] += jnp.sum(grad, 0, keepdims=True)

    @pl.loop(n // 2, n)
    def _(i):
        extra(i)

    @pl.when(ends.takes)
    def _():
        @pl.loop(0, n)
        def _(i):
            for put in blocks(i):
                put.wait()

        @pl.loop(0, n - 1)
        def _(i):
            for put in late_blocks(i):
                put.wait()

    for put in puts:
        put.wait()

    gather.drain()
    scatter.drain()

    @pl.when(ends.gives)
    def _():
        first.wait_send()

        @pl.loop(1, n)
        def _(i):
            hand(i).wait_send()


def mlp(raw, attn, cot, gain, bias, og_all, wg, wu, wd, cid):
    n = lax.axis_size("tp")
    chips = lax.axis_size("seq") // 2
    rows, model = raw.shape
    width = wg.shape[1]
    total = n * rows
    dma = pltpu.SemaphoreType.DMA
    sems = max(10, n - 1)
    vmem = pl.BlockSpec(memory_space=pltpu.VMEM)
    hbm = pl.BlockSpec(memory_space=pl.ANY)
    shape = jax.ShapeDtypeStruct
    return pl.pallas_call(
        functools.partial(mlp_kernel, n, chips),
        out_shape=(
            shape((2 * n, rows, model), BF),
            shape((2 * total, width), BF),
            shape((2 * total - rows, width), BF),
            shape((2 * total - rows, width), BF),
            shape((n, rows, model), BF),
            shape((rows, model), F32),
            shape((rows, model), BF),
            shape((8, model), F32),
            shape((rows, width), F32),
            shape((rows, width), F32),
        ),
        in_specs=[vmem] * 5 + [hbm] * 4,
        out_specs=(hbm,) * 5 + (vmem,) * 5,
        scratch_shapes=[
            pltpu.VMEM(og_all.shape, BF),
            pltpu.VMEM((rows, model), BF),
            pltpu.VMEM((rows, model), F32),
            pltpu.VMEM((2 * n, rows, model), BF),
            pltpu.VMEM((2 * total, width), BF),
            pltpu.VMEM((2 * total, width), BF),
            pltpu.VMEM((2 * total, width), BF),
            pltpu.VMEM((n, rows, model), BF),
        ]
        + [pltpu.VMEM(w.shape, BF) for w in (wg, wu, wd)]
        + [
            pltpu.VMEM((total, width), F32),
            pltpu.VMEM((rows, width), F32),
            pltpu.VMEM((rows, width), F32),
            pltpu.VMEM((rows, model), F32),
            pltpu.VMEM((n, rows, model), BF),
        ]
        + scatter_scratch(n, rows, model)
        + [dma((4,))]
        + [dma((sems,))] * 4
        + [dma((n,)), dma((n,)), dma((5,)), dma((4, n))],
        compiler_params=params(cid),
        name="mlp",
    )(raw, attn, cot, gain, bias, og_all, wg, wu, wd)


def mixer_back_kernel(n, chips, heads, *refs):
    (
        fac, res, wo_h, wq_h, wk_h, wv_h, ws_h, q_h, k_h, v_h, sp_h, mx_h, prior_h, mlp_h, decay, qfac, kfac, cos, sin, og_h, wd_h, gate_late, up_late,
        res_o, swish_o, value_o, qk_o, grad_one, mlp_out, og_late, gate_low, upper_low,
        q, k, v, sp, mx, prior, mlp_parts, res_all, swish_low, value_low, qk_low, wo, wq, wk, wv, ws, mixed_low, sums, parts, local, later, key_part, value_part,
    ) = refs[:55]
    near, far, hold, mlp_near, mlp_far, mlp_hold = refs[55:61]
    chain_refs = refs[61:69]
    wsem, gs, gr, ss, sr, ms, mr, es, er, isem, lsem, osem, bsem = refs[69:]
    rows = res.shape[0]
    gather = Gather(n, res, res_all, gs, gr)
    scatter = Scatter(n, parts, near, far, hold, ss, sr)
    scatter_mlp = Scatter(n, mlp_parts, mlp_near, mlp_far, mlp_hold, ms, mr)
    chain = Chain(chips, heads, True, fac, local, later, *chain_refs)
    ends = Ends(chips)
    late = remote(og_h.at[gather.source(n - 1)], og_late, es, er, 0, ends.mate)
    load_late = pltpu.make_async_copy(wd_h, wo, wsem.at[5])
    loads = [
        pltpu.make_async_copy(a, w, wsem.at[i])
        for i, (a, w) in enumerate(((wo_h, wo), (ws_h, ws), (wq_h, wq), (wk_h, wk), (wv_h, wv)))
    ]
    def entering(i):
        j = gather.source(i)
        at = pl.ds(pl.multiple_of(j * rows, rows), rows)
        return [
            pltpu.make_async_copy(a.at[at], b.at[at], isem.at[w, j])
            for w, (a, b) in enumerate(((mx_h, mx), (sp_h, sp), (q_h, q)))
        ]

    loads += [
        pltpu.make_async_copy(a, b, lsem.at[i])
        for i, (a, b) in enumerate(((k_h, k), (v_h, v), (prior_h, prior), (mlp_h, mlp_parts)))
    ]
    loads[0].start()
    for i in range(n):
        for load in entering(i):
            load.start()
    for load in loads[1:]:
        load.start()
    greet(gather.peers + chain.peers)
    gather.start()
    me = gather.source(0)
    res_all[me] = res[...]
    loads[0].wait()

    @pl.loop(0, n)
    def _(i):
        j = gather.source(i)
        gather.arrive(i)
        at = pl.ds(pl.multiple_of(j * rows, rows), rows)
        for load in entering(i):
            load.wait()
        sums[j, :, : heads * DV] = dot(res_all[j], wo[...], 1, 1).astype(sums.dtype)

        for h in range(heads):
            vc = slice(h * DV, (h + 1) * DV)
            kc = slice(h * DK, (h + 1) * DK)
            back = sums[j, :, vc].astype(F32)
            normed, inv = norm_of(mx[at, vc])
            pre = sp[at, vc]
            sig = jax.nn.sigmoid(pre)
            swish_low[at, vc] = (back * normed * (sig * (1.0 + pre * (1.0 - sig)))).astype(BF)
            g = back * (pre * sig)
            g = inv * (
                g
                - jnp.mean(g, -1, keepdims=True)
                - normed * jnp.mean(g * normed, -1, keepdims=True)
            )
            g = g.astype(BF)
            mixed_low[at, vc] = g
            query_dec = (q[at, kc].astype(F32) * qfac[h]).astype(BF)
            p = j * heads + h
            local[p] = dot(query_dec, g, 0, 0).astype(BF)
            chain.begin(p)

        chain.open(gather, i)

        @pl.when(i == 0)
        def _():
            gather.relays()

    puts = [
        pltpu.make_async_copy(res_all, res_o, osem.at[0]),
        pltpu.make_async_copy(swish_low, swish_o, osem.at[1]),
    ]
    for put in puts:
        put.start()

    def leaving(j):
        at = pl.ds(pl.multiple_of(j * rows, rows), rows)
        return [
            pltpu.make_async_copy(value_low.at[at], value_o.at[at], bsem.at[0, j]),
            pltpu.make_async_copy(qk_low.at[at], qk_o.at[at], bsem.at[1, j]),
        ]

    for load in loads[1:]:
        load.wait()
    for i in range(1, n):
        scatter_mlp.send(i)

    @pl.when(ends.gives)
    def _():
        late.start()

    @pl.when(ends.takes)
    def _():
        load_late.start()

    @pl.loop(0, n)
    def _(i):
        j = gather.source(i)
        at = pl.ds(pl.multiple_of(j * rows, rows), rows)
        for h in range(heads):
            vc = slice(h * DV, (h + 1) * DV)
            kc = slice(h * DK, (h + 1) * DK)
            g, query, key = mixed_low[at, vc], q[at, kc], k[at, kc]
            chain.tick(gather, i * heads + h)
            raw_low = (dot(g, v[at, vc], 1, 1) * decay[h]).astype(BF)
            query_back = dot(raw_low, key) + dot(g, prior[j * heads + h], 1, 1) * qfac[h]
            qk_low[at, kc] = turn_back(query_back, cos[...], sin[...]).astype(BF)
            scores = (dot(query, key, 1, 1) * decay[h]).astype(BF)
            key_part[at, kc] = dot(raw_low, query, 0, 0).astype(key_part.dtype)
            value_part[at, vc] = dot(scores, g, 0, 0).astype(value_part.dtype)
        sums[j] = dot(swish_low[at], ws[...], 1, 1).astype(sums.dtype)
        sums[j] += dot(qk_low[at, : heads * DK], wq[...], 1, 1).astype(sums.dtype)

    scatter_mlp.relay()

    @pl.loop(0, n)
    def _(step):
        i = (step + 1) % n
        j = gather.source(i)
        at = pl.ds(pl.multiple_of(j * rows, rows), rows)
        for h in range(heads):
            vc = slice(h * DV, (h + 1) * DV)
            kc = slice(h * DK, (h + 1) * DK)
            chain.tick(gather, (n + step) * heads + h)
            after = later[j * heads + h]
            key_dec = (k[at, kc].astype(F32) * kfac[h]).astype(BF)
            key_back = key_part[at, kc].astype(F32) + dot(v[at, vc], after, 1, 1) * kfac[h]
            qk_low[at, slice((heads + h) * DK, (heads + h + 1) * DK)] = turn_back(
                key_back, cos[...], sin[...]
            ).astype(BF)
            value_low[at, vc] = (value_part[at, vc] + dot(key_dec, after)).astype(BF)
        sums[j] += dot(value_low[at], wv[...], 1, 1).astype(sums.dtype)
        parts[j] = (sums[j].astype(F32) + dot(qk_low[at, heads * DK :], wk[...], 1, 1)).astype(BF)
        scatter.send(i)
        for put in leaving(j):
            put.start()

    scatter.relay()

    @pl.when(ends.takes)
    def _():
        width = gate_late.shape[1]
        load_late.wait()
        late.wait_recv()
        sums[0, :, :width] = dot(og_late[...], wo[...], 1, 1).astype(sums.dtype)
        slab = 16

        @pl.loop(0, rows // slab)
        def _(r):
            here = pl.ds(pl.multiple_of(r * slab, slab), slab)
            gelu, slope = gelu_of(gate_late[here])
            back = sums[0, here, :width].astype(F32)
            gate_low[here] = (back * up_late[here] * slope).astype(BF)
            upper_low[here] = (back * gelu).astype(BF)

    def write(cols, total):
        grad_one[:, cols] = total

    scatter.finish(write)

    def write_mlp(cols, total):
        mlp_out[:, cols] = total

    scatter_mlp.finish(write_mlp)
    gather.drain()
    scatter.drain()
    scatter_mlp.drain()

    @pl.when(ends.gives)
    def _():
        late.wait_send()

    for put in puts:
        put.wait()

    @pl.loop(0, n)
    def _(j):
        for put in leaving(j):
            put.wait()

    @pl.loop(0, n * heads)
    def _(p):
        chain.drain(p)


def mixer_back(fac, res, wo, wq, wk, wv, ws, q, k, v, sp, mx, prior, mlp_parts, decay, qfac, kfac, cos, sin, og_all, wd, gate_late, up_late, cid):
    n = lax.axis_size("tp")
    chips = lax.axis_size("seq") // 2
    rows, model = res.shape
    heads = q.shape[1] // DK
    pieces = n * heads
    total = n * rows
    keep = F32 if n <= 4 else BF
    dma = pltpu.SemaphoreType.DMA
    sems = max(10, n - 1)
    vmem = pl.BlockSpec(memory_space=pltpu.VMEM)
    hbm = pl.BlockSpec(memory_space=pl.ANY)
    shape = jax.ShapeDtypeStruct
    return pl.pallas_call(
        functools.partial(mixer_back_kernel, n, chips, heads),
        out_shape=(
            shape((n, rows, model), BF),
            shape((total, heads * DV), BF),
            shape((total, heads * DV), BF),
            shape((total, 2 * heads * DK), BF),
            shape((rows, model), F32),
            shape((rows, model), F32),
            shape((rows, model), BF),
            shape(gate_late.shape, BF),
            shape(gate_late.shape, BF),
        ),
        in_specs=[pl.BlockSpec(memory_space=pltpu.SMEM), vmem] + [hbm] * 12 + [vmem] * 5 + [hbm, hbm, vmem, vmem],
        out_specs=(hbm,) * 4 + (vmem,) * 5,
        scratch_shapes=[pltpu.VMEM(a.shape, a.dtype) for a in (q, k, v, sp, mx, prior, mlp_parts)]
        + [
            pltpu.VMEM((n, rows, model), BF),
            pltpu.VMEM((total, heads * DV), BF),
            pltpu.VMEM((total, heads * DV), BF),
            pltpu.VMEM((total, 2 * heads * DK), BF),
        ]
        + [pltpu.VMEM(w.shape, BF) for w in (wo, wq, wk, wv, ws)]
        + [
            pltpu.VMEM((total, heads * DV), BF),
            pltpu.VMEM((n, rows, model), keep),
            pltpu.VMEM((n, rows, model), BF),
            pltpu.VMEM((pieces, DK, DV), BF),
            pltpu.VMEM((pieces, DK, DV), BF),
            pltpu.VMEM((total, heads * DK), keep),
            pltpu.VMEM((total, heads * DV), BF),
        ]
        + scatter_scratch(n, rows, model)
        + scatter_scratch(n, rows, model)
        + chain_scratch(pieces)
        + [dma((6,))]
        + [dma((sems,))] * 6
        + [dma((1,)), dma((1,)), dma((3, n)), dma((4,)), dma((2,)), dma((2, n))],
        compiler_params=params(cid),
        name="mixer_back",
    )(fac, res, wo, wq, wk, wv, ws, q, k, v, sp, mx, prior, mlp_parts, decay, qfac, kfac, cos, sin, og_all, wd, gate_late, up_late)


def weights_kernel(chips, *refs):
    (
        two, og, og_late, hidden, gate_low, gate_late, up_low, up_late,
        one, res, swish_low, gated, value_low, qk_low,
        vec_two, gain, grad_h, raw_h, res_h, attn_h, mlp_h,
        down_o, gate_o, up_o, swish_o, mixer_o, value_o, query_o, key_o, back_o, outs_o, vec_out,
    ) = refs[:32]
    mlp = LineSums(
        chips, 1, chips - 2, ((two,), (og, og_late)),
        ((gate_low, gate_late), (up_low, up_late), (hidden,)), (0, 0, 1), refs[32:44],
    )
    mix = LineSums(
        chips, 0, chips - 1, ((one,), (res,)), ((swish_low,), (gated,), (value_low,), (qk_low,)),
        (0, 1, 0, 0), refs[44:56],
    )
    (
        turned, osem, grad, raw, res_grad, attn, mlp_out, back, outs, csem, dsem,
        vec, vec_near, vec_mid, vec_far, vs, vr, us, ur,
    ) = refs[56:]
    s, t = lax.axis_index("seq"), lax.axis_index("tp")
    span, tp = 2 * chips, vec_far.shape[0] + 1
    share = vec_mid.shape[1]
    ring = [((s + d) % span, t) for d in range(1, span)]
    cross = [(s, (t + d) % tp) for d in range(1, tp)]

    def part(who):
        return pl.ds(pl.multiple_of(who * share, share), share)

    greet(ring + cross)
    vec_first = [
        remote(vec.at[:, part((s + d) % span)], vec_near.at[d - 1], vs, vr, d - 1, ring[d - 1])
        for d in range(1, span)
    ]
    vec_last = [
        remote(vec_mid, vec_far.at[d - 1], us, ur, d - 1, cross[d - 1]) for d in range(1, tp)
    ]
    vec[...] = vec_two[...]
    for u in range(mix.units):
        if u < mlp.units:
            mlp.share(u)
        mix.share(u)

    @pl.loop(0, mix.units)
    def _(u):
        for w in range(mix.units):

            @pl.when(u == w)
            def _(w=w):
                if w < mlp.units:
                    mlp.ready(w)

        @pl.when(u < mlp.units)
        def _():
            mlp.step(u, 0)

        for w in range(mix.units):

            @pl.when(u == w)
            def _(w=w):
                mix.ready(w)

        @pl.loop(0, chips - 1)
        def _(k):
            @pl.when((u < mlp.units) & (k > 0))
            def _():
                mlp.step(u, k)

            mix.step(u, k)

        @pl.when(u == 0)
        def _():
            chunk = raw.shape[0]

            @pl.loop(0, grad_h.shape[0] // chunk)
            def _(c):
                here = pl.ds(pl.multiple_of(c * chunk, chunk), chunk)
                pairs = (grad_h, grad), (raw_h, raw), (res_h, res_grad), (attn_h, attn), (mlp_h, mlp_out)
                ins = [
                    pltpu.make_async_copy(a.at[here], b, csem.at[i])
                    for i, (a, b) in enumerate(pairs)
                ]
                for copy in ins:
                    copy.start()
                for copy in ins:
                    copy.wait()
                value = raw[...].astype(F32)
                outs[...] = (value + attn[...] + mlp_out[...]).astype(BF)
                center, inv = row_stats(value)
                hat = center * inv
                vec[0:1] += jnp.sum(grad[...] * hat, 0, keepdims=True)
                vec[1:2] += jnp.sum(grad[...], 0, keepdims=True)
                back[...] = (res_grad[...] + norm_pull(grad[...], hat, inv, gain[...])).astype(BF)
                puts = [
                    pltpu.make_async_copy(a, b.at[0, here], dsem.at[i])
                    for i, (a, b) in enumerate(((back, back_o), (outs, outs_o)))
                ]
                for copy in puts:
                    copy.start()
                for copy in puts:
                    copy.wait()

            for copy in vec_first:
                copy.start()

        @pl.when(u == 1)
        def _():
            for copy in vec_first:
                copy.wait_recv()
            vec_mid[...] = vec[:, part(s)] + jnp.sum(vec_near[...], 0)
            for copy in vec_last:
                copy.start()

        @pl.when(u > 0)
        def _():
            mlp.finish(u - 1)
            mix.finish(u - 1)

    half = mix.out.shape[2] // 2
    lo, hi = pl.ds(0, half), pl.ds(half, half)
    turned[...] = mlp.out[2].T
    pairs = [
        (mlp.out.at[0], gate_o),
        (mlp.out.at[1], up_o),
        (mix.out.at[0], swish_o),
        (turned, down_o),
        (turned, mixer_o),
        (mix.out.at[2], value_o),
        (mix.out.at[3, :, lo], query_o),
        (mix.out.at[3, :, hi], key_o),
    ]
    copies = [pltpu.make_async_copy(a, b, osem.at[i]) for i, (a, b) in enumerate(pairs)]
    for i in (3, 0, 1, 2, 5):
        copies[i].start()
    copies[3].wait()
    turned[...] = mix.out[1].T
    copies[4].start()
    mix.finish(mix.units - 1)
    for copy in copies[6:]:
        copy.start()
    for copy in vec_last:
        copy.wait_recv()
    vec_out[...] = vec_mid[...] + jnp.sum(vec_far[...], 0)
    for copy in vec_first + vec_last:
        copy.wait_send()
    mlp.drain()
    mix.drain()
    for i, copy in enumerate(copies):
        if i != 3:
            copy.wait()


def weight_sums(
    two, og, og_late, hidden, gate_low, gate_late, up_low, up_late, one, res, swish_low, gated, value_low,
    qk_low, vec_two, gain, grad, raw, res_grad, attn, mlp_out, cid,
):
    chips = lax.axis_size("seq") // 2
    tokens, model = one.shape
    width = gated.shape[1]
    mlp_tokens, mlp_width = hidden.shape
    keys = qk_low.shape[1] // 2
    cut = model // (2 * chips)
    dma = pltpu.SemaphoreType.DMA
    vmem = pl.BlockSpec(memory_space=pltpu.VMEM)
    hbm = pl.BlockSpec(memory_space=pl.ANY)
    shape = lambda *a: jax.ShapeDtypeStruct(a, F32)
    ring, cross = 2 * chips - 1, lax.axis_size("tp") - 1
    rows, share, chunk = raw.shape[0], model // (2 * chips), 16
    part = lambda dtype: pltpu.VMEM((chunk, model), dtype)
    return pl.pallas_call(
        functools.partial(weights_kernel, chips),
        out_shape=(
            shape(mlp_width, cut),
            shape(cut, mlp_width),
            shape(cut, mlp_width),
            shape(cut, width),
            shape(width, cut),
            shape(cut, width),
            shape(cut, keys),
            shape(cut, keys),
            jax.ShapeDtypeStruct((1, rows, model), BF),
            jax.ShapeDtypeStruct((1, rows, model), BF),
            shape(8, share),
        ),
        in_specs=[hbm] * 14 + [vmem] * 2 + [hbm] * 5,
        out_specs=(hbm,) * 10 + (vmem,),
        scratch_shapes=line_scratch(chips, 3, 2, mlp_tokens, cut, mlp_width)
        + line_scratch(chips, 4, 2, tokens, cut, width)
        + [
            pltpu.VMEM((width, cut), F32),
            dma((8,)),
            part(F32),
            part(BF),
            part(F32),
            part(F32),
            part(F32),
            part(BF),
            part(BF),
            dma((5,)),
            dma((2,)),
            pltpu.VMEM((8, model), F32),
            pltpu.VMEM((ring, 8, share), F32),
            pltpu.VMEM((8, share), F32),
            pltpu.VMEM((cross, 8, share), F32),
            dma((ring,)),
            dma((ring,)),
            dma((cross,)),
            dma((cross,)),
        ],
        compiler_params=params(cid),
        name="weights",
    )(two, og, og_late, hidden, gate_low, gate_late, up_low, up_late, one, res, swish_low, gated, value_low,
      qk_low, vec_two, gain, grad, raw, res_grad, attn, mlp_out)


def shards(
    inputs,
    query_weight,
    key_weight,
    value_weight,
    swish_weight,
    output_weight,
    gate_weight,
    up_weight,
    down_weight,
    attn_gain,
    attn_bias,
    mlp_gain,
    mlp_bias,
    output_grad,
):
    _, rows, model = inputs.shape
    heads = query_weight.shape[1] // DK
    seqs, tps = lax.axis_size("seq"), lax.axis_size("tp")
    raw, cotangent = inputs[0], output_grad[0]
    row = lambda v: v.reshape(1, model)
    flat = lambda a: a.reshape(-1, model)

    half_width = DK // 2
    frequencies = np.power(
        np.float32(10000.0), -np.arange(half_width, dtype=np.float32) / np.float32(half_width)
    )[None]
    decays = 1.0 - np.exp2(-5.0 - np.arange(heads * tps))
    factors = np.stack([np.power(decays, rows), np.log(decays)]).astype(np.float32)

    (
        one_all, grad_all, query, key, value, swish_pre, mixed, prior, gated, attn_out,
        decay_mat, query_fac, key_fac, cosine, sine,
    ) = mixer(
        factors, raw, cotangent, key_weight, value_weight, query_weight, swish_weight,
        output_weight, row(attn_gain), row(attn_bias), frequencies, 0,
    )
    two_all, hidden, gate_low, upper_low, mlp_parts, res_grad, res_low, vectors, gate_pre, up_pre = mlp(
        raw, attn_out, cotangent, row(mlp_gain), row(mlp_bias), grad_all, gate_weight, up_weight,
        down_weight, 1,
    )
    (
        res_all, swish_low, value_low, qk_low, normed_one_grad, mlp_out, og_late, gate_late, up_late,
    ) = mixer_back(
        factors, res_low, output_weight, query_weight, key_weight, value_weight, swish_weight,
        query, key, value, swish_pre, mixed, prior, mlp_parts, decay_mat, query_fac, key_fac,
        cosine, sine, grad_all, down_weight, gate_pre, up_pre, 2,
    )
    (
        down_grad, gate_grad, up_grad, swish_grad, mixer_grad, value_grad, query_grad, key_grad,
        input_grad, outputs, vector_sums,
    ) = weight_sums(
        flat(two_all), flat(grad_all), og_late, hidden, gate_low, gate_late, upper_low, up_late,
        flat(one_all), flat(res_all), swish_low, gated, value_low, qk_low, vectors, row(attn_gain),
        normed_one_grad, raw, res_grad, attn_out, mlp_out, 3,
    )
    each = model // (seqs * tps)
    vector_sums = lax.dynamic_slice(vector_sums, (0, lax.axis_index("tp") * each), (4, each))
    return (
        outputs,
        input_grad,
        query_grad,
        key_grad,
        value_grad,
        swish_grad,
        mixer_grad,
        gate_grad,
        up_grad,
        down_grad,
        vector_sums[0],
        vector_sums[1],
        vector_sums[2],
        vector_sums[3],
    )


def solution(mesh):
    return jax.shard_map(
        shards,
        mesh=mesh,
        in_specs=(
            P("tp", "seq", None),
            P(None, "tp"),
            P(None, "tp"),
            P(None, "tp"),
            P(None, "tp"),
            P("tp", None),
            P(None, "tp"),
            P(None, "tp"),
            P("tp", None),
            P(),
            P(),
            P(),
            P(),
            P("tp", "seq", None),
        ),
        out_specs=(
            P("tp", "seq", None),
            P("tp", "seq", None),
            P("seq", "tp"),
            P("seq", "tp"),
            P("seq", "tp"),
            P("seq", "tp"),
            P("tp", "seq"),
            P("seq", "tp"),
            P("seq", "tp"),
            P("tp", "seq"),
            P(("seq", "tp")),
            P(("seq", "tp")),
            P(("seq", "tp")),
            P(("seq", "tp")),
        ),
        check_vma=False,
    )
```

```python
import functools

import jax
import jax.numpy as jnp
import numpy as np
from jax import lax
from jax.experimental import pallas as pl
from jax.experimental.pallas import tpu as pltpu
from jax.sharding import PartitionSpec as P

DK = 256
DV = 512


EPS = 1e-05
MESH = pl.DeviceIdType.MESH
BF = jnp.bfloat16
F32 = jnp.float32
VMEM_LIMIT = 63 * 1024 * 1024 - 512 * 1024


def remote(src, dst, ssem, rsem, slot, dev):
    return pltpu.make_async_remote_copy(
        src_ref=src,
        dst_ref=dst,
        send_sem=ssem.at[slot],
        recv_sem=rsem.at[slot],
        device_id=dev,
        device_id_type=MESH,
    )


def greet(devs):
    barrier = pltpu.get_barrier_semaphore()
    for dev in devs:
        pl.semaphore_signal(barrier, inc=1, device_id=dev, device_id_type=MESH)
    pl.semaphore_wait(barrier, len(devs))


def params(cid):
    return pltpu.CompilerParams(
        collective_id=cid, has_side_effects=True, vmem_limit_bytes=VMEM_LIMIT
    )


class Gather:
    def __init__(self, n, x, o, ssem, rsem, base=0):
        s, t = lax.axis_index("seq"), lax.axis_index("tp")
        self.n, self.t = n, t
        rows = x.shape[0]
        if n == 4:
            px, py = t + 1 - 2 * (t % 2), (t + 2) % 4
            dx, dy = (s, px), (s, py)
            self.peers = [dx, dy]
            half = rows // 2
            lo, hi = pl.ds(0, half), pl.ds(half, half)
            self.first = [
                remote(x.at[lo], o.at[base + t, lo], ssem, rsem, 0, dx),
                remote(x.at[hi], o.at[base + t, hi], ssem, rsem, 1, dy),
                remote(x.at[hi], o.at[base + t, hi], ssem, rsem, 2, dx),
                remote(x.at[lo], o.at[base + t, lo], ssem, rsem, 3, dy),
            ]
            self.relay = [
                remote(o.at[base + px, lo], o.at[base + px, lo], ssem, rsem, 4, dy),
                remote(o.at[base + py, hi], o.at[base + py, hi], ssem, rsem, 5, dx),
            ]
        else:
            self.peers = [(s, (t + k) % n) for k in range(1, n)]
            self.first = [
                remote(x, o.at[base + t], ssem, rsem, k, dev) for k, dev in enumerate(self.peers)
            ]
            self.relay = []

    def source(self, i):
        t = self.t
        if self.n == 4:
            near = jnp.where(i == 1, t + 1 - 2 * (t % 2), (t + 2) % 4)
            return jnp.where(i == 0, t, jnp.where(i == 3, 3 - t, near))
        return (t - i + self.n) % self.n

    def start(self):
        for copy in self.first:
            copy.start()

    def relays(self):
        for copy, onward in zip(self.first, self.relay):
            copy.wait_recv()
            onward.start()

    def arrive(self, i):
        if self.n == 4:

            @pl.when(i == 1)
            def _():
                self.first[2].wait_recv()

            @pl.when(i == 2)
            def _():
                self.first[3].wait_recv()

            @pl.when(i == 3)
            def _():
                self.relay[0].wait_recv()
                self.relay[1].wait_recv()

        else:
            for k, copy in enumerate(self.first):

                @pl.when(i == k + 1)
                def _(copy=copy):
                    copy.wait_recv()

    def drain(self):
        for copy in self.first + self.relay:
            copy.wait_send()


class Scatter:
    def __init__(self, n, parts, near, far, hold, ssem, rsem):
        s, t = lax.axis_index("seq"), lax.axis_index("tp")
        self.n, self.t = n, t
        self.parts, self.near, self.far, self.hold = parts, near, far, hold
        if n == 4:
            self.px, self.py, pd = t + 1 - 2 * (t % 2), (t + 2) % 4, 3 - t
            dx, dy = (s, self.px), (s, self.py)
            self.peers = [dx, dy]
            half = parts.shape[-1] // 2
            self.cols = a, b = pl.ds(0, half), pl.ds(half, half)
            rows = parts.shape[1] // 2
            self.halves = (pl.ds(0, rows), pl.ds(rows, rows))
            self.far_a = [
                remote(parts.at[pd, r, a], near.at[0, 1, r], ssem, rsem, i, dx)
                for i, r in enumerate(self.halves)
            ]
            self.far_b = [
                remote(parts.at[pd, r, b], near.at[1, 1, r], ssem, rsem, 6 + i, dy)
                for i, r in enumerate(self.halves)
            ]
            self.near_a = remote(parts.at[self.px, :, a], near.at[0, 0], ssem, rsem, 2, dx)
            self.near_b = remote(parts.at[self.py, :, b], near.at[1, 0], ssem, rsem, 3, dy)
            self.sum_a = [
                remote(hold.at[0, r], far.at[0, r], ssem, rsem, 4 + i, dy)
                for i, r in enumerate(self.halves)
            ]
            self.sum_b = [
                remote(hold.at[1, r], far.at[1, r], ssem, rsem, 8 + i, dx)
                for i, r in enumerate(self.halves)
            ]
            self.copies = self.far_a + self.far_b + [self.near_a, self.near_b]
            self.copies += self.sum_a + self.sum_b
        else:
            self.peers = [(s, (t + k) % n) for k in range(1, n)]
            self.copies = [
                remote(parts.at[(t - k + n) % n], near.at[k - 1], ssem, rsem, k - 1, (s, (t - k + n) % n))
                for k in range(1, n)
            ]

    def send(self, i):
        if self.n == 4:

            @pl.when(i == 1)
            def _():
                self.near_a.start()

            @pl.when(i == 2)
            def _():
                self.near_b.start()

            @pl.when(i == 3)
            def _():
                for copy_a, copy_b in zip(self.far_a, self.far_b):
                    copy_a.start()
                    copy_b.start()

        else:
            for k, copy in enumerate(self.copies):

                @pl.when(i == k + 1)
                def _(copy=copy):
                    copy.start()

    def relay(self):
        if self.n == 4:
            sides = (self.cols[0], self.py, self.far_a, self.sum_a), (
                self.cols[1], self.px, self.far_b, self.sum_b
            )
            for i, r in enumerate(self.halves):
                for side, (cols, who, came, onward) in enumerate(sides):
                    came[i].wait_recv()
                    self.hold[side, r] = (
                        self.parts[who, r, cols].astype(F32) + self.near[side, 1, r].astype(F32)
                    ).astype(BF)
                    onward[i].start()

    def finish(self, write):
        if self.n == 4:
            for side, (one, two) in enumerate(
                ((self.near_a, self.sum_a), (self.near_b, self.sum_b))
            ):
                one.wait_recv()
                for copy in two:
                    copy.wait_recv()
                write(
                    slice(None),
                    self.cols[side],
                    self.parts[self.t, :, self.cols[side]].astype(F32)
                    + self.near[side, 0].astype(F32)
                    + self.far[side].astype(F32),
                )
        else:
            for copy in self.copies:
                copy.wait_recv()

            @pl.loop(0, self.parts.shape[1] // 16)
            def _(r):
                at = pl.ds(pl.multiple_of(r * 16, 16), 16)
                total = self.parts[self.t, at].astype(F32)
                for k in range(self.n - 1):
                    total = total + self.near[k, at].astype(F32)
                write(at, slice(None), total)

    def drain(self):
        for copy in self.copies:
            copy.wait_send()


def scatter_scratch(n, rows, width):
    if n == 4:
        near, far = (2, 2, rows, width // 2), (2, rows, width // 2)
    else:
        near, far = (n - 1, rows, width), (1, 16, 128)
    return [pltpu.VMEM(near, BF), pltpu.VMEM(far, BF), pltpu.VMEM(far, BF)]


class Ends:
    def __init__(self, chips):
        s, t = lax.axis_index("seq"), lax.axis_index("tp")
        chip, span = s // 2, 2 * chips
        self.gives = (chip == 0) | (chip == chips - 1)
        self.takes = (chip == 1) | (chip == chips - 2)
        self.peers = [((s + 2) % span, t), ((s - 2 + span) % span, t)]
        step = jnp.where(chip == 0, 2, jnp.where(chip == chips - 1, span - 2, 0))
        self.mate = ((s + step) % span, t)


class Chain:
    def __init__(self, chips, heads, flip, fac, local, out, pair, enter, ps, pr, zs, zr, bs, br):
        s, t = lax.axis_index("seq"), lax.axis_index("tp")
        core, chip, span = s % 2, s // 2, 2 * chips
        self.chips, self.heads, self.fac = chips, heads, fac
        self.local, self.out, self.pair, self.enter, self.leave = local, out, pair, enter, local
        self.sems = ps, pr, zs, zr, bs, br
        self.partner = (s + 1 - 2 * core, t)
        above, below = ((s + 2) % span, t), ((s - 2 + span) % span, t)
        self.peers = [self.partner, above, below]
        if flip:
            self.first, self.place, self.ahead = core == 1, chips - 1 - chip, below
        else:
            self.first, self.place, self.ahead = core == 0, chip, above
        self.last = jnp.logical_not(self.first)

    def give(self, p):
        return remote(self.local.at[p], self.pair.at[p], self.sems[0], self.sems[1], p, self.partner)

    def back(self, p):
        return remote(self.enter.at[p], self.out.at[p], self.sems[4], self.sems[5], p, self.partner)

    def onward(self, p):
        return remote(self.leave.at[p], self.enter.at[p], self.sems[2], self.sems[3], p, self.ahead)

    def piece(self, gather, index):
        return gather.source(index // self.heads) * self.heads + index % self.heads

    def open(self, gather, i):
        @pl.when(self.place == 0)
        def _():
            @pl.loop(0, self.heads)
            def _(h):
                self.step(self.piece(gather, i * self.heads + h))

    def tick(self, gather, now):
        total = self.local.shape[0]
        ends = self.place == self.chips - 1
        lag = jnp.minimum(3 * (self.place - 1), total - self.heads)
        index = jnp.where(ends, (self.heads + now) % total, now - lag)
        due = (self.place > 0) & (index >= 0) & (index < total)

        @pl.when(due & (jnp.logical_not(ends) | (now >= total)))
        def _():
            self.step(self.piece(gather, jnp.maximum(index, 0)))

    def planned(self, gather, i, plan):
        block = jnp.int32(0)
        for place, turn, ahead in plan:
            block = jnp.where((self.place == place) & (i == turn), ahead, block)

        @pl.when(block > 0)
        def _():
            @pl.loop(0, self.heads)
            def _(h):
                self.step(self.piece(gather, block * self.heads + h))

    def due(self, gather, i, plan):
        now = self.place > 0
        for place, _, ahead in plan:
            now = now & ((self.place != place) | (i != ahead))

        @pl.when(now)
        def _():
            @pl.loop(0, self.heads)
            def _(h):
                self.step(self.piece(gather, i * self.heads + h))

    def begin(self, p):
        @pl.when(self.first)
        def _():
            self.give(p).start()

            @pl.when(self.place == 0)
            def _():
                self.out[p] = jnp.zeros(self.out.shape[1:], BF)

    def step(self, p):
        @pl.when(self.first)
        def _():
            @pl.when(self.place > 0)
            def _():
                self.back(p).wait_recv()

        @pl.when(self.last)
        def _():
            fac = self.fac[0, lax.axis_index("tp") * self.heads + p % self.heads]
            self.give(p).wait_recv()
            early = self.pair[p].astype(F32)
            chip_sum = early * fac + self.local[p].astype(F32)

            @pl.when(self.place == 0)
            def _():
                self.leave[p] = chip_sum.astype(BF)
                self.out[p] = self.pair[p]

            @pl.when(self.place > 0)
            def _():
                self.onward(p).wait_recv()
                self.back(p).start()
                came = self.enter[p].astype(F32)
                self.leave[p] = (came * (fac * fac) + chip_sum).astype(BF)
                self.out[p] = (came * fac + early).astype(BF)

            @pl.when(self.place < self.chips - 1)
            def _():
                self.onward(p).start()

    def drain(self, p):
        @pl.when(self.first)
        def _():
            self.give(p).wait_send()

        @pl.when(self.last)
        def _():
            @pl.when(self.place > 0)
            def _():
                self.back(p).wait_send()

            @pl.when(self.place < self.chips - 1)
            def _():
                self.onward(p).wait_send()


def chain_scratch(pieces):
    dma = pltpu.SemaphoreType.DMA
    return [pltpu.VMEM((pieces, DK, DV), BF)] * 2 + [dma((pieces,))] * 6


def dot(a, b, ca=1, cb=0):
    return lax.dot_general(a, b, (((ca,), (cb,)), ((), ())), preferred_element_type=F32)


def turn(v, cos, sin):
    lo, hi = v[:, : DK // 2], v[:, DK // 2 :]
    return jnp.concatenate([lo * cos - hi * sin, hi * cos + lo * sin], 1)


def turn_back(g, cos, sin):
    lo, hi = g[:, : DK // 2], g[:, DK // 2 :]
    return jnp.concatenate([lo * cos + hi * sin, hi * cos - lo * sin], 1)


def row_stats(v):
    center = v - jnp.mean(v, -1, keepdims=True)
    return center, lax.rsqrt(jnp.mean(center * center, -1, keepdims=True) + EPS)


def norm_pull(grad, hat, inv, gain):
    g = grad * gain
    return (g - jnp.mean(g, -1, keepdims=True) - hat * jnp.mean(g * hat, -1, keepdims=True)) * inv


def norm_of(m):
    center = m - jnp.mean(m, -1, keepdims=True)
    inv = lax.rsqrt(jnp.mean(center * center, -1, keepdims=True) + EPS)
    return center * inv, inv


class LineSums:
    def __init__(self, chips, lo, hi, wide, deep, kinds, refs, swap=False):
        s, t = lax.axis_index("seq"), lax.axis_index("tp")
        self.core, self.chip, self.chips, self.lo, self.hi = s % 2, s // 2, chips, lo, hi
        self.wide, self.deep, self.kinds = wide, deep, kinds
        (
            self.xs, self.ys, self.buf, self.out,
            self.xsem, self.ysem, self.psx, self.prx, self.psy, self.pry, self.ssem, self.rsem,
        ) = refs
        self.units = len(deep)
        self.swap = swap
        self.tokens = self.ys.shape[1] // 2
        self.cut = self.xs.shape[3]
        self.spans = [self.places(parts) for parts in wide], [self.places(parts) for parts in deep]
        span = 2 * chips
        self.partner = (s + 1 - 2 * self.core, t)
        self.above = ((s + 2) % span, t)
        self.below = ((s - 2 + span) % span, t)
        self.peers = [self.partner, self.above, self.below]

    def cols(self, j, core):
        return pl.ds(pl.multiple_of((2 * j + core) * self.cut, self.cut), self.cut)

    def places(self, parts):
        found, start = [], 0
        for part in parts:
            found.append((start, part.shape[0]))
            start += part.shape[0]
        assert start == self.tokens
        return found

    def wide_own(self, kind, j):
        return [
            pltpu.make_async_copy(
                part.at[:, self.cols(j, self.core)],
                self.xs.at[kind, j, pl.ds(start, size)],
                self.xsem.at[kind, j, i],
            )
            for i, (part, (start, size)) in enumerate(zip(self.wide[kind], self.spans[0][kind]))
        ]

    def wide_give(self, kind, j):
        return [
            remote(
                part.at[:, self.cols(j, 1 - self.core)],
                self.xs.at[kind, j, pl.ds(self.tokens + start, size)],
                self.psx.at[kind, j],
                self.prx.at[kind, j],
                i,
                self.partner,
            )
            for i, (part, (start, size)) in enumerate(zip(self.wide[kind], self.spans[0][kind]))
        ]

    def deep_own(self, u):
        return [
            pltpu.make_async_copy(
                part, self.ys.at[u, pl.ds(start, size)], self.ysem.at[u, i]
            )
            for i, (part, (start, size)) in enumerate(zip(self.deep[u], self.spans[1][u]))
        ]

    def deep_give(self, u):
        return [
            remote(
                part,
                self.ys.at[u, pl.ds(self.tokens + start, size)],
                self.psy.at[u],
                self.pry.at[u],
                i,
                self.partner,
            )
            for i, (part, (start, size)) in enumerate(zip(self.deep[u], self.spans[1][u]))
        ]

    def adds(self):
        return (self.chip >= self.lo) & (self.chip <= self.hi)

    def share(self, u):
        @pl.when(self.adds())
        def _():
            if self.kinds[u] not in self.kinds[:u]:
                for j in range(self.chips):
                    for copy in self.wide_give(self.kinds[u], j) + self.wide_own(self.kinds[u], j):
                        copy.start()
            for copy in self.deep_give(u) + self.deep_own(u):
                copy.start()

    def ready(self, u):
        @pl.when(self.adds())
        def _():
            own, given = self.deep_own(u), self.deep_give(u)
            if self.kinds[u] not in self.kinds[:u]:
                for j in range(self.chips):
                    own += self.wide_own(self.kinds[u], j)
                    given += self.wide_give(self.kinds[u], j)
            for copy in own:
                copy.wait()
            for copy in given:
                copy.wait_recv()

    def up(self, u, j):
        return remote(
            self.buf.at[u, j], self.buf.at[u, j], self.ssem.at[u], self.rsem.at[u], j, self.above
        )

    def down(self, u, j):
        slot = jnp.where(j == self.chip - 1, self.chips, j)
        return pltpu.make_async_remote_copy(
            src_ref=self.buf.at[u, j],
            dst_ref=self.buf.at[u, slot],
            send_sem=self.ssem.at[u, j],
            recv_sem=self.rsem.at[u, slot],
            device_id=self.below,
            device_id_type=MESH,
        )

    def arrived(self, u, slot):
        remote(
            self.buf.at[u, slot], self.buf.at[u, slot], self.ssem.at[u], self.rsem.at[u], slot,
            self.above,
        ).wait_recv()
        return self.buf[u, slot].astype(F32)

    def product(self, u, j):
        kind = 0
        for w in range(self.units):
            if self.kinds[w]:
                kind = kind + jnp.where(u == w, self.kinds[w], 0)
        if self.swap:
            return dot(self.ys[u], self.xs[kind, j], 0, 0)
        return dot(self.xs[kind, j], self.ys[u], 0, 0)

    def order(self, k):
        rights = self.chips - 1 - self.chip
        return jnp.where(
            self.chip < self.chips // 2,
            jnp.where(k < rights, self.chips - 1 - k, k - rights),
            jnp.where(k < self.chip, k, self.chips - 1 - (k - self.chip)),
        )

    def step(self, u, k):
        chip = self.chip
        j = self.order(k)

        @pl.when(self.adds())
        def _():
            total = self.product(u, j)

            @pl.when(((j > chip) & (chip == self.lo)) | ((j < chip) & (chip == self.hi)))
            def _():
                self.buf[u, j] = total.astype(BF)

            @pl.when(((j > chip) & (chip > self.lo)) | ((j < chip) & (chip < self.hi)))
            def _():
                self.buf[u, j] = (total + self.arrived(u, j)).astype(BF)

            @pl.when(j > chip)
            def _():
                self.up(u, j).start()

            @pl.when(j < chip)
            def _():
                self.down(u, j).start()

    def finish(self, u):
        chip = self.chip

        @pl.when(self.adds())
        def _():
            self.out[0] = self.product(u, chip)

        @pl.when((chip < self.lo) | (chip > self.hi))
        def _():
            self.out[0] = jnp.zeros(self.out.shape[1:], F32)

        @pl.when(chip > self.lo)
        def _():
            self.out[0] += self.arrived(u, chip)

        @pl.when(chip < self.hi)
        def _():
            self.out[0] += self.arrived(u, self.chips)

    def drain(self):
        @pl.when(self.adds())
        def _():
            @pl.loop(0, self.units)
            def _(u):
                @pl.loop(0, self.chips)
                def _(j):
                    @pl.when(j > self.chip)
                    def _():
                        self.up(u, j).wait_send()

                    @pl.when(j < self.chip)
                    def _():
                        self.down(u, j).wait_send()

            for u in range(self.units):
                for copy in self.deep_give(u):
                    copy.wait_send()
            for kind in range(max(self.kinds) + 1):
                for j in range(self.chips):
                    for copy in self.wide_give(kind, j):
                        copy.wait_send()


def line_scratch(chips, units, kinds, tokens, cut, width, swap=False):
    dma = pltpu.SemaphoreType.DMA
    block = (width, cut) if swap else (cut, width)
    return [
        pltpu.VMEM((kinds, chips, 2 * tokens, cut), BF),
        pltpu.VMEM((units, 2 * tokens, width), BF),
        pltpu.VMEM((units, chips + 1) + block, BF),
        pltpu.VMEM((1,) + block, F32),
        dma((kinds, chips, 2)),
        dma((units, 2)),
        dma((kinds, chips, 2)),
        dma((kinds, chips, 2)),
        dma((units, 2)),
        dma((units, 2)),
        dma((units, chips + 1)),
        dma((units, chips + 1)),
    ]


def mixer_kernel(n, chips, heads, *refs):
    (
        fac, raw, og, wk_h, wv_h, wq_h, ws_h, wo_h, gain, bias, freq,
        x_o, og_o, q_o, k_o, v_o, sp_o, mx_o, prior_o, gated_o, attn, decay, qfac, kfac, cos, sin,
        x_all, og_all, q, k, v, sp, mx, prior, gated, x, wk, wv, wq, ws, wo, acc, parts, local,
    ) = refs[:44]
    near, far, hold = refs[44:47]
    chain_refs = refs[47:55]
    wsem, gs, gr, os, orr, ss, sr, es, er, osem, bsem = refs[55:]
    rows = raw.shape[0]
    gather = Gather(n, x, x_all, gs, gr)
    gather_og = Gather(n, og, og_all, os, orr)
    ends = Ends(chips)
    hand_own = remote(og, og_o.at[n], es, er, 0, ends.mate)

    def hand(i):
        return remote(og_all.at[gather.source(i)], og_o.at[n + i], es, er, i, ends.mate)

    scatter = Scatter(n, parts, near, far, hold, ss, sr)
    chain = Chain(chips, heads, False, fac, local, prior, *chain_refs)
    loads = [
        pltpu.make_async_copy(a, w, wsem.at[i])
        for i, (a, w) in enumerate(((wk_h, wk), (wv_h, wv), (wq_h, wq), (ws_h, ws), (wo_h, wo)))
    ]
    for load in loads:
        load.start()
    slab = 16
    plan = ((1, 1, 1), (1, 3, 2)) if n == 4 else ()

    @pl.loop(0, rows // slab)
    def _(r):
        here = pl.ds(pl.multiple_of(r * slab, slab), slab)
        center, inv = row_stats(raw[here].astype(F32))
        x[here] = (center * inv * gain[...] + bias[...]).astype(BF)

    greet(gather.peers + chain.peers)
    gather.start()
    place = lax.broadcasted_iota(jnp.int32, (rows, 1), 0).astype(F32)
    angles = (lax.axis_index("seq").astype(F32) * rows + place) * freq[...]
    cos[...] = jnp.cos(angles)
    sin[...] = jnp.sin(angles)
    lag = place - lax.broadcasted_iota(jnp.int32, (rows, rows), 1).astype(F32)
    for h in range(heads):
        rate = fac[1, lax.axis_index("tp") * heads + h]
        decay[h] = jnp.where(lag >= 0, jnp.exp(jnp.maximum(lag, 0.0) * rate), 0.0)
        qfac[h] = jnp.exp((place + 1.0) * rate)
        kfac[h] = jnp.exp((rows - 1.0 - place) * rate)

    @pl.when(ends.gives)
    def _():
        hand_own.start()

    me = gather.source(0)
    x_all[me] = x[...]
    og_all[me] = og[...]
    for load in loads[:2]:
        load.wait()

    @pl.loop(0, n)
    def _(i):
        j = gather.source(i)
        gather.arrive(i)
        at = pl.ds(pl.multiple_of(j * rows, rows), rows)
        acc[:, : heads * DK] = dot(x_all[j], wk[...])

        v[at] = dot(x_all[j], wv[...]).astype(BF)
        for h in range(heads):
            vc = slice(h * DV, (h + 1) * DV)
            kc = slice(h * DK, (h + 1) * DK)
            key = turn(acc[:, kc], cos[...], sin[...]).astype(BF)
            k[at, kc] = key
            key_dec = (key.astype(F32) * kfac[h]).astype(BF)
            p = j * heads + h
            local[p] = dot(key_dec, v[at, vc], 0, 0).astype(BF)
            chain.begin(p)

        chain.open(gather, i)

        @pl.when(i == 0)
        def _():
            gather.relays()
            gather_og.start()

    puts = [
        pltpu.make_async_copy(a, b, osem.at[i])
        for i, (a, b) in enumerate(
            ((x_all, x_o), (k, k_o), (v, v_o), (q, q_o), (sp, sp_o), (og_all, og_o.at[pl.ds(0, n)]))
        )
    ]
    for put in puts[:3]:
        put.start()
    for load in loads[2:]:
        load.wait()

    @pl.loop(0, n)
    def _(i):
        j = gather.source(i)
        at = pl.ds(pl.multiple_of(j * rows, rows), rows)
        acc[:, : heads * DK] = dot(x_all[j], wq[...])
        for h in range(heads):
            kc = slice(h * DK, (h + 1) * DK)
            vc = slice(h * DV, (h + 1) * DV)
            query = turn(acc[:, kc], cos[...], sin[...]).astype(BF)
            q[at, kc] = query
            scores = (dot(query, k[at, kc], 1, 1) * decay[h]).astype(BF)
            mx[at, vc] = dot(scores, v[at, vc])
            sp[at, vc] = dot(x_all[j], ws[:, vc])
        chain.planned(gather, i, plan)

    for put in puts[3:5]:
        put.start()
    gather_og.relays()

    def blocks(j):
        at = pl.ds(pl.multiple_of(j * rows, rows), rows)
        of = pl.ds(j * heads, heads)
        return [
            pltpu.make_async_copy(mx.at[at], mx_o.at[at], bsem.at[0, j]),
            pltpu.make_async_copy(gated.at[at], gated_o.at[at], bsem.at[1, j]),
            pltpu.make_async_copy(prior.at[of], prior_o.at[of], bsem.at[2, j]),
        ]


    @pl.loop(0, n)
    def _(step):
        i = (step + 1) % n
        j = gather.source(i)
        chain.due(gather, i, plan)
        gather_og.arrive(i)

        @pl.when(ends.gives & (chain.place > 0) & (i > 0) & (i < n - 1))
        def _():
            hand(i).start()

        at = pl.ds(pl.multiple_of(j * rows, rows), rows)
        for h in range(heads):
            vc = slice(h * DV, (h + 1) * DV)
            kc = slice(h * DK, (h + 1) * DK)
            p = j * heads + h
            query_dec = (q[at, kc].astype(F32) * qfac[h]).astype(BF)
            mx[at, vc] += dot(query_dec, prior[p])
            pre = sp[at, vc]
            gated[at, vc] = (pre * jax.nn.sigmoid(pre) * norm_of(mx[at, vc])[0]).astype(BF)
        parts[j] = dot(gated[at], wo[...]).astype(BF)
        scatter.send(i)

        @pl.when(ends.gives & (chain.place == 0) & (step == n - 2))
        def _():
            @pl.loop(1, n - 1)
            def _(c):
                hand(c).start()

        for put in blocks(j):
            put.start()

    puts[5].start()
    scatter.relay()

    def write(at, cols, total):
        attn[at, cols] = total

    scatter.finish(write)
    gather.drain()
    gather_og.drain()
    for put in puts:
        put.wait()

    @pl.loop(0, n)
    def _(j):
        for put in blocks(j):
            put.wait()

    @pl.when(ends.gives)
    def _():
        hand_own.wait_send()

        @pl.loop(1, n - 1)
        def _(i):
            hand(i).wait_send()

    @pl.when(ends.takes)
    def _():
        @pl.loop(0, n - 1)
        def _(i):
            hand(i).wait_recv()

    scatter.drain()

    @pl.loop(0, n * heads)
    def _(p):
        chain.drain(p)


def mixer(fac, x, og, wk, wv, wq, ws, wo, gain, bias, freq, cid):
    n = lax.axis_size("tp")
    chips = lax.axis_size("seq") // 2
    rows, model = x.shape
    heads = wk.shape[1] // DK
    pieces = n * heads
    total = n * rows
    dma = pltpu.SemaphoreType.DMA
    sems = max(10, n - 1)
    vmem = pl.BlockSpec(memory_space=pltpu.VMEM)
    hbm = pl.BlockSpec(memory_space=pl.ANY)
    shape = jax.ShapeDtypeStruct
    return pl.pallas_call(
        functools.partial(mixer_kernel, n, chips, heads),
        out_shape=(
            shape((n, rows, model), BF),
            shape((2 * n - 1, rows, model), BF),
            shape((total, heads * DK), BF),
            shape((total, heads * DK), BF),
            shape((total, heads * DV), BF),
            shape((total, heads * DV), F32),
            shape((total, heads * DV), F32),
            shape((pieces, DK, DV), BF),
            shape((total, heads * DV), BF),
            shape((rows, model), F32),
            shape((heads, rows, rows), F32),
            shape((heads, rows, 1), F32),
            shape((heads, rows, 1), F32),
            shape((rows, DK // 2), F32),
            shape((rows, DK // 2), F32),
        ),
        in_specs=[pl.BlockSpec(memory_space=pltpu.SMEM), vmem, vmem] + [hbm] * 5 + [vmem] * 3,
        out_specs=(hbm,) * 9 + (vmem,) * 6,
        scratch_shapes=[
            pltpu.VMEM((n, rows, model), BF),
            pltpu.VMEM((n, rows, model), BF),
            pltpu.VMEM((total, heads * DK), BF),
            pltpu.VMEM((total, heads * DK), BF),
            pltpu.VMEM((total, heads * DV), BF),
            pltpu.VMEM((total, heads * DV), F32),
            pltpu.VMEM((total, heads * DV), F32),
            pltpu.VMEM((pieces, DK, DV), BF),
            pltpu.VMEM((total, heads * DV), BF),
            pltpu.VMEM((rows, model), BF),
        ]
        + [pltpu.VMEM(w.shape, BF) for w in (wk, wv, wq, ws, wo)]
        + [
            pltpu.VMEM((rows, heads * DK), F32),
            pltpu.VMEM((n, rows, model), BF),
            pltpu.VMEM((pieces, DK, DV), BF),
        ]
        + scatter_scratch(n, rows, model)
        + chain_scratch(pieces)
        + [dma((5,))]
        + [dma((sems,))] * 6
        + [dma((n - 1,)), dma((n - 1,)), dma((6,)), dma((3, n))],
        compiler_params=params(cid),
        name="mixer",
    )(fac, x, og, wk, wv, wq, ws, wo, gain, bias, freq)


GELU_C = 0.7978845608028654
GELU_A = 0.044715


def gelu_of(g):
    square = g * g
    th = jnp.tanh(GELU_C * (g + GELU_A * (square * g)))
    half = 0.5 * (1.0 + th)
    slope = half + 0.5 * g * (1.0 - th * th) * (GELU_C * (1.0 + 3.0 * GELU_A * square))
    return g * half, slope


def mlp_kernel(n, chips, *refs):
    (
        raw, attn, cot, gain, bias, og_h, wg_h, wu_h, wd_h,
        x_o, hidden_o, gate_o, upper_o, mlp_o, res_grad, res_low, vec, gate_late, up_late,
        og_all, x, grad_two, x_all, hidden, gate_low, upper_low, mlp_parts, wg, wu, wd, hg, acc_g, acc_u, acc, parts, near, far, hold,
        wsem, gs, gr, ss, sr, es, er, osem, bsem,
    ) = refs
    rows = raw.shape[0]
    slab = 16
    gather = Gather(n, x, x_all, gs, gr)
    scatter = Scatter(n, parts, near, far, hold, ss, sr)
    ends = Ends(chips)
    loads = [
        pltpu.make_async_copy(a, w, wsem.at[i])
        for i, (a, w) in enumerate(((wd_h, wd), (wg_h, wg), (wu_h, wu)))
    ]
    loads.append(pltpu.make_async_copy(og_h, og_all, wsem.at[3]))
    for load in [loads[0], loads[3], loads[1], loads[2]]:
        load.start()
    @pl.loop(0, rows // slab)
    def _(r):
        here = pl.ds(pl.multiple_of(r * slab, slab), slab)
        center, inv = row_stats(raw[here].astype(F32) + attn[here])
        x[here] = (center * inv * gain[...] + bias[...]).astype(BF)

    greet(gather.peers + ends.peers)
    gather.start()
    me = gather.source(0)

    def hand(i):
        j = gather.source(i)
        return remote(x_all.at[j], x_all.at[n + i], es, er, i, ends.mate)

    first = remote(x, x_all.at[n], es, er, 0, ends.mate)

    @pl.when(ends.gives)
    def _():
        first.start()

    x_all[me] = x[...]
    loads[0].wait()
    loads[3].wait()
    pair = 2 * rows

    @pl.loop(0, n // 2)
    def _(c):
        two = pl.ds(pl.multiple_of(2 * c, 2), 2)
        at = pl.ds(pl.multiple_of(c * pair, pair), pair)
        hg[at] = dot(og_all[two].reshape(pair, x.shape[1]), wd[...], 1, 1)

    gather.relays()
    loads[1].wait()
    loads[2].wait()

    def units(block, back_at, extra):
        start = pl.multiple_of(block * rows, rows)
        acc_g[...] = dot(x_all[block], wg[...])
        acc_u[...] = dot(x_all[block], wu[...])
        if extra:
            gate_late[...] = acc_g[...]
            up_late[...] = acc_u[...]

        @pl.loop(0, rows // slab)
        def _(r):
            here = pl.ds(pl.multiple_of(r * slab, slab), slab)
            there = pl.ds(pl.multiple_of(start + r * slab, slab), slab)
            g, u = acc_g[here], acc_u[here]
            gelu, slope = gelu_of(g)
            hidden[there] = (gelu * u).astype(BF)
            back = hg[pl.ds(pl.multiple_of(back_at + r * slab, slab), slab)]
            gate_low[there] = (back * u * slope).astype(BF)
            upper_low[there] = (back * gelu).astype(BF)

    @pl.loop(0, n)
    def _(turn):
        i = jnp.where(turn == 2, 3, jnp.where(turn == 3, 2, turn)) if n == 4 else turn
        j = gather.source(i)
        gather.arrive(i)

        @pl.when(ends.gives & (i > 0))
        def _():
            hand(i).start()

        units(j, j * rows, False)
        at = pl.ds(pl.multiple_of(j * rows, rows), rows)
        acc[...] = dot(gate_low[at], wg[...], 1, 1)
        parts[j] = (acc[...] + dot(upper_low[at], wu[...], 1, 1)).astype(BF)
        scatter.send(i)

    whole = pl.ds(0, n * rows)
    puts = [
        pltpu.make_async_copy(a, b, osem.at[i])
        for i, (a, b) in enumerate(
            (
                (x_all.at[pl.ds(0, n)], x_o.at[pl.ds(0, n)]),
                (hidden.at[whole], hidden_o.at[whole]),
                (gate_low.at[whole], gate_o.at[whole]),
                (upper_low.at[whole], upper_o.at[whole]),
                (mlp_parts, mlp_o),
            )
        )
    ]
    for put in puts[:4]:
        put.start()

    def blocks(i):
        at = pl.ds(pl.multiple_of((n + i) * rows, rows), rows)
        return [
            pltpu.make_async_copy(x_all.at[n + i], x_o.at[n + i], bsem.at[0, i]),
            pltpu.make_async_copy(hidden.at[at], hidden_o.at[at], bsem.at[1, i]),
        ]

    def late_blocks(i):
        at = pl.ds(pl.multiple_of((n + i) * rows, rows), rows)
        return [
            pltpu.make_async_copy(gate_low.at[at], gate_o.at[at], bsem.at[2, i]),
            pltpu.make_async_copy(upper_low.at[at], upper_o.at[at], bsem.at[3, i]),
        ]

    def extra(i):
        @pl.when(ends.takes)
        def _():
            hg[pl.ds(0, rows)] = dot(og_all[n + jnp.minimum(i, n - 2)], wd[...], 1, 1)
            hand(i).wait_recv()
            units(n + i, 0, True)
            for put in blocks(i):
                put.start()

            @pl.when(i < n - 1)
            def _():
                for put in late_blocks(i):
                    put.start()

    @pl.loop(0, n // 2)
    def _(i):
        extra(i)

    scatter.relay()

    @pl.loop(0, n // 2)
    def _(c):
        two = pl.ds(pl.multiple_of(2 * c, 2), 2)
        at = pl.ds(pl.multiple_of(c * pair, pair), pair)
        mlp_parts[two] = dot(hidden[at], wd[...]).astype(BF).reshape(2, rows, x.shape[1])

    puts[4].start()

    def write(at, cols, total):
        grad_two[at, cols] = total

    scatter.finish(write)
    vec[...] = jnp.zeros_like(vec)

    @pl.loop(0, rows // slab)
    def _(r):
        here = pl.ds(pl.multiple_of(r * slab, slab), slab)
        center, inv = row_stats(raw[here].astype(F32) + attn[here])
        hat, grad = center * inv, grad_two[here]
        total = cot[here].astype(F32) + norm_pull(grad, hat, inv, gain[...])
        res_grad[here] = total
        res_low[here] = total.astype(BF)
        vec[2:3] += jnp.sum(grad * hat, 0, keepdims=True)
        vec[3:4] += jnp.sum(grad, 0, keepdims=True)

    @pl.loop(n // 2, n)
    def _(i):
        extra(i)

    @pl.when(ends.takes)
    def _():
        @pl.loop(0, n)
        def _(i):
            for put in blocks(i):
                put.wait()

        @pl.loop(0, n - 1)
        def _(i):
            for put in late_blocks(i):
                put.wait()

    for put in puts:
        put.wait()

    gather.drain()
    scatter.drain()

    @pl.when(ends.gives)
    def _():
        first.wait_send()

        @pl.loop(1, n)
        def _(i):
            hand(i).wait_send()


def mlp(raw, attn, cot, gain, bias, og_all, wg, wu, wd, cid):
    n = lax.axis_size("tp")
    chips = lax.axis_size("seq") // 2
    rows, model = raw.shape
    width = wg.shape[1]
    total = n * rows
    dma = pltpu.SemaphoreType.DMA
    sems = max(10, n - 1)
    vmem = pl.BlockSpec(memory_space=pltpu.VMEM)
    hbm = pl.BlockSpec(memory_space=pl.ANY)
    shape = jax.ShapeDtypeStruct
    return pl.pallas_call(
        functools.partial(mlp_kernel, n, chips),
        out_shape=(
            shape((2 * n, rows, model), BF),
            shape((2 * total, width), BF),
            shape((2 * total - rows, width), BF),
            shape((2 * total - rows, width), BF),
            shape((n, rows, model), BF),
            shape((rows, model), F32),
            shape((rows, model), BF),
            shape((8, model), F32),
            shape((rows, width), F32),
            shape((rows, width), F32),
        ),
        in_specs=[vmem] * 5 + [hbm] * 4,
        out_specs=(hbm,) * 5 + (vmem,) * 5,
        scratch_shapes=[
            pltpu.VMEM(og_all.shape, BF),
            pltpu.VMEM((rows, model), BF),
            pltpu.VMEM((rows, model), F32),
            pltpu.VMEM((2 * n, rows, model), BF),
            pltpu.VMEM((2 * total, width), BF),
            pltpu.VMEM((2 * total, width), BF),
            pltpu.VMEM((2 * total, width), BF),
            pltpu.VMEM((n, rows, model), BF),
        ]
        + [pltpu.VMEM(w.shape, BF) for w in (wg, wu, wd)]
        + [
            pltpu.VMEM((total, width), F32),
            pltpu.VMEM((rows, width), F32),
            pltpu.VMEM((rows, width), F32),
            pltpu.VMEM((rows, model), F32),
            pltpu.VMEM((n, rows, model), BF),
        ]
        + scatter_scratch(n, rows, model)
        + [dma((4,))]
        + [dma((sems,))] * 4
        + [dma((n,)), dma((n,)), dma((5,)), dma((4, n))],
        compiler_params=params(cid),
        name="mlp",
    )(raw, attn, cot, gain, bias, og_all, wg, wu, wd)


def mixer_back_kernel(n, chips, heads, *refs):
    (
        fac, res, wo_h, wq_h, wk_h, wv_h, ws_h, q_h, k_h, v_h, sp_h, mx_h, prior_h, mlp_h, decay, qfac, kfac, cos, sin, og_h, wd_h, gate_late, up_late,
        res_o, swish_o, value_o, qk_o, parts_o, mlp_out, og_late, gate_low, upper_low,
        q, k, v, sp, mx, prior, mlp_parts, res_all, swish_low, value_low, qk_low, wo, wq, wk, wv, ws, mixed_low, sums, parts, local, later, key_part, value_part,
    ) = refs[:55]
    mlp_near, mlp_far, mlp_hold = refs[55:58]
    chain_refs = refs[58:66]
    wsem, gs, gr, ms, mr, es, er, isem, lsem, osem, bsem = refs[66:]
    rows = res.shape[0]
    gather = Gather(n, res, res_all, gs, gr)
    scatter_mlp = Scatter(n, mlp_parts, mlp_near, mlp_far, mlp_hold, ms, mr)
    chain = Chain(chips, heads, True, fac, local, later, *chain_refs)
    ends = Ends(chips)
    late = remote(og_h.at[gather.source(n - 1)], og_late, es, er, 0, ends.mate)
    load_late = pltpu.make_async_copy(wd_h, wo, wsem.at[5])
    loads = [
        pltpu.make_async_copy(a, w, wsem.at[i])
        for i, (a, w) in enumerate(((wo_h, wo), (ws_h, ws), (wq_h, wq), (wk_h, wk), (wv_h, wv)))
    ]
    def entering(i):
        j = gather.source(i)
        at = pl.ds(pl.multiple_of(j * rows, rows), rows)
        return [
            pltpu.make_async_copy(a.at[at], b.at[at], isem.at[w, j])
            for w, (a, b) in enumerate(((mx_h, mx), (sp_h, sp), (q_h, q)))
        ]

    loads += [
        pltpu.make_async_copy(a, b, lsem.at[i])
        for i, (a, b) in enumerate(((k_h, k), (v_h, v), (prior_h, prior), (mlp_h, mlp_parts)))
    ]
    loads[0].start()
    for i in range(n):
        for load in entering(i):
            load.start()
    for load in loads[1:]:
        load.start()
    greet(gather.peers + chain.peers)
    gather.start()
    me = gather.source(0)
    res_all[me] = res[...]
    loads[0].wait()

    @pl.loop(0, n)
    def _(i):
        j = gather.source(i)
        gather.arrive(i)
        at = pl.ds(pl.multiple_of(j * rows, rows), rows)
        for load in entering(i):
            load.wait()
        sums[j, :, : heads * DV] = dot(res_all[j], wo[...], 1, 1).astype(sums.dtype)

        for h in range(heads):
            vc = slice(h * DV, (h + 1) * DV)
            kc = slice(h * DK, (h + 1) * DK)
            back = sums[j, :, vc].astype(F32)
            normed, inv = norm_of(mx[at, vc])
            pre = sp[at, vc]
            sig = jax.nn.sigmoid(pre)
            swish_low[at, vc] = (back * normed * (sig * (1.0 + pre * (1.0 - sig)))).astype(BF)
            g = back * (pre * sig)
            g = inv * (
                g
                - jnp.mean(g, -1, keepdims=True)
                - normed * jnp.mean(g * normed, -1, keepdims=True)
            )
            g = g.astype(BF)
            mixed_low[at, vc] = g
            query_dec = (q[at, kc].astype(F32) * qfac[h]).astype(BF)
            p = j * heads + h
            local[p] = dot(query_dec, g, 0, 0).astype(BF)
            chain.begin(p)

        chain.open(gather, i)

        @pl.when(i == 0)
        def _():
            gather.relays()

    puts = [
        pltpu.make_async_copy(res_all, res_o, osem.at[0]),
        pltpu.make_async_copy(swish_low, swish_o, osem.at[1]),
    ]
    for put in puts:
        put.start()

    def leaving(j):
        at = pl.ds(pl.multiple_of(j * rows, rows), rows)
        return [
            pltpu.make_async_copy(value_low.at[at], value_o.at[at], bsem.at[0, j]),
            pltpu.make_async_copy(qk_low.at[at], qk_o.at[at], bsem.at[1, j]),
            pltpu.make_async_copy(parts.at[j], parts_o.at[j], bsem.at[2, j]),
        ]

    for load in loads[1:]:
        load.wait()
    for i in range(1, n):
        scatter_mlp.send(i)

    @pl.when(ends.gives)
    def _():
        late.start()

    @pl.when(ends.takes)
    def _():
        load_late.start()

    @pl.loop(0, n)
    def _(i):
        j = gather.source(i)
        at = pl.ds(pl.multiple_of(j * rows, rows), rows)
        for h in range(heads):
            vc = slice(h * DV, (h + 1) * DV)
            kc = slice(h * DK, (h + 1) * DK)
            g, query, key = mixed_low[at, vc], q[at, kc], k[at, kc]
            chain.tick(gather, i * heads + h)
            raw_low = (dot(g, v[at, vc], 1, 1) * decay[h]).astype(BF)
            query_back = dot(raw_low, key) + dot(g, prior[j * heads + h], 1, 1) * qfac[h]
            qk_low[at, kc] = turn_back(query_back, cos[...], sin[...]).astype(BF)
            scores = (dot(query, key, 1, 1) * decay[h]).astype(BF)
            key_part[at, kc] = dot(raw_low, query, 0, 0).astype(key_part.dtype)
            value_part[at, vc] = dot(scores, g, 0, 0).astype(value_part.dtype)
        sums[j] = dot(swish_low[at], ws[...], 1, 1).astype(sums.dtype)
        sums[j] += dot(qk_low[at, : heads * DK], wq[...], 1, 1).astype(sums.dtype)

    scatter_mlp.relay()

    @pl.loop(0, n)
    def _(step):
        i = (step + 1) % n
        j = gather.source(i)
        at = pl.ds(pl.multiple_of(j * rows, rows), rows)
        for h in range(heads):
            vc = slice(h * DV, (h + 1) * DV)
            kc = slice(h * DK, (h + 1) * DK)
            chain.tick(gather, (n + step) * heads + h)
            after = later[j * heads + h]
            key_dec = (k[at, kc].astype(F32) * kfac[h]).astype(BF)
            key_back = key_part[at, kc].astype(F32) + dot(v[at, vc], after, 1, 1) * kfac[h]
            qk_low[at, slice((heads + h) * DK, (heads + h + 1) * DK)] = turn_back(
                key_back, cos[...], sin[...]
            ).astype(BF)
            value_low[at, vc] = (value_part[at, vc] + dot(key_dec, after)).astype(BF)
        sums[j] += dot(value_low[at], wv[...], 1, 1).astype(sums.dtype)
        parts[j] = (sums[j].astype(F32) + dot(qk_low[at, heads * DK :], wk[...], 1, 1)).astype(BF)
        for put in leaving(j):
            put.start()

    @pl.when(ends.takes)
    def _():
        width = gate_late.shape[1]
        load_late.wait()
        late.wait_recv()
        sums[0, :, :width] = dot(og_late[...], wo[...], 1, 1).astype(sums.dtype)
        slab = 16

        @pl.loop(0, rows // slab)
        def _(r):
            here = pl.ds(pl.multiple_of(r * slab, slab), slab)
            gelu, slope = gelu_of(gate_late[here])
            back = sums[0, here, :width].astype(F32)
            gate_low[here] = (back * up_late[here] * slope).astype(BF)
            upper_low[here] = (back * gelu).astype(BF)

    def write_mlp(at, cols, total):
        mlp_out[at, cols] = total

    scatter_mlp.finish(write_mlp)
    gather.drain()
    scatter_mlp.drain()

    @pl.when(ends.gives)
    def _():
        late.wait_send()

    for put in puts:
        put.wait()

    @pl.loop(0, n)
    def _(j):
        for put in leaving(j):
            put.wait()

    @pl.loop(0, n * heads)
    def _(p):
        chain.drain(p)


def mixer_back(fac, res, wo, wq, wk, wv, ws, q, k, v, sp, mx, prior, mlp_parts, decay, qfac, kfac, cos, sin, og_all, wd, gate_late, up_late, cid):
    n = lax.axis_size("tp")
    chips = lax.axis_size("seq") // 2
    rows, model = res.shape
    heads = q.shape[1] // DK
    pieces = n * heads
    total = n * rows
    keep = F32 if n <= 4 else BF
    dma = pltpu.SemaphoreType.DMA
    sems = max(10, n - 1)
    vmem = pl.BlockSpec(memory_space=pltpu.VMEM)
    hbm = pl.BlockSpec(memory_space=pl.ANY)
    shape = jax.ShapeDtypeStruct
    return pl.pallas_call(
        functools.partial(mixer_back_kernel, n, chips, heads),
        out_shape=(
            shape((n, rows, model), BF),
            shape((total, heads * DV), BF),
            shape((total, heads * DV), BF),
            shape((total, 2 * heads * DK), BF),
            shape((n, rows, model), BF),
            shape((rows, model), F32),
            shape((rows, model), BF),
            shape(gate_late.shape, BF),
            shape(gate_late.shape, BF),
        ),
        in_specs=[pl.BlockSpec(memory_space=pltpu.SMEM), vmem] + [hbm] * 12 + [vmem] * 5 + [hbm, hbm, vmem, vmem],
        out_specs=(hbm,) * 5 + (vmem,) * 4,
        scratch_shapes=[pltpu.VMEM(a.shape, a.dtype) for a in (q, k, v, sp, mx, prior, mlp_parts)]
        + [
            pltpu.VMEM((n, rows, model), BF),
            pltpu.VMEM((total, heads * DV), BF),
            pltpu.VMEM((total, heads * DV), BF),
            pltpu.VMEM((total, 2 * heads * DK), BF),
        ]
        + [pltpu.VMEM(w.shape, BF) for w in (wo, wq, wk, wv, ws)]
        + [
            pltpu.VMEM((total, heads * DV), BF),
            pltpu.VMEM((n, rows, model), keep),
            pltpu.VMEM((n, rows, model), BF),
            pltpu.VMEM((pieces, DK, DV), BF),
            pltpu.VMEM((pieces, DK, DV), BF),
            pltpu.VMEM((total, heads * DK), keep),
            pltpu.VMEM((total, heads * DV), BF),
        ]
        + scatter_scratch(n, rows, model)
        + chain_scratch(pieces)
        + [dma((6,))]
        + [dma((sems,))] * 4
        + [dma((1,)), dma((1,)), dma((3, n)), dma((4,)), dma((2,)), dma((3, n))],
        compiler_params=params(cid),
        name="mixer_back",
    )(fac, res, wo, wq, wk, wv, ws, q, k, v, sp, mx, prior, mlp_parts, decay, qfac, kfac, cos, sin, og_all, wd, gate_late, up_late)


def weights_kernel(chips, *refs):
    (
        two, og, og_late, hidden, gate_low, gate_late, up_low, up_late,
        one, res, swish_low, gated, value_low, qk_low,
        vec_two, gain, parts_h, raw_h, res_h, attn_h, mlp_h,
        down_o, gate_o, up_o, swish_o, mixer_o, value_o, query_o, key_o, back_o, outs_o, vec_out,
    ) = refs[:32]
    mlp = LineSums(
        chips, 1, chips - 2, ((two,), (og, og_late)),
        ((gate_low, gate_late), (up_low, up_late), (hidden,)), (0, 0, 1), refs[32:44],
    )
    mix = LineSums(
        chips, 0, chips - 1, ((one,), (res,)), ((swish_low,), (gated,), (value_low,), (qk_low,)),
        (0, 1, 0, 0), refs[44:56],
    )
    (
        turned, osem, grad, raw, res_grad, attn, mlp_out, back, outs, csem, dsem,
        vec, vec_near, vec_mid, vec_far, vs, vr, us, ur, parts, near, far, hold, lsem, ss, sr,
    ) = refs[56:]
    grad = grad if parts.shape[0] == 4 else near.at[0]
    scatter = Scatter(parts.shape[0], parts, near, far, hold, ss, sr)
    load = pltpu.make_async_copy(parts_h, parts, lsem.at[0])
    load.start()
    s, t = lax.axis_index("seq"), lax.axis_index("tp")
    span, tp = 2 * chips, vec_far.shape[0] + 1
    share = vec_mid.shape[1]
    ring = [((s + d) % span, t) for d in range(1, span)]
    cross = [(s, (t + d) % tp) for d in range(1, tp)]

    def part(who):
        return pl.ds(pl.multiple_of(who * share, share), share)

    greet(ring + cross)
    vec_first = [
        remote(vec.at[:, part((s + d) % span)], vec_near.at[d - 1], vs, vr, d - 1, ring[d - 1])
        for d in range(1, span)
    ]
    vec_last = [
        remote(vec_mid, vec_far.at[d - 1], us, ur, d - 1, cross[d - 1]) for d in range(1, tp)
    ]
    vec[...] = vec_two[...]
    for u in range(mix.units):
        if u < mlp.units:
            mlp.share(u)
        mix.share(u)

    half = mix.out.shape[2] // 2
    lo, hi = pl.ds(0, half), pl.ds(half, half)

    def put(pairs):
        copies = [pltpu.make_async_copy(a, b, osem.at[i]) for i, (a, b) in enumerate(pairs)]
        for copy in copies:
            copy.start()
        for copy in copies:
            copy.wait()

    def put_mlp(w):
        if w == 2:
            turned[...] = mlp.out[0].T
            put([(turned, down_o)])
        else:
            put([(mlp.out.at[0], (gate_o, up_o)[w])])

    def put_mix(w):
        if w == 1:
            turned[...] = mix.out[0].T
            put([(turned, mixer_o)])
        elif w == 3:
            put([(mix.out.at[0, :, lo], query_o), (mix.out.at[0, :, hi], key_o)])
        else:
            put([(mix.out.at[0], (swish_o, None, value_o)[w])])

    load.wait()
    for i in range(1, scatter.n):
        scatter.send(i)

    @pl.loop(0, mix.units)
    def _(u):
        for w in range(mix.units):

            @pl.when(u == w)
            def _(w=w):
                if w < mlp.units:
                    mlp.ready(w)

        @pl.when(u < mlp.units)
        def _():
            mlp.step(u, 0)

        for w in range(mix.units):

            @pl.when(u == w)
            def _(w=w):
                mix.ready(w)

        @pl.loop(0, chips - 1)
        def _(k):
            @pl.when((u < mlp.units) & (k > 0))
            def _():
                mlp.step(u, k)

            mix.step(u, k)

        @pl.when(u == 0)
        def _():
            chunk = raw.shape[0]

            scatter.relay()

            def write(at, cols, total):
                grad[at, cols] = total.astype(grad.dtype)

            scatter.finish(write)

            @pl.loop(0, parts.shape[1] // chunk)
            def _(c):
                here = pl.ds(pl.multiple_of(c * chunk, chunk), chunk)
                pairs = (raw_h, raw), (res_h, res_grad), (attn_h, attn), (mlp_h, mlp_out)
                ins = [
                    pltpu.make_async_copy(a.at[here], b, csem.at[i])
                    for i, (a, b) in enumerate(pairs)
                ]
                for copy in ins:
                    copy.start()
                for copy in ins:
                    copy.wait()
                value = raw[...].astype(F32)
                outs[...] = (value + attn[...] + mlp_out[...]).astype(BF)
                center, inv = row_stats(value)
                hat, given = center * inv, grad[here].astype(F32)
                vec[0:1] += jnp.sum(given * hat, 0, keepdims=True)
                vec[1:2] += jnp.sum(given, 0, keepdims=True)
                back[...] = (res_grad[...] + norm_pull(given, hat, inv, gain[...])).astype(BF)
                puts = [
                    pltpu.make_async_copy(a, b.at[0, here], dsem.at[i])
                    for i, (a, b) in enumerate(((back, back_o), (outs, outs_o)))
                ]
                for copy in puts:
                    copy.start()
                for copy in puts:
                    copy.wait()

            for copy in vec_first:
                copy.start()

        @pl.when(u == 1)
        def _():
            for copy in vec_first:
                copy.wait_recv()
            vec_mid[...] = vec[:, part(s)] + jnp.sum(vec_near[...], 0)
            for copy in vec_last:
                copy.start()

        @pl.when(u > 0)
        def _():
            mlp.finish(u - 1)
            mix.finish(u - 1)
            for w in range(mix.units - 1):

                @pl.when(u - 1 == w)
                def _(w=w):
                    put_mlp(w)
                    put_mix(w)

    mix.finish(mix.units - 1)
    put_mix(mix.units - 1)
    for copy in vec_last:
        copy.wait_recv()
    vec_out[...] = vec_mid[...] + jnp.sum(vec_far[...], 0)
    for copy in vec_first + vec_last:
        copy.wait_send()
    scatter.drain()
    mlp.drain()
    mix.drain()


def weight_sums(
    two, og, og_late, hidden, gate_low, gate_late, up_low, up_late, one, res, swish_low, gated, value_low,
    qk_low, vec_two, gain, grad, raw, res_grad, attn, mlp_out, cid,
):
    chips = lax.axis_size("seq") // 2
    tokens, model = one.shape
    width = gated.shape[1]
    mlp_tokens, mlp_width = hidden.shape
    keys = qk_low.shape[1] // 2
    cut = model // (2 * chips)
    dma = pltpu.SemaphoreType.DMA
    vmem = pl.BlockSpec(memory_space=pltpu.VMEM)
    hbm = pl.BlockSpec(memory_space=pl.ANY)
    shape = lambda *a: jax.ShapeDtypeStruct(a, F32)
    ring, cross = 2 * chips - 1, lax.axis_size("tp") - 1
    rows, share, chunk = raw.shape[0], model // (2 * chips), 16
    part = lambda dtype: pltpu.VMEM((chunk, model), dtype)
    return pl.pallas_call(
        functools.partial(weights_kernel, chips),
        out_shape=(
            shape(mlp_width, cut),
            shape(cut, mlp_width),
            shape(cut, mlp_width),
            shape(cut, width),
            shape(width, cut),
            shape(cut, width),
            shape(cut, keys),
            shape(cut, keys),
            jax.ShapeDtypeStruct((1, rows, model), BF),
            jax.ShapeDtypeStruct((1, rows, model), BF),
            shape(8, share),
        ),
        in_specs=[hbm] * 14 + [vmem] * 2 + [hbm] * 5,
        out_specs=(hbm,) * 10 + (vmem,),
        scratch_shapes=line_scratch(chips, 3, 2, mlp_tokens, cut, mlp_width)
        + line_scratch(chips, 4, 2, tokens, cut, width)
        + [
            pltpu.VMEM((width, cut), F32),
            dma((8,)),
            pltpu.VMEM((rows, model) if cross < 4 else (16, 128), F32),
            part(BF),
            part(F32),
            part(F32),
            part(F32),
            part(BF),
            part(BF),
            dma((5,)),
            dma((2,)),
            pltpu.VMEM((8, model), F32),
            pltpu.VMEM((ring, 8, share), F32),
            pltpu.VMEM((8, share), F32),
            pltpu.VMEM((cross, 8, share), F32),
            dma((ring,)),
            dma((ring,)),
            dma((cross,)),
            dma((cross,)),
            pltpu.VMEM((cross + 1, rows, model), BF),
        ]
        + scatter_scratch(cross + 1, rows, model)
        + [
            dma((1,)),
            dma((max(10, cross),)),
            dma((max(10, cross),)),
        ],
        compiler_params=params(cid),
        name="weights",
    )(two, og, og_late, hidden, gate_low, gate_late, up_low, up_late, one, res, swish_low, gated, value_low,
      qk_low, vec_two, gain, grad, raw, res_grad, attn, mlp_out)


def shards(
    inputs,
    query_weight,
    key_weight,
    value_weight,
    swish_weight,
    output_weight,
    gate_weight,
    up_weight,
    down_weight,
    attn_gain,
    attn_bias,
    mlp_gain,
    mlp_bias,
    output_grad,
):
    _, rows, model = inputs.shape
    heads = query_weight.shape[1] // DK
    seqs, tps = lax.axis_size("seq"), lax.axis_size("tp")
    raw, cotangent = inputs[0], output_grad[0]
    row = lambda v: v.reshape(1, model)
    flat = lambda a: a.reshape(-1, model)

    half_width = DK // 2
    frequencies = np.power(
        np.float32(10000.0), -np.arange(half_width, dtype=np.float32) / np.float32(half_width)
    )[None]
    decays = 1.0 - np.exp2(-5.0 - np.arange(heads * tps))
    factors = np.stack([np.power(decays, rows), np.log(decays)]).astype(np.float32)

    (
        one_all, grad_all, query, key, value, swish_pre, mixed, prior, gated, attn_out,
        decay_mat, query_fac, key_fac, cosine, sine,
    ) = mixer(
        factors, raw, cotangent, key_weight, value_weight, query_weight, swish_weight,
        output_weight, row(attn_gain), row(attn_bias), frequencies, 0,
    )
    two_all, hidden, gate_low, upper_low, mlp_parts, res_grad, res_low, vectors, gate_pre, up_pre = mlp(
        raw, attn_out, cotangent, row(mlp_gain), row(mlp_bias), grad_all, gate_weight, up_weight,
        down_weight, 1,
    )
    (
        res_all, swish_low, value_low, qk_low, normed_one_grad, mlp_out, og_late, gate_late, up_late,
    ) = mixer_back(
        factors, res_low, output_weight, query_weight, key_weight, value_weight, swish_weight,
        query, key, value, swish_pre, mixed, prior, mlp_parts, decay_mat, query_fac, key_fac,
        cosine, sine, grad_all, down_weight, gate_pre, up_pre, 2,
    )
    (
        down_grad, gate_grad, up_grad, swish_grad, mixer_grad, value_grad, query_grad, key_grad,
        input_grad, outputs, vector_sums,
    ) = weight_sums(
        flat(two_all), flat(grad_all), og_late, hidden, gate_low, gate_late, upper_low, up_late,
        flat(one_all), flat(res_all), swish_low, gated, value_low, qk_low, vectors, row(attn_gain),
        normed_one_grad, raw, res_grad, attn_out, mlp_out, 3,
    )
    each = model // (seqs * tps)
    vector_sums = lax.dynamic_slice(vector_sums, (0, lax.axis_index("tp") * each), (4, each))
    return (
        outputs,
        input_grad,
        query_grad,
        key_grad,
        value_grad,
        swish_grad,
        mixer_grad,
        gate_grad,
        up_grad,
        down_grad,
        vector_sums[0],
        vector_sums[1],
        vector_sums[2],
        vector_sums[3],
    )


def solution(mesh):
    return jax.shard_map(
        shards,
        mesh=mesh,
        in_specs=(
            P("tp", "seq", None),
            P(None, "tp"),
            P(None, "tp"),
            P(None, "tp"),
            P(None, "tp"),
            P("tp", None),
            P(None, "tp"),
            P(None, "tp"),
            P("tp", None),
            P(),
            P(),
            P(),
            P(),
            P("tp", "seq", None),
        ),
        out_specs=(
            P("tp", "seq", None),
            P("tp", "seq", None),
            P("seq", "tp"),
            P("seq", "tp"),
            P("seq", "tp"),
            P("seq", "tp"),
            P("tp", "seq"),
            P("seq", "tp"),
            P("seq", "tp"),
            P("tp", "seq"),
            P(("seq", "tp")),
            P(("seq", "tp")),
            P(("seq", "tp")),
            P(("seq", "tp")),
        ),
        check_vma=False,
    )
```

```python
import functools

import jax
import jax.numpy as jnp
import numpy as np
from jax import lax
from jax.experimental import pallas as pl
from jax.experimental.pallas import tpu as pltpu
from jax.sharding import PartitionSpec as P

DK = 256
DV = 512


EPS = 1e-05
MESH = pl.DeviceIdType.MESH
BF = jnp.bfloat16
F32 = jnp.float32
VMEM_LIMIT = 63 * 1024 * 1024 - 512 * 1024


def remote(src, dst, ssem, rsem, slot, dev):
    return pltpu.make_async_remote_copy(
        src_ref=src,
        dst_ref=dst,
        send_sem=ssem.at[slot],
        recv_sem=rsem.at[slot],
        device_id=dev,
        device_id_type=MESH,
    )


def greet(devs):
    barrier = pltpu.get_barrier_semaphore()
    for dev in devs:
        pl.semaphore_signal(barrier, inc=1, device_id=dev, device_id_type=MESH)
    pl.semaphore_wait(barrier, len(devs))


def params(cid):
    return pltpu.CompilerParams(
        collective_id=cid, has_side_effects=True, vmem_limit_bytes=VMEM_LIMIT
    )


class Gather:
    def __init__(self, n, x, o, ssem, rsem, base=0):
        s, t = lax.axis_index("seq"), lax.axis_index("tp")
        self.n, self.t = n, t
        rows = x.shape[0]
        if n == 4:
            px, py = t + 1 - 2 * (t % 2), (t + 2) % 4
            dx, dy = (s, px), (s, py)
            self.peers = [dx, dy]
            half = rows // 2
            lo, hi = pl.ds(0, half), pl.ds(half, half)
            self.first = [
                remote(x.at[lo], o.at[base + t, lo], ssem, rsem, 0, dx),
                remote(x.at[hi], o.at[base + t, hi], ssem, rsem, 1, dy),
                remote(x.at[hi], o.at[base + t, hi], ssem, rsem, 2, dx),
                remote(x.at[lo], o.at[base + t, lo], ssem, rsem, 3, dy),
            ]
            self.relay = [
                remote(o.at[base + px, lo], o.at[base + px, lo], ssem, rsem, 4, dy),
                remote(o.at[base + py, hi], o.at[base + py, hi], ssem, rsem, 5, dx),
            ]
        else:
            self.peers = [(s, (t + k) % n) for k in range(1, n)]
            self.first = [
                remote(x, o.at[base + t], ssem, rsem, k, dev) for k, dev in enumerate(self.peers)
            ]
            self.relay = []

    def source(self, i):
        t = self.t
        if self.n == 4:
            near = jnp.where(i == 1, t + 1 - 2 * (t % 2), (t + 2) % 4)
            return jnp.where(i == 0, t, jnp.where(i == 3, 3 - t, near))
        return (t - i + self.n) % self.n

    def start(self):
        for copy in self.first:
            copy.start()

    def relays(self):
        for copy, onward in zip(self.first, self.relay):
            copy.wait_recv()
            onward.start()

    def arrive(self, i):
        if self.n == 4:

            @pl.when(i == 1)
            def _():
                self.first[2].wait_recv()

            @pl.when(i == 2)
            def _():
                self.first[3].wait_recv()

            @pl.when(i == 3)
            def _():
                self.relay[0].wait_recv()
                self.relay[1].wait_recv()

        else:
            for k, copy in enumerate(self.first):

                @pl.when(i == k + 1)
                def _(copy=copy):
                    copy.wait_recv()

    def drain(self):
        for copy in self.first + self.relay:
            copy.wait_send()


class Scatter:
    def __init__(self, n, parts, near, far, hold, ssem, rsem):
        s, t = lax.axis_index("seq"), lax.axis_index("tp")
        self.n, self.t = n, t
        self.parts, self.near, self.far, self.hold = parts, near, far, hold
        if n == 4:
            self.px, self.py, pd = t + 1 - 2 * (t % 2), (t + 2) % 4, 3 - t
            dx, dy = (s, self.px), (s, self.py)
            self.peers = [dx, dy]
            half = parts.shape[-1] // 2
            self.cols = a, b = pl.ds(0, half), pl.ds(half, half)
            rows = parts.shape[1] // 2
            self.halves = (pl.ds(0, rows), pl.ds(rows, rows))
            self.far_a = [
                remote(parts.at[pd, r, a], near.at[0, 1, r], ssem, rsem, i, dx)
                for i, r in enumerate(self.halves)
            ]
            self.far_b = [
                remote(parts.at[pd, r, b], near.at[1, 1, r], ssem, rsem, 6 + i, dy)
                for i, r in enumerate(self.halves)
            ]
            self.near_a = remote(parts.at[self.px, :, a], near.at[0, 0], ssem, rsem, 2, dx)
            self.near_b = remote(parts.at[self.py, :, b], near.at[1, 0], ssem, rsem, 3, dy)
            self.sum_a = [
                remote(hold.at[0, r], far.at[0, r], ssem, rsem, 4 + i, dy)
                for i, r in enumerate(self.halves)
            ]
            self.sum_b = [
                remote(hold.at[1, r], far.at[1, r], ssem, rsem, 8 + i, dx)
                for i, r in enumerate(self.halves)
            ]
            self.copies = self.far_a + self.far_b + [self.near_a, self.near_b]
            self.copies += self.sum_a + self.sum_b
        else:
            self.peers = [(s, (t + k) % n) for k in range(1, n)]
            self.copies = [
                remote(parts.at[(t - k + n) % n], near.at[k - 1], ssem, rsem, k - 1, (s, (t - k + n) % n))
                for k in range(1, n)
            ]

    def send(self, i):
        if self.n == 4:

            @pl.when(i == 1)
            def _():
                self.near_a.start()

            @pl.when(i == 2)
            def _():
                self.near_b.start()

            @pl.when(i == 3)
            def _():
                for copy_a, copy_b in zip(self.far_a, self.far_b):
                    copy_a.start()
                    copy_b.start()

        else:
            for k, copy in enumerate(self.copies):

                @pl.when(i == k + 1)
                def _(copy=copy):
                    copy.start()

    def relay(self):
        if self.n == 4:
            sides = (self.cols[0], self.py, self.far_a, self.sum_a), (
                self.cols[1], self.px, self.far_b, self.sum_b
            )
            for i, r in enumerate(self.halves):
                for side, (cols, who, came, onward) in enumerate(sides):
                    came[i].wait_recv()
                    self.hold[side, r] = (
                        self.parts[who, r, cols].astype(F32) + self.near[side, 1, r].astype(F32)
                    ).astype(BF)
                    onward[i].start()

    def finish(self, write):
        if self.n == 4:
            for side, (one, two) in enumerate(
                ((self.near_a, self.sum_a), (self.near_b, self.sum_b))
            ):
                one.wait_recv()
                for copy in two:
                    copy.wait_recv()
                write(
                    slice(None),
                    self.cols[side],
                    self.parts[self.t, :, self.cols[side]].astype(F32)
                    + self.near[side, 0].astype(F32)
                    + self.far[side].astype(F32),
                )
        else:
            for copy in self.copies:
                copy.wait_recv()

            @pl.loop(0, self.parts.shape[1] // 16)
            def _(r):
                at = pl.ds(pl.multiple_of(r * 16, 16), 16)
                total = self.parts[self.t, at].astype(F32)
                for k in range(self.n - 1):
                    total = total + self.near[k, at].astype(F32)
                write(at, slice(None), total)

    def drain(self):
        for copy in self.copies:
            copy.wait_send()


def scatter_scratch(n, rows, width):
    if n == 4:
        near, far = (2, 2, rows, width // 2), (2, rows, width // 2)
    else:
        near, far = (n - 1, rows, width), (1, 16, 128)
    return [pltpu.VMEM(near, BF), pltpu.VMEM(far, BF), pltpu.VMEM(far, BF)]


class Ends:
    def __init__(self, chips):
        s, t = lax.axis_index("seq"), lax.axis_index("tp")
        chip, span = s // 2, 2 * chips
        self.gives = (chip == 0) | (chip == chips - 1)
        self.takes = (chip == 1) | (chip == chips - 2)
        self.peers = [((s + 2) % span, t), ((s - 2 + span) % span, t)]
        step = jnp.where(chip == 0, 2, jnp.where(chip == chips - 1, span - 2, 0))
        self.mate = ((s + step) % span, t)


class Chain:
    def __init__(self, chips, heads, flip, fac, local, out, pair, enter, ps, pr, zs, zr, bs, br):
        s, t = lax.axis_index("seq"), lax.axis_index("tp")
        core, chip, span = s % 2, s // 2, 2 * chips
        self.chips, self.heads, self.fac = chips, heads, fac
        self.local, self.out, self.pair, self.enter, self.leave = local, out, pair, enter, local
        self.sems = ps, pr, zs, zr, bs, br
        self.partner = (s + 1 - 2 * core, t)
        above, below = ((s + 2) % span, t), ((s - 2 + span) % span, t)
        self.peers = [self.partner, above, below]
        if flip:
            self.first, self.place, self.ahead = core == 1, chips - 1 - chip, below
        else:
            self.first, self.place, self.ahead = core == 0, chip, above
        self.last = jnp.logical_not(self.first)

    def give(self, p):
        return remote(self.local.at[p], self.pair.at[p], self.sems[0], self.sems[1], p, self.partner)

    def back(self, p):
        return remote(self.enter.at[p], self.out.at[p], self.sems[4], self.sems[5], p, self.partner)

    def onward(self, p):
        return remote(self.leave.at[p], self.enter.at[p], self.sems[2], self.sems[3], p, self.ahead)

    def piece(self, gather, index):
        return gather.source(index // self.heads) * self.heads + index % self.heads

    def open(self, gather, i):
        @pl.when(self.place == 0)
        def _():
            @pl.loop(0, self.heads)
            def _(h):
                self.step(self.piece(gather, i * self.heads + h))

    def tick(self, gather, now):
        total = self.local.shape[0]
        ends = self.place == self.chips - 1
        lag = jnp.minimum(3 * (self.place - 1), total - self.heads)
        index = jnp.where(ends, (self.heads + now) % total, now - lag)
        due = (self.place > 0) & (index >= 0) & (index < total)

        @pl.when(due & (jnp.logical_not(ends) | (now >= total)))
        def _():
            self.step(self.piece(gather, jnp.maximum(index, 0)))

    def planned(self, gather, i, plan):
        block = jnp.int32(0)
        for place, turn, ahead in plan:
            block = jnp.where((self.place == place) & (i == turn), ahead, block)

        @pl.when(block > 0)
        def _():
            @pl.loop(0, self.heads)
            def _(h):
                self.step(self.piece(gather, block * self.heads + h))

    def due(self, gather, i, plan):
        now = self.place > 0
        for place, _, ahead in plan:
            now = now & ((self.place != place) | (i != ahead))

        @pl.when(now)
        def _():
            @pl.loop(0, self.heads)
            def _(h):
                self.step(self.piece(gather, i * self.heads + h))

    def begin(self, p):
        @pl.when(self.first)
        def _():
            self.give(p).start()

            @pl.when(self.place == 0)
            def _():
                self.out[p] = jnp.zeros(self.out.shape[1:], BF)

    def step(self, p):
        @pl.when(self.first)
        def _():
            @pl.when(self.place > 0)
            def _():
                self.back(p).wait_recv()

        @pl.when(self.last)
        def _():
            fac = self.fac[0, lax.axis_index("tp") * self.heads + p % self.heads]
            self.give(p).wait_recv()
            early = self.pair[p].astype(F32)
            chip_sum = early * fac + self.local[p].astype(F32)

            @pl.when(self.place == 0)
            def _():
                self.leave[p] = chip_sum.astype(BF)
                self.out[p] = self.pair[p]

            @pl.when(self.place > 0)
            def _():
                self.onward(p).wait_recv()
                self.back(p).start()
                came = self.enter[p].astype(F32)
                self.leave[p] = (came * (fac * fac) + chip_sum).astype(BF)
                self.out[p] = (came * fac + early).astype(BF)

            @pl.when(self.place < self.chips - 1)
            def _():
                self.onward(p).start()

    def drain(self, p):
        @pl.when(self.first)
        def _():
            self.give(p).wait_send()

        @pl.when(self.last)
        def _():
            @pl.when(self.place > 0)
            def _():
                self.back(p).wait_send()

            @pl.when(self.place < self.chips - 1)
            def _():
                self.onward(p).wait_send()


def chain_scratch(pieces):
    dma = pltpu.SemaphoreType.DMA
    return [pltpu.VMEM((pieces, DK, DV), BF)] * 2 + [dma((pieces,))] * 6


def dot(a, b, ca=1, cb=0):
    return lax.dot_general(a, b, (((ca,), (cb,)), ((), ())), preferred_element_type=F32)


def turn(v, cos, sin):
    lo, hi = v[:, : DK // 2], v[:, DK // 2 :]
    return jnp.concatenate([lo * cos - hi * sin, hi * cos + lo * sin], 1)


def turn_back(g, cos, sin):
    lo, hi = g[:, : DK // 2], g[:, DK // 2 :]
    return jnp.concatenate([lo * cos + hi * sin, hi * cos - lo * sin], 1)


def row_stats(v):
    center = v - jnp.mean(v, -1, keepdims=True)
    return center, lax.rsqrt(jnp.mean(center * center, -1, keepdims=True) + EPS)


def norm_pull(grad, hat, inv, gain):
    g = grad * gain
    return (g - jnp.mean(g, -1, keepdims=True) - hat * jnp.mean(g * hat, -1, keepdims=True)) * inv


def norm_of(m):
    center = m - jnp.mean(m, -1, keepdims=True)
    inv = lax.rsqrt(jnp.mean(center * center, -1, keepdims=True) + EPS)
    return center * inv, inv


class LineSums:
    def __init__(self, chips, lo, hi, wide, deep, kinds, refs, swap=False):
        s, t = lax.axis_index("seq"), lax.axis_index("tp")
        self.core, self.chip, self.chips, self.lo, self.hi = s % 2, s // 2, chips, lo, hi
        self.wide, self.deep, self.kinds = wide, deep, kinds
        (
            self.xs, self.ys, self.buf, self.out,
            self.xsem, self.ysem, self.psx, self.prx, self.psy, self.pry, self.ssem, self.rsem,
        ) = refs
        self.units = len(deep)
        self.swap = swap
        self.tokens = self.ys.shape[1] // 2
        self.cut = self.xs.shape[3]
        self.spans = [self.places(parts) for parts in wide], [self.places(parts) for parts in deep]
        span = 2 * chips
        self.partner = (s + 1 - 2 * self.core, t)
        self.above = ((s + 2) % span, t)
        self.below = ((s - 2 + span) % span, t)
        self.peers = [self.partner, self.above, self.below]

    def cols(self, j, core):
        return pl.ds(pl.multiple_of((2 * j + core) * self.cut, self.cut), self.cut)

    def places(self, parts):
        found, start = [], 0
        for part in parts:
            found.append((start, part.shape[0]))
            start += part.shape[0]
        assert start == self.tokens
        return found

    def wide_own(self, kind, j):
        return [
            pltpu.make_async_copy(
                part.at[:, self.cols(j, self.core)],
                self.xs.at[kind, j, pl.ds(start, size)],
                self.xsem.at[kind, j, i],
            )
            for i, (part, (start, size)) in enumerate(zip(self.wide[kind], self.spans[0][kind]))
        ]

    def wide_give(self, kind, j):
        return [
            remote(
                part.at[:, self.cols(j, 1 - self.core)],
                self.xs.at[kind, j, pl.ds(self.tokens + start, size)],
                self.psx.at[kind, j],
                self.prx.at[kind, j],
                i,
                self.partner,
            )
            for i, (part, (start, size)) in enumerate(zip(self.wide[kind], self.spans[0][kind]))
        ]

    def deep_own(self, u):
        return [
            pltpu.make_async_copy(
                part, self.ys.at[u, pl.ds(start, size)], self.ysem.at[u, i]
            )
            for i, (part, (start, size)) in enumerate(zip(self.deep[u], self.spans[1][u]))
        ]

    def deep_give(self, u):
        return [
            remote(
                part,
                self.ys.at[u, pl.ds(self.tokens + start, size)],
                self.psy.at[u],
                self.pry.at[u],
                i,
                self.partner,
            )
            for i, (part, (start, size)) in enumerate(zip(self.deep[u], self.spans[1][u]))
        ]

    def adds(self):
        return (self.chip >= self.lo) & (self.chip <= self.hi)

    def share(self, u):
        @pl.when(self.adds())
        def _():
            if self.kinds[u] not in self.kinds[:u]:
                for j in range(self.chips):
                    for copy in self.wide_give(self.kinds[u], j) + self.wide_own(self.kinds[u], j):
                        copy.start()
            for copy in self.deep_give(u) + self.deep_own(u):
                copy.start()

    def ready(self, u):
        @pl.when(self.adds())
        def _():
            own, given = self.deep_own(u), self.deep_give(u)
            if self.kinds[u] not in self.kinds[:u]:
                for j in range(self.chips):
                    own += self.wide_own(self.kinds[u], j)
                    given += self.wide_give(self.kinds[u], j)
            for copy in own:
                copy.wait()
            for copy in given:
                copy.wait_recv()

    def up(self, u, j):
        return remote(
            self.buf.at[u, j], self.buf.at[u, j], self.ssem.at[u], self.rsem.at[u], j, self.above
        )

    def down(self, u, j):
        slot = jnp.where(j == self.chip - 1, self.chips, j)
        return pltpu.make_async_remote_copy(
            src_ref=self.buf.at[u, j],
            dst_ref=self.buf.at[u, slot],
            send_sem=self.ssem.at[u, j],
            recv_sem=self.rsem.at[u, slot],
            device_id=self.below,
            device_id_type=MESH,
        )

    def arrived(self, u, slot):
        remote(
            self.buf.at[u, slot], self.buf.at[u, slot], self.ssem.at[u], self.rsem.at[u], slot,
            self.above,
        ).wait_recv()
        return self.buf[u, slot].astype(F32)

    def product(self, u, j):
        kind = 0
        for w in range(self.units):
            if self.kinds[w]:
                kind = kind + jnp.where(u == w, self.kinds[w], 0)
        if self.swap:
            return dot(self.ys[u], self.xs[kind, j], 0, 0)
        return dot(self.xs[kind, j], self.ys[u], 0, 0)

    def order(self, k):
        rights = self.chips - 1 - self.chip
        return jnp.where(
            self.chip < self.chips // 2,
            jnp.where(k < rights, self.chips - 1 - k, k - rights),
            jnp.where(k < self.chip, k, self.chips - 1 - (k - self.chip)),
        )

    def step(self, u, k):
        chip = self.chip
        j = self.order(k)

        @pl.when(self.adds())
        def _():
            total = self.product(u, j)

            @pl.when(((j > chip) & (chip == self.lo)) | ((j < chip) & (chip == self.hi)))
            def _():
                self.buf[u, j] = total.astype(BF)

            @pl.when(((j > chip) & (chip > self.lo)) | ((j < chip) & (chip < self.hi)))
            def _():
                self.buf[u, j] = (total + self.arrived(u, j)).astype(BF)

            @pl.when(j > chip)
            def _():
                self.up(u, j).start()

            @pl.when(j < chip)
            def _():
                self.down(u, j).start()

    def finish(self, u):
        chip = self.chip

        @pl.when(self.adds())
        def _():
            self.out[0] = self.product(u, chip)

        @pl.when((chip < self.lo) | (chip > self.hi))
        def _():
            self.out[0] = jnp.zeros(self.out.shape[1:], F32)

        @pl.when(chip > self.lo)
        def _():
            self.out[0] += self.arrived(u, chip)

        @pl.when(chip < self.hi)
        def _():
            self.out[0] += self.arrived(u, self.chips)

    def drain(self):
        @pl.when(self.adds())
        def _():
            @pl.loop(0, self.units)
            def _(u):
                @pl.loop(0, self.chips)
                def _(j):
                    @pl.when(j > self.chip)
                    def _():
                        self.up(u, j).wait_send()

                    @pl.when(j < self.chip)
                    def _():
                        self.down(u, j).wait_send()

            for u in range(self.units):
                for copy in self.deep_give(u):
                    copy.wait_send()
            for kind in range(max(self.kinds) + 1):
                for j in range(self.chips):
                    for copy in self.wide_give(kind, j):
                        copy.wait_send()


def line_scratch(chips, units, kinds, tokens, cut, width, swap=False):
    dma = pltpu.SemaphoreType.DMA
    block = (width, cut) if swap else (cut, width)
    return [
        pltpu.VMEM((kinds, chips, 2 * tokens, cut), BF),
        pltpu.VMEM((units, 2 * tokens, width), BF),
        pltpu.VMEM((units, chips + 1) + block, BF),
        pltpu.VMEM((1,) + block, F32),
        dma((kinds, chips, 2)),
        dma((units, 2)),
        dma((kinds, chips, 2)),
        dma((kinds, chips, 2)),
        dma((units, 2)),
        dma((units, 2)),
        dma((units, chips + 1)),
        dma((units, chips + 1)),
    ]


def mixer_kernel(n, chips, heads, *refs):
    (
        fac, raw, og, wk_h, wv_h, wq_h, ws_h, wo_h, gain, bias, freq,
        x_o, og_o, q_o, k_o, v_o, sp_o, mx_o, prior_o, gated_o, attn, decay, qfac, kfac, cos, sin,
        x_all, og_all, q, k, v, sp, mx, prior, gated, x, wk, wv, wq, ws, wo, acc, parts, local,
    ) = refs[:44]
    near, far, hold = refs[44:47]
    chain_refs = refs[47:55]
    wsem, gs, gr, os, orr, ss, sr, es, er, osem, bsem = refs[55:]
    rows = raw.shape[0]
    gather = Gather(n, x, x_all, gs, gr)
    gather_og = Gather(n, og, og_all, os, orr)
    ends = Ends(chips)
    hand_own = remote(og, og_o.at[n], es, er, 0, ends.mate)

    def hand(i):
        return remote(og_all.at[gather.source(i)], og_o.at[n + i], es, er, i, ends.mate)

    scatter = Scatter(n, parts, near, far, hold, ss, sr)
    chain = Chain(chips, heads, False, fac, local, prior, *chain_refs)
    loads = [
        pltpu.make_async_copy(a, w, wsem.at[i])
        for i, (a, w) in enumerate(((wk_h, wk), (wv_h, wv), (wq_h, wq), (ws_h, ws), (wo_h, wo)))
    ]
    for load in loads:
        load.start()
    slab = 16
    plan = ((1, 1, 1), (1, 3, 2)) if n == 4 else ()

    @pl.loop(0, rows // slab)
    def _(r):
        here = pl.ds(pl.multiple_of(r * slab, slab), slab)
        center, inv = row_stats(raw[here].astype(F32))
        x[here] = (center * inv * gain[...] + bias[...]).astype(BF)

    greet(gather.peers + chain.peers)
    gather.start()
    place = lax.broadcasted_iota(jnp.int32, (rows, 1), 0).astype(F32)
    angles = (lax.axis_index("seq").astype(F32) * rows + place) * freq[...]
    cos[...] = jnp.cos(angles)
    sin[...] = jnp.sin(angles)
    lag = place - lax.broadcasted_iota(jnp.int32, (rows, rows), 1).astype(F32)
    for h in range(heads):
        rate = fac[1, lax.axis_index("tp") * heads + h]
        decay[h] = jnp.where(lag >= 0, jnp.exp(jnp.maximum(lag, 0.0) * rate), 0.0)
        qfac[h] = jnp.exp((place + 1.0) * rate)
        kfac[h] = jnp.exp((rows - 1.0 - place) * rate)

    @pl.when(ends.gives)
    def _():
        hand_own.start()

    me = gather.source(0)
    x_all[me] = x[...]
    og_all[me] = og[...]
    for load in loads[:2]:
        load.wait()

    @pl.loop(0, n)
    def _(i):
        j = gather.source(i)
        gather.arrive(i)
        at = pl.ds(pl.multiple_of(j * rows, rows), rows)
        acc[:, : heads * DK] = dot(x_all[j], wk[...])

        v[at] = dot(x_all[j], wv[...]).astype(BF)
        for h in range(heads):
            vc = slice(h * DV, (h + 1) * DV)
            kc = slice(h * DK, (h + 1) * DK)
            key = turn(acc[:, kc], cos[...], sin[...]).astype(BF)
            k[at, kc] = key
            key_dec = (key.astype(F32) * kfac[h]).astype(BF)
            p = j * heads + h
            local[p] = dot(key_dec, v[at, vc], 0, 0).astype(BF)
            chain.begin(p)

        chain.open(gather, i)

        @pl.when(i == 0)
        def _():
            gather.relays()
            gather_og.start()

    puts = [
        pltpu.make_async_copy(a, b, osem.at[i])
        for i, (a, b) in enumerate(
            ((x_all, x_o), (k, k_o), (v, v_o), (q, q_o), (sp, sp_o), (og_all, og_o.at[pl.ds(0, n)]))
        )
    ]
    for put in puts[:3]:
        put.start()
    for load in loads[2:]:
        load.wait()

    @pl.loop(0, n)
    def _(i):
        j = gather.source(i)
        at = pl.ds(pl.multiple_of(j * rows, rows), rows)
        acc[:, : heads * DK] = dot(x_all[j], wq[...])
        for h in range(heads):
            kc = slice(h * DK, (h + 1) * DK)
            vc = slice(h * DV, (h + 1) * DV)
            query = turn(acc[:, kc], cos[...], sin[...]).astype(BF)
            q[at, kc] = query
            scores = (dot(query, k[at, kc], 1, 1) * decay[h]).astype(BF)
            mx[at, vc] = dot(scores, v[at, vc])
            sp[at, vc] = dot(x_all[j], ws[:, vc])
        chain.planned(gather, i, plan)

    for put in puts[3:5]:
        put.start()
    gather_og.relays()

    def blocks(j):
        at = pl.ds(pl.multiple_of(j * rows, rows), rows)
        of = pl.ds(j * heads, heads)
        return [
            pltpu.make_async_copy(mx.at[at], mx_o.at[at], bsem.at[0, j]),
            pltpu.make_async_copy(gated.at[at], gated_o.at[at], bsem.at[1, j]),
            pltpu.make_async_copy(prior.at[of], prior_o.at[of], bsem.at[2, j]),
        ]


    @pl.loop(0, n)
    def _(step):
        i = (step + 1) % n
        j = gather.source(i)
        chain.due(gather, i, plan)
        gather_og.arrive(i)

        @pl.when(ends.gives & (chain.place > 0) & (i > 0) & (i < n - 1))
        def _():
            hand(i).start()

        at = pl.ds(pl.multiple_of(j * rows, rows), rows)
        for h in range(heads):
            vc = slice(h * DV, (h + 1) * DV)
            kc = slice(h * DK, (h + 1) * DK)
            p = j * heads + h
            query_dec = (q[at, kc].astype(F32) * qfac[h]).astype(BF)
            mx[at, vc] += dot(query_dec, prior[p])
            pre = sp[at, vc]
            gated[at, vc] = (pre * jax.nn.sigmoid(pre) * norm_of(mx[at, vc])[0]).astype(BF)
        parts[j] = dot(gated[at], wo[...]).astype(BF)
        scatter.send(i)

        @pl.when(ends.gives & (chain.place == 0) & (step == n - 2))
        def _():
            @pl.loop(1, n - 1)
            def _(c):
                hand(c).start()

        for put in blocks(j):
            put.start()

    puts[5].start()
    scatter.relay()

    def write(at, cols, total):
        attn[at, cols] = total

    scatter.finish(write)
    gather.drain()
    gather_og.drain()
    for put in puts:
        put.wait()

    @pl.loop(0, n)
    def _(j):
        for put in blocks(j):
            put.wait()

    @pl.when(ends.gives)
    def _():
        hand_own.wait_send()

        @pl.loop(1, n - 1)
        def _(i):
            hand(i).wait_send()

    @pl.when(ends.takes)
    def _():
        @pl.loop(0, n - 1)
        def _(i):
            hand(i).wait_recv()

    scatter.drain()

    @pl.loop(0, n * heads)
    def _(p):
        chain.drain(p)


def mixer(fac, x, og, wk, wv, wq, ws, wo, gain, bias, freq, cid):
    n = lax.axis_size("tp")
    chips = lax.axis_size("seq") // 2
    rows, model = x.shape
    heads = wk.shape[1] // DK
    pieces = n * heads
    total = n * rows
    dma = pltpu.SemaphoreType.DMA
    sems = max(10, n - 1)
    vmem = pl.BlockSpec(memory_space=pltpu.VMEM)
    hbm = pl.BlockSpec(memory_space=pl.ANY)
    shape = jax.ShapeDtypeStruct
    return pl.pallas_call(
        functools.partial(mixer_kernel, n, chips, heads),
        out_shape=(
            shape((n, rows, model), BF),
            shape((2 * n - 1, rows, model), BF),
            shape((total, heads * DK), BF),
            shape((total, heads * DK), BF),
            shape((total, heads * DV), BF),
            shape((total, heads * DV), F32),
            shape((total, heads * DV), F32),
            shape((pieces, DK, DV), BF),
            shape((total, heads * DV), BF),
            shape((rows, model), F32),
            shape((heads, rows, rows), F32),
            shape((heads, rows, 1), F32),
            shape((heads, rows, 1), F32),
            shape((rows, DK // 2), F32),
            shape((rows, DK // 2), F32),
        ),
        in_specs=[pl.BlockSpec(memory_space=pltpu.SMEM), vmem, vmem] + [hbm] * 5 + [vmem] * 3,
        out_specs=(hbm,) * 9 + (vmem,) * 6,
        scratch_shapes=[
            pltpu.VMEM((n, rows, model), BF),
            pltpu.VMEM((n, rows, model), BF),
            pltpu.VMEM((total, heads * DK), BF),
            pltpu.VMEM((total, heads * DK), BF),
            pltpu.VMEM((total, heads * DV), BF),
            pltpu.VMEM((total, heads * DV), F32),
            pltpu.VMEM((total, heads * DV), F32),
            pltpu.VMEM((pieces, DK, DV), BF),
            pltpu.VMEM((total, heads * DV), BF),
            pltpu.VMEM((rows, model), BF),
        ]
        + [pltpu.VMEM(w.shape, BF) for w in (wk, wv, wq, ws, wo)]
        + [
            pltpu.VMEM((rows, heads * DK), F32),
            pltpu.VMEM((n, rows, model), BF),
            pltpu.VMEM((pieces, DK, DV), BF),
        ]
        + scatter_scratch(n, rows, model)
        + chain_scratch(pieces)
        + [dma((5,))]
        + [dma((sems,))] * 6
        + [dma((n - 1,)), dma((n - 1,)), dma((6,)), dma((3, n))],
        compiler_params=params(cid),
        name="mixer",
    )(fac, x, og, wk, wv, wq, ws, wo, gain, bias, freq)


GELU_C = 0.7978845608028654
GELU_A = 0.044715


def gelu_of(g):
    square = g * g
    th = jnp.tanh(GELU_C * (g + GELU_A * (square * g)))
    half = 0.5 * (1.0 + th)
    slope = half + 0.5 * g * (1.0 - th * th) * (GELU_C * (1.0 + 3.0 * GELU_A * square))
    return g * half, slope


def mlp_kernel(n, chips, *refs):
    (
        raw, attn, cot, gain, bias, og_h, wg_h, wu_h, wd_h,
        x_o, hidden_o, gate_o, upper_o, mlp_o, res_grad, res_low, vec, gate_late, up_late,
        og_all, x, grad_two, x_all, hidden, gate_low, upper_low, mlp_parts, wg, wu, wd, hg, acc_g, acc_u, acc, parts, near, far, hold,
        wsem, gs, gr, ss, sr, es, er, osem, bsem,
    ) = refs
    rows = raw.shape[0]
    slab = 16
    gather = Gather(n, x, x_all, gs, gr)
    scatter = Scatter(n, parts, near, far, hold, ss, sr)
    ends = Ends(chips)
    loads = [
        pltpu.make_async_copy(a, w, wsem.at[i])
        for i, (a, w) in enumerate(((wd_h, wd), (wg_h, wg), (wu_h, wu)))
    ]
    loads.append(pltpu.make_async_copy(og_h, og_all, wsem.at[3]))
    for load in [loads[0], loads[3], loads[1], loads[2]]:
        load.start()
    @pl.loop(0, rows // slab)
    def _(r):
        here = pl.ds(pl.multiple_of(r * slab, slab), slab)
        center, inv = row_stats(raw[here].astype(F32) + attn[here])
        x[here] = (center * inv * gain[...] + bias[...]).astype(BF)

    greet(gather.peers + ends.peers)
    gather.start()
    me = gather.source(0)

    def hand(i):
        j = gather.source(i)
        return remote(x_all.at[j], x_all.at[n + i], es, er, i, ends.mate)

    first = remote(x, x_all.at[n], es, er, 0, ends.mate)

    @pl.when(ends.gives)
    def _():
        first.start()

    x_all[me] = x[...]
    loads[0].wait()
    loads[3].wait()
    pair = 2 * rows

    @pl.loop(0, n // 2)
    def _(c):
        two = pl.ds(pl.multiple_of(2 * c, 2), 2)
        at = pl.ds(pl.multiple_of(c * pair, pair), pair)
        hg[at] = dot(og_all[two].reshape(pair, x.shape[1]), wd[...], 1, 1)

    gather.relays()
    loads[1].wait()
    loads[2].wait()

    def units(block, back_at, extra):
        start = pl.multiple_of(block * rows, rows)
        acc_g[...] = dot(x_all[block], wg[...])
        acc_u[...] = dot(x_all[block], wu[...])
        if extra:
            gate_late[...] = acc_g[...]
            up_late[...] = acc_u[...]

        @pl.loop(0, rows // slab)
        def _(r):
            here = pl.ds(pl.multiple_of(r * slab, slab), slab)
            there = pl.ds(pl.multiple_of(start + r * slab, slab), slab)
            g, u = acc_g[here], acc_u[here]
            gelu, slope = gelu_of(g)
            hidden[there] = (gelu * u).astype(BF)
            back = hg[pl.ds(pl.multiple_of(back_at + r * slab, slab), slab)]
            gate_low[there] = (back * u * slope).astype(BF)
            upper_low[there] = (back * gelu).astype(BF)

    @pl.loop(0, n)
    def _(turn):
        i = jnp.where(turn == 2, 3, jnp.where(turn == 3, 2, turn)) if n == 4 else turn
        j = gather.source(i)
        gather.arrive(i)

        @pl.when(ends.gives & (i > 0))
        def _():
            hand(i).start()

        units(j, j * rows, False)
        at = pl.ds(pl.multiple_of(j * rows, rows), rows)
        acc[...] = dot(gate_low[at], wg[...], 1, 1)
        parts[j] = (acc[...] + dot(upper_low[at], wu[...], 1, 1)).astype(BF)
        scatter.send(i)

    whole = pl.ds(0, n * rows)
    puts = [
        pltpu.make_async_copy(a, b, osem.at[i])
        for i, (a, b) in enumerate(
            (
                (x_all.at[pl.ds(0, n)], x_o.at[pl.ds(0, n)]),
                (hidden.at[whole], hidden_o.at[whole]),
                (gate_low.at[whole], gate_o.at[whole]),
                (upper_low.at[whole], upper_o.at[whole]),
                (mlp_parts, mlp_o),
            )
        )
    ]
    for put in puts[:4]:
        put.start()

    def blocks(i):
        at = pl.ds(pl.multiple_of((n + i) * rows, rows), rows)
        return [
            pltpu.make_async_copy(x_all.at[n + i], x_o.at[n + i], bsem.at[0, i]),
            pltpu.make_async_copy(hidden.at[at], hidden_o.at[at], bsem.at[1, i]),
        ]

    def late_blocks(i):
        at = pl.ds(pl.multiple_of((n + i) * rows, rows), rows)
        return [
            pltpu.make_async_copy(gate_low.at[at], gate_o.at[at], bsem.at[2, i]),
            pltpu.make_async_copy(upper_low.at[at], upper_o.at[at], bsem.at[3, i]),
        ]

    def extra(i):
        @pl.when(ends.takes)
        def _():
            hg[pl.ds(0, rows)] = dot(og_all[n + jnp.minimum(i, n - 2)], wd[...], 1, 1)
            hand(i).wait_recv()
            units(n + i, 0, True)
            for put in blocks(i):
                put.start()

            @pl.when(i < n - 1)
            def _():
                for put in late_blocks(i):
                    put.start()

    @pl.loop(0, n // 2)
    def _(i):
        extra(i)

    scatter.relay()

    @pl.loop(0, n // 2)
    def _(c):
        two = pl.ds(pl.multiple_of(2 * c, 2), 2)
        at = pl.ds(pl.multiple_of(c * pair, pair), pair)
        mlp_parts[two] = dot(hidden[at], wd[...]).astype(BF).reshape(2, rows, x.shape[1])

    puts[4].start()

    def write(at, cols, total):
        grad_two[at, cols] = total

    scatter.finish(write)
    vec[...] = jnp.zeros_like(vec)

    @pl.loop(0, rows // slab)
    def _(r):
        here = pl.ds(pl.multiple_of(r * slab, slab), slab)
        center, inv = row_stats(raw[here].astype(F32) + attn[here])
        hat, grad = center * inv, grad_two[here]
        total = cot[here].astype(F32) + norm_pull(grad, hat, inv, gain[...])
        res_grad[here] = total
        res_low[here] = total.astype(BF)
        vec[2:3] += jnp.sum(grad * hat, 0, keepdims=True)
        vec[3:4] += jnp.sum(grad, 0, keepdims=True)

    @pl.loop(n // 2, n)
    def _(i):
        extra(i)

    @pl.when(ends.takes)
    def _():
        @pl.loop(0, n)
        def _(i):
            for put in blocks(i):
                put.wait()

        @pl.loop(0, n - 1)
        def _(i):
            for put in late_blocks(i):
                put.wait()

    for put in puts:
        put.wait()

    gather.drain()
    scatter.drain()

    @pl.when(ends.gives)
    def _():
        first.wait_send()

        @pl.loop(1, n)
        def _(i):
            hand(i).wait_send()


def mlp(raw, attn, cot, gain, bias, og_all, wg, wu, wd, cid):
    n = lax.axis_size("tp")
    chips = lax.axis_size("seq") // 2
    rows, model = raw.shape
    width = wg.shape[1]
    total = n * rows
    dma = pltpu.SemaphoreType.DMA
    sems = max(10, n - 1)
    vmem = pl.BlockSpec(memory_space=pltpu.VMEM)
    hbm = pl.BlockSpec(memory_space=pl.ANY)
    shape = jax.ShapeDtypeStruct
    return pl.pallas_call(
        functools.partial(mlp_kernel, n, chips),
        out_shape=(
            shape((2 * n, rows, model), BF),
            shape((2 * total, width), BF),
            shape((2 * total - rows, width), BF),
            shape((2 * total - rows, width), BF),
            shape((n, rows, model), BF),
            shape((rows, model), F32),
            shape((rows, model), BF),
            shape((8, model), F32),
            shape((rows, width), F32),
            shape((rows, width), F32),
        ),
        in_specs=[vmem] * 5 + [hbm] * 4,
        out_specs=(hbm,) * 5 + (vmem,) * 5,
        scratch_shapes=[
            pltpu.VMEM(og_all.shape, BF),
            pltpu.VMEM((rows, model), BF),
            pltpu.VMEM((rows, model), F32),
            pltpu.VMEM((2 * n, rows, model), BF),
            pltpu.VMEM((2 * total, width), BF),
            pltpu.VMEM((2 * total, width), BF),
            pltpu.VMEM((2 * total, width), BF),
            pltpu.VMEM((n, rows, model), BF),
        ]
        + [pltpu.VMEM(w.shape, BF) for w in (wg, wu, wd)]
        + [
            pltpu.VMEM((total, width), F32),
            pltpu.VMEM((rows, width), F32),
            pltpu.VMEM((rows, width), F32),
            pltpu.VMEM((rows, model), F32),
            pltpu.VMEM((n, rows, model), BF),
        ]
        + scatter_scratch(n, rows, model)
        + [dma((4,))]
        + [dma((sems,))] * 4
        + [dma((n,)), dma((n,)), dma((5,)), dma((4, n))],
        compiler_params=params(cid),
        name="mlp",
    )(raw, attn, cot, gain, bias, og_all, wg, wu, wd)


def mixer_back_kernel(n, chips, heads, *refs):
    (
        fac, res, wo_h, wq_h, wk_h, wv_h, ws_h, q_h, k_h, v_h, sp_h, mx_h, prior_h, mlp_h, decay, qfac, kfac, cos, sin, og_h, wd_h, gate_late, up_late,
        res_o, swish_o, value_o, qk_o, parts_o, mlp_out, og_late, gate_low, upper_low,
        q, k, v, sp, mx, prior, mlp_parts, res_all, swish_low, value_low, qk_low, wo, wq, wk, wv, ws, mixed_low, sums, parts, local, later, key_part, value_part,
    ) = refs[:55]
    mlp_near, mlp_far, mlp_hold = refs[55:58]
    chain_refs = refs[58:66]
    wsem, gs, gr, ms, mr, es, er, isem, lsem, osem, bsem = refs[66:]
    rows = res.shape[0]
    gather = Gather(n, res, res_all, gs, gr)
    scatter_mlp = Scatter(n, mlp_parts, mlp_near, mlp_far, mlp_hold, ms, mr)
    chain = Chain(chips, heads, True, fac, local, later, *chain_refs)
    ends = Ends(chips)
    late = remote(og_h.at[gather.source(n - 1)], og_late, es, er, 0, ends.mate)
    load_late = pltpu.make_async_copy(wd_h, wo, wsem.at[5])
    loads = [
        pltpu.make_async_copy(a, w, wsem.at[i])
        for i, (a, w) in enumerate(((wo_h, wo), (ws_h, ws), (wq_h, wq), (wk_h, wk), (wv_h, wv)))
    ]
    def entering(i):
        j = gather.source(i)
        at = pl.ds(pl.multiple_of(j * rows, rows), rows)
        return [
            pltpu.make_async_copy(a.at[at], b.at[at], isem.at[w, j])
            for w, (a, b) in enumerate(((mx_h, mx), (sp_h, sp), (q_h, q)))
        ]

    loads += [
        pltpu.make_async_copy(a, b, lsem.at[i])
        for i, (a, b) in enumerate(((k_h, k), (v_h, v), (prior_h, prior), (mlp_h, mlp_parts)))
    ]
    loads[0].start()
    for i in range(n):
        for load in entering(i):
            load.start()
    for load in loads[1:]:
        load.start()
    greet(gather.peers + chain.peers)
    gather.start()
    me = gather.source(0)
    res_all[me] = res[...]
    loads[0].wait()

    @pl.loop(0, n)
    def _(i):
        j = gather.source(i)
        gather.arrive(i)
        at = pl.ds(pl.multiple_of(j * rows, rows), rows)
        for load in entering(i):
            load.wait()
        sums[j, :, : heads * DV] = dot(res_all[j], wo[...], 1, 1).astype(sums.dtype)

        for h in range(heads):
            vc = slice(h * DV, (h + 1) * DV)
            kc = slice(h * DK, (h + 1) * DK)
            back = sums[j, :, vc].astype(F32)
            normed, inv = norm_of(mx[at, vc])
            pre = sp[at, vc]
            sig = jax.nn.sigmoid(pre)
            swish_low[at, vc] = (back * normed * (sig * (1.0 + pre * (1.0 - sig)))).astype(BF)
            g = back * (pre * sig)
            g = inv * (
                g
                - jnp.mean(g, -1, keepdims=True)
                - normed * jnp.mean(g * normed, -1, keepdims=True)
            )
            g = g.astype(BF)
            mixed_low[at, vc] = g
            query_dec = (q[at, kc].astype(F32) * qfac[h]).astype(BF)
            p = j * heads + h
            local[p] = dot(query_dec, g, 0, 0).astype(BF)
            chain.begin(p)

        chain.open(gather, i)

        @pl.when(i == 0)
        def _():
            gather.relays()

    puts = [
        pltpu.make_async_copy(res_all, res_o, osem.at[0]),
        pltpu.make_async_copy(swish_low, swish_o, osem.at[1]),
    ]
    for put in puts:
        put.start()

    def leaving(j):
        at = pl.ds(pl.multiple_of(j * rows, rows), rows)
        return [
            pltpu.make_async_copy(value_low.at[at], value_o.at[at], bsem.at[0, j]),
            pltpu.make_async_copy(qk_low.at[at], qk_o.at[at], bsem.at[1, j]),
            pltpu.make_async_copy(parts.at[j], parts_o.at[j], bsem.at[2, j]),
        ]

    for load in loads[1:]:
        load.wait()
    for i in range(1, n):
        scatter_mlp.send(i)

    @pl.when(ends.gives)
    def _():
        late.start()

    @pl.when(ends.takes)
    def _():
        load_late.start()

    @pl.loop(0, n)
    def _(i):
        j = gather.source(i)
        at = pl.ds(pl.multiple_of(j * rows, rows), rows)
        for h in range(heads):
            vc = slice(h * DV, (h + 1) * DV)
            kc = slice(h * DK, (h + 1) * DK)
            g, query, key = mixed_low[at, vc], q[at, kc], k[at, kc]
            chain.tick(gather, i * heads + h)
            raw_low = (dot(g, v[at, vc], 1, 1) * decay[h]).astype(BF)
            query_back = dot(raw_low, key) + dot(g, prior[j * heads + h], 1, 1) * qfac[h]
            qk_low[at, kc] = turn_back(query_back, cos[...], sin[...]).astype(BF)
            scores = (dot(query, key, 1, 1) * decay[h]).astype(BF)
            key_part[at, kc] = dot(raw_low, query, 0, 0).astype(key_part.dtype)
            value_part[at, vc] = dot(scores, g, 0, 0).astype(value_part.dtype)
        sums[j] = dot(swish_low[at], ws[...], 1, 1).astype(sums.dtype)
        sums[j] += dot(qk_low[at, : heads * DK], wq[...], 1, 1).astype(sums.dtype)

    scatter_mlp.relay()

    @pl.loop(0, n)
    def _(step):
        i = (step + 1) % n
        j = gather.source(i)
        at = pl.ds(pl.multiple_of(j * rows, rows), rows)
        for h in range(heads):
            vc = slice(h * DV, (h + 1) * DV)
            kc = slice(h * DK, (h + 1) * DK)
            chain.tick(gather, (n + step) * heads + h)
            after = later[j * heads + h]
            key_dec = (k[at, kc].astype(F32) * kfac[h]).astype(BF)
            key_back = key_part[at, kc].astype(F32) + dot(v[at, vc], after, 1, 1) * kfac[h]
            qk_low[at, slice((heads + h) * DK, (heads + h + 1) * DK)] = turn_back(
                key_back, cos[...], sin[...]
            ).astype(BF)
            value_low[at, vc] = (value_part[at, vc] + dot(key_dec, after)).astype(BF)
        sums[j] += dot(value_low[at], wv[...], 1, 1).astype(sums.dtype)
        parts[j] = (sums[j].astype(F32) + dot(qk_low[at, heads * DK :], wk[...], 1, 1)).astype(BF)
        for put in leaving(j):
            put.start()

    @pl.when(ends.takes)
    def _():
        width = gate_late.shape[1]
        load_late.wait()
        late.wait_recv()
        sums[0, :, :width] = dot(og_late[...], wo[...], 1, 1).astype(sums.dtype)
        slab = 16

        @pl.loop(0, rows // slab)
        def _(r):
            here = pl.ds(pl.multiple_of(r * slab, slab), slab)
            gelu, slope = gelu_of(gate_late[here])
            back = sums[0, here, :width].astype(F32)
            gate_low[here] = (back * up_late[here] * slope).astype(BF)
            upper_low[here] = (back * gelu).astype(BF)

    def write_mlp(at, cols, total):
        mlp_out[at, cols] = total

    scatter_mlp.finish(write_mlp)
    gather.drain()
    scatter_mlp.drain()

    @pl.when(ends.gives)
    def _():
        late.wait_send()

    for put in puts:
        put.wait()

    @pl.loop(0, n)
    def _(j):
        for put in leaving(j):
            put.wait()

    @pl.loop(0, n * heads)
    def _(p):
        chain.drain(p)


def mixer_back(fac, res, wo, wq, wk, wv, ws, q, k, v, sp, mx, prior, mlp_parts, decay, qfac, kfac, cos, sin, og_all, wd, gate_late, up_late, cid):
    n = lax.axis_size("tp")
    chips = lax.axis_size("seq") // 2
    rows, model = res.shape
    heads = q.shape[1] // DK
    pieces = n * heads
    total = n * rows
    keep = F32 if n <= 4 else BF
    dma = pltpu.SemaphoreType.DMA
    sems = max(10, n - 1)
    vmem = pl.BlockSpec(memory_space=pltpu.VMEM)
    hbm = pl.BlockSpec(memory_space=pl.ANY)
    shape = jax.ShapeDtypeStruct
    return pl.pallas_call(
        functools.partial(mixer_back_kernel, n, chips, heads),
        out_shape=(
            shape((n, rows, model), BF),
            shape((total, heads * DV), BF),
            shape((total, heads * DV), BF),
            shape((total, 2 * heads * DK), BF),
            shape((n, rows, model), BF),
            shape((rows, model), F32),
            shape((rows, model), BF),
            shape(gate_late.shape, BF),
            shape(gate_late.shape, BF),
        ),
        in_specs=[pl.BlockSpec(memory_space=pltpu.SMEM), vmem] + [hbm] * 12 + [vmem] * 5 + [hbm, hbm, vmem, vmem],
        out_specs=(hbm,) * 5 + (vmem,) * 4,
        scratch_shapes=[pltpu.VMEM(a.shape, a.dtype) for a in (q, k, v, sp, mx, prior, mlp_parts)]
        + [
            pltpu.VMEM((n, rows, model), BF),
            pltpu.VMEM((total, heads * DV), BF),
            pltpu.VMEM((total, heads * DV), BF),
            pltpu.VMEM((total, 2 * heads * DK), BF),
        ]
        + [pltpu.VMEM(w.shape, BF) for w in (wo, wq, wk, wv, ws)]
        + [
            pltpu.VMEM((total, heads * DV), BF),
            pltpu.VMEM((n, rows, model), keep),
            pltpu.VMEM((n, rows, model), BF),
            pltpu.VMEM((pieces, DK, DV), BF),
            pltpu.VMEM((pieces, DK, DV), BF),
            pltpu.VMEM((total, heads * DK), keep),
            pltpu.VMEM((total, heads * DV), BF),
        ]
        + scatter_scratch(n, rows, model)
        + chain_scratch(pieces)
        + [dma((6,))]
        + [dma((sems,))] * 4
        + [dma((1,)), dma((1,)), dma((3, n)), dma((4,)), dma((2,)), dma((3, n))],
        compiler_params=params(cid),
        name="mixer_back",
    )(fac, res, wo, wq, wk, wv, ws, q, k, v, sp, mx, prior, mlp_parts, decay, qfac, kfac, cos, sin, og_all, wd, gate_late, up_late)


def weights_kernel(chips, *refs):
    (
        two, og, og_late, hidden, gate_low, gate_late, up_low, up_late,
        one, res, swish_low, gated, value_low, qk_low,
        vec_two, gain, parts_h, raw_h, res_h, attn_h, mlp_h,
        down_o, gate_o, up_o, swish_o, mixer_o, value_o, query_o, key_o, back_o, outs_o, vec_out,
    ) = refs[:32]
    mlp = LineSums(
        chips, 1, chips - 2, ((two,), (og, og_late)),
        ((gate_low, gate_late), (up_low, up_late), (hidden,)), (0, 0, 1), refs[32:44],
    )
    mix = LineSums(
        chips, 0, chips - 1, ((one,), (res,)), ((swish_low,), (gated,), (value_low,), (qk_low,)),
        (0, 1, 0, 0), refs[44:56],
    )
    (
        turned, osem, grad, raw, res_grad, attn, mlp_out, back, outs, csem, dsem,
        vec, vec_near, vec_mid, vec_far, vs, vr, us, ur, parts, near, far, hold, lsem, ss, sr,
    ) = refs[56:]
    grad = grad if parts.shape[0] == 4 else near.at[0]
    scatter = Scatter(parts.shape[0], parts, near, far, hold, ss, sr)
    load = pltpu.make_async_copy(parts_h, parts, lsem.at[0])
    load.start()
    s, t = lax.axis_index("seq"), lax.axis_index("tp")
    span, tp = 2 * chips, vec_far.shape[0] + 1
    share = vec_mid.shape[1]
    ring = [((s + d) % span, t) for d in range(1, span)]
    cross = [(s, (t + d) % tp) for d in range(1, tp)]

    def part(who):
        return pl.ds(pl.multiple_of(who * share, share), share)

    greet(ring + cross)
    vec_first = [
        remote(vec.at[:, part((s + d) % span)], vec_near.at[d - 1], vs, vr, d - 1, ring[d - 1])
        for d in range(1, span)
    ]
    vec_last = [
        remote(vec_mid, vec_far.at[d - 1], us, ur, d - 1, cross[d - 1]) for d in range(1, tp)
    ]
    vec[...] = vec_two[...]
    for u in range(mix.units):
        if u < mlp.units:
            mlp.share(u)
        mix.share(u)

    half = mix.out.shape[2] // 2
    lo, hi = pl.ds(0, half), pl.ds(half, half)

    def put(pairs):
        copies = [pltpu.make_async_copy(a, b, osem.at[i]) for i, (a, b) in enumerate(pairs)]
        for copy in copies:
            copy.start()
        for copy in copies:
            copy.wait()

    def put_mlp(w):
        if w == 2:
            turned[...] = mlp.out[0].T
            put([(turned, down_o)])
        else:
            put([(mlp.out.at[0], (gate_o, up_o)[w])])

    def put_mix(w):
        if w == 1:
            turned[...] = mix.out[0].T
            put([(turned, mixer_o)])
        elif w == 3:
            put([(mix.out.at[0, :, lo], query_o), (mix.out.at[0, :, hi], key_o)])
        else:
            put([(mix.out.at[0], (swish_o, None, value_o)[w])])

    @pl.loop(0, mix.units)
    def _(u):
        for w in range(mix.units):

            @pl.when(u == w)
            def _(w=w):
                if w < mlp.units:
                    mlp.ready(w)

        @pl.when(u < mlp.units)
        def _():
            mlp.step(u, 0)

        @pl.when(u == 0)
        def _():
            load.wait()
            for i in range(1, scatter.n):
                scatter.send(i)

        for w in range(mix.units):

            @pl.when(u == w)
            def _(w=w):
                mix.ready(w)

        @pl.loop(0, chips - 1)
        def _(k):
            @pl.when((u < mlp.units) & (k > 0))
            def _():
                mlp.step(u, k)

            mix.step(u, k)

        @pl.when(u == 0)
        def _():
            chunk = raw.shape[0]

            scatter.relay()

            def write(at, cols, total):
                grad[at, cols] = total.astype(grad.dtype)

            scatter.finish(write)

            @pl.loop(0, parts.shape[1] // chunk)
            def _(c):
                here = pl.ds(pl.multiple_of(c * chunk, chunk), chunk)
                pairs = (raw_h, raw), (res_h, res_grad), (attn_h, attn), (mlp_h, mlp_out)
                ins = [
                    pltpu.make_async_copy(a.at[here], b, csem.at[i])
                    for i, (a, b) in enumerate(pairs)
                ]
                for copy in ins:
                    copy.start()
                for copy in ins:
                    copy.wait()
                value = raw[...].astype(F32)
                outs[...] = value + attn[...] + mlp_out[...]
                center, inv = row_stats(value)
                hat, given = center * inv, grad[here].astype(F32)
                vec[0:1] += jnp.sum(given * hat, 0, keepdims=True)
                vec[1:2] += jnp.sum(given, 0, keepdims=True)
                back[...] = res_grad[...] + norm_pull(given, hat, inv, gain[...])
                puts = [
                    pltpu.make_async_copy(a, b.at[here], dsem.at[i])
                    for i, (a, b) in enumerate(((back, back_o), (outs, outs_o)))
                ]
                for copy in puts:
                    copy.start()
                for copy in puts:
                    copy.wait()

            for copy in vec_first:
                copy.start()

        @pl.when(u == 1)
        def _():
            for copy in vec_first:
                copy.wait_recv()
            vec_mid[...] = vec[:, part(s)] + jnp.sum(vec_near[...], 0)
            for copy in vec_last:
                copy.start()

        @pl.when(u > 0)
        def _():
            mlp.finish(u - 1)
            mix.finish(u - 1)
            for w in range(mix.units - 1):

                @pl.when(u - 1 == w)
                def _(w=w):
                    put_mlp(w)
                    put_mix(w)

    mix.finish(mix.units - 1)
    put_mix(mix.units - 1)
    for copy in vec_last:
        copy.wait_recv()
    vec_out[...] = vec_mid[...] + jnp.sum(vec_far[...], 0)
    for copy in vec_first + vec_last:
        copy.wait_send()
    scatter.drain()
    mlp.drain()
    mix.drain()


def weight_sums(
    two, og, og_late, hidden, gate_low, gate_late, up_low, up_late, one, res, swish_low, gated, value_low,
    qk_low, vec_two, gain, grad, raw, res_grad, attn, mlp_out, cid,
):
    chips = lax.axis_size("seq") // 2
    tokens, model = one.shape
    width = gated.shape[1]
    mlp_tokens, mlp_width = hidden.shape
    keys = qk_low.shape[1] // 2
    cut = model // (2 * chips)
    dma = pltpu.SemaphoreType.DMA
    vmem = pl.BlockSpec(memory_space=pltpu.VMEM)
    hbm = pl.BlockSpec(memory_space=pl.ANY)
    shape = lambda *a: jax.ShapeDtypeStruct(a, F32)
    ring, cross = 2 * chips - 1, lax.axis_size("tp") - 1
    rows, share, chunk = raw.shape[0], model // (2 * chips), 16
    part = lambda dtype: pltpu.VMEM((chunk, model), dtype)
    return pl.pallas_call(
        functools.partial(weights_kernel, chips),
        out_shape=(
            shape(mlp_width, cut),
            shape(cut, mlp_width),
            shape(cut, mlp_width),
            shape(cut, width),
            shape(width, cut),
            shape(cut, width),
            shape(cut, keys),
            shape(cut, keys),
            shape(rows, model),
            shape(rows, model),
            shape(8, share),
        ),
        in_specs=[hbm] * 14 + [vmem] * 2 + [hbm] * 5,
        out_specs=(hbm,) * 10 + (vmem,),
        scratch_shapes=line_scratch(chips, 3, 2, mlp_tokens, cut, mlp_width)
        + line_scratch(chips, 4, 2, tokens, cut, width)
        + [
            pltpu.VMEM((width, cut), F32),
            dma((8,)),
            pltpu.VMEM((rows, model) if cross < 4 else (16, 128), F32),
            part(BF),
            part(F32),
            part(F32),
            part(F32),
            part(F32),
            part(F32),
            dma((5,)),
            dma((2,)),
            pltpu.VMEM((8, model), F32),
            pltpu.VMEM((ring, 8, share), F32),
            pltpu.VMEM((8, share), F32),
            pltpu.VMEM((cross, 8, share), F32),
            dma((ring,)),
            dma((ring,)),
            dma((cross,)),
            dma((cross,)),
            pltpu.VMEM((cross + 1, rows, model), BF),
        ]
        + scatter_scratch(cross + 1, rows, model)
        + [
            dma((1,)),
            dma((max(10, cross),)),
            dma((max(10, cross),)),
        ],
        compiler_params=params(cid),
        name="weights",
    )(two, og, og_late, hidden, gate_low, gate_late, up_low, up_late, one, res, swish_low, gated, value_low,
      qk_low, vec_two, gain, grad, raw, res_grad, attn, mlp_out)


def shards(
    inputs,
    query_weight,
    key_weight,
    value_weight,
    swish_weight,
    output_weight,
    gate_weight,
    up_weight,
    down_weight,
    attn_gain,
    attn_bias,
    mlp_gain,
    mlp_bias,
    output_grad,
):
    _, rows, model = inputs.shape
    heads = query_weight.shape[1] // DK
    seqs, tps = lax.axis_size("seq"), lax.axis_size("tp")
    raw, cotangent = inputs[0], output_grad[0]
    row = lambda v: v.reshape(1, model)
    flat = lambda a: a.reshape(-1, model)

    half_width = DK // 2
    frequencies = np.power(
        np.float32(10000.0), -np.arange(half_width, dtype=np.float32) / np.float32(half_width)
    )[None]
    decays = 1.0 - np.exp2(-5.0 - np.arange(heads * tps))
    factors = np.stack([np.power(decays, rows), np.log(decays)]).astype(np.float32)

    (
        one_all, grad_all, query, key, value, swish_pre, mixed, prior, gated, attn_out,
        decay_mat, query_fac, key_fac, cosine, sine,
    ) = mixer(
        factors, raw, cotangent, key_weight, value_weight, query_weight, swish_weight,
        output_weight, row(attn_gain), row(attn_bias), frequencies, 0,
    )
    two_all, hidden, gate_low, upper_low, mlp_parts, res_grad, res_low, vectors, gate_pre, up_pre = mlp(
        raw, attn_out, cotangent, row(mlp_gain), row(mlp_bias), grad_all, gate_weight, up_weight,
        down_weight, 1,
    )
    (
        res_all, swish_low, value_low, qk_low, normed_one_grad, mlp_out, og_late, gate_late, up_late,
    ) = mixer_back(
        factors, res_low, output_weight, query_weight, key_weight, value_weight, swish_weight,
        query, key, value, swish_pre, mixed, prior, mlp_parts, decay_mat, query_fac, key_fac,
        cosine, sine, grad_all, down_weight, gate_pre, up_pre, 2,
    )
    (
        down_grad, gate_grad, up_grad, swish_grad, mixer_grad, value_grad, query_grad, key_grad,
        input_grad, outputs, vector_sums,
    ) = weight_sums(
        flat(two_all), flat(grad_all), og_late, hidden, gate_low, gate_late, upper_low, up_late,
        flat(one_all), flat(res_all), swish_low, gated, value_low, qk_low, vectors, row(attn_gain),
        normed_one_grad, raw, res_grad, attn_out, mlp_out, 3,
    )
    each = model // (seqs * tps)
    vector_sums = lax.dynamic_slice(vector_sums, (0, lax.axis_index("tp") * each), (4, each))
    return (
        outputs.astype(BF)[None],
        input_grad.astype(BF)[None],
        query_grad,
        key_grad,
        value_grad,
        swish_grad,
        mixer_grad,
        gate_grad,
        up_grad,
        down_grad,
        vector_sums[0],
        vector_sums[1],
        vector_sums[2],
        vector_sums[3],
    )


def solution(mesh):
    return jax.shard_map(
        shards,
        mesh=mesh,
        in_specs=(
            P("tp", "seq", None),
            P(None, "tp"),
            P(None, "tp"),
            P(None, "tp"),
            P(None, "tp"),
            P("tp", None),
            P(None, "tp"),
            P(None, "tp"),
            P("tp", None),
            P(),
            P(),
            P(),
            P(),
            P("tp", "seq", None),
        ),
        out_specs=(
            P("tp", "seq", None),
            P("tp", "seq", None),
            P("seq", "tp"),
            P("seq", "tp"),
            P("seq", "tp"),
            P("seq", "tp"),
            P("tp", "seq"),
            P("seq", "tp"),
            P("seq", "tp"),
            P("tp", "seq"),
            P(("seq", "tp")),
            P(("seq", "tp")),
            P(("seq", "tp")),
            P(("seq", "tp")),
        ),
        check_vma=False,
    )
```

```python
import functools

import jax
import jax.numpy as jnp
import numpy as np
from jax import lax
from jax.experimental import pallas as pl
from jax.experimental.pallas import tpu as pltpu
from jax.sharding import PartitionSpec as P

DK = 256
DV = 512


EPS = 1e-05
MESH = pl.DeviceIdType.MESH
BF = jnp.bfloat16
F32 = jnp.float32
VMEM_LIMIT = 63 * 1024 * 1024 - 512 * 1024


def remote(src, dst, ssem, rsem, slot, dev):
    return pltpu.make_async_remote_copy(
        src_ref=src,
        dst_ref=dst,
        send_sem=ssem.at[slot],
        recv_sem=rsem.at[slot],
        device_id=dev,
        device_id_type=MESH,
    )


def greet(devs):
    barrier = pltpu.get_barrier_semaphore()
    for dev in devs:
        pl.semaphore_signal(barrier, inc=1, device_id=dev, device_id_type=MESH)
    pl.semaphore_wait(barrier, len(devs))


def params(cid):
    return pltpu.CompilerParams(
        collective_id=cid, has_side_effects=True, vmem_limit_bytes=VMEM_LIMIT
    )


class Gather:
    def __init__(self, n, x, o, ssem, rsem, base=0):
        s, t = lax.axis_index("seq"), lax.axis_index("tp")
        self.n, self.t = n, t
        rows = x.shape[0]
        if n == 4:
            px, py = t + 1 - 2 * (t % 2), (t + 2) % 4
            dx, dy = (s, px), (s, py)
            self.peers = [dx, dy]
            half = rows // 2
            lo, hi = pl.ds(0, half), pl.ds(half, half)
            self.first = [
                remote(x.at[lo], o.at[base + t, lo], ssem, rsem, 0, dx),
                remote(x.at[hi], o.at[base + t, hi], ssem, rsem, 1, dy),
                remote(x.at[hi], o.at[base + t, hi], ssem, rsem, 2, dx),
                remote(x.at[lo], o.at[base + t, lo], ssem, rsem, 3, dy),
            ]
            self.relay = [
                remote(o.at[base + px, lo], o.at[base + px, lo], ssem, rsem, 4, dy),
                remote(o.at[base + py, hi], o.at[base + py, hi], ssem, rsem, 5, dx),
            ]
        else:
            self.peers = [(s, (t + k) % n) for k in range(1, n)]
            self.first = [
                remote(x, o.at[base + t], ssem, rsem, k, dev) for k, dev in enumerate(self.peers)
            ]
            self.relay = []

    def source(self, i):
        t = self.t
        if self.n == 4:
            near = jnp.where(i == 1, t + 1 - 2 * (t % 2), (t + 2) % 4)
            return jnp.where(i == 0, t, jnp.where(i == 3, 3 - t, near))
        return (t - i + self.n) % self.n

    def start(self):
        for copy in self.first:
            copy.start()

    def relays(self):
        for copy, onward in zip(self.first, self.relay):
            copy.wait_recv()
            onward.start()

    def arrive(self, i):
        if self.n == 4:

            @pl.when(i == 1)
            def _():
                self.first[2].wait_recv()

            @pl.when(i == 2)
            def _():
                self.first[3].wait_recv()

            @pl.when(i == 3)
            def _():
                self.relay[0].wait_recv()
                self.relay[1].wait_recv()

        else:
            for k, copy in enumerate(self.first):

                @pl.when(i == k + 1)
                def _(copy=copy):
                    copy.wait_recv()

    def drain(self):
        for copy in self.first + self.relay:
            copy.wait_send()


class Scatter:
    def __init__(self, n, parts, near, far, hold, ssem, rsem):
        s, t = lax.axis_index("seq"), lax.axis_index("tp")
        self.n, self.t = n, t
        self.parts, self.near, self.far, self.hold = parts, near, far, hold
        if n == 4:
            self.px, self.py, pd = t + 1 - 2 * (t % 2), (t + 2) % 4, 3 - t
            dx, dy = (s, self.px), (s, self.py)
            self.peers = [dx, dy]
            half = parts.shape[-1] // 2
            self.cols = a, b = pl.ds(0, half), pl.ds(half, half)
            rows = parts.shape[1] // 2
            self.halves = (pl.ds(0, rows), pl.ds(rows, rows))
            self.far_a = [
                remote(parts.at[pd, r, a], near.at[0, 1, r], ssem, rsem, i, dx)
                for i, r in enumerate(self.halves)
            ]
            self.far_b = [
                remote(parts.at[pd, r, b], near.at[1, 1, r], ssem, rsem, 6 + i, dy)
                for i, r in enumerate(self.halves)
            ]
            self.near_a = remote(parts.at[self.px, :, a], near.at[0, 0], ssem, rsem, 2, dx)
            self.near_b = remote(parts.at[self.py, :, b], near.at[1, 0], ssem, rsem, 3, dy)
            self.sum_a = [
                remote(hold.at[0, r], far.at[0, r], ssem, rsem, 4 + i, dy)
                for i, r in enumerate(self.halves)
            ]
            self.sum_b = [
                remote(hold.at[1, r], far.at[1, r], ssem, rsem, 8 + i, dx)
                for i, r in enumerate(self.halves)
            ]
            self.copies = self.far_a + self.far_b + [self.near_a, self.near_b]
            self.copies += self.sum_a + self.sum_b
        else:
            self.peers = [(s, (t + k) % n) for k in range(1, n)]
            self.copies = [
                remote(parts.at[(t - k + n) % n], near.at[k - 1], ssem, rsem, k - 1, (s, (t - k + n) % n))
                for k in range(1, n)
            ]

    def send(self, i):
        if self.n == 4:

            @pl.when(i == 1)
            def _():
                self.near_a.start()

            @pl.when(i == 2)
            def _():
                self.near_b.start()

            @pl.when(i == 3)
            def _():
                for copy_a, copy_b in zip(self.far_a, self.far_b):
                    copy_a.start()
                    copy_b.start()

        else:
            for k, copy in enumerate(self.copies):

                @pl.when(i == k + 1)
                def _(copy=copy):
                    copy.start()

    def relay(self):
        if self.n == 4:
            sides = (self.cols[0], self.py, self.far_a, self.sum_a), (
                self.cols[1], self.px, self.far_b, self.sum_b
            )
            for i, r in enumerate(self.halves):
                for side, (cols, who, came, onward) in enumerate(sides):
                    came[i].wait_recv()
                    self.hold[side, r] = (
                        self.parts[who, r, cols].astype(F32) + self.near[side, 1, r].astype(F32)
                    ).astype(BF)
                    onward[i].start()

    def finish(self, write):
        if self.n == 4:
            for side, (one, two) in enumerate(
                ((self.near_a, self.sum_a), (self.near_b, self.sum_b))
            ):
                one.wait_recv()
                for copy in two:
                    copy.wait_recv()
                write(
                    slice(None),
                    self.cols[side],
                    self.parts[self.t, :, self.cols[side]].astype(F32)
                    + self.near[side, 0].astype(F32)
                    + self.far[side].astype(F32),
                )
        else:
            for copy in self.copies:
                copy.wait_recv()

            @pl.loop(0, self.parts.shape[1] // 16)
            def _(r):
                at = pl.ds(pl.multiple_of(r * 16, 16), 16)
                total = self.parts[self.t, at].astype(F32)
                for k in range(self.n - 1):
                    total = total + self.near[k, at].astype(F32)
                write(at, slice(None), total)

    def drain(self):
        for copy in self.copies:
            copy.wait_send()


def scatter_scratch(n, rows, width):
    if n == 4:
        near, far = (2, 2, rows, width // 2), (2, rows, width // 2)
    else:
        near, far = (n - 1, rows, width), (1, 16, 128)
    return [pltpu.VMEM(near, BF), pltpu.VMEM(far, BF), pltpu.VMEM(far, BF)]


class Ends:
    def __init__(self, chips):
        s, t = lax.axis_index("seq"), lax.axis_index("tp")
        chip, span = s // 2, 2 * chips
        self.gives = (chip == 0) | (chip == chips - 1)
        self.takes = (chip == 1) | (chip == chips - 2)
        self.peers = [((s + 2) % span, t), ((s - 2 + span) % span, t)]
        step = jnp.where(chip == 0, 2, jnp.where(chip == chips - 1, span - 2, 0))
        self.mate = ((s + step) % span, t)


class Chain:
    def __init__(self, chips, heads, flip, fac, local, out, pair, enter, ps, pr, zs, zr, bs, br):
        s, t = lax.axis_index("seq"), lax.axis_index("tp")
        core, chip, span = s % 2, s // 2, 2 * chips
        self.chips, self.heads, self.fac = chips, heads, fac
        self.local, self.out, self.pair, self.enter, self.leave = local, out, pair, enter, local
        self.sems = ps, pr, zs, zr, bs, br
        self.partner = (s + 1 - 2 * core, t)
        above, below = ((s + 2) % span, t), ((s - 2 + span) % span, t)
        self.peers = [self.partner, above, below]
        if flip:
            self.first, self.place, self.ahead = core == 1, chips - 1 - chip, below
        else:
            self.first, self.place, self.ahead = core == 0, chip, above
        self.last = jnp.logical_not(self.first)

    def give(self, p):
        return remote(self.local.at[p], self.pair.at[p], self.sems[0], self.sems[1], p, self.partner)

    def back(self, p):
        return remote(self.enter.at[p], self.out.at[p], self.sems[4], self.sems[5], p, self.partner)

    def onward(self, p):
        return remote(self.leave.at[p], self.enter.at[p], self.sems[2], self.sems[3], p, self.ahead)

    def piece(self, gather, index):
        return gather.source(index // self.heads) * self.heads + index % self.heads

    def open(self, gather, i):
        @pl.when(self.place == 0)
        def _():
            @pl.loop(0, self.heads)
            def _(h):
                self.step(self.piece(gather, i * self.heads + h))

    def tick(self, gather, now):
        total = self.local.shape[0]
        ends = self.place == self.chips - 1
        lag = jnp.minimum(3 * (self.place - 1), total - self.heads)
        index = jnp.where(ends, (self.heads + now) % total, now - lag)
        due = (self.place > 0) & (index >= 0) & (index < total)

        @pl.when(due & (jnp.logical_not(ends) | (now >= total)))
        def _():
            self.step(self.piece(gather, jnp.maximum(index, 0)))

    def planned(self, gather, i, plan):
        block = jnp.int32(0)
        for place, turn, ahead in plan:
            block = jnp.where((self.place == place) & (i == turn), ahead, block)

        @pl.when(block > 0)
        def _():
            @pl.loop(0, self.heads)
            def _(h):
                self.step(self.piece(gather, block * self.heads + h))

    def due(self, gather, i, plan):
        now = self.place > 0
        for place, _, ahead in plan:
            now = now & ((self.place != place) | (i != ahead))

        @pl.when(now)
        def _():
            @pl.loop(0, self.heads)
            def _(h):
                self.step(self.piece(gather, i * self.heads + h))

    def begin(self, p):
        @pl.when(self.first)
        def _():
            self.give(p).start()

            @pl.when(self.place == 0)
            def _():
                self.out[p] = jnp.zeros(self.out.shape[1:], BF)

    def step(self, p):
        @pl.when(self.first)
        def _():
            @pl.when(self.place > 0)
            def _():
                self.back(p).wait_recv()

        @pl.when(self.last)
        def _():
            fac = self.fac[0, lax.axis_index("tp") * self.heads + p % self.heads]
            self.give(p).wait_recv()
            early = self.pair[p].astype(F32)
            chip_sum = early * fac + self.local[p].astype(F32)

            @pl.when(self.place == 0)
            def _():
                self.leave[p] = chip_sum.astype(BF)
                self.out[p] = self.pair[p]

            @pl.when(self.place > 0)
            def _():
                self.onward(p).wait_recv()
                self.back(p).start()
                came = self.enter[p].astype(F32)
                self.leave[p] = (came * (fac * fac) + chip_sum).astype(BF)
                self.out[p] = (came * fac + early).astype(BF)

            @pl.when(self.place < self.chips - 1)
            def _():
                self.onward(p).start()

    def drain(self, p):
        @pl.when(self.first)
        def _():
            self.give(p).wait_send()

        @pl.when(self.last)
        def _():
            @pl.when(self.place > 0)
            def _():
                self.back(p).wait_send()

            @pl.when(self.place < self.chips - 1)
            def _():
                self.onward(p).wait_send()


def chain_scratch(pieces):
    dma = pltpu.SemaphoreType.DMA
    return [pltpu.VMEM((pieces, DK, DV), BF)] * 2 + [dma((pieces,))] * 6


def dot(a, b, ca=1, cb=0):
    return lax.dot_general(a, b, (((ca,), (cb,)), ((), ())), preferred_element_type=F32)


def turn(v, cos, sin):
    lo, hi = v[:, : DK // 2], v[:, DK // 2 :]
    return jnp.concatenate([lo * cos - hi * sin, hi * cos + lo * sin], 1)


def turn_back(g, cos, sin):
    lo, hi = g[:, : DK // 2], g[:, DK // 2 :]
    return jnp.concatenate([lo * cos + hi * sin, hi * cos - lo * sin], 1)


def row_stats(v):
    center = v - jnp.mean(v, -1, keepdims=True)
    return center, lax.rsqrt(jnp.mean(center * center, -1, keepdims=True) + EPS)


def norm_pull(grad, hat, inv, gain):
    g = grad * gain
    return (g - jnp.mean(g, -1, keepdims=True) - hat * jnp.mean(g * hat, -1, keepdims=True)) * inv


def norm_of(m):
    center = m - jnp.mean(m, -1, keepdims=True)
    inv = lax.rsqrt(jnp.mean(center * center, -1, keepdims=True) + EPS)
    return center * inv, inv


class LineSums:
    def __init__(self, chips, lo, hi, wide, deep, kinds, refs, swap=False):
        s, t = lax.axis_index("seq"), lax.axis_index("tp")
        self.core, self.chip, self.chips, self.lo, self.hi = s % 2, s // 2, chips, lo, hi
        self.wide, self.deep, self.kinds = wide, deep, kinds
        (
            self.xs, self.ys, self.buf, self.out,
            self.xsem, self.ysem, self.psx, self.prx, self.psy, self.pry, self.ssem, self.rsem,
        ) = refs
        self.units = len(deep)
        self.swap = swap
        self.tokens = self.ys.shape[1] // 2
        self.cut = self.xs.shape[3]
        self.spans = [self.places(parts) for parts in wide], [self.places(parts) for parts in deep]
        span = 2 * chips
        self.partner = (s + 1 - 2 * self.core, t)
        self.above = ((s + 2) % span, t)
        self.below = ((s - 2 + span) % span, t)
        self.peers = [self.partner, self.above, self.below]

    def cols(self, j, core):
        return pl.ds(pl.multiple_of((2 * j + core) * self.cut, self.cut), self.cut)

    def places(self, parts):
        found, start = [], 0
        for part in parts:
            found.append((start, part.shape[0]))
            start += part.shape[0]
        assert start == self.tokens
        return found

    def wide_own(self, kind, j):
        return [
            pltpu.make_async_copy(
                part.at[:, self.cols(j, self.core)],
                self.xs.at[kind, j, pl.ds(start, size)],
                self.xsem.at[kind, j, i],
            )
            for i, (part, (start, size)) in enumerate(zip(self.wide[kind], self.spans[0][kind]))
        ]

    def wide_give(self, kind, j):
        return [
            remote(
                part.at[:, self.cols(j, 1 - self.core)],
                self.xs.at[kind, j, pl.ds(self.tokens + start, size)],
                self.psx.at[kind, j],
                self.prx.at[kind, j],
                i,
                self.partner,
            )
            for i, (part, (start, size)) in enumerate(zip(self.wide[kind], self.spans[0][kind]))
        ]

    def deep_own(self, u):
        return [
            pltpu.make_async_copy(
                part, self.ys.at[u, pl.ds(start, size)], self.ysem.at[u, i]
            )
            for i, (part, (start, size)) in enumerate(zip(self.deep[u], self.spans[1][u]))
        ]

    def deep_give(self, u):
        return [
            remote(
                part,
                self.ys.at[u, pl.ds(self.tokens + start, size)],
                self.psy.at[u],
                self.pry.at[u],
                i,
                self.partner,
            )
            for i, (part, (start, size)) in enumerate(zip(self.deep[u], self.spans[1][u]))
        ]

    def adds(self):
        return (self.chip >= self.lo) & (self.chip <= self.hi)

    def share(self, u):
        @pl.when(self.adds())
        def _():
            if self.kinds[u] not in self.kinds[:u]:
                for j in range(self.chips):
                    for copy in self.wide_give(self.kinds[u], j) + self.wide_own(self.kinds[u], j):
                        copy.start()
            for copy in self.deep_give(u) + self.deep_own(u):
                copy.start()

    def ready(self, u):
        @pl.when(self.adds())
        def _():
            own, given = self.deep_own(u), self.deep_give(u)
            if self.kinds[u] not in self.kinds[:u]:
                for j in range(self.chips):
                    own += self.wide_own(self.kinds[u], j)
                    given += self.wide_give(self.kinds[u], j)
            for copy in own:
                copy.wait()
            for copy in given:
                copy.wait_recv()

    def up(self, u, j):
        return remote(
            self.buf.at[u, j], self.buf.at[u, j], self.ssem.at[u], self.rsem.at[u], j, self.above
        )

    def down(self, u, j):
        slot = jnp.where(j == self.chip - 1, self.chips, j)
        return pltpu.make_async_remote_copy(
            src_ref=self.buf.at[u, j],
            dst_ref=self.buf.at[u, slot],
            send_sem=self.ssem.at[u, j],
            recv_sem=self.rsem.at[u, slot],
            device_id=self.below,
            device_id_type=MESH,
        )

    def arrived(self, u, slot):
        remote(
            self.buf.at[u, slot], self.buf.at[u, slot], self.ssem.at[u], self.rsem.at[u], slot,
            self.above,
        ).wait_recv()
        return self.buf[u, slot].astype(F32)

    def product(self, u, j):
        kind = 0
        for w in range(self.units):
            if self.kinds[w]:
                kind = kind + jnp.where(u == w, self.kinds[w], 0)
        if self.swap:
            return dot(self.ys[u], self.xs[kind, j], 0, 0)
        return dot(self.xs[kind, j], self.ys[u], 0, 0)

    def order(self, k):
        rights = self.chips - 1 - self.chip
        return jnp.where(
            self.chip < self.chips // 2,
            jnp.where(k < rights, self.chips - 1 - k, k - rights),
            jnp.where(k < self.chip, k, self.chips - 1 - (k - self.chip)),
        )

    def step(self, u, k):
        chip = self.chip
        j = self.order(k)

        @pl.when(self.adds())
        def _():
            total = self.product(u, j)

            @pl.when(((j > chip) & (chip == self.lo)) | ((j < chip) & (chip == self.hi)))
            def _():
                self.buf[u, j] = total.astype(BF)

            @pl.when(((j > chip) & (chip > self.lo)) | ((j < chip) & (chip < self.hi)))
            def _():
                self.buf[u, j] = (total + self.arrived(u, j)).astype(BF)

            @pl.when(j > chip)
            def _():
                self.up(u, j).start()

            @pl.when(j < chip)
            def _():
                self.down(u, j).start()

    def finish(self, u):
        chip = self.chip

        @pl.when(self.adds())
        def _():
            self.out[0] = self.product(u, chip)

        @pl.when((chip < self.lo) | (chip > self.hi))
        def _():
            self.out[0] = jnp.zeros(self.out.shape[1:], F32)

        @pl.when(chip > self.lo)
        def _():
            self.out[0] += self.arrived(u, chip)

        @pl.when(chip < self.hi)
        def _():
            self.out[0] += self.arrived(u, self.chips)

    def drain(self):
        @pl.when(self.adds())
        def _():
            @pl.loop(0, self.units)
            def _(u):
                @pl.loop(0, self.chips)
                def _(j):
                    @pl.when(j > self.chip)
                    def _():
                        self.up(u, j).wait_send()

                    @pl.when(j < self.chip)
                    def _():
                        self.down(u, j).wait_send()

            for u in range(self.units):
                for copy in self.deep_give(u):
                    copy.wait_send()
            for kind in range(max(self.kinds) + 1):
                for j in range(self.chips):
                    for copy in self.wide_give(kind, j):
                        copy.wait_send()


def line_scratch(chips, units, kinds, tokens, cut, width, swap=False):
    dma = pltpu.SemaphoreType.DMA
    block = (width, cut) if swap else (cut, width)
    return [
        pltpu.VMEM((kinds, chips, 2 * tokens, cut), BF),
        pltpu.VMEM((units, 2 * tokens, width), BF),
        pltpu.VMEM((units, chips + 1) + block, BF),
        pltpu.VMEM((1,) + block, F32),
        dma((kinds, chips, 2)),
        dma((units, 2)),
        dma((kinds, chips, 2)),
        dma((kinds, chips, 2)),
        dma((units, 2)),
        dma((units, 2)),
        dma((units, chips + 1)),
        dma((units, chips + 1)),
    ]


def mixer_kernel(n, chips, heads, *refs):
    (
        fac, raw, og, wk_h, wv_h, wq_h, ws_h, wo_h, gain, bias, freq,
        x_o, og_o, q_o, k_o, v_o, sp_o, mx_o, prior_o, gated_o, attn, decay, qfac, kfac, cos, sin,
        x_all, og_all, q, k, v, sp, mx, prior, gated, x, wk, wv, wq, ws, wo, acc, parts, local,
    ) = refs[:44]
    near, far, hold = refs[44:47]
    chain_refs = refs[47:55]
    wsem, gs, gr, os, orr, ss, sr, es, er, osem, bsem = refs[55:]
    rows = raw.shape[0]
    gather = Gather(n, x, x_all, gs, gr)
    gather_og = Gather(n, og, og_all, os, orr)
    ends = Ends(chips)
    hand_own = remote(og, og_o.at[n], es, er, 0, ends.mate)

    def hand(i):
        return remote(og_all.at[gather.source(i)], og_o.at[n + i], es, er, i, ends.mate)

    scatter = Scatter(n, parts, near, far, hold, ss, sr)
    chain = Chain(chips, heads, False, fac, local, prior, *chain_refs)
    loads = [
        pltpu.make_async_copy(a, w, wsem.at[i])
        for i, (a, w) in enumerate(((wk_h, wk), (wv_h, wv), (wq_h, wq), (ws_h, ws), (wo_h, wo)))
    ]
    for load in loads:
        load.start()
    slab = 16
    plan = ((1, 1, 1), (1, 3, 2)) if n == 4 else ()

    @pl.loop(0, rows // slab)
    def _(r):
        here = pl.ds(pl.multiple_of(r * slab, slab), slab)
        center, inv = row_stats(raw[here].astype(F32))
        x[here] = (center * inv * gain[...] + bias[...]).astype(BF)

    greet(gather.peers + chain.peers)
    gather.start()
    place = lax.broadcasted_iota(jnp.int32, (rows, 1), 0).astype(F32)
    angles = (lax.axis_index("seq").astype(F32) * rows + place) * freq[...]
    cos[...] = jnp.cos(angles)
    sin[...] = jnp.sin(angles)
    lag = place - lax.broadcasted_iota(jnp.int32, (rows, rows), 1).astype(F32)
    for h in range(heads):
        rate = fac[1, lax.axis_index("tp") * heads + h]
        decay[h] = jnp.where(lag >= 0, jnp.exp(jnp.maximum(lag, 0.0) * rate), 0.0)
        qfac[h] = jnp.exp((place + 1.0) * rate)
        kfac[h] = jnp.exp((rows - 1.0 - place) * rate)

    @pl.when(ends.gives)
    def _():
        hand_own.start()

    me = gather.source(0)
    x_all[me] = x[...]
    og_all[me] = og[...]
    for load in loads[:2]:
        load.wait()

    @pl.loop(0, n)
    def _(i):
        j = gather.source(i)
        gather.arrive(i)
        at = pl.ds(pl.multiple_of(j * rows, rows), rows)
        acc[:, : heads * DK] = dot(x_all[j], wk[...])

        v[at] = dot(x_all[j], wv[...]).astype(BF)
        for h in range(heads):
            vc = slice(h * DV, (h + 1) * DV)
            kc = slice(h * DK, (h + 1) * DK)
            key = turn(acc[:, kc], cos[...], sin[...]).astype(BF)
            k[at, kc] = key
            key_dec = (key.astype(F32) * kfac[h]).astype(BF)
            p = j * heads + h
            local[p] = dot(key_dec, v[at, vc], 0, 0).astype(BF)
            chain.begin(p)

        chain.open(gather, i)

        @pl.when(i == 0)
        def _():
            gather.relays()
            gather_og.start()

    puts = [
        pltpu.make_async_copy(a, b, osem.at[i])
        for i, (a, b) in enumerate(
            ((x_all, x_o), (k, k_o), (v, v_o), (q, q_o), (sp, sp_o), (og_all, og_o.at[pl.ds(0, n)]))
        )
    ]
    for put in puts[:3]:
        put.start()
    for load in loads[2:]:
        load.wait()

    @pl.loop(0, n)
    def _(i):
        j = gather.source(i)
        at = pl.ds(pl.multiple_of(j * rows, rows), rows)
        acc[:, : heads * DK] = dot(x_all[j], wq[...])
        for h in range(heads):
            kc = slice(h * DK, (h + 1) * DK)
            vc = slice(h * DV, (h + 1) * DV)
            query = turn(acc[:, kc], cos[...], sin[...]).astype(BF)
            q[at, kc] = query
            scores = (dot(query, k[at, kc], 1, 1) * decay[h]).astype(BF)
            mx[at, vc] = dot(scores, v[at, vc])
            sp[at, vc] = dot(x_all[j], ws[:, vc])
        chain.planned(gather, i, plan)

    for put in puts[3:5]:
        put.start()
    gather_og.relays()

    def blocks(j):
        at = pl.ds(pl.multiple_of(j * rows, rows), rows)
        of = pl.ds(j * heads, heads)
        return [
            pltpu.make_async_copy(mx.at[at], mx_o.at[at], bsem.at[0, j]),
            pltpu.make_async_copy(gated.at[at], gated_o.at[at], bsem.at[1, j]),
            pltpu.make_async_copy(prior.at[of], prior_o.at[of], bsem.at[2, j]),
        ]


    @pl.loop(0, n)
    def _(step):
        i = (step + 1) % n
        j = gather.source(i)
        chain.due(gather, i, plan)
        gather_og.arrive(i)

        @pl.when(ends.gives & (chain.place > 0) & (i > 0) & (i < n - 1))
        def _():
            hand(i).start()

        at = pl.ds(pl.multiple_of(j * rows, rows), rows)
        for h in range(heads):
            vc = slice(h * DV, (h + 1) * DV)
            kc = slice(h * DK, (h + 1) * DK)
            p = j * heads + h
            query_dec = (q[at, kc].astype(F32) * qfac[h]).astype(BF)
            mx[at, vc] += dot(query_dec, prior[p])
            pre = sp[at, vc]
            gated[at, vc] = (pre * jax.nn.sigmoid(pre) * norm_of(mx[at, vc])[0]).astype(BF)
        parts[j] = dot(gated[at], wo[...]).astype(BF)
        scatter.send(i)

        @pl.when(ends.gives & (chain.place == 0) & (step == n - 2))
        def _():
            @pl.loop(1, n - 1)
            def _(c):
                hand(c).start()

        for put in blocks(j):
            put.start()

    puts[5].start()
    scatter.relay()

    def write(at, cols, total):
        attn[at, cols] = total

    scatter.finish(write)
    gather.drain()
    gather_og.drain()
    for put in puts:
        put.wait()

    @pl.loop(0, n)
    def _(j):
        for put in blocks(j):
            put.wait()

    @pl.when(ends.gives)
    def _():
        hand_own.wait_send()

        @pl.loop(1, n - 1)
        def _(i):
            hand(i).wait_send()

    @pl.when(ends.takes)
    def _():
        @pl.loop(0, n - 1)
        def _(i):
            hand(i).wait_recv()

    scatter.drain()

    @pl.loop(0, n * heads)
    def _(p):
        chain.drain(p)


def mixer(fac, x, og, wk, wv, wq, ws, wo, gain, bias, freq, cid):
    n = lax.axis_size("tp")
    chips = lax.axis_size("seq") // 2
    rows, model = x.shape
    heads = wk.shape[1] // DK
    pieces = n * heads
    total = n * rows
    dma = pltpu.SemaphoreType.DMA
    sems = max(10, n - 1)
    vmem = pl.BlockSpec(memory_space=pltpu.VMEM)
    hbm = pl.BlockSpec(memory_space=pl.ANY)
    shape = jax.ShapeDtypeStruct
    return pl.pallas_call(
        functools.partial(mixer_kernel, n, chips, heads),
        out_shape=(
            shape((n, rows, model), BF),
            shape((2 * n - 1, rows, model), BF),
            shape((total, heads * DK), BF),
            shape((total, heads * DK), BF),
            shape((total, heads * DV), BF),
            shape((total, heads * DV), F32),
            shape((total, heads * DV), F32),
            shape((pieces, DK, DV), BF),
            shape((total, heads * DV), BF),
            shape((rows, model), F32),
            shape((heads, rows, rows), F32),
            shape((heads, rows, 1), F32),
            shape((heads, rows, 1), F32),
            shape((rows, DK // 2), F32),
            shape((rows, DK // 2), F32),
        ),
        in_specs=[pl.BlockSpec(memory_space=pltpu.SMEM), vmem, vmem] + [hbm] * 5 + [vmem] * 3,
        out_specs=(hbm,) * 9 + (vmem,) * 6,
        scratch_shapes=[
            pltpu.VMEM((n, rows, model), BF),
            pltpu.VMEM((n, rows, model), BF),
            pltpu.VMEM((total, heads * DK), BF),
            pltpu.VMEM((total, heads * DK), BF),
            pltpu.VMEM((total, heads * DV), BF),
            pltpu.VMEM((total, heads * DV), F32),
            pltpu.VMEM((total, heads * DV), F32),
            pltpu.VMEM((pieces, DK, DV), BF),
            pltpu.VMEM((total, heads * DV), BF),
            pltpu.VMEM((rows, model), BF),
        ]
        + [pltpu.VMEM(w.shape, BF) for w in (wk, wv, wq, ws, wo)]
        + [
            pltpu.VMEM((rows, heads * DK), F32),
            pltpu.VMEM((n, rows, model), BF),
            pltpu.VMEM((pieces, DK, DV), BF),
        ]
        + scatter_scratch(n, rows, model)
        + chain_scratch(pieces)
        + [dma((5,))]
        + [dma((sems,))] * 6
        + [dma((n - 1,)), dma((n - 1,)), dma((6,)), dma((3, n))],
        compiler_params=params(cid),
        name="mixer",
    )(fac, x, og, wk, wv, wq, ws, wo, gain, bias, freq)


GELU_C = 0.7978845608028654
GELU_A = 0.044715


def gelu_of(g):
    square = g * g
    th = jnp.tanh(GELU_C * (g + GELU_A * (square * g)))
    half = 0.5 * (1.0 + th)
    slope = half + 0.5 * g * (1.0 - th * th) * (GELU_C * (1.0 + 3.0 * GELU_A * square))
    return g * half, slope


def mlp_kernel(n, chips, *refs):
    (
        raw, attn, cot, gain, bias, og_h, wg_h, wu_h, wd_h,
        x_o, hidden_o, gate_o, upper_o, mlp_o, res_grad, res_low, vec, gate_late, up_late,
        og_all, x, grad_two, x_all, hidden, gate_low, upper_low, mlp_parts, wg, wu, wd, hg, acc_g, acc_u, acc, parts, near, far, hold,
        wsem, gs, gr, ss, sr, es, er, osem, bsem,
    ) = refs
    rows = raw.shape[0]
    slab = 16
    gather = Gather(n, x, x_all, gs, gr)
    scatter = Scatter(n, parts, near, far, hold, ss, sr)
    ends = Ends(chips)
    loads = [
        pltpu.make_async_copy(a, w, wsem.at[i])
        for i, (a, w) in enumerate(((wd_h, wd), (wg_h, wg), (wu_h, wu)))
    ]
    loads.append(pltpu.make_async_copy(og_h, og_all, wsem.at[3]))
    for load in [loads[0], loads[3], loads[1], loads[2]]:
        load.start()
    @pl.loop(0, rows // slab)
    def _(r):
        here = pl.ds(pl.multiple_of(r * slab, slab), slab)
        center, inv = row_stats(raw[here].astype(F32) + attn[here])
        x[here] = (center * inv * gain[...] + bias[...]).astype(BF)

    greet(gather.peers + ends.peers)
    gather.start()
    me = gather.source(0)

    def hand(i):
        j = gather.source(i)
        return remote(x_all.at[j], x_all.at[n + i], es, er, i, ends.mate)

    first = remote(x, x_all.at[n], es, er, 0, ends.mate)

    @pl.when(ends.gives)
    def _():
        first.start()

    x_all[me] = x[...]
    loads[0].wait()
    loads[3].wait()
    pair = 2 * rows

    @pl.loop(0, n // 2)
    def _(c):
        two = pl.ds(pl.multiple_of(2 * c, 2), 2)
        at = pl.ds(pl.multiple_of(c * pair, pair), pair)
        hg[at] = dot(og_all[two].reshape(pair, x.shape[1]), wd[...], 1, 1)

    gather.relays()
    loads[1].wait()
    loads[2].wait()

    def units(block, back_at, extra):
        start = pl.multiple_of(block * rows, rows)
        acc_g[...] = dot(x_all[block], wg[...])
        acc_u[...] = dot(x_all[block], wu[...])
        if extra:
            gate_late[...] = acc_g[...]
            up_late[...] = acc_u[...]

        @pl.loop(0, rows // slab)
        def _(r):
            here = pl.ds(pl.multiple_of(r * slab, slab), slab)
            there = pl.ds(pl.multiple_of(start + r * slab, slab), slab)
            g, u = acc_g[here], acc_u[here]
            gelu, slope = gelu_of(g)
            hidden[there] = (gelu * u).astype(BF)
            back = hg[pl.ds(pl.multiple_of(back_at + r * slab, slab), slab)]
            gate_low[there] = (back * u * slope).astype(BF)
            upper_low[there] = (back * gelu).astype(BF)

    @pl.loop(0, n)
    def _(turn):
        i = jnp.where(turn == 2, 3, jnp.where(turn == 3, 2, turn)) if n == 4 else turn
        j = gather.source(i)
        gather.arrive(i)

        @pl.when(ends.gives & (i > 0))
        def _():
            hand(i).start()

        units(j, j * rows, False)
        at = pl.ds(pl.multiple_of(j * rows, rows), rows)
        acc[...] = dot(gate_low[at], wg[...], 1, 1)
        parts[j] = (acc[...] + dot(upper_low[at], wu[...], 1, 1)).astype(BF)
        scatter.send(i)

    whole = pl.ds(0, n * rows)
    puts = [
        pltpu.make_async_copy(a, b, osem.at[i])
        for i, (a, b) in enumerate(
            (
                (x_all.at[pl.ds(0, n)], x_o.at[pl.ds(0, n)]),
                (hidden.at[whole], hidden_o.at[whole]),
                (gate_low.at[whole], gate_o.at[whole]),
                (upper_low.at[whole], upper_o.at[whole]),
                (mlp_parts, mlp_o),
            )
        )
    ]
    for put in puts[:4]:
        put.start()

    def blocks(i):
        at = pl.ds(pl.multiple_of((n + i) * rows, rows), rows)
        return [
            pltpu.make_async_copy(x_all.at[n + i], x_o.at[n + i], bsem.at[0, i]),
            pltpu.make_async_copy(hidden.at[at], hidden_o.at[at], bsem.at[1, i]),
        ]

    def late_blocks(i):
        at = pl.ds(pl.multiple_of((n + i) * rows, rows), rows)
        return [
            pltpu.make_async_copy(gate_low.at[at], gate_o.at[at], bsem.at[2, i]),
            pltpu.make_async_copy(upper_low.at[at], upper_o.at[at], bsem.at[3, i]),
        ]

    def extra(i):
        @pl.when(ends.takes)
        def _():
            hg[pl.ds(0, rows)] = dot(og_all[n + jnp.minimum(i, n - 2)], wd[...], 1, 1)
            hand(i).wait_recv()
            units(n + i, 0, True)
            for put in blocks(i):
                put.start()

            @pl.when(i < n - 1)
            def _():
                for put in late_blocks(i):
                    put.start()

    @pl.loop(0, n // 2)
    def _(i):
        extra(i)

    scatter.relay()

    @pl.loop(0, n // 2)
    def _(c):
        two = pl.ds(pl.multiple_of(2 * c, 2), 2)
        at = pl.ds(pl.multiple_of(c * pair, pair), pair)
        mlp_parts[two] = dot(hidden[at], wd[...]).astype(BF).reshape(2, rows, x.shape[1])

    puts[4].start()

    def write(at, cols, total):
        grad_two[at, cols] = total

    scatter.finish(write)
    vec[...] = jnp.zeros_like(vec)

    @pl.loop(0, rows // slab)
    def _(r):
        here = pl.ds(pl.multiple_of(r * slab, slab), slab)
        center, inv = row_stats(raw[here].astype(F32) + attn[here])
        hat, grad = center * inv, grad_two[here]
        total = cot[here].astype(F32) + norm_pull(grad, hat, inv, gain[...])
        res_grad[here] = total
        res_low[here] = total.astype(BF)
        vec[2:3] += jnp.sum(grad * hat, 0, keepdims=True)
        vec[3:4] += jnp.sum(grad, 0, keepdims=True)

    @pl.loop(n // 2, n)
    def _(i):
        extra(i)

    @pl.when(ends.takes)
    def _():
        @pl.loop(0, n)
        def _(i):
            for put in blocks(i):
                put.wait()

        @pl.loop(0, n - 1)
        def _(i):
            for put in late_blocks(i):
                put.wait()

    for put in puts:
        put.wait()

    gather.drain()
    scatter.drain()

    @pl.when(ends.gives)
    def _():
        first.wait_send()

        @pl.loop(1, n)
        def _(i):
            hand(i).wait_send()


def mlp(raw, attn, cot, gain, bias, og_all, wg, wu, wd, cid):
    n = lax.axis_size("tp")
    chips = lax.axis_size("seq") // 2
    rows, model = raw.shape
    width = wg.shape[1]
    total = n * rows
    dma = pltpu.SemaphoreType.DMA
    sems = max(10, n - 1)
    vmem = pl.BlockSpec(memory_space=pltpu.VMEM)
    hbm = pl.BlockSpec(memory_space=pl.ANY)
    shape = jax.ShapeDtypeStruct
    return pl.pallas_call(
        functools.partial(mlp_kernel, n, chips),
        out_shape=(
            shape((2 * n, rows, model), BF),
            shape((2 * total, width), BF),
            shape((2 * total - rows, width), BF),
            shape((2 * total - rows, width), BF),
            shape((n, rows, model), BF),
            shape((rows, model), F32),
            shape((rows, model), BF),
            shape((8, model), F32),
            shape((rows, width), F32),
            shape((rows, width), F32),
        ),
        in_specs=[vmem] * 5 + [hbm] * 4,
        out_specs=(hbm,) * 5 + (vmem,) * 5,
        scratch_shapes=[
            pltpu.VMEM(og_all.shape, BF),
            pltpu.VMEM((rows, model), BF),
            pltpu.VMEM((rows, model), F32),
            pltpu.VMEM((2 * n, rows, model), BF),
            pltpu.VMEM((2 * total, width), BF),
            pltpu.VMEM((2 * total, width), BF),
            pltpu.VMEM((2 * total, width), BF),
            pltpu.VMEM((n, rows, model), BF),
        ]
        + [pltpu.VMEM(w.shape, BF) for w in (wg, wu, wd)]
        + [
            pltpu.VMEM((total, width), F32),
            pltpu.VMEM((rows, width), F32),
            pltpu.VMEM((rows, width), F32),
            pltpu.VMEM((rows, model), F32),
            pltpu.VMEM((n, rows, model), BF),
        ]
        + scatter_scratch(n, rows, model)
        + [dma((4,))]
        + [dma((sems,))] * 4
        + [dma((n,)), dma((n,)), dma((5,)), dma((4, n))],
        compiler_params=params(cid),
        name="mlp",
    )(raw, attn, cot, gain, bias, og_all, wg, wu, wd)


def mixer_back_kernel(n, chips, heads, *refs):
    (
        fac, res, wo_h, wq_h, wk_h, wv_h, ws_h, q_h, k_h, v_h, sp_h, mx_h, prior_h, mlp_h, decay, qfac, kfac, cos, sin, og_h, wd_h, gate_late, up_late,
        res_o, swish_o, value_o, qk_o, parts_o, mlp_out, og_late, gate_low, upper_low,
        q, k, v, sp, mx, prior, mlp_parts, res_all, swish_low, value_low, qk_low, wo, wq, wk, wv, ws, mixed_low, sums, parts, local, later, key_part, value_part,
    ) = refs[:55]
    mlp_near, mlp_far, mlp_hold = refs[55:58]
    chain_refs = refs[58:66]
    wsem, gs, gr, ms, mr, es, er, isem, lsem, osem, bsem = refs[66:]
    rows = res.shape[0]
    gather = Gather(n, res, res_all, gs, gr)
    scatter_mlp = Scatter(n, mlp_parts, mlp_near, mlp_far, mlp_hold, ms, mr)
    chain = Chain(chips, heads, True, fac, local, later, *chain_refs)
    ends = Ends(chips)
    late = remote(og_h.at[gather.source(n - 1)], og_late, es, er, 0, ends.mate)
    load_late = pltpu.make_async_copy(wd_h, wo, wsem.at[5])
    loads = [
        pltpu.make_async_copy(a, w, wsem.at[i])
        for i, (a, w) in enumerate(((wo_h, wo), (ws_h, ws), (wq_h, wq), (wk_h, wk), (wv_h, wv)))
    ]
    def entering(i):
        j = gather.source(i)
        at = pl.ds(pl.multiple_of(j * rows, rows), rows)
        return [
            pltpu.make_async_copy(a.at[at], b.at[at], isem.at[w, j])
            for w, (a, b) in enumerate(((mx_h, mx), (sp_h, sp), (q_h, q)))
        ]

    loads += [
        pltpu.make_async_copy(a, b, lsem.at[i])
        for i, (a, b) in enumerate(((k_h, k), (v_h, v), (prior_h, prior), (mlp_h, mlp_parts)))
    ]
    loads[0].start()
    for i in range(n):
        for load in entering(i):
            load.start()
    for load in loads[1:]:
        load.start()
    greet(gather.peers + chain.peers)
    gather.start()
    me = gather.source(0)
    res_all[me] = res[...]
    loads[0].wait()

    @pl.loop(0, n)
    def _(i):
        j = gather.source(i)
        gather.arrive(i)
        at = pl.ds(pl.multiple_of(j * rows, rows), rows)
        for load in entering(i):
            load.wait()
        sums[j, :, : heads * DV] = dot(res_all[j], wo[...], 1, 1).astype(sums.dtype)

        for h in range(heads):
            vc = slice(h * DV, (h + 1) * DV)
            kc = slice(h * DK, (h + 1) * DK)
            back = sums[j, :, vc].astype(F32)
            normed, inv = norm_of(mx[at, vc])
            pre = sp[at, vc]
            sig = jax.nn.sigmoid(pre)
            swish_low[at, vc] = (back * normed * (sig * (1.0 + pre * (1.0 - sig)))).astype(BF)
            g = back * (pre * sig)
            g = inv * (
                g
                - jnp.mean(g, -1, keepdims=True)
                - normed * jnp.mean(g * normed, -1, keepdims=True)
            )
            g = g.astype(BF)
            mixed_low[at, vc] = g
            query_dec = (q[at, kc].astype(F32) * qfac[h]).astype(BF)
            p = j * heads + h
            local[p] = dot(query_dec, g, 0, 0).astype(BF)
            chain.begin(p)

        chain.open(gather, i)

        @pl.when(i == 0)
        def _():
            gather.relays()

    puts = [
        pltpu.make_async_copy(res_all, res_o, osem.at[0]),
        pltpu.make_async_copy(swish_low, swish_o, osem.at[1]),
    ]
    for put in puts:
        put.start()

    def leaving(j):
        at = pl.ds(pl.multiple_of(j * rows, rows), rows)
        return [
            pltpu.make_async_copy(value_low.at[at], value_o.at[at], bsem.at[0, j]),
            pltpu.make_async_copy(qk_low.at[at], qk_o.at[at], bsem.at[1, j]),
            pltpu.make_async_copy(parts.at[j], parts_o.at[j], bsem.at[2, j]),
        ]

    for load in loads[1:]:
        load.wait()
    for i in range(1, n):
        scatter_mlp.send(i)

    @pl.when(ends.gives)
    def _():
        late.start()

    @pl.when(ends.takes)
    def _():
        load_late.start()

    @pl.loop(0, n)
    def _(i):
        j = gather.source(i)
        at = pl.ds(pl.multiple_of(j * rows, rows), rows)
        for h in range(heads):
            vc = slice(h * DV, (h + 1) * DV)
            kc = slice(h * DK, (h + 1) * DK)
            g, query, key = mixed_low[at, vc], q[at, kc], k[at, kc]
            chain.tick(gather, i * heads + h)
            raw_low = (dot(g, v[at, vc], 1, 1) * decay[h]).astype(BF)
            query_back = dot(raw_low, key) + dot(g, prior[j * heads + h], 1, 1) * qfac[h]
            qk_low[at, kc] = turn_back(query_back, cos[...], sin[...]).astype(BF)
            scores = (dot(query, key, 1, 1) * decay[h]).astype(BF)
            key_part[at, kc] = dot(raw_low, query, 0, 0).astype(key_part.dtype)
            value_part[at, vc] = dot(scores, g, 0, 0).astype(value_part.dtype)
        sums[j] = dot(swish_low[at], ws[...], 1, 1).astype(sums.dtype)
        sums[j] += dot(qk_low[at, : heads * DK], wq[...], 1, 1).astype(sums.dtype)

    scatter_mlp.relay()

    @pl.loop(0, n)
    def _(step):
        i = (step + 1) % n
        j = gather.source(i)
        at = pl.ds(pl.multiple_of(j * rows, rows), rows)
        for h in range(heads):
            vc = slice(h * DV, (h + 1) * DV)
            kc = slice(h * DK, (h + 1) * DK)
            chain.tick(gather, (n + step) * heads + h)
            after = later[j * heads + h]
            key_dec = (k[at, kc].astype(F32) * kfac[h]).astype(BF)
            key_back = key_part[at, kc].astype(F32) + dot(v[at, vc], after, 1, 1) * kfac[h]
            qk_low[at, slice((heads + h) * DK, (heads + h + 1) * DK)] = turn_back(
                key_back, cos[...], sin[...]
            ).astype(BF)
            value_low[at, vc] = (value_part[at, vc] + dot(key_dec, after)).astype(BF)
        sums[j] += dot(value_low[at], wv[...], 1, 1).astype(sums.dtype)
        parts[j] = (sums[j].astype(F32) + dot(qk_low[at, heads * DK :], wk[...], 1, 1)).astype(BF)
        for put in leaving(j):
            put.start()

    @pl.when(ends.takes)
    def _():
        width = gate_late.shape[1]
        load_late.wait()
        late.wait_recv()
        sums[0, :, :width] = dot(og_late[...], wo[...], 1, 1).astype(sums.dtype)
        slab = 16

        @pl.loop(0, rows // slab)
        def _(r):
            here = pl.ds(pl.multiple_of(r * slab, slab), slab)
            gelu, slope = gelu_of(gate_late[here])
            back = sums[0, here, :width].astype(F32)
            gate_low[here] = (back * up_late[here] * slope).astype(BF)
            upper_low[here] = (back * gelu).astype(BF)

    def write_mlp(at, cols, total):
        mlp_out[at, cols] = total

    scatter_mlp.finish(write_mlp)
    gather.drain()
    scatter_mlp.drain()

    @pl.when(ends.gives)
    def _():
        late.wait_send()

    for put in puts:
        put.wait()

    @pl.loop(0, n)
    def _(j):
        for put in leaving(j):
            put.wait()

    @pl.loop(0, n * heads)
    def _(p):
        chain.drain(p)


def mixer_back(fac, res, wo, wq, wk, wv, ws, q, k, v, sp, mx, prior, mlp_parts, decay, qfac, kfac, cos, sin, og_all, wd, gate_late, up_late, cid):
    n = lax.axis_size("tp")
    chips = lax.axis_size("seq") // 2
    rows, model = res.shape
    heads = q.shape[1] // DK
    pieces = n * heads
    total = n * rows
    keep = F32 if n <= 4 else BF
    dma = pltpu.SemaphoreType.DMA
    sems = max(10, n - 1)
    vmem = pl.BlockSpec(memory_space=pltpu.VMEM)
    hbm = pl.BlockSpec(memory_space=pl.ANY)
    shape = jax.ShapeDtypeStruct
    return pl.pallas_call(
        functools.partial(mixer_back_kernel, n, chips, heads),
        out_shape=(
            shape((n, rows, model), BF),
            shape((total, heads * DV), BF),
            shape((total, heads * DV), BF),
            shape((total, 2 * heads * DK), BF),
            shape((n, rows, model), BF),
            shape((rows, model), F32),
            shape((rows, model), BF),
            shape(gate_late.shape, BF),
            shape(gate_late.shape, BF),
        ),
        in_specs=[pl.BlockSpec(memory_space=pltpu.SMEM), vmem] + [hbm] * 12 + [vmem] * 5 + [hbm, hbm, vmem, vmem],
        out_specs=(hbm,) * 5 + (vmem,) * 4,
        scratch_shapes=[pltpu.VMEM(a.shape, a.dtype) for a in (q, k, v, sp, mx, prior, mlp_parts)]
        + [
            pltpu.VMEM((n, rows, model), BF),
            pltpu.VMEM((total, heads * DV), BF),
            pltpu.VMEM((total, heads * DV), BF),
            pltpu.VMEM((total, 2 * heads * DK), BF),
        ]
        + [pltpu.VMEM(w.shape, BF) for w in (wo, wq, wk, wv, ws)]
        + [
            pltpu.VMEM((total, heads * DV), BF),
            pltpu.VMEM((n, rows, model), keep),
            pltpu.VMEM((n, rows, model), BF),
            pltpu.VMEM((pieces, DK, DV), BF),
            pltpu.VMEM((pieces, DK, DV), BF),
            pltpu.VMEM((total, heads * DK), keep),
            pltpu.VMEM((total, heads * DV), BF),
        ]
        + scatter_scratch(n, rows, model)
        + chain_scratch(pieces)
        + [dma((6,))]
        + [dma((sems,))] * 4
        + [dma((1,)), dma((1,)), dma((3, n)), dma((4,)), dma((2,)), dma((3, n))],
        compiler_params=params(cid),
        name="mixer_back",
    )(fac, res, wo, wq, wk, wv, ws, q, k, v, sp, mx, prior, mlp_parts, decay, qfac, kfac, cos, sin, og_all, wd, gate_late, up_late)


def weights_kernel(chips, *refs):
    (
        two, og, og_late, hidden, gate_low, gate_late, up_low, up_late,
        one, res, swish_low, gated, value_low, qk_low,
        vec_two, gain, parts_h, raw_h, res_h, attn_h, mlp_h,
        down_o, gate_o, up_o, swish_o, mixer_o, value_o, query_o, key_o, back_o, outs_o, vec_out,
    ) = refs[:32]
    mlp = LineSums(
        chips, 1, chips - 2, ((two,), (og, og_late)),
        ((gate_low, gate_late), (up_low, up_late), (hidden,)), (0, 0, 1), refs[32:44],
    )
    mix = LineSums(
        chips, 0, chips - 1, ((one,), (res,)), ((swish_low,), (gated,), (value_low,), (qk_low,)),
        (0, 1, 0, 0), refs[44:56],
    )
    (
        turned, osem, grad, raw, res_grad, attn, mlp_out, back, outs, csem, dsem,
        vec, vec_near, vec_mid, vec_far, vs, vr, us, ur, parts, near, far, hold, lsem, ss, sr,
    ) = refs[56:]
    grad = grad if parts.shape[0] == 4 else near.at[0]
    scatter = Scatter(parts.shape[0], parts, near, far, hold, ss, sr)
    load = pltpu.make_async_copy(parts_h, parts, lsem.at[0])
    load.start()
    s, t = lax.axis_index("seq"), lax.axis_index("tp")
    span, tp = 2 * chips, vec_far.shape[0] + 1
    share = vec_mid.shape[1]
    ring = [((s + d) % span, t) for d in range(1, span)]
    cross = [(s, (t + d) % tp) for d in range(1, tp)]

    def part(who):
        return pl.ds(pl.multiple_of(who * share, share), share)

    greet(ring + cross)
    vec_first = [
        remote(vec.at[:, part((s + d) % span)], vec_near.at[d - 1], vs, vr, d - 1, ring[d - 1])
        for d in range(1, span)
    ]
    vec_last = [
        remote(vec_mid, vec_far.at[d - 1], us, ur, d - 1, cross[d - 1]) for d in range(1, tp)
    ]
    vec[...] = vec_two[...]
    for u in range(mix.units):
        if u < mlp.units:
            mlp.share(u)
        mix.share(u)

    half = mix.out.shape[2] // 2
    lo, hi = pl.ds(0, half), pl.ds(half, half)

    def put(pairs):
        copies = [pltpu.make_async_copy(a, b, osem.at[i]) for i, (a, b) in enumerate(pairs)]
        for copy in copies:
            copy.start()
        for copy in copies:
            copy.wait()

    def put_mlp(w):
        if w == 2:
            turned[...] = mlp.out[0].T
            put([(turned, down_o)])
        else:
            put([(mlp.out.at[0], (gate_o, up_o)[w])])

    def put_mix(w):
        if w == 1:
            turned[...] = mix.out[0].T
            put([(turned, mixer_o)])
        elif w == 3:
            put([(mix.out.at[0, :, lo], query_o), (mix.out.at[0, :, hi], key_o)])
        else:
            put([(mix.out.at[0], (swish_o, None, value_o)[w])])

    @pl.loop(0, mix.units)
    def _(u):
        for w in range(mix.units):

            @pl.when(u == w)
            def _(w=w):
                if w < mlp.units:
                    mlp.ready(w)

        @pl.when(u < mlp.units)
        def _():
            mlp.step(u, 0)

        @pl.when(u == 0)
        def _():
            load.wait()
            for i in range(1, scatter.n):
                scatter.send(i)

        for w in range(mix.units):

            @pl.when(u == w)
            def _(w=w):
                mix.ready(w)

        @pl.loop(0, chips - 1)
        def _(k):
            @pl.when((u < mlp.units) & (k > 0))
            def _():
                mlp.step(u, k)

            mix.step(u, k)

        @pl.when(u == 0)
        def _():
            chunk = raw.shape[0]

            scatter.relay()

            def write(at, cols, total):
                grad[at, cols] = total.astype(grad.dtype)

            scatter.finish(write)

            @pl.loop(0, parts.shape[1] // chunk)
            def _(c):
                here = pl.ds(pl.multiple_of(c * chunk, chunk), chunk)
                pairs = (raw_h, raw), (res_h, res_grad), (attn_h, attn), (mlp_h, mlp_out)
                ins = [
                    pltpu.make_async_copy(a.at[here], b, csem.at[i])
                    for i, (a, b) in enumerate(pairs)
                ]
                for copy in ins:
                    copy.start()
                for copy in ins:
                    copy.wait()
                value = raw[...].astype(F32)
                outs[...] = value + attn[...] + mlp_out[...]
                center, inv = row_stats(value)
                hat, given = center * inv, grad[here].astype(F32)
                vec[0:1] += jnp.sum(given * hat, 0, keepdims=True)
                vec[1:2] += jnp.sum(given, 0, keepdims=True)
                back[...] = res_grad[...] + norm_pull(given, hat, inv, gain[...])
                puts = [
                    pltpu.make_async_copy(a, b.at[here], dsem.at[i])
                    for i, (a, b) in enumerate(((back, back_o), (outs, outs_o)))
                ]
                for copy in puts:
                    copy.start()
                for copy in puts:
                    copy.wait()

            for copy in vec_first:
                copy.start()

        @pl.when(u == 1)
        def _():
            for copy in vec_first:
                copy.wait_recv()
            vec_mid[...] = vec[:, part(s)] + jnp.sum(vec_near[...], 0)
            for copy in vec_last:
                copy.start()

        @pl.when(u > 0)
        def _():
            mlp.finish(u - 1)
            mix.finish(u - 1)
            for w in range(mix.units - 1):

                @pl.when(u - 1 == w)
                def _(w=w):
                    put_mlp(w)
                    put_mix(w)

    mix.finish(mix.units - 1)
    put_mix(mix.units - 1)
    for copy in vec_last:
        copy.wait_recv()
    vec_out[...] = vec_mid[...] + jnp.sum(vec_far[...], 0)
    for copy in vec_first + vec_last:
        copy.wait_send()
    scatter.drain()
    mlp.drain()
    mix.drain()


def weight_sums(
    two, og, og_late, hidden, gate_low, gate_late, up_low, up_late, one, res, swish_low, gated, value_low,
    qk_low, vec_two, gain, grad, raw, res_grad, attn, mlp_out, cid,
):
    chips = lax.axis_size("seq") // 2
    tokens, model = one.shape
    width = gated.shape[1]
    mlp_tokens, mlp_width = hidden.shape
    keys = qk_low.shape[1] // 2
    cut = model // (2 * chips)
    dma = pltpu.SemaphoreType.DMA
    vmem = pl.BlockSpec(memory_space=pltpu.VMEM)
    hbm = pl.BlockSpec(memory_space=pl.ANY)
    shape = lambda *a: jax.ShapeDtypeStruct(a, F32)
    ring, cross = 2 * chips - 1, lax.axis_size("tp") - 1
    rows, share, chunk = raw.shape[0], model // (2 * chips), 32 if cross < 4 else 16
    part = lambda dtype: pltpu.VMEM((chunk, model), dtype)
    return pl.pallas_call(
        functools.partial(weights_kernel, chips),
        out_shape=(
            shape(mlp_width, cut),
            shape(cut, mlp_width),
            shape(cut, mlp_width),
            shape(cut, width),
            shape(width, cut),
            shape(cut, width),
            shape(cut, keys),
            shape(cut, keys),
            shape(rows, model),
            shape(rows, model),
            shape(8, share),
        ),
        in_specs=[hbm] * 14 + [vmem] * 2 + [hbm] * 5,
        out_specs=(hbm,) * 10 + (vmem,),
        scratch_shapes=line_scratch(chips, 3, 2, mlp_tokens, cut, mlp_width)
        + line_scratch(chips, 4, 2, tokens, cut, width)
        + [
            pltpu.VMEM((width, cut), F32),
            dma((8,)),
            pltpu.VMEM((rows, model) if cross < 4 else (16, 128), F32),
            part(BF),
            part(F32),
            part(F32),
            part(F32),
            part(F32),
            part(F32),
            dma((5,)),
            dma((2,)),
            pltpu.VMEM((8, model), F32),
            pltpu.VMEM((ring, 8, share), F32),
            pltpu.VMEM((8, share), F32),
            pltpu.VMEM((cross, 8, share), F32),
            dma((ring,)),
            dma((ring,)),
            dma((cross,)),
            dma((cross,)),
            pltpu.VMEM((cross + 1, rows, model), BF),
        ]
        + scatter_scratch(cross + 1, rows, model)
        + [
            dma((1,)),
            dma((max(10, cross),)),
            dma((max(10, cross),)),
        ],
        compiler_params=params(cid),
        name="weights",
    )(two, og, og_late, hidden, gate_low, gate_late, up_low, up_late, one, res, swish_low, gated, value_low,
      qk_low, vec_two, gain, grad, raw, res_grad, attn, mlp_out)


def shards(
    inputs,
    query_weight,
    key_weight,
    value_weight,
    swish_weight,
    output_weight,
    gate_weight,
    up_weight,
    down_weight,
    attn_gain,
    attn_bias,
    mlp_gain,
    mlp_bias,
    output_grad,
):
    _, rows, model = inputs.shape
    heads = query_weight.shape[1] // DK
    seqs, tps = lax.axis_size("seq"), lax.axis_size("tp")
    raw, cotangent = inputs[0], output_grad[0]
    row = lambda v: v.reshape(1, model)
    flat = lambda a: a.reshape(-1, model)

    half_width = DK // 2
    frequencies = np.power(
        np.float32(10000.0), -np.arange(half_width, dtype=np.float32) / np.float32(half_width)
    )[None]
    decays = 1.0 - np.exp2(-5.0 - np.arange(heads * tps))
    factors = np.stack([np.power(decays, rows), np.log(decays)]).astype(np.float32)

    (
        one_all, grad_all, query, key, value, swish_pre, mixed, prior, gated, attn_out,
        decay_mat, query_fac, key_fac, cosine, sine,
    ) = mixer(
        factors, raw, cotangent, key_weight, value_weight, query_weight, swish_weight,
        output_weight, row(attn_gain), row(attn_bias), frequencies, 0,
    )
    two_all, hidden, gate_low, upper_low, mlp_parts, res_grad, res_low, vectors, gate_pre, up_pre = mlp(
        raw, attn_out, cotangent, row(mlp_gain), row(mlp_bias), grad_all, gate_weight, up_weight,
        down_weight, 1,
    )
    (
        res_all, swish_low, value_low, qk_low, normed_one_grad, mlp_out, og_late, gate_late, up_late,
    ) = mixer_back(
        factors, res_low, output_weight, query_weight, key_weight, value_weight, swish_weight,
        query, key, value, swish_pre, mixed, prior, mlp_parts, decay_mat, query_fac, key_fac,
        cosine, sine, grad_all, down_weight, gate_pre, up_pre, 2,
    )
    (
        down_grad, gate_grad, up_grad, swish_grad, mixer_grad, value_grad, query_grad, key_grad,
        input_grad, outputs, vector_sums,
    ) = weight_sums(
        flat(two_all), flat(grad_all), og_late, hidden, gate_low, gate_late, upper_low, up_late,
        flat(one_all), flat(res_all), swish_low, gated, value_low, qk_low, vectors, row(attn_gain),
        normed_one_grad, raw, res_grad, attn_out, mlp_out, 3,
    )
    each = model // (seqs * tps)
    vector_sums = lax.dynamic_slice(vector_sums, (0, lax.axis_index("tp") * each), (4, each))
    return (
        outputs.astype(BF)[None],
        input_grad.astype(BF)[None],
        query_grad,
        key_grad,
        value_grad,
        swish_grad,
        mixer_grad,
        gate_grad,
        up_grad,
        down_grad,
        vector_sums[0],
        vector_sums[1],
        vector_sums[2],
        vector_sums[3],
    )


def solution(mesh):
    return jax.shard_map(
        shards,
        mesh=mesh,
        in_specs=(
            P("tp", "seq", None),
            P(None, "tp"),
            P(None, "tp"),
            P(None, "tp"),
            P(None, "tp"),
            P("tp", None),
            P(None, "tp"),
            P(None, "tp"),
            P("tp", None),
            P(),
            P(),
            P(),
            P(),
            P("tp", "seq", None),
        ),
        out_specs=(
            P("tp", "seq", None),
            P("tp", "seq", None),
            P("seq", "tp"),
            P("seq", "tp"),
            P("seq", "tp"),
            P("seq", "tp"),
            P("tp", "seq"),
            P("seq", "tp"),
            P("seq", "tp"),
            P("tp", "seq"),
            P(("seq", "tp")),
            P(("seq", "tp")),
            P(("seq", "tp")),
            P(("seq", "tp")),
        ),
        check_vma=False,
    )
```
